32 devices in a mesh: dp: 8 (over z, x), tensor: 4 (over y, core).
Axes of the slice: x: 2, y: 2, z: 4, core: 2. Of those that a mesh axis runs over, the one named last changes fastest.
Arguments:
- image_tokens: bfloat16 [16, 1024, 1536], P('dp', 'tensor'), may hold values from -6 to 6
- text_tokens: bfloat16 [16, 154, 1536], P('dp'), may hold values from -6 to 6
- condition: bfloat16 [16, 1536], P('dp'), may hold values from -6 to 6
- group_size: int32 [8], P('dp'), may hold values from 1 to 2, as said below
- image_modulation: bfloat16 [1536, 6, 1536], P('dp', None, 'tensor'), may hold values from -0.15625 to 0.15625
- image_attention_in: bfloat16 [1536, 3, 1536], P('dp', None, 'tensor'), may hold values from -0.15625 to 0.15625
- image_attention_out: bfloat16 [1536, 1536], P('tensor', 'dp'), may hold values from -1.25 to 1.25
- image_hidden_in: bfloat16 [1536, 6144], P('dp', 'tensor'), may hold values from -0.15625 to 0.15625
- image_hidden_out: bfloat16 [6144, 1536], P('tensor', 'dp'), may hold values from -0.078125 to 0.078125
- text_modulation: bfloat16 [1536, 6, 1536], P('dp', None, 'tensor'), may hold values from -0.15625 to 0.15625
- text_attention_in: bfloat16 [1536, 3, 1536], P('dp', None, 'tensor'), may hold values from -0.15625 to 0.15625
- text_attention_out: bfloat16 [1536, 1536], P('tensor', 'dp'), may hold values from -1.25 to 1.25
- text_hidden_in: bfloat16 [1536, 6144], P('dp', 'tensor'), may hold values from -0.15625 to 0.15625
- text_hidden_out: bfloat16 [6144, 1536], P('tensor', 'dp'), may hold values from -0.078125 to 0.078125
- image_cotangent: bfloat16 [16, 1024, 1536], P('dp', 'tensor'), may hold values from -6 to 6
- text_cotangent: bfloat16 [16, 154, 1536], P('dp'), may hold values from -6 to 6
Outputs:
- image_output: bfloat16 [16, 1024, 1536], P('dp', 'tensor')
- text_output: bfloat16 [16, 154, 1536], P('dp')
- image_gradient: float32 [16, 1024, 1536], P('dp', 'tensor')
- text_gradient: float32 [16, 154, 1536], P('dp')
- condition_gradient: float32 [16, 1536], P('dp')
- image_modulation_gradient: float32 [1536, 6, 1536], P('dp', None, 'tensor')
- image_attention_in_gradient: float32 [1536, 3, 1536], P('dp', None, 'tensor')
- image_attention_out_gradient: float32 [1536, 1536], P('tensor', 'dp')
- image_hidden_in_gradient: float32 [1536, 6144], P('dp', 'tensor')
- image_hidden_out_gradient: float32 [6144, 1536], P('tensor', 'dp')
- text_modulation_gradient: float32 [1536, 6, 1536], P('dp', None, 'tensor')
- text_attention_in_gradient: float32 [1536, 3, 1536], P('dp', None, 'tensor')
- text_attention_out_gradient: float32 [1536, 1536], P('tensor', 'dp')
- text_hidden_in_gradient: float32 [1536, 6144], P('dp', 'tensor')
- text_hidden_out_gradient: float32 [6144, 1536], P('tensor', 'dp')
The draws below stay inside these ranges and needn't reach their ends.
Inputs may be any that keep to these rules, and one draw needn't show every extreme that they name: `group_size`: each entry is the number of live sequences of that group; the entries sum to 13.
All inputs are finite; a program needn't handle non-finite values.
Results may differ from the reference program's by a relative error of at most 0.018.
The reference program's roundings to bfloat16 on the way count: a program that leaves them out, or rounds other values in their place, can miss the bound.
Values may be sent and summed in bfloat16 or wider, within the bound.
No kernel may reach another device: no remote copies, remote signals or barrier semaphores. Data moves between devices by JAX's collectives and lax.ppermute only.
A program may use at most 248 MiB of HBM per device.

```python
import jax
import jax.numpy as jnp
from jax import lax

D = 1536
HEADS = 24
HEAD = 64
FF = 6144
IMG = 1024
TXT = 154
SEQS = 13
SLOTS = 16


def draw_group_size(key, part):
    groups = SLOTS // 2
    order = jax.random.permutation(key, groups)
    return jnp.where(order < SEQS - groups, 2, 1).astype(jnp.int32)


def levels(rng, shape, cuts, least, largest):
    level, own = 1.0, jax.random.fold_in(rng, 6)
    for position, parts in cuts:
        draws = jnp.exp(jax.random.uniform(jax.random.fold_in(own, position), (parts,), jnp.float32, least / len(cuts), largest / len(cuts)))
        level = level * jnp.repeat(draws, shape[position] // parts).reshape([-1 if axis == position else 1 for axis in range(len(shape))])
    return level


def bell_draw(rng, extent, width, bound, shards=(), kind=jnp.bfloat16):
    level = levels(rng, extent, shards, -0.22, 0.18) if shards else 1.0
    result = jax.random.normal(rng, extent, jnp.float32) * width * level
    return jnp.minimum(jnp.maximum(result, -bound), bound).astype(kind)


def setup_inputs(seed: int = 0) -> dict:
    seeds = jax.random.split(jax.random.key(seed), 17)
    image_tokens = bell_draw(seeds[0], (SLOTS, IMG, D), 1.0, 6.0, ((0, 8), (1, 4)))
    text_tokens = bell_draw(seeds[1], (SLOTS, TXT, D), 1.0, 6.0, ((0, 8),))
    condition = bell_draw(seeds[2], (SLOTS, D), 1.0, 6.0, ((0, 8),))
    group_size = draw_group_size(jax.random.fold_in(seeds[16], 71), 0)
    image_modulation = bell_draw(seeds[4], (D, 6, D), D ** -0.5, 0.15625, ((0, 8), (2, 4)))
    image_attention_in = bell_draw(seeds[5], (D, 3, D), D ** -0.5, 0.15625, ((0, 8), (2, 4)))
    image_attention_out = bell_draw(seeds[6], (D, D), (max(D // 64, 1)) ** -0.5, 1.25, ((0, 4), (1, 8)))
    image_hidden_in = bell_draw(seeds[7], (D, FF), D ** -0.5, 0.15625, ((0, 8), (1, 4)))
    image_hidden_out = bell_draw(seeds[8], (FF, D), FF ** -0.5, 0.078125, ((0, 4), (1, 8)))
    text_modulation = bell_draw(seeds[9], (D, 6, D), D ** -0.5, 0.15625, ((0, 8), (2, 4)))
    text_attention_in = bell_draw(seeds[10], (D, 3, D), D ** -0.5, 0.15625, ((0, 8), (2, 4)))
    text_attention_out = bell_draw(seeds[11], (D, D), (max(D // 64, 1)) ** -0.5, 1.25, ((0, 4), (1, 8)))
    text_hidden_in = bell_draw(seeds[12], (D, FF), D ** -0.5, 0.15625, ((0, 8), (1, 4)))
    text_hidden_out = bell_draw(seeds[13], (FF, D), FF ** -0.5, 0.078125, ((0, 4), (1, 8)))
    image_cotangent = bell_draw(seeds[14], (SLOTS, IMG, D), 1.0, 6.0, ((0, 8), (1, 4)))
    text_cotangent = bell_draw(seeds[15], (SLOTS, TXT, D), 1.0, 6.0, ((0, 8),))
    return {"image_tokens": image_tokens, "text_tokens": text_tokens, "condition": condition, "group_size": group_size, "image_modulation": image_modulation, "image_attention_in": image_attention_in, "image_attention_out": image_attention_out, "image_hidden_in": image_hidden_in, "image_hidden_out": image_hidden_out, "text_modulation": text_modulation, "text_attention_in": text_attention_in, "text_attention_out": text_attention_out, "text_hidden_in": text_hidden_in, "text_hidden_out": text_hidden_out, "image_cotangent": image_cotangent, "text_cotangent": text_cotangent}


@jax.custom_vjp
def low(v):
    return lax.optimization_barrier(v.astype(jnp.bfloat16)).astype(jnp.float32)

@jax.custom_vjp
def low_back(v):
    return v

def low_keep(v):
    return (low(v), None)

def low_pass(kept, grad):
    return (grad,)

def back_keep(v):
    return (v, None)

def back_low(kept, grad):
    return (low(grad),)
low.defvjp(low_keep, low_pass)
low_back.defvjp(back_keep, back_low)

def layer_norm(values):
    center = values - lax.optimization_barrier(jnp.mean(values, axis=-1, keepdims=True))
    return center * lax.rsqrt(lax.optimization_barrier(jnp.mean(center * center, axis=-1, keepdims=True)) + 1e-06)

def product(left, right):
    return jnp.dot(left, right, precision=lax.Precision.HIGHEST)

def joint_attention(queries, key_rows, value_rows):
    scores = jnp.einsum('qhe,khe->hqk', queries, key_rows, precision=lax.Precision.HIGHEST)
    scores = low_back(scores * HEAD ** (-0.5))
    layer_weights = jax.nn.softmax(scores, axis=-1)
    mixed = jnp.einsum('hqk,khe->qhe', low(layer_weights), value_rows, precision=lax.Precision.HIGHEST)
    return low(low_back(mixed.reshape(-1, HEADS * HEAD)))

def block(params, image_in, text_in, cond_in):
    activated = low(jax.nn.silu(cond_in))
    streams = (image_in, text_in)
    modulations = []
    packs = []
    for stream in range(2):
        modulation = low_back(product(activated, params[5 * stream].reshape(D, 6 * D))).reshape(6, D)
        first_in = low(layer_norm(streams[stream]) * (1.0 + modulation[1]) + modulation[0])
        packed = low(low_back(product(first_in, params[5 * stream + 1].reshape(D, 3 * D))))
        modulations.append(modulation)
        packs.append(packed.reshape(-1, 3, HEADS, HEAD))
    together = jnp.concatenate([packs[1], packs[0]], axis=0)
    mixed = joint_attention(together[:, 0], together[:, 1], together[:, 2])
    pieces = (mixed[TXT:], mixed[:TXT])
    results = []
    for stream in range(2):
        modulation = modulations[stream]
        branch = low_back(product(pieces[stream], params[5 * stream + 2]))
        middle = streams[stream] + modulation[2] * branch
        second_in = low(layer_norm(middle) * (1.0 + modulation[4]) + modulation[3])
        hidden = low_back(product(second_in, params[5 * stream + 3]))
        active_rows = low(jax.nn.gelu(hidden, approximate=True))
        branch_two = low_back(product(active_rows, params[5 * stream + 4]))
        results.append(middle + modulation[5] * branch_two)
    return (results[0], results[1])

def reference(image_tokens, text_tokens, condition, group_size, image_modulation, image_attention_in, image_attention_out, image_hidden_in, image_hidden_out, text_modulation, text_attention_in, text_attention_out, text_hidden_in, text_hidden_out, image_cotangent, text_cotangent):
    params = tuple((weight.astype(jnp.float32) for weight in (image_modulation, image_attention_in, image_attention_out, image_hidden_in, image_hidden_out, text_modulation, text_attention_in, text_attention_out, text_hidden_in, text_hidden_out)))
    alive = (jnp.arange(2).astype(jnp.int32)[None, :] < group_size[:, None]).reshape(-1).astype(jnp.float32)

    def one_slot(totals, item):
        image_in, text_in, cond_in, image_back, text_back, alive_one = item
        outputs, pull = jax.vjp(block, params, image_in.astype(jnp.float32), text_in.astype(jnp.float32), cond_in.astype(jnp.float32))
        grads = pull((image_back.astype(jnp.float32) * alive_one, text_back.astype(jnp.float32) * alive_one))
        totals = tuple((total + grad for total, grad in zip(totals, grads[0])))
        return (totals, (outputs[0] * alive_one, outputs[1] * alive_one, grads[1], grads[2], grads[3]))
    initial = tuple((jnp.zeros_like(weight) for weight in params))
    totals, collected = lax.scan(one_slot, initial, (image_tokens, text_tokens, condition, image_cotangent, text_cotangent, alive))
    image_out, text_out, image_grad, text_grad, cond_grad = collected
    return (image_out.astype(jnp.bfloat16), text_out.astype(jnp.bfloat16), image_grad, text_grad, cond_grad, totals[0], totals[1], totals[2], totals[3], totals[4], totals[5], totals[6], totals[7], totals[8], totals[9])
```

```python
import functools

import jax
import jax.numpy as jnp
from jax import lax
from jax.experimental import pallas as pl
from jax.experimental.pallas import tpu as pltpu
from jax.sharding import PartitionSpec as P

HEAD = 64
LANES = 128
F32 = jnp.float32
BF16 = jnp.bfloat16


def norm_rows(values):
    center = values - jnp.mean(values, axis=-1, keepdims=True)
    inverse = lax.rsqrt(jnp.mean(center * center, axis=-1, keepdims=True) + 1e-06)
    return (center * inverse, inverse)


def norm_back(upstream, normed, inverse):
    first = jnp.mean(upstream, axis=-1, keepdims=True)
    second = jnp.mean(upstream * normed, axis=-1, keepdims=True)
    return inverse * (upstream - first - normed * second)


def gelu_tanh(values):
    return jax.nn.gelu(values, approximate=True)


def spread(vector):
    return vector[:, None, :]


def dot(left, right, left_dim, right_dim):
    return lax.dot_general(
        left, right, (((left_dim,), (right_dim,)), ((), ())), preferred_element_type=F32
    )


def swap(value, bit, size, axis="tensor"):
    return lax.ppermute(value, axis, [(i, i ^ bit) for i in range(size)])


def bits_of(size):
    bits = []
    bit = 1
    while bit < size:
        bits.append(bit)
        bit *= 2
    return bits


def gather_pieces(value, size, axis="tensor"):
    have = {0: value}
    for bit in reversed(bits_of(size)):
        have.update({k ^ bit: swap(v, bit, size, axis) for k, v in list(have.items())})
    return [have[k] for k in range(size)]


def exchange(blocks, size, axis):
    return [blocks[0]] + [swap(blocks[k], k, size, axis) for k in range(1, size)]


def sum_all(value, size, axis):
    for bit in bits_of(size):
        value = value + swap(value, bit, size, axis)
    return value


def scatter_sum(make_piece, size):
    have = {k: make_piece(k) for k in reversed(range(size))}
    for bit in bits_of(size):
        kept = {}
        for k in sorted(have, reverse=True):
            if not k & bit:
                other = swap(have[k ^ bit].astype(BF16), bit, size)
                kept[k] = have[k].astype(F32) + other.astype(F32)
        have = kept
    return have[0]


def ring_of(count):
    return list(range(0, count, 2)) + list(range(1, count, 2))[::-1]


def ring_member(place, count):
    place = lax.rem(place + count, count)
    return jnp.where(place < (count + 1) // 2, 2 * place, 2 * (count - 1 - place) + 1)


def ring_place(member, count):
    return jnp.where(member % 2 == 0, member // 2, count - 1 - member // 2)


def ring_step(value, way, count):
    ring = ring_of(count)
    hops = [(ring[i], ring[(i + way) % count]) for i in range(count)]
    return lax.ppermute(value, "dp", hops)


def ring_gather(block, count):
    share, wide = block.shape
    half = wide // 2 // LANES * LANES
    place = ring_place(lax.axis_index("dp"), count)
    whole = jnp.zeros((count * share, wide), block.dtype)

    def put(whole, value, offset, column):
        row = ring_member(place + offset, count) * share
        return lax.dynamic_update_slice(whole, value, (row, column))

    whole = put(whole, block, 0, 0)
    behind = ahead = block
    for hop in range(1, count // 2):
        behind = ring_step(behind, 1, count)
        ahead = ring_step(ahead, -1, count)
        whole = put(put(whole, behind, -hop, 0), ahead, hop, 0)
    behind = ring_step(behind[:, :half], 1, count)
    ahead = ring_step(ahead[:, half:], -1, count)
    return put(put(whole, behind, -(count // 2), 0), ahead, count // 2, half)


def ring_scatter(grad, count):
    wide = grad.shape[1]
    share = grad.shape[0] // count
    half = wide // 2 // LANES * LANES
    place = ring_place(lax.axis_index("dp"), count)

    def own(offset):
        row = ring_member(place + offset, count) * share
        return lax.dynamic_slice_in_dim(grad, row, share, 0).astype(F32)

    far = own(count // 2).astype(BF16)
    behind = ring_step(far[:, :half], 1, count)
    ahead = ring_step(far[:, half:], -1, count)
    behind, ahead = yield behind, ahead
    behind = jnp.pad(behind.astype(F32), ((0, 0), (0, wide - half)))
    ahead = jnp.pad(ahead.astype(F32), ((0, 0), (half, 0)))
    for hop in range(count // 2 - 1, 0, -1):
        behind = ring_step((own(hop) + behind).astype(BF16), 1, count)
        ahead = ring_step((own(-hop) + ahead).astype(BF16), -1, count)
        behind, ahead = yield behind, ahead
        behind, ahead = behind.astype(F32), ahead.astype(F32)
    yield own(0) + behind + ahead


def text_sum(value, size):
    for bit in bits_of(size):
        if bit == 1:
            value = value + swap(value, bit, size)
        else:
            value = lax.reduce_precision(value, 8, 7)
            value = value + swap(value.astype(BF16), bit, size).astype(F32)
    return value


def lane_mask(half, shape):
    lane = lax.broadcasted_iota(jnp.int32, shape, 1)
    return (lane >= HEAD) if half else (lane < HEAD)


def pick(value, half):
    return jnp.where(lane_mask(half, value.shape), value, jnp.zeros_like(value))


def load_rows(refs, store):
    start = 0
    for ref in refs:
        rows = ref.shape[1]
        store[start : start + rows, :] = ref[0]
        start += rows


def attend_kernel(count, *refs):
    queries, keys, values = refs[:count], refs[count : 2 * count], refs[2 * count : 3 * count]
    outs = refs[3 * count : 4 * count]
    sums = refs[4 * count : 5 * count]
    key_all, value_all = refs[5 * count :]
    load_rows(keys, key_all)
    load_rows(values, value_all)
    for index in range(count):
        query = queries[index][0] * jnp.asarray(HEAD**-0.5, BF16)
        halves = []
        for half in range(2):
            scores = dot(key_all[...], pick(query, half), 1, 1)
            highest = jnp.max(scores, axis=0, keepdims=True)
            weights = jnp.exp(scores - highest)
            total = jnp.sum(weights, axis=0, keepdims=True)
            weights = (weights * (1.0 / total)).astype(BF16)
            mixed = dot(value_all[...], weights, 0, 0)
            halves.append(mixed[half * HEAD : (half + 1) * HEAD])
            sums[index][0, 0, half : half + 1, :] = highest + jnp.log(total)
        outs[index][0] = jnp.concatenate(halves, axis=0).T.astype(BF16)


def attend_back_kernel(count, groups, *refs):
    queries, keys, values = refs[:count], refs[count : 2 * count], refs[2 * count : 3 * count]
    upstreams = refs[3 * count : 4 * count]
    sums = refs[4 * count : 5 * count]
    outs = refs[5 * count : 6 * count]
    key_all, value_all, key_grad, value_grad = refs[6 * count :]
    load_rows(keys, key_all)
    load_rows(values, value_all)
    pair = pl.program_id(1)
    scale = jnp.asarray(HEAD**-0.5, BF16)
    query_lanes = pl.ds(pl.multiple_of(pair * LANES, LANES), LANES)
    key_lanes = pl.ds(pl.multiple_of((groups + pair) * LANES, LANES), LANES)
    value_lanes = pl.ds(pl.multiple_of((2 * groups + pair) * LANES, LANES), LANES)
    for index in range(count):
        query = queries[index][0] * scale
        upstream = upstreams[index][0]
        halves = []
        for half in range(2):
            query_half = pick(query, half)
            upstream_half = pick(upstream, half)
            scores = dot(key_all[...], query_half, 1, 1)
            weights = jnp.exp(scores - sums[index][0, 0, half : half + 1, :])
            along = dot(value_all[...], upstream_half, 1, 1)
            value_part = dot(weights.astype(BF16), upstream_half, 1, 0)
            product = weights * along
            score_grad = (product - weights * jnp.sum(product, axis=0, keepdims=True)).astype(BF16)
            key_part = dot(score_grad, query_half, 1, 0)
            if index == 0 and half == 0:
                value_grad[...] = value_part
                key_grad[...] = key_part
            else:
                value_grad[...] += value_part
                key_grad[...] += key_part
            mixed = dot(key_all[...], score_grad, 0, 0)
            halves.append(mixed[half * HEAD : (half + 1) * HEAD])
        query_grad = jnp.concatenate(halves, axis=0).T * HEAD**-0.5
        outs[index][0, :, query_lanes] = query_grad.astype(BF16)
    start = 0
    for index in range(count):
        rows = outs[index].shape[1]
        outs[index][0, :, key_lanes] = key_grad[start : start + rows, :].astype(BF16)
        outs[index][0, :, value_lanes] = value_grad[start : start + rows, :].astype(BF16)
        start += rows


def lane_blocks(parts, offset):
    return [
        pl.BlockSpec((1, part.shape[1], LANES), lambda s, p, o=offset: (s, 0, o + p))
        for part in parts
    ]


def widen(part, copies):
    slots, rows, width = part.shape
    width = width // copies
    extra = -width % LANES
    if not extra:
        return part
    part = jnp.pad(part.reshape(slots, rows, copies, width), ((0, 0), (0, 0), (0, 0), (0, extra)))
    return part.reshape(slots, rows, copies * (width + extra))


def narrow(part, copies, width):
    slots, rows, wide = part.shape
    wide = wide // copies
    if wide == width:
        return part
    return part.reshape(slots, rows, copies, wide)[..., :width].reshape(slots, rows, -1)


def attention_cost(slots, rows, width, products):
    return pl.CostEstimate(
        flops=products * 8 * slots * rows * rows * width,
        transcendentals=slots * rows * rows * (width // HEAD),
        bytes_accessed=slots * rows * width * 2 * (4 + 3 * (products > 2)),
    )


def attend(parts):
    slots = parts[0].shape[0]
    width = parts[0].shape[2] // 3
    parts = [widen(part, 3) for part in parts]
    count = len(parts)
    wide = parts[0].shape[2] // 3
    groups = wide // LANES
    total = sum(part.shape[1] for part in parts)
    outs = pl.pallas_call(
        functools.partial(attend_kernel, count),
        grid=(slots, groups),
        in_specs=lane_blocks(parts, 0) + lane_blocks(parts, groups) + lane_blocks(parts, 2 * groups),
        out_specs=lane_blocks(parts, 0)
        + [
            pl.BlockSpec((1, 1, 2, part.shape[1]), lambda s, p: (s, p, 0, 0)) for part in parts
        ],
        out_shape=[jax.ShapeDtypeStruct((slots, part.shape[1], wide), BF16) for part in parts]
        + [jax.ShapeDtypeStruct((slots, groups, 2, part.shape[1]), F32) for part in parts],
        scratch_shapes=[pltpu.VMEM((total, LANES), BF16)] * 2,
        compiler_params=pltpu.CompilerParams(vmem_limit_bytes=48 * 1024 * 1024),
        cost_estimate=attention_cost(slots, total, wide, 2),
        name="attend",
    )(*parts, *parts, *parts)
    return [narrow(out, 1, width) for out in outs[:count]], outs[count:]


def attend_back(parts, upstreams, sums):
    slots = parts[0].shape[0]
    width = parts[0].shape[2] // 3
    parts = [widen(part, 3) for part in parts]
    upstreams = [widen(part, 1) for part in upstreams]
    count = len(parts)
    wide = parts[0].shape[2] // 3
    groups = wide // LANES
    total = sum(part.shape[1] for part in parts)
    outs = pl.pallas_call(
        functools.partial(attend_back_kernel, count, groups),
        grid=(slots, groups),
        in_specs=lane_blocks(parts, 0)
        + lane_blocks(parts, groups)
        + lane_blocks(parts, 2 * groups)
        + lane_blocks(upstreams, 0)
        + [
            pl.BlockSpec((1, 1, 2, part.shape[1]), lambda s, p: (s, p, 0, 0)) for part in parts
        ],
        out_specs=[
            pl.BlockSpec((1, part.shape[1], 3 * wide), lambda s, p: (s, 0, 0)) for part in parts
        ],
        out_shape=[jax.ShapeDtypeStruct((slots, part.shape[1], 3 * wide), BF16) for part in parts],
        scratch_shapes=[pltpu.VMEM((total, LANES), BF16)] * 2 + [pltpu.VMEM((total, LANES), F32)] * 2,
        compiler_params=pltpu.CompilerParams(vmem_limit_bytes=48 * 1024 * 1024),
        cost_estimate=attention_cost(slots, total, wide, 5),
        name="attend_back",
    )(*parts, *parts, *parts, *upstreams, *sums)
    return [narrow(out, 3, width) for out in outs]


def rows_kernel(count, *refs):
    lefts, rights, out = refs[:count], refs[count : 2 * count], refs[-1]
    total = None
    for left, right in zip(lefts, rights):
        for slot in range(left.shape[0]):
            part = dot(left[slot], right[slot], 0, 0)
            total = part if total is None else total + part
    out[...] = total.astype(BF16)


def weight_grad(pairs):
    joined = None
    rows = pairs[0][0][0].shape[-1]
    wide = sum(rights[0].shape[-1] for _, rights in pairs)
    start = 0
    for lefts, rights in pairs:
        part = rights[0].shape[-1]
        if part % LANES or start % part:
            return jnp.concatenate([plain_grad(*pair) for pair in pairs], axis=1)
        count = len(lefts)
        step = 256
        length = sum(left.shape[0] * left.shape[1] for left in lefts)
        ins = [
            pl.BlockSpec((left.shape[0], left.shape[1], step), lambda i: (0, 0, i))
            for left in lefts
        ] + [
            pl.BlockSpec(right.shape, lambda i: (0, 0, 0), pipeline_mode=pl.Buffered(1))
            for right in rights
        ]
        operands = (*lefts, *rights)
        if joined is not None:
            ins.append(pl.BlockSpec(memory_space=pl.ANY))
            operands += (joined,)
        joined = pl.pallas_call(
            functools.partial(rows_kernel, count),
            grid=(rows // step,),
            in_specs=ins,
            out_specs=pl.BlockSpec((step, part), lambda i, c=start // part: (i, c)),
            out_shape=jax.ShapeDtypeStruct((rows, wide), BF16),
            input_output_aliases={} if joined is None else {2 * count: 0},
            compiler_params=pltpu.CompilerParams(vmem_limit_bytes=48 * 1024 * 1024),
            cost_estimate=pl.CostEstimate(
                flops=2 * length * rows * part,
                transcendentals=0,
                bytes_accessed=2 * (length * (rows + part) + rows * part),
            ),
            name="weight_grad",
        )(*operands)
        start += part
    return joined


def plain_grad(lefts, rights):
    left = jnp.concatenate([v.reshape(-1, v.shape[-1]) for v in lefts], axis=0)
    right = jnp.concatenate([v.reshape(-1, v.shape[-1]) for v in rights], axis=0)
    return dot(left, right, 0, 0).astype(BF16)


def on_device(
    group_count,
    tensor_size,
    image_tokens,
    text_tokens,
    condition,
    group_size,
    image_modulation,
    image_attention_in,
    image_attention_out,
    image_hidden_in,
    image_hidden_out,
    text_modulation,
    text_attention_in,
    text_attention_out,
    text_hidden_in,
    text_hidden_out,
    image_cotangent,
    text_cotangent,
):
    size = tensor_size
    slots, image_length, model = image_tokens.shape
    text_length = text_tokens.shape[1]
    share, _, width = image_attention_in.shape
    units = image_hidden_in.shape[1]
    tensor_rank = lax.axis_index("tensor")
    group_rank = lax.axis_index("dp")

    def gathered(*blocks):
        joined = blocks[0] if len(blocks) == 1 else jnp.concatenate(blocks, axis=1)
        return lax.all_gather(joined, "dp", axis=0, tiled=True)

    packed_in = gathered(
        image_attention_in.reshape(share, 3 * width), text_attention_in.reshape(share, 3 * width)
    )
    packed_mid = gathered(image_attention_out.T, text_attention_out.T, image_hidden_in)
    image_down = gathered(image_hidden_out.T)
    weight_in = (packed_in[:, : 3 * width], packed_in[:, 3 * width :])
    weight_out = (packed_mid[:, :width], packed_mid[:, width : 2 * width])

    alive = (jnp.arange(slots) < group_size[0]).astype(F32)[:, None, None]
    cond_full = condition.astype(F32)
    group_order = group_rank ^ jnp.arange(group_count)
    activated_low = jax.nn.silu(cond_full).astype(BF16)
    activated_blocks = [
        lax.dynamic_slice_in_dim(activated_low, group_order[k] * share, share, 1)
        for k in range(group_count)
    ]
    activated_own = jnp.concatenate(exchange(activated_blocks, group_count, "dp"), axis=0)
    all_slots = activated_own.shape[0]
    mod_parts = jnp.concatenate(
        [
            dot(activated_own, image_modulation.reshape(share, 6 * width), 1, 0),
            dot(activated_own, text_modulation.reshape(share, 6 * width), 1, 0),
        ],
        axis=1,
    ).reshape(group_count, slots, 12 * width)
    mod_own = sum(exchange([mod_parts[k] for k in range(group_count)], group_count, "dp"))
    modulations = lax.all_gather(
        mod_own.reshape(slots, 2, 6, width), "tensor", axis=3, tiled=True
    )
    mods = (modulations[:, 0], modulations[:, 1])

    tokens = (image_tokens.astype(F32), text_tokens.astype(F32))
    outgoing = (image_cotangent.astype(F32) * alive, text_cotangent.astype(F32) * alive)

    def image_rows(values):
        return gather_pieces(values.astype(BF16), size)

    def text_rows(values):
        return [values.astype(BF16)]

    collect = (image_rows, text_rows)

    def flat(values):
        return values.reshape(-1, values.shape[-1])

    def apply(pieces, weight, weight_dim, low):
        return [
            dot(flat(piece), weight, 1, weight_dim)
            .astype(BF16 if low else F32)
            .reshape(slots, piece.shape[1], -1)
            for piece in pieces
        ]

    def reduced(stream, pieces, weight, weight_dim):
        if stream == 1:
            return text_sum(
                dot(flat(pieces[0]), weight, 1, weight_dim).reshape(slots, text_length, model), size
            )

        def make_piece(k):
            return dot(flat(pieces[k]), weight, 1, weight_dim).reshape(slots, image_length, model)

        return scatter_sum(make_piece, size)

    first_saved = []
    packed = []
    for stream in range(2):
        mod = mods[stream]
        normed, inverse = norm_rows(tokens[stream])
        first_in = normed * (1.0 + spread(mod[:, 1])) + spread(mod[:, 0])
        pieces = collect[stream](first_in)
        packed.append(apply(pieces, weight_in[stream], 0, True))
        first_saved.append((normed, inverse, pieces))
    parts = packed[0] + packed[1]
    down_pieces = [
        collect[stream](outgoing[stream] * spread(mods[stream][:, 5])) for stream in range(2)
    ]
    text_mlp_own = jnp.concatenate([text_hidden_in, text_hidden_out.T], axis=1)
    parts, down_pieces, text_mlp_own = lax.optimization_barrier((parts, down_pieces, text_mlp_own))
    packed_text = ring_gather(text_mlp_own, group_count)
    weight_up = (packed_mid[:, 2 * width :], packed_text[:, :units])
    weight_down = (image_down, packed_text[:, units:])
    attended, sums = attend(parts)
    attended_parts = (attended[:-1], attended[-1:])
    outputs = []
    second_saved = []
    for stream in range(2):
        mod = mods[stream]
        branch = reduced(stream, attended_parts[stream], weight_out[stream], 1)
        middle = tokens[stream] + spread(mod[:, 2]) * branch
        normed_two, inverse_two = norm_rows(middle)
        second_in = normed_two * (1.0 + spread(mod[:, 4])) + spread(mod[:, 3])
        pieces = collect[stream](second_in)
        hidden = apply(pieces, weight_up[stream], 0, False)
        active = [gelu_tanh(piece).astype(BF16) for piece in hidden]
        branch_two = reduced(stream, active, weight_down[stream], 1)
        result = middle + spread(mod[:, 5]) * branch_two
        outputs.append((result * alive).astype(BF16))
        second_saved.append((branch, normed_two, inverse_two, pieces, hidden, active, branch_two))

    def scattered(grad):
        return lax.psum_scatter(grad, "dp", scatter_dimension=0, tiled=True).astype(F32)

    mlp_grads = []
    middle_grads = []
    stats = []
    upstreams = []
    out_pairs = []
    for stream in range(2):
        mod = mods[stream]
        branch, normed_two, inverse_two, pieces, hidden, active, branch_two = second_saved[stream]
        gate_two_grad = jnp.sum(outgoing[stream] * branch_two, axis=1)
        active_grad = apply(down_pieces[stream], weight_down[stream], 0, False)
        hidden_grad = [
            jax.vjp(gelu_tanh, value)[1](grad)[0].astype(BF16)
            for value, grad in zip(hidden, active_grad)
        ]
        mlp_grads.append(weight_grad([(down_pieces[stream], active), (pieces, hidden_grad)]))
        second_grad = reduced(stream, hidden_grad, weight_up[stream], 1)
        shift_two_grad = jnp.sum(second_grad, axis=1)
        scale_two_grad = jnp.sum(second_grad * normed_two, axis=1)
        middle_grad = outgoing[stream] + norm_back(
            second_grad * (1.0 + spread(mod[:, 4])), normed_two, inverse_two
        )
        gate_one_grad = jnp.sum(middle_grad * branch, axis=1)
        branch_grad = collect[stream](middle_grad * spread(mod[:, 2]))
        out_pairs.append((branch_grad, attended_parts[stream]))
        upstreams.extend(apply(branch_grad, weight_out[stream], 0, True))
        middle_grads.append(middle_grad)
        stats.append((gate_one_grad, shift_two_grad, scale_two_grad, gate_two_grad))
    image_mlp = scattered(mlp_grads[0])
    text_grad, upstreams = lax.optimization_barrier((mlp_grads[1], upstreams))
    text_ring = ring_scatter(text_grad, group_count)
    text_hop = next(text_ring)
    packed_grads = attend_back(parts, upstreams, sums)
    packed_grads, text_hop = lax.optimization_barrier((packed_grads, text_hop))
    text_hop = text_ring.send(text_hop)
    late_grads, image_mlp = lax.optimization_barrier((packed_grads, image_mlp))
    packed_grads = (packed_grads[:-1], packed_grads[-1:])
    late_grads = (late_grads[:-1], late_grads[-1:])
    in_pairs = [(first_saved[stream][2], late_grads[stream]) for stream in range(2)]
    attention_grad = weight_grad(in_pairs + out_pairs)
    for _ in range(group_count // 2 - 3):
        attention_grad, text_hop = lax.optimization_barrier((attention_grad, text_hop))
        text_hop = text_ring.send(text_hop)
    attention_sum = scattered(attention_grad)
    input_grads = [None, None]
    mod_grads = [None, None]
    for stream in (1, 0):
        mod = mods[stream]
        normed, inverse, pieces = first_saved[stream]
        gate_one_grad, shift_two_grad, scale_two_grad, gate_two_grad = stats[stream]
        first_grad = reduced(stream, packed_grads[stream], weight_in[stream], 1)
        first_grad, text_hop = lax.optimization_barrier((first_grad, text_hop))
        text_hop = text_ring.send(text_hop)
        shift_one_grad = jnp.sum(first_grad, axis=1)
        scale_one_grad = jnp.sum(first_grad * normed, axis=1)
        input_grads[stream] = middle_grads[stream] + norm_back(
            first_grad * (1.0 + spread(mod[:, 1])), normed, inverse
        )
        mod_grads[stream] = jnp.stack(
            [
                shift_one_grad,
                scale_one_grad,
                gate_one_grad,
                shift_two_grad,
                scale_two_grad,
                gate_two_grad,
            ],
            axis=1,
        )
    text_mlp = text_hop

    image_share = sum(
        exchange(
            [
                lax.dynamic_slice_in_dim(mod_grads[0], (tensor_rank ^ k) * width, width, 2)
                for k in range(size)
            ],
            size,
            "tensor",
        )
    )
    text_share = lax.dynamic_slice_in_dim(mod_grads[1], tensor_rank * width, width, 2)
    share_low = jnp.stack([image_share, text_share], axis=1).astype(BF16)
    share_all = jnp.concatenate(gather_pieces(share_low, group_count, "dp"), axis=0)
    image_all = share_all[:, 0].reshape(all_slots, 6 * width)
    text_all = share_all[:, 1].reshape(all_slots, 6 * width)
    image_ada = dot(activated_own, image_all, 0, 0).reshape(share, 6, width)
    text_ada = dot(activated_own, text_all, 0, 0).reshape(share, 6, width)
    activated_part = dot(image_all, image_modulation.reshape(share, 6 * width), 1, 1) + dot(
        text_all, text_modulation.reshape(share, 6 * width), 1, 1
    )
    activated_part = sum_all(activated_part, size, "tensor").reshape(group_count, slots, share)
    activated_rows = jnp.stack(
        exchange([activated_part[k] for k in range(group_count)], group_count, "dp")
    )
    activated_grad = jnp.concatenate(
        [
            lax.dynamic_index_in_dim(activated_rows, group_order[k], 0, keepdims=False)
            for k in range(group_count)
        ],
        axis=1,
    )
    condition_gradient = jax.vjp(jax.nn.silu, cond_full)[1](activated_grad)[0]

    return (
        outputs[0],
        outputs[1],
        input_grads[0],
        input_grads[1],
        condition_gradient,
        image_ada,
        attention_sum[:, : 3 * width].reshape(share, 3, width),
        attention_sum[:, 6 * width : 7 * width].T,
        image_mlp[:, units:],
        image_mlp[:, :units].T,
        text_ada,
        attention_sum[:, 3 * width : 6 * width].reshape(share, 3, width),
        attention_sum[:, 7 * width :].T,
        text_mlp[:, units:],
        text_mlp[:, :units].T,
    )


def solution(mesh):
    image = P("dp", "tensor", None)
    text = P("dp", None, None)
    columns = P("dp", None, "tensor")
    rows = P("tensor", "dp")
    plain = P("dp", "tensor")
    weights = (columns, columns, rows, plain, rows)
    return jax.shard_map(
        functools.partial(on_device, mesh.shape["dp"], mesh.shape["tensor"]),
        mesh=mesh,
        in_specs=(image, text, P("dp", None), P("dp")) + weights + weights + (image, text),
        out_specs=(image, text, image, text, P("dp", None)) + weights + weights,
        check_vma=False,
    )
```

```python
import functools

import jax
import jax.numpy as jnp
from jax import lax
from jax.experimental import pallas as pl
from jax.experimental.pallas import tpu as pltpu
from jax.sharding import PartitionSpec as P

HEAD = 64
LANES = 128
F32 = jnp.float32
BF16 = jnp.bfloat16


def norm_rows(values):
    center = values - jnp.mean(values, axis=-1, keepdims=True)
    inverse = lax.rsqrt(jnp.mean(center * center, axis=-1, keepdims=True) + 1e-06)
    return (center * inverse, inverse)


def norm_back(upstream, normed, inverse):
    first = jnp.mean(upstream, axis=-1, keepdims=True)
    second = jnp.mean(upstream * normed, axis=-1, keepdims=True)
    return inverse * (upstream - first - normed * second)


def gelu_tanh(values):
    return jax.nn.gelu(values, approximate=True)


def spread(vector):
    return vector[:, None, :]


def dot(left, right, left_dim, right_dim):
    return lax.dot_general(
        left, right, (((left_dim,), (right_dim,)), ((), ())), preferred_element_type=F32
    )


def swap(value, bit, size, axis="tensor"):
    return lax.ppermute(value, axis, [(i, i ^ bit) for i in range(size)])


def bits_of(size):
    bits = []
    bit = 1
    while bit < size:
        bits.append(bit)
        bit *= 2
    return bits


def gather_pieces(value, size, axis="tensor"):
    have = {0: value}
    for bit in reversed(bits_of(size)):
        have.update({k ^ bit: swap(v, bit, size, axis) for k, v in list(have.items())})
    return [have[k] for k in range(size)]


def gather_stack(value, size, axis):
    value = value[None]
    for bit in bits_of(size):
        value = jnp.concatenate([value, swap(value, bit, size, axis)], axis=0)
    return value


def scatter_stack(value, size, axis):
    for bit in reversed(bits_of(size)):
        value = value[:bit] + swap(value[bit:], bit, size, axis)
    return value[0]


def sum_all(value, size, axis):
    for bit in bits_of(size):
        value = value + swap(value, bit, size, axis)
    return value


def scatter_sum(pieces, size):
    have = dict(enumerate(pieces))
    for bit in bits_of(size):
        kept = {}
        for k in sorted(have, reverse=True):
            if not k & bit:
                other = swap(have[k ^ bit].astype(BF16), bit, size)
                kept[k] = have[k].astype(F32) + other.astype(F32)
        have = kept
    return have[0]


def after(values, *others):
    return lax.optimization_barrier((values, others))[0]


def ring_of(count):
    return list(range(0, count, 2)) + list(range(1, count, 2))[::-1]


def ring_member(place, count):
    place = lax.rem(place + count, count)
    return jnp.where(place < (count + 1) // 2, 2 * place, 2 * (count - 1 - place) + 1)


def ring_place(member, count):
    return jnp.where(member % 2 == 0, member // 2, count - 1 - member // 2)


def ring_step(value, way, count):
    ring = ring_of(count)
    hops = [(ring[i], ring[(i + way) % count]) for i in range(count)]
    return lax.ppermute(value, "dp", hops)


def ring_gather(block, count):
    share, wide = block.shape
    half = wide // 2 // LANES * LANES
    place = ring_place(lax.axis_index("dp"), count)
    whole = jnp.zeros((count * share, wide), block.dtype)

    def put(whole, value, offset, column):
        row = ring_member(place + offset, count) * share
        return lax.dynamic_update_slice(whole, value, (row, column))

    whole = put(whole, block, 0, 0)
    behind = ahead = block
    for hop in range(1, count // 2):
        behind = ring_step(behind, 1, count)
        ahead = ring_step(ahead, -1, count)
        whole = put(put(whole, behind, -hop, 0), ahead, hop, 0)
    behind = ring_step(behind[:, :half], 1, count)
    ahead = ring_step(ahead[:, half:], -1, count)
    return put(put(whole, behind, -(count // 2), 0), ahead, count // 2, half)


def ring_scatter(grad, count):
    wide = grad.shape[1]
    share = grad.shape[0] // count
    half = wide // 2 // LANES * LANES
    place = ring_place(lax.axis_index("dp"), count)

    def own(offset):
        row = ring_member(place + offset, count) * share
        return lax.dynamic_slice_in_dim(grad, row, share, 0).astype(F32)

    far = own(count // 2).astype(BF16)
    behind = ring_step(far[:, :half], 1, count)
    ahead = ring_step(far[:, half:], -1, count)
    behind, ahead = yield behind, ahead
    behind = jnp.pad(behind.astype(F32), ((0, 0), (0, wide - half)))
    ahead = jnp.pad(ahead.astype(F32), ((0, 0), (half, 0)))
    for hop in range(count // 2 - 1, 0, -1):
        behind = ring_step((own(hop) + behind).astype(BF16), 1, count)
        ahead = ring_step((own(-hop) + ahead).astype(BF16), -1, count)
        behind, ahead = yield behind, ahead
        behind, ahead = behind.astype(F32), ahead.astype(F32)
    yield own(0) + behind + ahead


def text_sum(value, size):
    for bit in bits_of(size):
        if bit == 1:
            value = value + swap(value, bit, size)
        else:
            value = lax.reduce_precision(value, 8, 7)
            value = value + swap(value.astype(BF16), bit, size).astype(F32)
    return value


def lane_mask(half, shape):
    lane = lax.broadcasted_iota(jnp.int32, shape, 1)
    return (lane >= HEAD) if half else (lane < HEAD)


def pick(value, half):
    return jnp.where(lane_mask(half, value.shape), value, jnp.zeros_like(value))


def load_rows(refs, store):
    start = 0
    for ref in refs:
        rows = ref.shape[1]
        store[start : start + rows, :] = ref[0]
        start += rows


def attend_kernel(count, *refs):
    queries, keys, values = refs[:count], refs[count : 2 * count], refs[2 * count : 3 * count]
    outs = refs[3 * count : 4 * count]
    sums = refs[4 * count : 5 * count]
    key_all, value_all = refs[5 * count :]
    load_rows(keys, key_all)
    load_rows(values, value_all)
    for index in range(count):
        query = queries[index][0] * jnp.asarray(HEAD**-0.5, BF16)
        halves = []
        for half in range(2):
            scores = dot(key_all[...], pick(query, half), 1, 1)
            highest = jnp.max(scores, axis=0, keepdims=True)
            weights = jnp.exp(scores - highest)
            total = jnp.sum(weights, axis=0, keepdims=True)
            weights = (weights * (1.0 / total)).astype(BF16)
            mixed = dot(value_all[...], weights, 0, 0)
            halves.append(mixed[half * HEAD : (half + 1) * HEAD])
            sums[index][0, 0, half : half + 1, :] = highest + jnp.log(total)
        outs[index][0] = jnp.concatenate(halves, axis=0).T.astype(BF16)


def attend_back_kernel(count, groups, *refs):
    queries, keys, values = refs[:count], refs[count : 2 * count], refs[2 * count : 3 * count]
    upstreams = refs[3 * count : 4 * count]
    sums = refs[4 * count : 5 * count]
    outs = refs[5 * count : 6 * count]
    key_all, value_all, key_grad, value_grad = refs[6 * count :]
    load_rows(keys, key_all)
    load_rows(values, value_all)
    pair = pl.program_id(1)
    scale = jnp.asarray(HEAD**-0.5, BF16)
    query_lanes = pl.ds(pl.multiple_of(pair * LANES, LANES), LANES)
    key_lanes = pl.ds(pl.multiple_of((groups + pair) * LANES, LANES), LANES)
    value_lanes = pl.ds(pl.multiple_of((2 * groups + pair) * LANES, LANES), LANES)
    for index in range(count):
        query = queries[index][0] * scale
        upstream = upstreams[index][0]
        halves = []
        for half in range(2):
            query_half = pick(query, half)
            upstream_half = pick(upstream, half)
            scores = dot(key_all[...], query_half, 1, 1)
            weights = jnp.exp(scores - sums[index][0, 0, half : half + 1, :])
            along = dot(value_all[...], upstream_half, 1, 1)
            value_part = dot(weights.astype(BF16), upstream_half, 1, 0)
            product = weights * along
            score_grad = (product - weights * jnp.sum(product, axis=0, keepdims=True)).astype(BF16)
            key_part = dot(score_grad, query_half, 1, 0)
            if index == 0 and half == 0:
                value_grad[...] = value_part
                key_grad[...] = key_part
            else:
                value_grad[...] += value_part
                key_grad[...] += key_part
            mixed = dot(key_all[...], score_grad, 0, 0)
            halves.append(mixed[half * HEAD : (half + 1) * HEAD])
        query_grad = jnp.concatenate(halves, axis=0).T * HEAD**-0.5
        outs[index][0, :, query_lanes] = query_grad.astype(BF16)
    start = 0
    for index in range(count):
        rows = outs[index].shape[1]
        outs[index][0, :, key_lanes] = key_grad[start : start + rows, :].astype(BF16)
        outs[index][0, :, value_lanes] = value_grad[start : start + rows, :].astype(BF16)
        start += rows


def lane_blocks(parts, offset):
    return [
        pl.BlockSpec((1, part.shape[1], LANES), lambda s, p, o=offset: (s, 0, o + p))
        for part in parts
    ]


def widen(part, copies):
    slots, rows, width = part.shape
    width = width // copies
    extra = -width % LANES
    if not extra:
        return part
    part = jnp.pad(part.reshape(slots, rows, copies, width), ((0, 0), (0, 0), (0, 0), (0, extra)))
    return part.reshape(slots, rows, copies * (width + extra))


def narrow(part, copies, width):
    slots, rows, wide = part.shape
    wide = wide // copies
    if wide == width:
        return part
    return part.reshape(slots, rows, copies, wide)[..., :width].reshape(slots, rows, -1)


def attention_cost(slots, rows, width, products):
    return pl.CostEstimate(
        flops=products * 8 * slots * rows * rows * width,
        transcendentals=slots * rows * rows * (width // HEAD),
        bytes_accessed=slots * rows * width * 2 * (4 + 3 * (products > 2)),
    )


def attend(parts):
    slots = parts[0].shape[0]
    width = parts[0].shape[2] // 3
    parts = [widen(part, 3) for part in parts]
    count = len(parts)
    wide = parts[0].shape[2] // 3
    groups = wide // LANES
    total = sum(part.shape[1] for part in parts)
    outs = pl.pallas_call(
        functools.partial(attend_kernel, count),
        grid=(slots, groups),
        in_specs=lane_blocks(parts, 0) + lane_blocks(parts, groups) + lane_blocks(parts, 2 * groups),
        out_specs=lane_blocks(parts, 0)
        + [
            pl.BlockSpec((1, 1, 2, part.shape[1]), lambda s, p: (s, p, 0, 0)) for part in parts
        ],
        out_shape=[jax.ShapeDtypeStruct((slots, part.shape[1], wide), BF16) for part in parts]
        + [jax.ShapeDtypeStruct((slots, groups, 2, part.shape[1]), F32) for part in parts],
        scratch_shapes=[pltpu.VMEM((total, LANES), BF16)] * 2,
        compiler_params=pltpu.CompilerParams(vmem_limit_bytes=48 * 1024 * 1024),
        cost_estimate=attention_cost(slots, total, wide, 2),
        name="attend",
    )(*parts, *parts, *parts)
    return [narrow(out, 1, width) for out in outs[:count]], outs[count:]


def attend_back(parts, upstreams, sums):
    slots = parts[0].shape[0]
    width = parts[0].shape[2] // 3
    parts = [widen(part, 3) for part in parts]
    upstreams = [widen(part, 1) for part in upstreams]
    count = len(parts)
    wide = parts[0].shape[2] // 3
    groups = wide // LANES
    total = sum(part.shape[1] for part in parts)
    outs = pl.pallas_call(
        functools.partial(attend_back_kernel, count, groups),
        grid=(slots, groups),
        in_specs=lane_blocks(parts, 0)
        + lane_blocks(parts, groups)
        + lane_blocks(parts, 2 * groups)
        + lane_blocks(upstreams, 0)
        + [
            pl.BlockSpec((1, 1, 2, part.shape[1]), lambda s, p: (s, p, 0, 0)) for part in parts
        ],
        out_specs=[
            pl.BlockSpec((1, part.shape[1], 3 * wide), lambda s, p: (s, 0, 0)) for part in parts
        ],
        out_shape=[jax.ShapeDtypeStruct((slots, part.shape[1], 3 * wide), BF16) for part in parts],
        scratch_shapes=[pltpu.VMEM((total, LANES), BF16)] * 2 + [pltpu.VMEM((total, LANES), F32)] * 2,
        compiler_params=pltpu.CompilerParams(vmem_limit_bytes=48 * 1024 * 1024),
        cost_estimate=attention_cost(slots, total, wide, 5),
        name="attend_back",
    )(*parts, *parts, *parts, *upstreams, *sums)
    return [narrow(out, 3, width) for out in outs]


def rows_kernel(count, *refs):
    lefts, rights, out = refs[:count], refs[count : 2 * count], refs[-1]
    total = None
    for left, right in zip(lefts, rights):
        for slot in range(left.shape[0]):
            part = dot(left[slot], right[slot], 0, 0)
            total = part if total is None else total + part
    out[...] = total.astype(BF16)


def weight_grad(pairs):
    joined = None
    rows = pairs[0][0][0].shape[-1]
    wide = sum(rights[0].shape[-1] for _, rights in pairs)
    start = 0
    for lefts, rights in pairs:
        part = rights[0].shape[-1]
        if part % LANES or start % part:
            return jnp.concatenate([plain_grad(*pair) for pair in pairs], axis=1)
        count = len(lefts)
        step = 256
        ins = [
            pl.BlockSpec((left.shape[0], left.shape[1], step), lambda i: (0, 0, i))
            for left in lefts
        ] + [
            pl.BlockSpec(right.shape, lambda i: (0, 0, 0), pipeline_mode=pl.Buffered(1))
            for right in rights
        ]
        operands = (*lefts, *rights)
        if joined is not None:
            ins.append(pl.BlockSpec(memory_space=pl.ANY))
            operands += (joined,)
        joined = pl.pallas_call(
            functools.partial(rows_kernel, count),
            grid=(rows // step,),
            in_specs=ins,
            out_specs=pl.BlockSpec((step, part), lambda i, c=start // part: (i, c)),
            out_shape=jax.ShapeDtypeStruct((rows, wide), BF16),
            input_output_aliases={} if joined is None else {2 * count: 0},
            compiler_params=pltpu.CompilerParams(vmem_limit_bytes=48 * 1024 * 1024),
            cost_estimate=pl.CostEstimate(flops=0, transcendentals=0, bytes_accessed=1024),
            name="weight_grad",
        )(*operands)
        start += part
    return joined


def plain_grad(lefts, rights):
    left = jnp.concatenate([v.reshape(-1, v.shape[-1]) for v in lefts], axis=0)
    right = jnp.concatenate([v.reshape(-1, v.shape[-1]) for v in rights], axis=0)
    return dot(left, right, 0, 0).astype(BF16)


def on_device(
    group_count,
    tensor_size,
    image_tokens,
    text_tokens,
    condition,
    group_size,
    image_modulation,
    image_attention_in,
    image_attention_out,
    image_hidden_in,
    image_hidden_out,
    text_modulation,
    text_attention_in,
    text_attention_out,
    text_hidden_in,
    text_hidden_out,
    image_cotangent,
    text_cotangent,
):
    size = tensor_size
    slots, image_length, model = image_tokens.shape
    text_length = text_tokens.shape[1]
    share, _, width = image_attention_in.shape
    units = image_hidden_in.shape[1]
    tensor_rank = lax.axis_index("tensor")
    group_rank = lax.axis_index("dp")

    def gathered(*blocks):
        joined = blocks[0] if len(blocks) == 1 else jnp.concatenate(blocks, axis=1)
        return lax.all_gather(joined, "dp", axis=0, tiled=True)

    image_in = gathered(image_attention_in.reshape(share, 3 * width))
    image_up = gathered(image_hidden_in)
    image_down = gathered(image_hidden_out.T)
    text_in = ring_gather(text_attention_in.reshape(share, 3 * width), group_count)
    both_out = ring_gather(
        after(jnp.concatenate([image_attention_out.T, text_attention_out.T], axis=1), text_in),
        group_count,
    )
    weight_in = (image_in, text_in)
    weight_out = (both_out[:, :width], both_out[:, width:])

    alive = (jnp.arange(slots) < group_size[0]).astype(F32)[:, None, None]
    cond_full = condition.astype(F32)
    activated_low = jax.nn.silu(cond_full).astype(BF16)
    activated_all = gather_stack(activated_low, group_count, "dp").reshape(-1, model)
    activated_own = lax.dynamic_slice_in_dim(activated_all, group_rank * share, share, 1)
    all_slots = activated_own.shape[0]
    mod_parts = jnp.concatenate(
        [
            dot(activated_own, image_modulation.reshape(share, 6 * width), 1, 0),
            dot(activated_own, text_modulation.reshape(share, 6 * width), 1, 0),
        ],
        axis=1,
    ).reshape(group_count, slots, 12 * width)
    mod_own = scatter_stack(mod_parts, group_count, "dp")
    modulations = lax.all_gather(
        mod_own.reshape(slots, 2, 6, width), "tensor", axis=3, tiled=True
    )
    mods = (modulations[:, 0], modulations[:, 1])

    tokens = (image_tokens.astype(F32), text_tokens.astype(F32))
    outgoing = (image_cotangent.astype(F32) * alive, text_cotangent.astype(F32) * alive)

    def collect(stream, values):
        values = values.astype(BF16)
        return [values] if stream else gather_pieces(values, size)

    def apply(pieces, weight, weight_dim, low):
        return [
            dot(piece, weight, 2, weight_dim).astype(BF16 if low else F32) for piece in pieces
        ]

    def reduced(stream, pieces):
        return text_sum(pieces[0], size) if stream else scatter_sum(pieces, size)

    def scattered(grad):
        return lax.psum_scatter(grad, "dp", scatter_dimension=0, tiled=True).astype(F32)

    first_saved = []
    packed = []
    down_pieces = []
    for stream in range(2):
        mod = mods[stream]
        normed, inverse = norm_rows(tokens[stream])
        first_in = normed * (1.0 + spread(mod[:, 1])) + spread(mod[:, 0])
        pieces = collect(stream, first_in)
        packed.append(apply(pieces, weight_in[stream], 0, True))
        first_saved.append((normed, inverse, pieces))
        down = (outgoing[stream] * spread(mod[:, 5])).astype(BF16)
        down_pieces.append(collect(stream, after(down, pieces)))
    parts = packed[0] + packed[1]
    packed_text = ring_gather(
        after(jnp.concatenate([text_hidden_in, text_hidden_out.T], axis=1), parts, both_out),
        group_count,
    )
    weight_up = (image_up, packed_text[:, :units])
    weight_down = (image_down, packed_text[:, units:])
    attended, sums = attend(parts)
    attended, down_pieces = lax.optimization_barrier((attended, down_pieces))
    attended_parts = (attended[:-1], attended[-1:])

    middles = [None, None]
    actives = [None, None]
    mlp_grads = [None, None]
    middle_grads = [None, None]
    branch_grads = [None, None]
    lows = [None, None]
    stats = [None, None]
    upstreams = [None, None]

    def stream_branch(stream):
        mod = mods[stream]
        branch = reduced(stream, apply(attended_parts[stream], weight_out[stream], 1, False))
        middle = tokens[stream] + spread(mod[:, 2]) * branch
        normed, inverse = norm_rows(middle)
        second_in = normed * (1.0 + spread(mod[:, 4])) + spread(mod[:, 3])
        middles[stream] = middle
        return branch, normed, inverse, collect(stream, second_in)

    def stream_back(stream, branch, normed, inverse, pieces):
        mod = mods[stream]
        hidden = apply(pieces, weight_up[stream], 0, False)
        active = [gelu_tanh(value).astype(BF16) for value in hidden]
        active_grad = apply(down_pieces[stream], weight_down[stream], 0, False)
        hidden_grad = [
            jax.vjp(gelu_tanh, value)[1](grad)[0].astype(BF16)
            for value, grad in zip(hidden, active_grad)
        ]
        products = apply(hidden_grad, weight_up[stream], 1, False)
        late = after((down_pieces[stream], active, pieces, hidden_grad), products)
        mlp_grads[stream] = weight_grad([late[:2], late[2:]])
        second_grad = reduced(stream, products)
        shift_two_grad = jnp.sum(second_grad, axis=1)
        scale_two_grad = jnp.sum(second_grad * normed, axis=1)
        middle_grad = outgoing[stream] + norm_back(
            second_grad * (1.0 + spread(mod[:, 4])), normed, inverse
        )
        gate_one_grad = jnp.sum(middle_grad * branch, axis=1)
        low = (middle_grad * spread(mod[:, 2])).astype(BF16)
        branch_grads[stream] = collect(stream, low)
        upstreams[stream] = apply(branch_grads[stream], weight_out[stream], 0, True)
        middle_grads[stream] = middle_grad
        actives[stream] = after(active, low)
        stats[stream] = (gate_one_grad, shift_two_grad, scale_two_grad)

    image_state = stream_branch(0)
    text_state = stream_branch(1)
    stream_back(0, *image_state)
    stream_back(1, *text_state)
    image_mlp = scattered(mlp_grads[0])
    text_ring = ring_scatter(mlp_grads[1], group_count)
    text_hop = next(text_ring)
    upstreams, text_hop = lax.optimization_barrier((upstreams, text_hop))
    text_hop = text_ring.send(text_hop)

    packed_grads = attend_back(parts, upstreams[0] + upstreams[1], sums)
    packed_grads, text_hop = lax.optimization_barrier((packed_grads, text_hop))
    text_hop = text_ring.send(text_hop)
    image_in_grad = weight_grad([(first_saved[0][2], packed_grads[:-1])])
    image_in_sum = scattered(image_in_grad)
    attention_grad = weight_grad(
        [
            (first_saved[1][2], packed_grads[-1:]),
            (branch_grads[0], attended_parts[0]),
            (branch_grads[1], attended_parts[1]),
        ]
    )
    packed_grads = after(packed_grads, image_in_grad, attention_grad)
    for _ in range(group_count // 2 - 2):
        attention_grad, text_hop = lax.optimization_barrier((attention_grad, text_hop))
        text_hop = text_ring.send(text_hop)
    text_mlp = text_hop
    attention_ring = ring_scatter(attention_grad, group_count)
    attention_hop = next(attention_ring)
    packed_grads = (packed_grads[:-1], packed_grads[-1:])
    outputs = [None, None]
    input_grads = [None, None]
    mod_grads = [None, None]
    for stream in (1, 0):
        mod = mods[stream]
        normed, inverse, _ = first_saved[stream]
        gate_one_grad, shift_two_grad, scale_two_grad = stats[stream]
        branch_two = reduced(stream, apply(actives[stream], weight_down[stream], 1, False))
        result = middles[stream] + spread(mod[:, 5]) * branch_two
        outputs[stream] = (result * alive).astype(BF16)
        gate_two_grad = jnp.sum(outgoing[stream] * branch_two, axis=1)
        first_grad = reduced(stream, apply(packed_grads[stream], weight_in[stream], 1, False))
        first_grad, attention_hop = lax.optimization_barrier((first_grad, attention_hop))
        if stream == 0:
            first_grad, image_mlp = lax.optimization_barrier((first_grad, image_mlp))
        attention_hop = attention_ring.send(attention_hop)
        shift_one_grad = jnp.sum(first_grad, axis=1)
        scale_one_grad = jnp.sum(first_grad * normed, axis=1)
        input_grads[stream] = middle_grads[stream] + norm_back(
            first_grad * (1.0 + spread(mod[:, 1])), normed, inverse
        )
        mod_grads[stream] = jnp.stack(
            [
                shift_one_grad,
                scale_one_grad,
                gate_one_grad,
                shift_two_grad,
                scale_two_grad,
                gate_two_grad,
            ],
            axis=1,
        )
    for _ in range(group_count // 2 - 2):
        attention_hop = attention_ring.send(attention_hop)
    attention_sum = attention_hop

    image_blocks = jnp.stack(
        [
            lax.dynamic_slice_in_dim(mod_grads[0], (tensor_rank ^ k) * width, width, 2)
            for k in range(size)
        ]
    )
    image_share = scatter_stack(image_blocks, size, "tensor")
    text_share = lax.dynamic_slice_in_dim(mod_grads[1], tensor_rank * width, width, 2)
    share_low = jnp.stack([image_share, text_share], axis=1).astype(BF16)
    share_all = gather_stack(share_low, group_count, "dp").reshape(all_slots, 2, 6, width)
    image_all = share_all[:, 0].reshape(all_slots, 6 * width)
    text_all = share_all[:, 1].reshape(all_slots, 6 * width)
    image_ada = dot(activated_own, image_all, 0, 0).reshape(share, 6, width)
    text_ada = dot(activated_own, text_all, 0, 0).reshape(share, 6, width)
    activated_part = dot(image_all, image_modulation.reshape(share, 6 * width), 1, 1) + dot(
        text_all, text_modulation.reshape(share, 6 * width), 1, 1
    )
    activated_part = sum_all(activated_part, size, "tensor").reshape(group_count, slots, share)
    activated_rows = gather_stack(activated_part, group_count, "dp")
    activated_rows = jnp.stack([activated_rows[k, k] for k in range(group_count)])
    group_order = group_rank ^ jnp.arange(group_count)
    activated_grad = jnp.concatenate(
        [
            lax.dynamic_index_in_dim(activated_rows, group_order[k], 0, keepdims=False)
            for k in range(group_count)
        ],
        axis=1,
    )
    condition_gradient = jax.vjp(jax.nn.silu, cond_full)[1](activated_grad)[0]

    return (
        outputs[0],
        outputs[1],
        input_grads[0],
        input_grads[1],
        condition_gradient,
        image_ada,
        image_in_sum.reshape(share, 3, width),
        attention_sum[:, 3 * width : 4 * width].T,
        image_mlp[:, units:],
        image_mlp[:, :units].T,
        text_ada,
        attention_sum[:, : 3 * width].reshape(share, 3, width),
        attention_sum[:, 4 * width :].T,
        text_mlp[:, units:],
        text_mlp[:, :units].T,
    )


def solution(mesh):
    image = P("dp", "tensor", None)
    text = P("dp", None, None)
    columns = P("dp", None, "tensor")
    rows = P("tensor", "dp")
    plain = P("dp", "tensor")
    weights = (columns, columns, rows, plain, rows)
    return jax.shard_map(
        functools.partial(on_device, mesh.shape["dp"], mesh.shape["tensor"]),
        mesh=mesh,
        in_specs=(image, text, P("dp", None), P("dp")) + weights + weights + (image, text),
        out_specs=(image, text, image, text, P("dp", None)) + weights + weights,
        check_vma=False,
    )
```

```python
import functools

import jax
import jax.numpy as jnp
from jax import lax
from jax.experimental import pallas as pl
from jax.experimental.pallas import tpu as pltpu
from jax.sharding import PartitionSpec as P

HEAD = 64
LANES = 128
F32 = jnp.float32
BF16 = jnp.bfloat16


def norm_rows(values):
    center = values - jnp.mean(values, axis=-1, keepdims=True)
    inverse = lax.rsqrt(jnp.mean(center * center, axis=-1, keepdims=True) + 1e-06)
    return (center * inverse, inverse)


def norm_back(upstream, normed, inverse):
    first = jnp.mean(upstream, axis=-1, keepdims=True)
    second = jnp.mean(upstream * normed, axis=-1, keepdims=True)
    return inverse * (upstream - first - normed * second)


def gelu_tanh(values):
    return jax.nn.gelu(values, approximate=True)


def spread(vector):
    return vector[:, None, :]


def dot(left, right, left_dim, right_dim):
    return lax.dot_general(
        left, right, (((left_dim,), (right_dim,)), ((), ())), preferred_element_type=F32
    )


def swap(value, bit, size, axis="tensor"):
    return lax.ppermute(value, axis, [(i, i ^ bit) for i in range(size)])


def bits_of(size):
    bits = []
    bit = 1
    while bit < size:
        bits.append(bit)
        bit *= 2
    return bits


def gather_pieces(value, size, axis="tensor"):
    have = {0: value}
    for bit in reversed(bits_of(size)):
        have.update({k ^ bit: swap(v, bit, size, axis) for k, v in list(have.items())})
    return [have[k] for k in range(size)]


def gather_stack(value, size, axis):
    value = value[None]
    for bit in bits_of(size):
        value = jnp.concatenate([value, swap(value, bit, size, axis)], axis=0)
    return value


def scatter_stack(value, size, axis):
    for bit in reversed(bits_of(size)):
        value = value[:bit] + swap(value[bit:], bit, size, axis)
    return value[0]


def sum_all(value, size, axis):
    for bit in bits_of(size):
        value = value + swap(value, bit, size, axis)
    return value


def scatter_sum(pieces, size):
    have = dict(enumerate(pieces))
    for bit in bits_of(size):
        kept = {}
        for k in sorted(have, reverse=True):
            if not k & bit:
                other = swap(have[k ^ bit].astype(BF16), bit, size)
                kept[k] = have[k].astype(F32) + other.astype(F32)
        have = kept
    return have[0]


def after(values, *others):
    return lax.optimization_barrier((values, others))[0]


def ring_of(count):
    return list(range(0, count, 2)) + list(range(1, count, 2))[::-1]


def ring_member(place, count):
    place = lax.rem(place + count, count)
    return jnp.where(place < (count + 1) // 2, 2 * place, 2 * (count - 1 - place) + 1)


def ring_place(member, count):
    return jnp.where(member % 2 == 0, member // 2, count - 1 - member // 2)


def ring_step(value, way, count):
    ring = ring_of(count)
    hops = [(ring[i], ring[(i + way) % count]) for i in range(count)]
    return lax.ppermute(value, "dp", hops)


def ring_gather(block, count):
    share, wide = block.shape
    half = wide // 2 // LANES * LANES
    place = ring_place(lax.axis_index("dp"), count)
    whole = jnp.zeros((count * share, wide), block.dtype)

    def put(whole, value, offset, column):
        row = ring_member(place + offset, count) * share
        return lax.dynamic_update_slice(whole, value, (row, column))

    whole = put(whole, block, 0, 0)
    behind = ahead = block
    for hop in range(1, count // 2):
        behind = ring_step(behind, 1, count)
        ahead = ring_step(ahead, -1, count)
        behind, ahead = yield behind, ahead
        whole = put(put(whole, behind, -hop, 0), ahead, hop, 0)
    behind = ring_step(behind[:, :half], 1, count)
    ahead = ring_step(ahead[:, half:], -1, count)
    behind, ahead = yield behind, ahead
    yield put(put(whole, behind, -(count // 2), 0), ahead, count // 2, half)


def ring_scatter(grad, count):
    wide = grad.shape[1]
    share = grad.shape[0] // count
    half = wide // 2 // LANES * LANES
    place = ring_place(lax.axis_index("dp"), count)

    def own(offset):
        row = ring_member(place + offset, count) * share
        return lax.dynamic_slice_in_dim(grad, row, share, 0).astype(F32)

    far = own(count // 2).astype(BF16)
    behind = ring_step(far[:, :half], 1, count)
    ahead = ring_step(far[:, half:], -1, count)
    behind, ahead = yield behind, ahead
    behind = jnp.pad(behind.astype(F32), ((0, 0), (0, wide - half)))
    ahead = jnp.pad(ahead.astype(F32), ((0, 0), (half, 0)))
    for hop in range(count // 2 - 1, 0, -1):
        behind = ring_step((own(hop) + behind).astype(BF16), 1, count)
        ahead = ring_step((own(-hop) + ahead).astype(BF16), -1, count)
        behind, ahead = yield behind, ahead
        behind, ahead = behind.astype(F32), ahead.astype(F32)
    yield own(0) + behind + ahead


def text_sum(value, size):
    for bit in bits_of(size):
        if bit == 1:
            value = value + swap(value, bit, size)
        else:
            value = lax.reduce_precision(value, 8, 7)
            value = value + swap(value.astype(BF16), bit, size).astype(F32)
    return value


def lane_mask(half, shape):
    lane = lax.broadcasted_iota(jnp.int32, shape, 1)
    return (lane >= HEAD) if half else (lane < HEAD)


def pick(value, half):
    return jnp.where(lane_mask(half, value.shape), value, jnp.zeros_like(value))


def load_rows(refs, store):
    start = 0
    for ref in refs:
        rows = ref.shape[1]
        store[start : start + rows, :] = ref[0]
        start += rows


def attend_kernel(count, *refs):
    queries, keys, values = refs[:count], refs[count : 2 * count], refs[2 * count : 3 * count]
    outs = refs[3 * count : 4 * count]
    sums = refs[4 * count : 5 * count]
    key_all, value_all = refs[5 * count :]
    load_rows(keys, key_all)
    load_rows(values, value_all)
    for index in range(count):
        query = queries[index][0] * jnp.asarray(HEAD**-0.5, BF16)
        halves = []
        for half in range(2):
            scores = dot(key_all[...], pick(query, half), 1, 1)
            highest = jnp.max(scores, axis=0, keepdims=True)
            weights = jnp.exp(scores - highest)
            total = jnp.sum(weights, axis=0, keepdims=True)
            weights = (weights * (1.0 / total)).astype(BF16)
            mixed = dot(value_all[...], weights, 0, 0)
            halves.append(mixed[half * HEAD : (half + 1) * HEAD])
            sums[index][0, 0, half : half + 1, :] = highest + jnp.log(total)
        outs[index][0] = jnp.concatenate(halves, axis=0).T.astype(BF16)


def attend_back_kernel(count, groups, *refs):
    queries, keys, values = refs[:count], refs[count : 2 * count], refs[2 * count : 3 * count]
    upstreams = refs[3 * count : 4 * count]
    sums = refs[4 * count : 5 * count]
    outs = refs[5 * count : 6 * count]
    key_all, value_all, key_grad, value_grad = refs[6 * count :]
    load_rows(keys, key_all)
    load_rows(values, value_all)
    pair = pl.program_id(1)
    scale = jnp.asarray(HEAD**-0.5, BF16)
    query_lanes = pl.ds(pl.multiple_of(pair * LANES, LANES), LANES)
    key_lanes = pl.ds(pl.multiple_of((groups + pair) * LANES, LANES), LANES)
    value_lanes = pl.ds(pl.multiple_of((2 * groups + pair) * LANES, LANES), LANES)
    for index in range(count):
        query = queries[index][0] * scale
        upstream = upstreams[index][0]
        halves = []
        for half in range(2):
            query_half = pick(query, half)
            upstream_half = pick(upstream, half)
            scores = dot(key_all[...], query_half, 1, 1)
            weights = jnp.exp(scores - sums[index][0, 0, half : half + 1, :])
            along = dot(value_all[...], upstream_half, 1, 1)
            value_part = dot(weights.astype(BF16), upstream_half, 1, 0)
            product = weights * along
            score_grad = (product - weights * jnp.sum(product, axis=0, keepdims=True)).astype(BF16)
            key_part = dot(score_grad, query_half, 1, 0)
            if index == 0 and half == 0:
                value_grad[...] = value_part
                key_grad[...] = key_part
            else:
                value_grad[...] += value_part
                key_grad[...] += key_part
            mixed = dot(key_all[...], score_grad, 0, 0)
            halves.append(mixed[half * HEAD : (half + 1) * HEAD])
        query_grad = jnp.concatenate(halves, axis=0).T * HEAD**-0.5
        outs[index][0, :, query_lanes] = query_grad.astype(BF16)
    start = 0
    for index in range(count):
        rows = outs[index].shape[1]
        outs[index][0, :, key_lanes] = key_grad[start : start + rows, :].astype(BF16)
        outs[index][0, :, value_lanes] = value_grad[start : start + rows, :].astype(BF16)
        start += rows


def lane_blocks(parts, offset):
    return [
        pl.BlockSpec((1, part.shape[1], LANES), lambda s, p, o=offset: (s, 0, o + p))
        for part in parts
    ]


def widen(part, copies):
    slots, rows, width = part.shape
    width = width // copies
    extra = -width % LANES
    if not extra:
        return part
    part = jnp.pad(part.reshape(slots, rows, copies, width), ((0, 0), (0, 0), (0, 0), (0, extra)))
    return part.reshape(slots, rows, copies * (width + extra))


def narrow(part, copies, width):
    slots, rows, wide = part.shape
    wide = wide // copies
    if wide == width:
        return part
    return part.reshape(slots, rows, copies, wide)[..., :width].reshape(slots, rows, -1)


def attention_cost(slots, rows, width, products):
    return pl.CostEstimate(
        flops=products * 8 * slots * rows * rows * width,
        transcendentals=slots * rows * rows * (width // HEAD),
        bytes_accessed=slots * rows * width * 2 * (4 + 3 * (products > 2)),
    )


def attend(parts):
    slots = parts[0].shape[0]
    width = parts[0].shape[2] // 3
    parts = [widen(part, 3) for part in parts]
    count = len(parts)
    wide = parts[0].shape[2] // 3
    groups = wide // LANES
    total = sum(part.shape[1] for part in parts)
    outs = pl.pallas_call(
        functools.partial(attend_kernel, count),
        grid=(slots, groups),
        in_specs=lane_blocks(parts, 0) + lane_blocks(parts, groups) + lane_blocks(parts, 2 * groups),
        out_specs=lane_blocks(parts, 0)
        + [
            pl.BlockSpec((1, 1, 2, part.shape[1]), lambda s, p: (s, p, 0, 0)) for part in parts
        ],
        out_shape=[jax.ShapeDtypeStruct((slots, part.shape[1], wide), BF16) for part in parts]
        + [jax.ShapeDtypeStruct((slots, groups, 2, part.shape[1]), F32) for part in parts],
        scratch_shapes=[pltpu.VMEM((total, LANES), BF16)] * 2,
        compiler_params=pltpu.CompilerParams(vmem_limit_bytes=48 * 1024 * 1024),
        cost_estimate=attention_cost(slots, total, wide, 2),
        name="attend",
    )(*parts, *parts, *parts)
    return [narrow(out, 1, width) for out in outs[:count]], outs[count:]


def attend_back(parts, upstreams, sums):
    slots = parts[0].shape[0]
    width = parts[0].shape[2] // 3
    parts = [widen(part, 3) for part in parts]
    upstreams = [widen(part, 1) for part in upstreams]
    count = len(parts)
    wide = parts[0].shape[2] // 3
    groups = wide // LANES
    total = sum(part.shape[1] for part in parts)
    outs = pl.pallas_call(
        functools.partial(attend_back_kernel, count, groups),
        grid=(slots, groups),
        in_specs=lane_blocks(parts, 0)
        + lane_blocks(parts, groups)
        + lane_blocks(parts, 2 * groups)
        + lane_blocks(upstreams, 0)
        + [
            pl.BlockSpec((1, 1, 2, part.shape[1]), lambda s, p: (s, p, 0, 0)) for part in parts
        ],
        out_specs=[
            pl.BlockSpec((1, part.shape[1], 3 * wide), lambda s, p: (s, 0, 0)) for part in parts
        ],
        out_shape=[jax.ShapeDtypeStruct((slots, part.shape[1], 3 * wide), BF16) for part in parts],
        scratch_shapes=[pltpu.VMEM((total, LANES), BF16)] * 2 + [pltpu.VMEM((total, LANES), F32)] * 2,
        compiler_params=pltpu.CompilerParams(vmem_limit_bytes=48 * 1024 * 1024),
        cost_estimate=attention_cost(slots, total, wide, 5),
        name="attend_back",
    )(*parts, *parts, *parts, *upstreams, *sums)
    return [narrow(out, 3, width) for out in outs]


def rows_kernel(count, *refs):
    lefts, rights, out = refs[:count], refs[count : 2 * count], refs[-1]
    total = None
    for left, right in zip(lefts, rights):
        for slot in range(left.shape[0]):
            part = dot(left[slot], right[slot], 0, 0)
            total = part if total is None else total + part
    out[...] = total.astype(BF16)


def weight_grad(pairs):
    joined = None
    rows = pairs[0][0][0].shape[-1]
    wide = sum(rights[0].shape[-1] for _, rights in pairs)
    start = 0
    for lefts, rights in pairs:
        part = rights[0].shape[-1]
        if part % LANES or start % part:
            return jnp.concatenate([plain_grad(*pair) for pair in pairs], axis=1)
        count = len(lefts)
        step = 256
        ins = [
            pl.BlockSpec((left.shape[0], left.shape[1], step), lambda i: (0, 0, i))
            for left in lefts
        ] + [
            pl.BlockSpec(right.shape, lambda i: (0, 0, 0), pipeline_mode=pl.Buffered(1))
            for right in rights
        ]
        operands = (*lefts, *rights)
        if joined is not None:
            ins.append(pl.BlockSpec(memory_space=pl.ANY))
            operands += (joined,)
        joined = pl.pallas_call(
            functools.partial(rows_kernel, count),
            grid=(rows // step,),
            in_specs=ins,
            out_specs=pl.BlockSpec((step, part), lambda i, c=start // part: (i, c)),
            out_shape=jax.ShapeDtypeStruct((rows, wide), BF16),
            input_output_aliases={} if joined is None else {2 * count: 0},
            compiler_params=pltpu.CompilerParams(vmem_limit_bytes=48 * 1024 * 1024),
            cost_estimate=pl.CostEstimate(flops=0, transcendentals=0, bytes_accessed=1024),
            name="weight_grad",
        )(*operands)
        start += part
    return joined


def plain_grad(lefts, rights):
    left = jnp.concatenate([v.reshape(-1, v.shape[-1]) for v in lefts], axis=0)
    right = jnp.concatenate([v.reshape(-1, v.shape[-1]) for v in rights], axis=0)
    return dot(left, right, 0, 0).astype(BF16)


def on_device(
    group_count,
    tensor_size,
    image_tokens,
    text_tokens,
    condition,
    group_size,
    image_modulation,
    image_attention_in,
    image_attention_out,
    image_hidden_in,
    image_hidden_out,
    text_modulation,
    text_attention_in,
    text_attention_out,
    text_hidden_in,
    text_hidden_out,
    image_cotangent,
    text_cotangent,
):
    size = tensor_size
    slots, image_length, model = image_tokens.shape
    text_length = text_tokens.shape[1]
    share, _, width = image_attention_in.shape
    units = image_hidden_in.shape[1]
    tensor_rank = lax.axis_index("tensor")
    group_rank = lax.axis_index("dp")

    def gathered(*blocks):
        joined = blocks[0] if len(blocks) == 1 else jnp.concatenate(blocks, axis=1)
        return lax.all_gather(joined, "dp", axis=0, tiled=True)

    packed_first = gathered(
        image_attention_in.reshape(share, 3 * width),
        text_attention_in.reshape(share, 3 * width),
        image_attention_out.T,
        text_attention_out.T,
    )
    packed_image = gathered(image_hidden_in, image_hidden_out.T)
    weight_in = (packed_first[:, : 3 * width], packed_first[:, 3 * width : 6 * width])
    weight_out = (packed_first[:, 6 * width : 7 * width], packed_first[:, 7 * width :])

    alive = (jnp.arange(slots) < group_size[0]).astype(F32)[:, None, None]
    cond_full = condition.astype(F32)
    activated_low = jax.nn.silu(cond_full).astype(BF16)
    activated_all = gather_stack(activated_low, group_count, "dp").reshape(-1, model)
    activated_own = lax.dynamic_slice_in_dim(activated_all, group_rank * share, share, 1)
    all_slots = activated_own.shape[0]
    mod_parts = jnp.concatenate(
        [
            dot(activated_own, image_modulation.reshape(share, 6 * width), 1, 0),
            dot(activated_own, text_modulation.reshape(share, 6 * width), 1, 0),
        ],
        axis=1,
    ).reshape(group_count, slots, 12 * width)
    mod_own = scatter_stack(mod_parts, group_count, "dp")
    modulations = lax.all_gather(
        mod_own.reshape(slots, 2, 6, width), "tensor", axis=3, tiled=True
    )
    mods = (modulations[:, 0], modulations[:, 1])

    tokens = (image_tokens.astype(F32), text_tokens.astype(F32))
    outgoing = (image_cotangent.astype(F32) * alive, text_cotangent.astype(F32) * alive)

    def collect(stream, values):
        values = values.astype(BF16)
        return [values] if stream else gather_pieces(values, size)

    def apply(pieces, weight, weight_dim, low):
        return [
            dot(piece, weight, 2, weight_dim).astype(BF16 if low else F32) for piece in pieces
        ]

    def reduced(stream, pieces):
        return text_sum(pieces[0], size) if stream else scatter_sum(pieces, size)

    def scattered(grad):
        return lax.psum_scatter(grad, "dp", scatter_dimension=0, tiled=True).astype(F32)

    first_saved = []
    packed = []
    down_pieces = []
    for stream in range(2):
        mod = mods[stream]
        normed, inverse = norm_rows(tokens[stream])
        first_in = normed * (1.0 + spread(mod[:, 1])) + spread(mod[:, 0])
        pieces = collect(stream, first_in)
        packed.append(apply(pieces, weight_in[stream], 0, True))
        first_saved.append((normed, inverse, pieces))
        down = (outgoing[stream] * spread(mod[:, 5])).astype(BF16)
        down_pieces.append(collect(stream, after(down, pieces)))
    parts = packed[0] + packed[1]
    text_ring = ring_gather(
        after(jnp.concatenate([text_hidden_in, text_hidden_out.T], axis=1), parts), group_count
    )
    text_hop = next(text_ring)
    attended, sums = attend(parts)
    attended, down_pieces, text_hop = lax.optimization_barrier((attended, down_pieces, text_hop))
    text_hop = text_ring.send(text_hop)
    attended_parts = (attended[:-1], attended[-1:])

    middles = [None, None]
    actives = [None, None]
    mlp_grads = [None, None]
    middle_grads = [None, None]
    branch_grads = [None, None]
    lows = [None, None]
    stats = [None, None]
    upstreams = [None, None]

    def stream_branch(stream, hop):
        mod = mods[stream]
        branch = reduced(stream, apply(attended_parts[stream], weight_out[stream], 1, False))
        branch, hop = lax.optimization_barrier((branch, hop))
        hop = text_ring.send(hop)
        middle = tokens[stream] + spread(mod[:, 2]) * branch
        normed, inverse = norm_rows(middle)
        second_in = normed * (1.0 + spread(mod[:, 4])) + spread(mod[:, 3])
        middles[stream] = middle
        return (branch, normed, inverse, collect(stream, second_in)), hop

    def stream_back(stream, branch, normed, inverse, pieces, hop=None):
        mod = mods[stream]
        hidden = apply(pieces, weight_up[stream], 0, False)
        active = [gelu_tanh(value).astype(BF16) for value in hidden]
        active_grad = apply(down_pieces[stream], weight_down[stream], 0, False)
        hidden_grad = [
            jax.vjp(gelu_tanh, value)[1](grad)[0].astype(BF16)
            for value, grad in zip(hidden, active_grad)
        ]
        products = apply(hidden_grad, weight_up[stream], 1, False)
        late = after((down_pieces[stream], active, pieces, hidden_grad), products)
        mlp_grads[stream] = weight_grad([late[:2], late[2:]])
        second_grad = reduced(stream, products)
        if hop is not None:
            second_grad, hop = lax.optimization_barrier((second_grad, hop))
            hop = text_ring.send(hop)
        shift_two_grad = jnp.sum(second_grad, axis=1)
        scale_two_grad = jnp.sum(second_grad * normed, axis=1)
        middle_grad = outgoing[stream] + norm_back(
            second_grad * (1.0 + spread(mod[:, 4])), normed, inverse
        )
        gate_one_grad = jnp.sum(middle_grad * branch, axis=1)
        low = (middle_grad * spread(mod[:, 2])).astype(BF16)
        branch_grads[stream] = collect(stream, low)
        upstreams[stream] = apply(branch_grads[stream], weight_out[stream], 0, True)
        middle_grads[stream] = middle_grad
        actives[stream] = after(active, low)
        stats[stream] = (gate_one_grad, shift_two_grad, scale_two_grad)
        return hop

    text_state, text_hop = stream_branch(1, text_hop)
    image_state, text_hop = stream_branch(0, text_hop)
    for _ in range(group_count // 2 - 4):
        text_hop = text_ring.send(text_hop)
    packed_text = text_ring.send(text_hop)
    weight_up = (packed_image[:, :units], packed_text[:, :units])
    weight_down = (packed_image[:, units:], packed_text[:, units:])
    stream_back(1, *text_state)
    text_ring = ring_scatter(mlp_grads[1], group_count)
    text_hop = stream_back(0, *image_state, hop=next(text_ring))
    image_mlp = scattered(mlp_grads[0])
    upstreams, text_hop = lax.optimization_barrier((upstreams, text_hop))
    text_hop = text_ring.send(text_hop)

    packed_grads = attend_back(parts, upstreams[0] + upstreams[1], sums)
    packed_grads, text_hop = lax.optimization_barrier((packed_grads, text_hop))
    text_hop = text_ring.send(text_hop)
    attention_grad = weight_grad(
        [
            (first_saved[0][2], packed_grads[:-1]),
            (first_saved[1][2], packed_grads[-1:]),
            (branch_grads[0], attended_parts[0]),
            (branch_grads[1], attended_parts[1]),
        ]
    )
    attention_sum = scattered(attention_grad)
    packed_grads = after(packed_grads, attention_grad)
    packed_grads = (packed_grads[:-1], packed_grads[-1:])
    outputs = [None, None]
    input_grads = [None, None]
    mod_grads = [None, None]
    for stream in (1, 0):
        mod = mods[stream]
        normed, inverse, _ = first_saved[stream]
        gate_one_grad, shift_two_grad, scale_two_grad = stats[stream]
        branch_two = reduced(stream, apply(actives[stream], weight_down[stream], 1, False))
        result = middles[stream] + spread(mod[:, 5]) * branch_two
        outputs[stream] = (result * alive).astype(BF16)
        gate_two_grad = jnp.sum(outgoing[stream] * branch_two, axis=1)
        first_grad = reduced(stream, apply(packed_grads[stream], weight_in[stream], 1, False))
        if stream == 0:
            first_grad, image_mlp, text_hop = lax.optimization_barrier(
                (first_grad, image_mlp, text_hop)
            )
            for _ in range(group_count // 2 - 3):
                text_hop = text_ring.send(text_hop)
        shift_one_grad = jnp.sum(first_grad, axis=1)
        scale_one_grad = jnp.sum(first_grad * normed, axis=1)
        input_grads[stream] = middle_grads[stream] + norm_back(
            first_grad * (1.0 + spread(mod[:, 1])), normed, inverse
        )
        mod_grads[stream] = jnp.stack(
            [
                shift_one_grad,
                scale_one_grad,
                gate_one_grad,
                shift_two_grad,
                scale_two_grad,
                gate_two_grad,
            ],
            axis=1,
        )
    text_mlp = text_hop

    image_blocks = jnp.stack(
        [
            lax.dynamic_slice_in_dim(mod_grads[0], (tensor_rank ^ k) * width, width, 2)
            for k in range(size)
        ]
    )
    image_share = scatter_stack(image_blocks, size, "tensor")
    text_share = lax.dynamic_slice_in_dim(mod_grads[1], tensor_rank * width, width, 2)
    share_low = jnp.stack([image_share, text_share], axis=1).astype(BF16)
    share_all = gather_stack(share_low, group_count, "dp").reshape(all_slots, 2, 6, width)
    image_all = share_all[:, 0].reshape(all_slots, 6 * width)
    text_all = share_all[:, 1].reshape(all_slots, 6 * width)
    image_ada = dot(activated_own, image_all, 0, 0).reshape(share, 6, width)
    text_ada = dot(activated_own, text_all, 0, 0).reshape(share, 6, width)
    activated_part = dot(image_all, image_modulation.reshape(share, 6 * width), 1, 1) + dot(
        text_all, text_modulation.reshape(share, 6 * width), 1, 1
    )
    activated_part = sum_all(activated_part, size, "tensor").reshape(group_count, slots, share)
    activated_rows = gather_stack(activated_part, group_count, "dp")
    activated_rows = jnp.stack([activated_rows[k, k] for k in range(group_count)])
    group_order = group_rank ^ jnp.arange(group_count)
    activated_grad = jnp.concatenate(
        [
            lax.dynamic_index_in_dim(activated_rows, group_order[k], 0, keepdims=False)
            for k in range(group_count)
        ],
        axis=1,
    )
    condition_gradient = jax.vjp(jax.nn.silu, cond_full)[1](activated_grad)[0]

    return (
        outputs[0],
        outputs[1],
        input_grads[0],
        input_grads[1],
        condition_gradient,
        image_ada,
        attention_sum[:, : 3 * width].reshape(share, 3, width),
        attention_sum[:, 6 * width : 7 * width].T,
        image_mlp[:, units:],
        image_mlp[:, :units].T,
        text_ada,
        attention_sum[:, 3 * width : 6 * width].reshape(share, 3, width),
        attention_sum[:, 7 * width :].T,
        text_mlp[:, units:],
        text_mlp[:, :units].T,
    )


def solution(mesh):
    image = P("dp", "tensor", None)
    text = P("dp", None, None)
    columns = P("dp", None, "tensor")
    rows = P("tensor", "dp")
    plain = P("dp", "tensor")
    weights = (columns, columns, rows, plain, rows)
    return jax.shard_map(
        functools.partial(on_device, mesh.shape["dp"], mesh.shape["tensor"]),
        mesh=mesh,
        in_specs=(image, text, P("dp", None), P("dp")) + weights + weights + (image, text),
        out_specs=(image, text, image, text, P("dp", None)) + weights + weights,
        check_vma=False,
    )
```

```python
import functools

import jax
import jax.numpy as jnp
from jax import lax
from jax.experimental import pallas as pl
from jax.experimental.pallas import tpu as pltpu
from jax.sharding import PartitionSpec as P

HEAD = 64
LANES = 128
F32 = jnp.float32
BF16 = jnp.bfloat16


def norm_rows(values):
    center = values - jnp.mean(values, axis=-1, keepdims=True)
    inverse = lax.rsqrt(jnp.mean(center * center, axis=-1, keepdims=True) + 1e-06)
    return (center * inverse, inverse)


def norm_back(upstream, normed, inverse):
    first = jnp.mean(upstream, axis=-1, keepdims=True)
    second = jnp.mean(upstream * normed, axis=-1, keepdims=True)
    return inverse * (upstream - first - normed * second)


def gelu_tanh(values):
    return jax.nn.gelu(values, approximate=True)


def spread(vector):
    return vector[:, None, :]


def dot(left, right, left_dim, right_dim):
    return lax.dot_general(
        left, right, (((left_dim,), (right_dim,)), ((), ())), preferred_element_type=F32
    )


def swap(value, bit, size, axis="tensor"):
    return lax.ppermute(value, axis, [(i, i ^ bit) for i in range(size)])


def bits_of(size):
    bits = []
    bit = 1
    while bit < size:
        bits.append(bit)
        bit *= 2
    return bits


def gather_pieces(value, size, axis="tensor"):
    have = {0: value}
    for bit in reversed(bits_of(size)):
        have.update({k ^ bit: swap(v, bit, size, axis) for k, v in list(have.items())})
    return [have[k] for k in range(size)]


def gather_stack(value, size, axis):
    value = value[None]
    for bit in bits_of(size):
        value = jnp.concatenate([value, swap(value, bit, size, axis)], axis=0)
    return value


def scatter_stack(value, size, axis):
    for bit in reversed(bits_of(size)):
        value = value[:bit] + swap(value[bit:], bit, size, axis)
    return value[0]


def sum_all(value, size, axis):
    for bit in bits_of(size):
        value = value + swap(value, bit, size, axis)
    return value


def scatter_sum(pieces, size):
    have = dict(enumerate(pieces))
    for bit in bits_of(size):
        kept = {}
        for k in sorted(have, reverse=True):
            if not k & bit:
                other = swap(have[k ^ bit].astype(BF16), bit, size)
                kept[k] = have[k].astype(F32) + other.astype(F32)
        have = kept
    return have[0]


def after(values, *others):
    return lax.optimization_barrier((values, others))[0]


def ring_of(count):
    return list(range(0, count, 2)) + list(range(1, count, 2))[::-1]


def ring_member(place, count):
    place = lax.rem(place + count, count)
    return jnp.where(place < (count + 1) // 2, 2 * place, 2 * (count - 1 - place) + 1)


def ring_place(member, count):
    return jnp.where(member % 2 == 0, member // 2, count - 1 - member // 2)


def ring_step(value, way, count):
    ring = ring_of(count)
    hops = [(ring[i], ring[(i + way) % count]) for i in range(count)]
    return lax.ppermute(value, "dp", hops)


def ring_gather(block, count):
    share, wide = block.shape
    half = wide // 2 // LANES * LANES
    place = ring_place(lax.axis_index("dp"), count)
    whole = jnp.zeros((count * share, wide), block.dtype)

    def put(whole, value, offset, column):
        row = ring_member(place + offset, count) * share
        return lax.dynamic_update_slice(whole, value, (row, column))

    whole = put(whole, block, 0, 0)
    behind = ahead = block
    for hop in range(1, count // 2):
        behind = ring_step(behind, 1, count)
        ahead = ring_step(ahead, -1, count)
        behind, ahead = yield behind, ahead
        whole = put(put(whole, behind, -hop, 0), ahead, hop, 0)
    behind = ring_step(behind[:, :half], 1, count)
    ahead = ring_step(ahead[:, half:], -1, count)
    behind, ahead = yield behind, ahead
    yield put(put(whole, behind, -(count // 2), 0), ahead, count // 2, half)


def ring_scatter(grad, count):
    wide = grad.shape[1]
    share = grad.shape[0] // count
    half = wide // 2 // LANES * LANES
    place = ring_place(lax.axis_index("dp"), count)

    def own(offset):
        row = ring_member(place + offset, count) * share
        return lax.dynamic_slice_in_dim(grad, row, share, 0).astype(F32)

    far = own(count // 2).astype(BF16)
    behind = ring_step(far[:, :half], 1, count)
    ahead = ring_step(far[:, half:], -1, count)
    behind, ahead = yield behind, ahead
    behind = jnp.pad(behind.astype(F32), ((0, 0), (0, wide - half)))
    ahead = jnp.pad(ahead.astype(F32), ((0, 0), (half, 0)))
    for hop in range(count // 2 - 1, 0, -1):
        behind = ring_step((own(hop) + behind).astype(BF16), 1, count)
        ahead = ring_step((own(-hop) + ahead).astype(BF16), -1, count)
        behind, ahead = yield behind, ahead
        behind, ahead = behind.astype(F32), ahead.astype(F32)
    yield own(0) + behind + ahead


def text_sum(value, size):
    for bit in bits_of(size):
        if bit == 1:
            value = value + swap(value, bit, size)
        else:
            value = lax.reduce_precision(value, 8, 7)
            value = value + swap(value.astype(BF16), bit, size).astype(F32)
    return value


def lane_mask(half, shape):
    lane = lax.broadcasted_iota(jnp.int32, shape, 1)
    return (lane >= HEAD) if half else (lane < HEAD)


def pick(value, half):
    return jnp.where(lane_mask(half, value.shape), value, jnp.zeros_like(value))


def load_rows(refs, store):
    start = 0
    for ref in refs:
        rows = ref.shape[1]
        store[start : start + rows, :] = ref[0]
        start += rows


def attend_kernel(count, *refs):
    queries, keys, values = refs[:count], refs[count : 2 * count], refs[2 * count : 3 * count]
    outs = refs[3 * count : 4 * count]
    sums = refs[4 * count : 5 * count]
    key_all, value_all = refs[5 * count :]
    load_rows(keys, key_all)
    load_rows(values, value_all)
    for index in range(count):
        query = queries[index][0] * jnp.asarray(HEAD**-0.5, BF16)
        halves = []
        for half in range(2):
            scores = dot(key_all[...], pick(query, half), 1, 1)
            highest = jnp.max(scores, axis=0, keepdims=True)
            weights = jnp.exp(scores - highest)
            total = jnp.sum(weights, axis=0, keepdims=True)
            weights = (weights * (1.0 / total)).astype(BF16)
            mixed = dot(value_all[...], weights, 0, 0)
            halves.append(mixed[half * HEAD : (half + 1) * HEAD])
            sums[index][0, 0, half : half + 1, :] = highest + jnp.log(total)
        outs[index][0] = jnp.concatenate(halves, axis=0).T.astype(BF16)


def attend_back_kernel(count, groups, *refs):
    queries, keys, values = refs[:count], refs[count : 2 * count], refs[2 * count : 3 * count]
    upstreams = refs[3 * count : 4 * count]
    sums = refs[4 * count : 5 * count]
    outs = refs[5 * count : 6 * count]
    key_all, value_all, key_grad, value_grad = refs[6 * count :]
    load_rows(keys, key_all)
    load_rows(values, value_all)
    pair = pl.program_id(1)
    scale = jnp.asarray(HEAD**-0.5, BF16)
    query_lanes = pl.ds(pl.multiple_of(pair * LANES, LANES), LANES)
    key_lanes = pl.ds(pl.multiple_of((groups + pair) * LANES, LANES), LANES)
    value_lanes = pl.ds(pl.multiple_of((2 * groups + pair) * LANES, LANES), LANES)
    for index in range(count):
        query = queries[index][0] * scale
        upstream = upstreams[index][0]
        halves = []
        for half in range(2):
            query_half = pick(query, half)
            upstream_half = pick(upstream, half)
            scores = dot(key_all[...], query_half, 1, 1)
            weights = jnp.exp(scores - sums[index][0, 0, half : half + 1, :])
            along = dot(value_all[...], upstream_half, 1, 1)
            value_part = dot(weights.astype(BF16), upstream_half, 1, 0)
            product = weights * along
            score_grad = (product - weights * jnp.sum(product, axis=0, keepdims=True)).astype(BF16)
            key_part = dot(score_grad, query_half, 1, 0)
            if index == 0 and half == 0:
                value_grad[...] = value_part
                key_grad[...] = key_part
            else:
                value_grad[...] += value_part
                key_grad[...] += key_part
            mixed = dot(key_all[...], score_grad, 0, 0)
            halves.append(mixed[half * HEAD : (half + 1) * HEAD])
        query_grad = jnp.concatenate(halves, axis=0).T * HEAD**-0.5
        outs[index][0, :, query_lanes] = query_grad.astype(BF16)
    start = 0
    for index in range(count):
        rows = outs[index].shape[1]
        outs[index][0, :, key_lanes] = key_grad[start : start + rows, :].astype(BF16)
        outs[index][0, :, value_lanes] = value_grad[start : start + rows, :].astype(BF16)
        start += rows


def lane_blocks(parts, offset):
    return [
        pl.BlockSpec((1, part.shape[1], LANES), lambda s, p, o=offset: (s, 0, o + p))
        for part in parts
    ]


def widen(part, copies):
    slots, rows, width = part.shape
    width = width // copies
    extra = -width % LANES
    if not extra:
        return part
    part = jnp.pad(part.reshape(slots, rows, copies, width), ((0, 0), (0, 0), (0, 0), (0, extra)))
    return part.reshape(slots, rows, copies * (width + extra))


def narrow(part, copies, width):
    slots, rows, wide = part.shape
    wide = wide // copies
    if wide == width:
        return part
    return part.reshape(slots, rows, copies, wide)[..., :width].reshape(slots, rows, -1)


def attention_cost(slots, rows, width, products):
    return pl.CostEstimate(
        flops=products * 8 * slots * rows * rows * width,
        transcendentals=slots * rows * rows * (width // HEAD),
        bytes_accessed=slots * rows * width * 2 * (4 + 3 * (products > 2)),
    )


def attend(parts):
    slots = parts[0].shape[0]
    width = parts[0].shape[2] // 3
    parts = [widen(part, 3) for part in parts]
    count = len(parts)
    wide = parts[0].shape[2] // 3
    groups = wide // LANES
    total = sum(part.shape[1] for part in parts)
    outs = pl.pallas_call(
        functools.partial(attend_kernel, count),
        grid=(slots, groups),
        in_specs=lane_blocks(parts, 0) + lane_blocks(parts, groups) + lane_blocks(parts, 2 * groups),
        out_specs=lane_blocks(parts, 0)
        + [
            pl.BlockSpec((1, 1, 2, part.shape[1]), lambda s, p: (s, p, 0, 0)) for part in parts
        ],
        out_shape=[jax.ShapeDtypeStruct((slots, part.shape[1], wide), BF16) for part in parts]
        + [jax.ShapeDtypeStruct((slots, groups, 2, part.shape[1]), F32) for part in parts],
        scratch_shapes=[pltpu.VMEM((total, LANES), BF16)] * 2,
        compiler_params=pltpu.CompilerParams(vmem_limit_bytes=48 * 1024 * 1024),
        cost_estimate=attention_cost(slots, total, wide, 2),
        name="attend",
    )(*parts, *parts, *parts)
    return [narrow(out, 1, width) for out in outs[:count]], outs[count:]


def attend_back(parts, upstreams, sums):
    slots = parts[0].shape[0]
    width = parts[0].shape[2] // 3
    parts = [widen(part, 3) for part in parts]
    upstreams = [widen(part, 1) for part in upstreams]
    count = len(parts)
    wide = parts[0].shape[2] // 3
    groups = wide // LANES
    total = sum(part.shape[1] for part in parts)
    outs = pl.pallas_call(
        functools.partial(attend_back_kernel, count, groups),
        grid=(slots, groups),
        in_specs=lane_blocks(parts, 0)
        + lane_blocks(parts, groups)
        + lane_blocks(parts, 2 * groups)
        + lane_blocks(upstreams, 0)
        + [
            pl.BlockSpec((1, 1, 2, part.shape[1]), lambda s, p: (s, p, 0, 0)) for part in parts
        ],
        out_specs=[
            pl.BlockSpec((1, part.shape[1], 3 * wide), lambda s, p: (s, 0, 0)) for part in parts
        ],
        out_shape=[jax.ShapeDtypeStruct((slots, part.shape[1], 3 * wide), BF16) for part in parts],
        scratch_shapes=[pltpu.VMEM((total, LANES), BF16)] * 2 + [pltpu.VMEM((total, LANES), F32)] * 2,
        compiler_params=pltpu.CompilerParams(vmem_limit_bytes=48 * 1024 * 1024),
        cost_estimate=attention_cost(slots, total, wide, 5),
        name="attend_back",
    )(*parts, *parts, *parts, *upstreams, *sums)
    return [narrow(out, 3, width) for out in outs]


def rows_kernel(count, *refs):
    lefts, rights, out = refs[:count], refs[count : 2 * count], refs[-1]
    total = None
    for left, right in zip(lefts, rights):
        for slot in range(left.shape[0]):
            part = dot(left[slot], right[slot], 0, 0)
            total = part if total is None else total + part
    out[...] = total.astype(BF16)


def weight_grad(pairs):
    joined = None
    rows = pairs[0][0][0].shape[-1]
    wide = sum(rights[0].shape[-1] for _, rights in pairs)
    start = 0
    for lefts, rights in pairs:
        part = rights[0].shape[-1]
        if part % LANES or start % part:
            return jnp.concatenate([plain_grad(*pair) for pair in pairs], axis=1)
        count = len(lefts)
        step = 256
        ins = [
            pl.BlockSpec((left.shape[0], left.shape[1], step), lambda i: (0, 0, i))
            for left in lefts
        ] + [
            pl.BlockSpec(right.shape, lambda i: (0, 0, 0), pipeline_mode=pl.Buffered(1))
            for right in rights
        ]
        operands = (*lefts, *rights)
        if joined is not None:
            ins.append(pl.BlockSpec(memory_space=pl.ANY))
            operands += (joined,)
        joined = pl.pallas_call(
            functools.partial(rows_kernel, count),
            grid=(rows // step,),
            in_specs=ins,
            out_specs=pl.BlockSpec((step, part), lambda i, c=start // part: (i, c)),
            out_shape=jax.ShapeDtypeStruct((rows, wide), BF16),
            input_output_aliases={} if joined is None else {2 * count: 0},
            compiler_params=pltpu.CompilerParams(vmem_limit_bytes=48 * 1024 * 1024),
            cost_estimate=pl.CostEstimate(flops=0, transcendentals=0, bytes_accessed=1024),
            name="weight_grad",
        )(*operands)
        start += part
    return joined


def plain_grad(lefts, rights):
    left = jnp.concatenate([v.reshape(-1, v.shape[-1]) for v in lefts], axis=0)
    right = jnp.concatenate([v.reshape(-1, v.shape[-1]) for v in rights], axis=0)
    return dot(left, right, 0, 0).astype(BF16)


def on_device(
    group_count,
    tensor_size,
    image_tokens,
    text_tokens,
    condition,
    group_size,
    image_modulation,
    image_attention_in,
    image_attention_out,
    image_hidden_in,
    image_hidden_out,
    text_modulation,
    text_attention_in,
    text_attention_out,
    text_hidden_in,
    text_hidden_out,
    image_cotangent,
    text_cotangent,
):
    size = tensor_size
    slots, image_length, model = image_tokens.shape
    text_length = text_tokens.shape[1]
    share, _, width = image_attention_in.shape
    units = image_hidden_in.shape[1]
    tensor_rank = lax.axis_index("tensor")
    group_rank = lax.axis_index("dp")

    def gathered(*blocks):
        joined = blocks[0] if len(blocks) == 1 else jnp.concatenate(blocks, axis=1)
        return lax.all_gather(joined, "dp", axis=0, tiled=True)

    image_in = gathered(image_attention_in.reshape(share, 3 * width))
    packed_mid = gathered(image_attention_out.T, text_attention_out.T, image_hidden_in)
    image_down = gathered(image_hidden_out.T)
    packed_text = gathered(text_hidden_in, text_hidden_out.T)
    text_ring = ring_gather(text_attention_in.reshape(share, 3 * width), group_count)
    text_hop = next(text_ring)
    weight_out = (packed_mid[:, :width], packed_mid[:, width : 2 * width])

    alive = (jnp.arange(slots) < group_size[0]).astype(F32)[:, None, None]
    cond_full = condition.astype(F32)
    activated_low = jax.nn.silu(cond_full).astype(BF16)
    activated_all = gather_stack(activated_low, group_count, "dp").reshape(-1, model)
    activated_all, text_hop = lax.optimization_barrier((activated_all, text_hop))
    text_hop = text_ring.send(text_hop)
    activated_own = lax.dynamic_slice_in_dim(activated_all, group_rank * share, share, 1)
    all_slots = activated_own.shape[0]
    mod_parts = jnp.concatenate(
        [
            dot(activated_own, image_modulation.reshape(share, 6 * width), 1, 0),
            dot(activated_own, text_modulation.reshape(share, 6 * width), 1, 0),
        ],
        axis=1,
    ).reshape(group_count, slots, 12 * width)
    for _ in range(group_count // 2 - 3):
        mod_parts, text_hop = lax.optimization_barrier((mod_parts, text_hop))
        text_hop = text_ring.send(text_hop)
    mod_own = scatter_stack(mod_parts, group_count, "dp")
    mod_own, text_hop = lax.optimization_barrier((mod_own, text_hop))
    text_hop = text_ring.send(text_hop)
    modulations = lax.all_gather(
        mod_own.reshape(slots, 2, 6, width), "tensor", axis=3, tiled=True
    )
    modulations, text_hop = lax.optimization_barrier((modulations, text_hop))
    weight_in = (image_in, text_ring.send(text_hop))
    mods = (modulations[:, 0], modulations[:, 1])

    tokens = (image_tokens.astype(F32), text_tokens.astype(F32))
    outgoing = (image_cotangent.astype(F32) * alive, text_cotangent.astype(F32) * alive)

    def collect(stream, values):
        values = values.astype(BF16)
        return [values] if stream else gather_pieces(values, size)

    def apply(pieces, weight, weight_dim, low):
        return [
            dot(piece, weight, 2, weight_dim).astype(BF16 if low else F32) for piece in pieces
        ]

    def reduced(stream, pieces):
        return text_sum(pieces[0], size) if stream else scatter_sum(pieces, size)

    def scattered(grad):
        return lax.psum_scatter(grad, "dp", scatter_dimension=0, tiled=True).astype(F32)

    first_saved = []
    packed = []
    down_pieces = []
    for stream in range(2):
        mod = mods[stream]
        normed, inverse = norm_rows(tokens[stream])
        first_in = normed * (1.0 + spread(mod[:, 1])) + spread(mod[:, 0])
        pieces = collect(stream, first_in)
        packed.append(apply(pieces, weight_in[stream], 0, True))
        first_saved.append((normed, inverse, pieces))
        down = (outgoing[stream] * spread(mod[:, 5])).astype(BF16)
        down_pieces.append(collect(stream, after(down, pieces)))
    parts = packed[0] + packed[1]
    attended, sums = attend(parts)
    attended, down_pieces = lax.optimization_barrier((attended, down_pieces))
    attended_parts = (attended[:-1], attended[-1:])

    middles = [None, None]
    actives = [None, None]
    middle_grads = [None, None]
    branch_grads = [None, None]
    lows = [None, None]
    stats = [None, None]
    upstreams = [None, None]

    def stream_branch(stream):
        mod = mods[stream]
        branch = reduced(stream, apply(attended_parts[stream], weight_out[stream], 1, False))
        middle = tokens[stream] + spread(mod[:, 2]) * branch
        normed, inverse = norm_rows(middle)
        second_in = normed * (1.0 + spread(mod[:, 4])) + spread(mod[:, 3])
        middles[stream] = middle
        return branch, normed, inverse, collect(stream, second_in)

    def stream_products(stream, pieces):
        hidden = apply(pieces, weight_up[stream], 0, False)
        active = [gelu_tanh(value).astype(BF16) for value in hidden]
        active_grad = apply(down_pieces[stream], weight_down[stream], 0, False)
        hidden_grad = [
            jax.vjp(gelu_tanh, value)[1](grad)[0].astype(BF16)
            for value, grad in zip(hidden, active_grad)
        ]
        products = apply(hidden_grad, weight_up[stream], 1, False)
        late = after((down_pieces[stream], active, pieces, hidden_grad), products)
        actives[stream] = active
        return products, late

    def stream_back(stream, products, branch, normed, inverse, pieces):
        mod = mods[stream]
        second_grad = reduced(stream, products)
        shift_two_grad = jnp.sum(second_grad, axis=1)
        scale_two_grad = jnp.sum(second_grad * normed, axis=1)
        middle_grad = outgoing[stream] + norm_back(
            second_grad * (1.0 + spread(mod[:, 4])), normed, inverse
        )
        gate_one_grad = jnp.sum(middle_grad * branch, axis=1)
        low = (middle_grad * spread(mod[:, 2])).astype(BF16)
        branch_grads[stream] = collect(stream, low)
        upstreams[stream] = apply(branch_grads[stream], weight_out[stream], 0, True)
        middle_grads[stream] = middle_grad
        stats[stream] = (gate_one_grad, shift_two_grad, scale_two_grad)
        return low
    image_state = stream_branch(0)
    text_state = stream_branch(1)
    weight_up = [packed_mid[:, 2 * width :], None]
    weight_down = [image_down, None]
    products, image_late = stream_products(0, image_state[-1])
    image_low = stream_back(0, products, *image_state)
    packed_text = after(packed_text, image_low)
    weight_up[1] = packed_text[:, :units]
    weight_down[1] = packed_text[:, units:]
    products, text_late = stream_products(1, text_state[-1])
    image_late = after(image_late, products)
    stream_back(1, products, *text_state)
    mlp_grads = [weight_grad([late[:2], late[2:]]) for late in (image_late, text_late)]
    text_ring = ring_scatter(mlp_grads[1], group_count)
    text_hop = next(text_ring)
    image_mlp = scattered(mlp_grads[0])
    upstreams, text_hop = lax.optimization_barrier((upstreams, text_hop))
    text_hop = text_ring.send(text_hop)

    packed_grads = attend_back(parts, upstreams[0] + upstreams[1], sums)
    packed_grads, text_hop = lax.optimization_barrier((packed_grads, text_hop))
    text_hop = text_ring.send(text_hop)
    attention_grad = weight_grad(
        [
            (first_saved[0][2], packed_grads[:-1]),
            (first_saved[1][2], packed_grads[-1:]),
            (branch_grads[0], attended_parts[0]),
            (branch_grads[1], attended_parts[1]),
        ]
    )
    attention_sum = scattered(attention_grad)
    packed_grads = after(packed_grads, attention_grad)
    actives = after(actives, packed_grads)
    packed_grads = (packed_grads[:-1], packed_grads[-1:])
    outputs = [None, None]
    input_grads = [None, None]
    mod_grads = [None, None]
    for stream in (1, 0):
        mod = mods[stream]
        normed, inverse, _ = first_saved[stream]
        gate_one_grad, shift_two_grad, scale_two_grad = stats[stream]
        branch_two = reduced(stream, apply(actives[stream], weight_down[stream], 1, False))
        result = middles[stream] + spread(mod[:, 5]) * branch_two
        outputs[stream] = (result * alive).astype(BF16)
        gate_two_grad = jnp.sum(outgoing[stream] * branch_two, axis=1)
        first_grad = reduced(stream, apply(packed_grads[stream], weight_in[stream], 1, False))
        first_grad, text_hop = lax.optimization_barrier((first_grad, text_hop))
        text_hop = text_ring.send(text_hop)
        shift_one_grad = jnp.sum(first_grad, axis=1)
        scale_one_grad = jnp.sum(first_grad * normed, axis=1)
        input_grads[stream] = middle_grads[stream] + norm_back(
            first_grad * (1.0 + spread(mod[:, 1])), normed, inverse
        )
        mod_grads[stream] = jnp.stack(
            [
                shift_one_grad,
                scale_one_grad,
                gate_one_grad,
                shift_two_grad,
                scale_two_grad,
                gate_two_grad,
            ],
            axis=1,
        )
    for _ in range(group_count // 2 - 4):
        text_hop = text_ring.send(text_hop)
    text_mlp = text_hop

    image_blocks = jnp.stack(
        [
            lax.dynamic_slice_in_dim(mod_grads[0], (tensor_rank ^ k) * width, width, 2)
            for k in range(size)
        ]
    )
    image_share = scatter_stack(image_blocks, size, "tensor")
    text_share = lax.dynamic_slice_in_dim(mod_grads[1], tensor_rank * width, width, 2)
    share_low = jnp.stack([image_share, text_share], axis=1).astype(BF16)
    share_all = gather_stack(share_low, group_count, "dp").reshape(all_slots, 2, 6, width)
    image_all = share_all[:, 0].reshape(all_slots, 6 * width)
    text_all = share_all[:, 1].reshape(all_slots, 6 * width)
    image_ada = dot(activated_own, image_all, 0, 0).reshape(share, 6, width)
    text_ada = dot(activated_own, text_all, 0, 0).reshape(share, 6, width)
    activated_part = dot(image_all, image_modulation.reshape(share, 6 * width), 1, 1) + dot(
        text_all, text_modulation.reshape(share, 6 * width), 1, 1
    )
    activated_part = sum_all(activated_part, size, "tensor").reshape(group_count, slots, share)
    activated_rows = gather_stack(activated_part, group_count, "dp")
    activated_rows = jnp.stack([activated_rows[k, k] for k in range(group_count)])
    group_order = group_rank ^ jnp.arange(group_count)
    activated_grad = jnp.concatenate(
        [
            lax.dynamic_index_in_dim(activated_rows, group_order[k], 0, keepdims=False)
            for k in range(group_count)
        ],
        axis=1,
    )
    condition_gradient = jax.vjp(jax.nn.silu, cond_full)[1](activated_grad)[0]

    return (
        outputs[0],
        outputs[1],
        input_grads[0],
        input_grads[1],
        condition_gradient,
        image_ada,
        attention_sum[:, : 3 * width].reshape(share, 3, width),
        attention_sum[:, 6 * width : 7 * width].T,
        image_mlp[:, units:],
        image_mlp[:, :units].T,
        text_ada,
        attention_sum[:, 3 * width : 6 * width].reshape(share, 3, width),
        attention_sum[:, 7 * width :].T,
        text_mlp[:, units:],
        text_mlp[:, :units].T,
    )


def solution(mesh):
    image = P("dp", "tensor", None)
    text = P("dp", None, None)
    columns = P("dp", None, "tensor")
    rows = P("tensor", "dp")
    plain = P("dp", "tensor")
    weights = (columns, columns, rows, plain, rows)
    return jax.shard_map(
        functools.partial(on_device, mesh.shape["dp"], mesh.shape["tensor"]),
        mesh=mesh,
        in_specs=(image, text, P("dp", None), P("dp")) + weights + weights + (image, text),
        out_specs=(image, text, image, text, P("dp", None)) + weights + weights,
        check_vma=False,
    )
```

```python
import functools
import math

import jax
import jax.numpy as jnp
from jax import lax
from jax.experimental import pallas as pl
from jax.experimental.pallas import tpu as pltpu
from jax.sharding import PartitionSpec as P

HEAD = 64
LANES = 128
F32 = jnp.float32
BF16 = jnp.bfloat16


def norm_rows(values):
    center = values - jnp.mean(values, axis=-1, keepdims=True)
    inverse = lax.rsqrt(jnp.mean(center * center, axis=-1, keepdims=True) + 1e-06)
    return (center * inverse, inverse)


def norm_back(upstream, normed, inverse):
    first = jnp.mean(upstream, axis=-1, keepdims=True)
    second = jnp.mean(upstream * normed, axis=-1, keepdims=True)
    return inverse * (upstream - first - normed * second)


def gelu_tanh(values):
    return jax.nn.gelu(values, approximate=True)


def spread(vector):
    return vector[:, None, :]


def dot(left, right, left_dim, right_dim):
    return lax.dot_general(
        left, right, (((left_dim,), (right_dim,)), ((), ())), preferred_element_type=F32
    )


def swap(value, bit, size, axis="tensor"):
    return lax.ppermute(value, axis, [(i, i ^ bit) for i in range(size)])


def bits_of(size):
    bits = []
    bit = 1
    while bit < size:
        bits.append(bit)
        bit *= 2
    return bits


def gather_pieces(value, size, axis="tensor", gate=None):
    have = {0: value}
    for bit in reversed(bits_of(size)):
        if bit == 1 and gate is not None:
            have = after(have, gate)
        have.update({k ^ bit: swap(v, bit, size, axis) for k, v in list(have.items())})
    return [have[k] for k in range(size)]


def gather_stack(value, size, axis):
    value = value[None]
    for bit in bits_of(size):
        value = jnp.concatenate([value, swap(value, bit, size, axis)], axis=0)
    return value


def scatter_stack(value, size, axis):
    for bit in reversed(bits_of(size)):
        value = value[:bit] + swap(value[bit:], bit, size, axis)
    return value[0]


def sum_all(value, size, axis):
    for bit in bits_of(size):
        value = value + swap(value, bit, size, axis)
    return value


def scatter_start(pieces, size):
    have = dict(enumerate(pieces))
    for bit in bits_of(size)[:-1]:
        kept = {}
        for k in sorted(have, reverse=True):
            if not k & bit:
                other = swap(have[k ^ bit].astype(BF16), bit, size)
                kept[k] = have[k].astype(F32) + other.astype(F32)
        have = kept
    kept, sent = (have[k] for k in sorted(have))
    return kept, sent.astype(BF16)


def scatter_end(kept, sent, size):
    return kept.astype(F32) + swap(sent, size // 2, size).astype(F32)


def after(values, *others):
    return lax.optimization_barrier((values, others))[0]


def ring_of(count):
    return list(range(0, count, 2)) + list(range(1, count, 2))[::-1]


def ring_member(place, count):
    place = lax.rem(place + count, count)
    return jnp.where(place < (count + 1) // 2, 2 * place, 2 * (count - 1 - place) + 1)


def ring_place(member, count):
    return jnp.where(member % 2 == 0, member // 2, count - 1 - member // 2)


def ring_step(value, way, count):
    ring = ring_of(count)
    hops = [(ring[i], ring[(i + way) % count]) for i in range(count)]
    return lax.ppermute(value, "dp", hops)


def ring_gather(block, count):
    share, wide = block.shape
    half = wide // 2 // LANES * LANES
    place = ring_place(lax.axis_index("dp"), count)
    whole = jnp.zeros((count * share, wide), block.dtype)

    def put(whole, value, offset, column):
        row = ring_member(place + offset, count) * share
        return lax.dynamic_update_slice(whole, value, (row, column))

    whole = put(whole, block, 0, 0)
    behind = ahead = block
    for hop in range(1, count // 2):
        behind = ring_step(behind, 1, count)
        ahead = ring_step(ahead, -1, count)
        behind, ahead = yield behind, ahead
        whole = put(put(whole, behind, -hop, 0), ahead, hop, 0)
    behind = ring_step(behind[:, :half], 1, count)
    ahead = ring_step(ahead[:, half:], -1, count)
    behind, ahead = yield behind, ahead
    yield put(put(whole, behind, -(count // 2), 0), ahead, count // 2, half)


def ring_scatter(grad, count):
    wide = grad.shape[1]
    share = grad.shape[0] // count
    half = wide // 2 // LANES * LANES
    place = ring_place(lax.axis_index("dp"), count)

    def own(offset):
        row = ring_member(place + offset, count) * share
        return lax.dynamic_slice_in_dim(grad, row, share, 0).astype(F32)

    far = own(count // 2).astype(BF16)
    behind = ring_step(far[:, :half], 1, count)
    ahead = ring_step(far[:, half:], -1, count)
    behind, ahead = yield behind, ahead
    behind = jnp.pad(behind.astype(F32), ((0, 0), (0, wide - half)))
    ahead = jnp.pad(ahead.astype(F32), ((0, 0), (half, 0)))
    for hop in range(count // 2 - 1, 0, -1):
        behind = ring_step((own(hop) + behind).astype(BF16), 1, count)
        ahead = ring_step((own(-hop) + ahead).astype(BF16), -1, count)
        behind, ahead = yield behind, ahead
        behind, ahead = behind.astype(F32), ahead.astype(F32)
    yield own(0) + behind + ahead


def text_start(value, size):
    for bit in bits_of(size)[:-1]:
        if bit > 1:
            value = lax.reduce_precision(value, 8, 7)
            value = value + swap(value.astype(BF16), bit, size).astype(F32)
        else:
            value = value + swap(value, bit, size)
    value = lax.reduce_precision(value, 8, 7)
    return value, value.astype(BF16)


def lane_mask(half, shape):
    lane = lax.broadcasted_iota(jnp.int32, shape, 1)
    return (lane >= HEAD) if half else (lane < HEAD)


def pick(value, half):
    return jnp.where(lane_mask(half, value.shape), value, jnp.zeros_like(value))


def load_rows(refs, store):
    start = 0
    for ref in refs:
        rows = ref.shape[1]
        store[start : start + rows, :] = ref[0]
        start += rows


def attend_kernel(count, *refs):
    queries, keys, values = refs[:count], refs[count : 2 * count], refs[2 * count : 3 * count]
    outs = refs[3 * count : 4 * count]
    sums = refs[4 * count : 5 * count]
    key_all, value_all = refs[5 * count :]
    load_rows(keys, key_all)
    load_rows(values, value_all)
    for index in range(count):
        query = queries[index][0] * jnp.asarray(HEAD**-0.5, BF16)
        halves = []
        for half in range(2):
            scores = dot(key_all[...], pick(query, half), 1, 1)
            highest = jnp.max(scores, axis=0, keepdims=True)
            weights = jnp.exp(scores - highest)
            total = jnp.sum(weights, axis=0, keepdims=True)
            weights = (weights * (1.0 / total)).astype(BF16)
            mixed = dot(value_all[...], weights, 0, 0)
            halves.append(mixed[half * HEAD : (half + 1) * HEAD])
            sums[index][0, 0, half : half + 1, :] = highest + jnp.log(total)
        outs[index][0] = jnp.concatenate(halves, axis=0).T.astype(BF16)


def attend_back_kernel(count, asked, groups, last, *refs):
    refs = list(refs)

    def take(number):
        return [refs.pop(0) for _ in range(number)]

    keys, values = take(count), take(count)
    queries, upstreams, sums = take(asked), take(asked), take(asked)
    if last:
        before = take(2)
        query_grads = take(count - asked)
        outs = take(count)
    else:
        outs = take(asked)
        totals = take(2)
    key_all, value_all, key_grad, value_grad = refs
    load_rows(keys, key_all)
    load_rows(values, value_all)
    pair = pl.program_id(1)
    scale = jnp.asarray(HEAD**-0.5, BF16)
    for index in range(asked):
        query = queries[index][0] * scale
        upstream = upstreams[index][0]
        halves = []
        for half in range(2):
            query_half = pick(query, half)
            upstream_half = pick(upstream, half)
            scores = dot(key_all[...], query_half, 1, 1)
            weights = jnp.exp(scores - sums[index][0, 0, half : half + 1, :])
            along = dot(value_all[...], upstream_half, 1, 1)
            value_part = dot(weights.astype(BF16), upstream_half, 1, 0)
            product = weights * along
            score_grad = (product - weights * jnp.sum(product, axis=0, keepdims=True)).astype(BF16)
            key_part = dot(score_grad, query_half, 1, 0)
            if index == 0 and half == 0 and last:
                value_grad[...] = before[1][0, 0] + value_part
                key_grad[...] = before[0][0, 0] + key_part
            elif index == 0 and half == 0:
                value_grad[...] = value_part
                key_grad[...] = key_part
            else:
                value_grad[...] += value_part
                key_grad[...] += key_part
            mixed = dot(key_all[...], score_grad, 0, 0)
            halves.append(mixed[half * HEAD : (half + 1) * HEAD])
        query_grad = (jnp.concatenate(halves, axis=0).T * HEAD**-0.5).astype(BF16)
        if last:
            lanes = pl.ds(pl.multiple_of(pair * LANES, LANES), LANES)
            outs[count - asked + index][0, :, lanes] = query_grad
        else:
            outs[index][0] = query_grad
    if not last:
        totals[0][0, 0] = key_grad[...]
        totals[1][0, 0] = value_grad[...]
        return
    for index, query_grad in enumerate(query_grads):
        lanes = pl.ds(pl.multiple_of(pair * LANES, LANES), LANES)
        outs[index][0, :, lanes] = query_grad[0]
    start = 0
    for out in outs:
        rows = out.shape[1]
        for number, grad in ((1, key_grad), (2, value_grad)):
            lanes = pl.ds(pl.multiple_of((number * groups + pair) * LANES, LANES), LANES)
            out[0, :, lanes] = grad[start : start + rows, :].astype(BF16)
        start += rows


def lane_blocks(parts, offset):
    return [
        pl.BlockSpec((1, part.shape[1], LANES), lambda s, p, o=offset: (s, 0, o + p))
        for part in parts
    ]


def widen(part, copies):
    slots, rows, width = part.shape
    width = width // copies
    extra = -width % LANES
    if not extra:
        return part
    part = jnp.pad(part.reshape(slots, rows, copies, width), ((0, 0), (0, 0), (0, 0), (0, extra)))
    return part.reshape(slots, rows, copies * (width + extra))


def narrow(part, copies, width):
    slots, rows, wide = part.shape
    wide = wide // copies
    if wide == width:
        return part
    return part.reshape(slots, rows, copies, wide)[..., :width].reshape(slots, rows, -1)


def attention_cost(slots, rows, width, products):
    return pl.CostEstimate(
        flops=products * 8 * slots * rows * rows * width,
        transcendentals=slots * rows * rows * (width // HEAD),
        bytes_accessed=slots * rows * width * 2 * (4 + 3 * (products > 2)),
    )


def attend(parts):
    slots = parts[0].shape[0]
    width = parts[0].shape[2] // 3
    parts = [widen(part, 3) for part in parts]
    count = len(parts)
    wide = parts[0].shape[2] // 3
    groups = wide // LANES
    total = sum(part.shape[1] for part in parts)
    outs = pl.pallas_call(
        functools.partial(attend_kernel, count),
        grid=(slots, groups),
        in_specs=lane_blocks(parts, 0) + lane_blocks(parts, groups) + lane_blocks(parts, 2 * groups),
        out_specs=lane_blocks(parts, 0)
        + [
            pl.BlockSpec((1, 1, 2, part.shape[1]), lambda s, p: (s, p, 0, 0)) for part in parts
        ],
        out_shape=[jax.ShapeDtypeStruct((slots, part.shape[1], wide), BF16) for part in parts]
        + [jax.ShapeDtypeStruct((slots, groups, 2, part.shape[1]), F32) for part in parts],
        scratch_shapes=[pltpu.VMEM((total, LANES), BF16)] * 2,
        compiler_params=pltpu.CompilerParams(vmem_limit_bytes=48 * 1024 * 1024),
        cost_estimate=attention_cost(slots, total, wide, 2),
        name="attend",
    )(*parts, *parts, *parts)
    return [narrow(out, 1, width) for out in outs[:count]], outs[count:]


def attend_back(parts, asked, upstreams, sums, before=None):
    slots = parts[0].shape[0]
    width = parts[0].shape[2] // 3
    parts = [widen(part, 3) for part in parts]
    upstreams = [widen(part, 1) for part in upstreams]
    last = before is not None
    count = len(parts)
    queries = parts[-asked:] if last else parts[:asked]
    wide = parts[0].shape[2] // 3
    groups = wide // LANES
    total = sum(part.shape[1] for part in parts)
    whole = pl.BlockSpec((1, 1, total, LANES), lambda s, p: (s, p, 0, 0))
    ins = lane_blocks(parts, groups) + lane_blocks(parts, 2 * groups) + lane_blocks(queries, 0)
    ins += lane_blocks(upstreams, 0)
    ins += [pl.BlockSpec((1, 1, 2, part.shape[1]), lambda s, p: (s, p, 0, 0)) for part in queries]
    operands = [*parts, *parts, *queries, *upstreams, *sums]
    if last:
        query_grads, totals = before
        ins += [whole, whole] + lane_blocks(query_grads, 0)
        operands += [*totals, *query_grads]
        out_specs = [
            pl.BlockSpec((1, part.shape[1], 3 * wide), lambda s, p: (s, 0, 0)) for part in parts
        ]
        out_shape = [
            jax.ShapeDtypeStruct((slots, part.shape[1], 3 * wide), BF16) for part in parts
        ]
    else:
        out_specs = lane_blocks(queries, 0) + [whole, whole]
        out_shape = [
            jax.ShapeDtypeStruct((slots, part.shape[1], wide), BF16) for part in queries
        ] + [jax.ShapeDtypeStruct((slots, groups, total, LANES), F32)] * 2
    outs = pl.pallas_call(
        functools.partial(attend_back_kernel, count, asked, groups, last),
        grid=(slots, groups),
        in_specs=ins,
        out_specs=out_specs,
        out_shape=out_shape,
        scratch_shapes=[pltpu.VMEM((total, LANES), BF16)] * 2 + [pltpu.VMEM((total, LANES), F32)] * 2,
        compiler_params=pltpu.CompilerParams(vmem_limit_bytes=48 * 1024 * 1024),
        cost_estimate=attention_cost(slots, total, wide, 2 if last else 5),
        name="attend_back",
    )(*operands)
    if last:
        return [narrow(out, 3, width) for out in outs]
    return outs[:asked], outs[asked:]


def rows_kernel(count, *refs):
    lefts, rights, out = refs[:count], refs[count : 2 * count], refs[-1]
    total = None
    for left, right in zip(lefts, rights):
        for slot in range(left.shape[0]):
            part = dot(left[slot], right[slot], 0, 0)
            total = part if total is None else total + part
    out[...] = total.astype(BF16)


def weight_grad(pairs):
    joined = None
    rows = pairs[0][0][0].shape[-1]
    wide = sum(rights[0].shape[-1] for _, rights in pairs)
    start = 0
    for lefts, rights in pairs:
        part = rights[0].shape[-1]
        if part % LANES or start % part:
            return jnp.concatenate([plain_grad(*pair) for pair in pairs], axis=1)
        count = len(lefts)
        step = 256
        ins = [
            pl.BlockSpec((left.shape[0], left.shape[1], step), lambda i: (0, 0, i))
            for left in lefts
        ] + [
            pl.BlockSpec(right.shape, lambda i: (0, 0, 0), pipeline_mode=pl.Buffered(1))
            for right in rights
        ]
        operands = (*lefts, *rights)
        if joined is not None:
            ins.append(pl.BlockSpec(memory_space=pl.ANY))
            operands += (joined,)
        joined = pl.pallas_call(
            functools.partial(rows_kernel, count),
            grid=(rows // step,),
            in_specs=ins,
            out_specs=pl.BlockSpec((step, part), lambda i, c=start // part: (i, c)),
            out_shape=jax.ShapeDtypeStruct((rows, wide), BF16),
            input_output_aliases={} if joined is None else {2 * count: 0},
            compiler_params=pltpu.CompilerParams(vmem_limit_bytes=48 * 1024 * 1024),
            cost_estimate=pl.CostEstimate(flops=0, transcendentals=0, bytes_accessed=1024),
            name="weight_grad",
        )(*operands)
        start += part
    return joined


NO_COST = pl.CostEstimate(flops=0, transcendentals=0, bytes_accessed=1024)
LIMIT = pltpu.CompilerParams(vmem_limit_bytes=48 * 1024 * 1024)


def tile_of(wide, start, most):
    return max(t for t in range(LANES, most + 1, LANES) if wide % t == 0 and start % t == 0)


def fits(weight):
    _, start, wide = weight
    return wide % LANES == 0 and start % LANES == 0


def cut(weight):
    array, start, wide = weight
    return array[:, start : start + wide]


def product_kernel(count, weight_dim, *refs):
    pieces, weight, outs, rows_all = refs[:count], refs[count], refs[count + 1 : -1], refs[-1]

    @pl.when(pl.program_id(1) == 0)
    def _():
        load_rows(pieces, rows_all)

    total = dot(rows_all[...], weight[...], 1, weight_dim)
    start = 0
    for out in outs:
        rows = out.shape[1]
        out[0] = total[start : start + rows].astype(out.dtype)
        start += rows


def products_of(pieces, weight, weight_dim, kinds):
    array, start, wide = weight
    if not fits(weight) or (weight_dim and start % wide):
        return [
            dot(piece, cut(weight), 2, weight_dim).astype(kind)
            for piece, kind in zip(pieces, kinds)
        ]
    count = len(pieces)
    slots, _, depth = pieces[0].shape
    total = sum(piece.shape[1] for piece in pieces)
    if weight_dim:
        result = array.shape[0]
        tile = tile_of(result, 0, 768)
        block = pl.BlockSpec((tile, wide), lambda s, j: (j, start // wide))
    else:
        result = wide
        tile = tile_of(wide, start, 768)
        block = pl.BlockSpec((depth, tile), lambda s, j: (0, start // tile + j))
    return pl.pallas_call(
        functools.partial(product_kernel, count, weight_dim),
        grid=(slots, result // tile),
        in_specs=[
            pl.BlockSpec((1, piece.shape[1], depth), lambda s, j: (s, 0, 0)) for piece in pieces
        ]
        + [block],
        out_specs=[
            pl.BlockSpec((1, piece.shape[1], tile), lambda s, j: (s, 0, j)) for piece in pieces
        ],
        out_shape=[
            jax.ShapeDtypeStruct((slots, piece.shape[1], result), kind)
            for piece, kind in zip(pieces, kinds)
        ],
        scratch_shapes=[pltpu.VMEM((total, depth), BF16)],
        compiler_params=LIMIT,
        cost_estimate=NO_COST,
        name="products",
    )(*pieces, array)


def hidden_kernel(count, *refs):
    pieces, downs, up, down = refs[:count], refs[count : 2 * count], refs[2 * count], refs[2 * count + 1]
    actives, grads = refs[2 * count + 2 : 3 * count + 2], refs[3 * count + 2 :]
    for piece, upstream, active, grad in zip(pieces, downs, actives, grads):
        hidden = dot(piece[0], up[...], 1, 0)
        active_grad = dot(upstream[0], down[...], 1, 0)
        square = hidden * hidden
        scale = (2 / math.pi) ** 0.5
        bend = jnp.tanh(hidden * (scale + scale * 0.044715 * square))
        half = 0.5 + 0.5 * bend
        slope = half + hidden * (0.5 - 0.5 * bend * bend) * (scale + scale * 0.134145 * square)
        active[0] = (hidden * half).astype(BF16)
        grad[0] = (active_grad * slope).astype(BF16)


def hidden_both(pieces, downs, up, down):
    count = len(pieces)
    if not (fits(up) and fits(down)):
        hidden = [dot(piece, cut(up), 2, 0) for piece in pieces]
        active_grad = [dot(piece, cut(down), 2, 0) for piece in downs]
        return (
            [gelu_tanh(value).astype(BF16) for value in hidden],
            [
                jax.vjp(gelu_tanh, value)[1](grad)[0].astype(BF16)
                for value, grad in zip(hidden, active_grad)
            ],
        )
    slots, _, depth = pieces[0].shape
    wide = up[2]
    tile = tile_of(wide, math.gcd(up[1], down[1]), 512)
    rows = [pl.BlockSpec((1, piece.shape[1], depth), lambda s, j: (s, 0, 0)) for piece in pieces]
    outs = pl.pallas_call(
        functools.partial(hidden_kernel, count),
        grid=(slots, wide // tile),
        in_specs=rows
        + rows
        + [
            pl.BlockSpec((depth, tile), lambda s, j, o=block[1] // tile: (0, o + j))
            for block in (up, down)
        ],
        out_specs=[
            pl.BlockSpec((1, piece.shape[1], tile), lambda s, j: (s, 0, j)) for piece in pieces
        ]
        * 2,
        out_shape=[
            jax.ShapeDtypeStruct((slots, piece.shape[1], wide), BF16) for piece in pieces
        ]
        * 2,
        compiler_params=LIMIT,
        cost_estimate=NO_COST,
        name="hidden_both",
    )(*pieces, *downs, up[0], down[0])
    return outs[:count], outs[count:]


def plain_grad(lefts, rights):
    left = jnp.concatenate([v.reshape(-1, v.shape[-1]) for v in lefts], axis=0)
    right = jnp.concatenate([v.reshape(-1, v.shape[-1]) for v in rights], axis=0)
    return dot(left, right, 0, 0).astype(BF16)


def on_device(
    group_count,
    tensor_size,
    image_tokens,
    text_tokens,
    condition,
    group_size,
    image_modulation,
    image_attention_in,
    image_attention_out,
    image_hidden_in,
    image_hidden_out,
    text_modulation,
    text_attention_in,
    text_attention_out,
    text_hidden_in,
    text_hidden_out,
    image_cotangent,
    text_cotangent,
):
    size = tensor_size
    slots, image_length, model = image_tokens.shape
    text_length = text_tokens.shape[1]
    share, _, width = image_attention_in.shape
    units = image_hidden_in.shape[1]
    tensor_rank = lax.axis_index("tensor")
    group_rank = lax.axis_index("dp")

    def gathered(*blocks):
        joined = blocks[0] if len(blocks) == 1 else jnp.concatenate(blocks, axis=1)
        return lax.all_gather(joined, "dp", axis=0, tiled=True)

    packed_in = gathered(
        image_attention_in.reshape(share, 3 * width), text_attention_in.reshape(share, 3 * width)
    )
    image_up = gathered(image_hidden_in)
    image_down = gathered(image_hidden_out.T)
    text_down = gathered(text_hidden_out.T)
    out_ring = ring_gather(
        jnp.concatenate([image_attention_out.T, text_attention_out.T], axis=1), group_count
    )
    out_hop = next(out_ring)
    weight_in = ((packed_in, 0, 3 * width), (packed_in, 3 * width, 3 * width))

    alive = (jnp.arange(slots) < group_size[0]).astype(F32)[:, None, None]
    cond_full = condition.astype(F32)
    activated_low = jax.nn.silu(cond_full).astype(BF16)
    activated_all = gather_stack(activated_low, group_count, "dp").reshape(-1, model)
    activated_all, out_hop = lax.optimization_barrier((activated_all, out_hop))
    out_hop = out_ring.send(out_hop)
    activated_own = lax.dynamic_slice_in_dim(activated_all, group_rank * share, share, 1)
    all_slots = activated_own.shape[0]
    mod_parts = jnp.concatenate(
        [
            dot(activated_own, image_modulation.reshape(share, 6 * width), 1, 0),
            dot(activated_own, text_modulation.reshape(share, 6 * width), 1, 0),
        ],
        axis=1,
    ).reshape(group_count, slots, 12 * width)
    mod_own = scatter_stack(mod_parts, group_count, "dp")
    modulations = lax.all_gather(
        mod_own.reshape(slots, 2, 6, width), "tensor", axis=3, tiled=True
    )
    modulations, out_hop = lax.optimization_barrier((modulations, out_hop))
    out_hop = out_ring.send(out_hop)
    mods = (modulations[:, 0], modulations[:, 1])

    tokens = (image_tokens.astype(F32), text_tokens.astype(F32))
    outgoing = (image_cotangent.astype(F32) * alive, text_cotangent.astype(F32) * alive)

    half = size // 2
    near_kinds = [F32] + [BF16] * (half - 1)

    def gathered_rows(values, gate=None):
        return gather_pieces(values, size, gate=gate)

    def scattered(grad):
        return lax.psum_scatter(grad, "dp", scatter_dimension=0, tiled=True).astype(F32)

    def row_products(pieces, weight, weight_dim):
        far = products_of(pieces[half:], weight, weight_dim, near_kinds)
        near = products_of(after(pieces[:half], far), weight, weight_dim, near_kinds)
        return [*near, *far]

    def image_sum(pieces, weight, weight_dim):
        return scatter_end(*scatter_start(row_products(pieces, weight, weight_dim), size), size)

    def text_sum(piece, weight, weight_dim):
        (product,) = products_of([piece], weight, weight_dim, [F32])
        return scatter_end(*text_start(product, size), size)

    def modulated(values, mod, shift, scale):
        normed, inverse = norm_rows(values)
        rows = normed * (1.0 + spread(mod[:, scale])) + spread(mod[:, shift])
        return normed, inverse, rows.astype(BF16)

    def second_back(stream, second_grad, normed, inverse):
        mod = mods[stream]
        shift_two_grad = jnp.sum(second_grad, axis=1)
        scale_two_grad = jnp.sum(second_grad * normed, axis=1)
        middle_grad = outgoing[stream] + norm_back(
            second_grad * (1.0 + spread(mod[:, 4])), normed, inverse
        )
        low = (middle_grad * spread(mod[:, 2])).astype(BF16)
        return middle_grad, low, shift_two_grad, scale_two_grad

    low_kinds = [BF16] * size

    normed_one, inverse_one, image_first = modulated(tokens[0], mods[0], 0, 1)
    text_normed_one, text_inverse_one, text_first = modulated(tokens[1], mods[1], 0, 1)
    first_pieces = gathered_rows(image_first)
    first_pieces, out_hop = lax.optimization_barrier((first_pieces, out_hop))
    for _ in range(group_count // 2 - 3):
        out_hop = out_ring.send(out_hop)
    packed = products_of(first_pieces, weight_in[0], 0, low_kinds)
    text_packed = products_of([text_first], weight_in[1], 0, [BF16])
    parts = [*packed, *text_packed]
    down_rows = [
        (outgoing[stream] * spread(mods[stream][:, 5])).astype(BF16) for stream in range(2)
    ]
    up_ring = ring_gather(after(text_hidden_in, first_pieces), group_count)
    up_hop = next(up_ring)
    attended, sums = attend(parts)
    down_pieces = gathered_rows(after(down_rows[0], first_pieces), attended)
    attended, out_hop, up_hop = lax.optimization_barrier((attended, out_hop, up_hop))
    both_out = out_ring.send(out_hop)
    up_hop = up_ring.send(up_hop)
    weight_out = ((both_out, 0, width), (both_out, width, width))
    attended_parts = (attended[:-1], attended[-1:])

    branch = image_sum(attended_parts[0], weight_out[0], 1)
    branch, up_hop = lax.optimization_barrier((branch, up_hop))
    up_hop = up_ring.send(up_hop)
    text_branch = text_sum(attended_parts[1][0], weight_out[1], 1)
    middle = tokens[0] + spread(mods[0][:, 2]) * branch
    normed_two, inverse_two, image_second = modulated(middle, mods[0], 3, 4)
    second_pieces = gathered_rows(image_second)
    up_weight, down_weight = (image_up, 0, units), (image_down, 0, units)
    near = hidden_both(second_pieces[:half], down_pieces[:half], up_weight, down_weight)
    far_pieces, up_hop = after((second_pieces[half:], up_hop), near)
    up_hop = up_ring.send(up_hop)
    far = hidden_both(far_pieces, down_pieces[half:], up_weight, down_weight)
    active = [*near[0], *far[0]]
    hidden_grad = [*near[1], *far[1]]
    kept, sent = scatter_start(row_products(hidden_grad, up_weight, 1), size)
    image_mlp_grad = weight_grad(
        after([(down_pieces, active), (second_pieces, hidden_grad)], sent)
    )
    second_grad, up_hop = after((scatter_end(kept, sent, size), up_hop), image_mlp_grad)
    image_mlp = scattered(image_mlp_grad)
    middle_grad, low, shift_two_grad, scale_two_grad = second_back(
        0, second_grad, normed_two, inverse_two
    )
    gate_one_grad = jnp.sum(middle_grad * branch, axis=1)

    for _ in range(group_count // 2 - 4):
        up_hop = up_ring.send(up_hop)
    text_up, text_down = after((up_ring.send(up_hop), text_down), low)
    up_weight, text_down_weight = (text_up, 0, units), (text_down, 0, units)
    text_middle = tokens[1] + spread(mods[1][:, 2]) * text_branch
    text_normed_two, text_inverse_two, text_second = modulated(text_middle, mods[1], 3, 4)
    text_active, text_hidden_grad = hidden_both(
        [text_second], [down_rows[1]], up_weight, text_down_weight
    )
    (text_product,) = products_of(text_hidden_grad, up_weight, 1, [F32])
    text_kept, text_sent = text_start(text_product, size)
    text_mlp_grad = weight_grad(
        after([([down_rows[1]], text_active), ([text_second], text_hidden_grad)], text_product)
    )
    text_ring = ring_scatter(text_mlp_grad, group_count)
    text_hop = next(text_ring)

    two_kept, two_sent = scatter_start(
        row_products(after(active, low), down_weight, 1), size
    )
    branch_grads = gathered_rows(low)
    branch_grads = after(branch_grads, two_sent)
    upstreams = products_of(branch_grads, weight_out[0], 0, low_kinds)
    upstreams = after(upstreams, text_sent, text_mlp_grad)
    first_part = attend_back(parts, size, upstreams, sums[:-1])
    text_second_grad = scatter_end(text_kept, text_sent, size)
    branch_two = scatter_end(two_kept, two_sent, size)
    first_part, text_second_grad, branch_two, text_hop = lax.optimization_barrier(
        (first_part, text_second_grad, branch_two, text_hop)
    )
    text_hop = text_ring.send(text_hop)
    text_middle_grad, text_low, text_shift_two_grad, text_scale_two_grad = second_back(
        1, text_second_grad, text_normed_two, text_inverse_two
    )
    text_gate_one_grad = jnp.sum(text_middle_grad * text_branch, axis=1)
    text_upstream = products_of([text_low], weight_out[1], 0, [BF16])
    packed_grads = attend_back(parts, 1, text_upstream, sums[-1:], first_part)
    attention_grad = weight_grad(
        [
            (first_pieces, packed_grads[:-1]),
            ([text_first], packed_grads[-1:]),
            (branch_grads, attended_parts[0]),
            ([text_low], attended_parts[1]),
        ]
    )
    attention_sum = scattered(attention_grad)
    packed_grads, text_hop = after((packed_grads, text_hop), attention_grad)
    text_hop = text_ring.send(text_hop)

    def first_back(stream, first_grad, normed, inverse, middle_grad):
        mod = mods[stream]
        shift_one_grad = jnp.sum(first_grad, axis=1)
        scale_one_grad = jnp.sum(first_grad * normed, axis=1)
        input_grad = middle_grad + norm_back(
            first_grad * (1.0 + spread(mod[:, 1])), normed, inverse
        )
        return input_grad, shift_one_grad, scale_one_grad

    def finish(stream, middle, branch_two):
        result = middle + spread(mods[stream][:, 5]) * branch_two
        gate_two_grad = jnp.sum(outgoing[stream] * branch_two, axis=1)
        return (result * alive).astype(BF16), gate_two_grad

    first_grad = image_sum(packed_grads[:-1], weight_in[0], 1)
    text_first_grad = text_sum(packed_grads[-1], weight_in[1], 1)
    text_branch_two = text_sum(text_active[0], text_down_weight, 1)
    text_first_grad, text_hop = lax.optimization_barrier((text_first_grad, text_hop))
    text_hop = text_ring.send(text_hop)
    for _ in range(group_count // 2 - 4):
        text_hop = text_ring.send(text_hop)
    first_grad, text_hop = lax.optimization_barrier((first_grad, text_hop))
    text_mlp = text_ring.send(text_hop)
    input_grads = [None, None]
    input_grads[0], shift_one_grad, scale_one_grad = first_back(
        0, first_grad, normed_one, inverse_one, middle_grad
    )
    input_grads[1], text_shift_one_grad, text_scale_one_grad = first_back(
        1, text_first_grad, text_normed_one, text_inverse_one, text_middle_grad
    )
    outputs = [None, None]
    outputs[0], gate_two_grad = finish(0, middle, branch_two)
    outputs[1], text_gate_two_grad = finish(1, text_middle, text_branch_two)
    mod_grads = (
        jnp.stack(
            [
                shift_one_grad,
                scale_one_grad,
                gate_one_grad,
                shift_two_grad,
                scale_two_grad,
                gate_two_grad,
            ],
            axis=1,
        ),
        jnp.stack(
            [
                text_shift_one_grad,
                text_scale_one_grad,
                text_gate_one_grad,
                text_shift_two_grad,
                text_scale_two_grad,
                text_gate_two_grad,
            ],
            axis=1,
        ),
    )

    image_blocks = jnp.stack(
        [
            lax.dynamic_slice_in_dim(mod_grads[0], (tensor_rank ^ k) * width, width, 2)
            for k in range(size)
        ]
    )
    image_share = scatter_stack(image_blocks, size, "tensor")
    text_share = lax.dynamic_slice_in_dim(mod_grads[1], tensor_rank * width, width, 2)
    share_low = jnp.stack([image_share, text_share], axis=1).astype(BF16)
    share_all = gather_stack(share_low, group_count, "dp").reshape(all_slots, 2, 6, width)
    image_all = share_all[:, 0].reshape(all_slots, 6 * width)
    text_all = share_all[:, 1].reshape(all_slots, 6 * width)
    image_ada = dot(activated_own, image_all, 0, 0).reshape(share, 6, width)
    text_ada = dot(activated_own, text_all, 0, 0).reshape(share, 6, width)
    activated_part = dot(image_all, image_modulation.reshape(share, 6 * width), 1, 1) + dot(
        text_all, text_modulation.reshape(share, 6 * width), 1, 1
    )
    activated_part = sum_all(activated_part, size, "tensor").reshape(group_count, slots, share)
    activated_rows = gather_stack(activated_part, group_count, "dp")
    activated_rows = jnp.stack([activated_rows[k, k] for k in range(group_count)])
    group_order = group_rank ^ jnp.arange(group_count)
    activated_grad = jnp.concatenate(
        [
            lax.dynamic_index_in_dim(activated_rows, group_order[k], 0, keepdims=False)
            for k in range(group_count)
        ],
        axis=1,
    )
    condition_gradient = jax.vjp(jax.nn.silu, cond_full)[1](activated_grad)[0]

    return (
        outputs[0],
        outputs[1],
        input_grads[0],
        input_grads[1],
        condition_gradient,
        image_ada,
        attention_sum[:, : 3 * width].reshape(share, 3, width),
        attention_sum[:, 6 * width : 7 * width].T,
        image_mlp[:, units:],
        image_mlp[:, :units].T,
        text_ada,
        attention_sum[:, 3 * width : 6 * width].reshape(share, 3, width),
        attention_sum[:, 7 * width :].T,
        text_mlp[:, units:],
        text_mlp[:, :units].T,
    )


def solution(mesh):
    image = P("dp", "tensor", None)
    text = P("dp", None, None)
    columns = P("dp", None, "tensor")
    rows = P("tensor", "dp")
    plain = P("dp", "tensor")
    weights = (columns, columns, rows, plain, rows)
    return jax.shard_map(
        functools.partial(on_device, mesh.shape["dp"], mesh.shape["tensor"]),
        mesh=mesh,
        in_specs=(image, text, P("dp", None), P("dp")) + weights + weights + (image, text),
        out_specs=(image, text, image, text, P("dp", None)) + weights + weights,
        check_vma=False,
    )
```

```python
import functools
import math

import jax
import jax.numpy as jnp
from jax import lax
from jax.experimental import pallas as pl
from jax.experimental.pallas import tpu as pltpu
from jax.sharding import PartitionSpec as P

HEAD = 64
LANES = 128
F32 = jnp.float32
BF16 = jnp.bfloat16


def norm_rows(values):
    center = values - jnp.mean(values, axis=-1, keepdims=True)
    inverse = lax.rsqrt(jnp.mean(center * center, axis=-1, keepdims=True) + 1e-06)
    return (center * inverse, inverse)


def norm_back(upstream, normed, inverse):
    first = jnp.mean(upstream, axis=-1, keepdims=True)
    second = jnp.mean(upstream * normed, axis=-1, keepdims=True)
    return inverse * (upstream - first - normed * second)


def gelu_tanh(values):
    return jax.nn.gelu(values, approximate=True)


def spread(vector):
    return vector[:, None, :]


def dot(left, right, left_dim, right_dim):
    return lax.dot_general(
        left, right, (((left_dim,), (right_dim,)), ((), ())), preferred_element_type=F32
    )


def swap(value, bit, size, axis="tensor"):
    return lax.ppermute(value, axis, [(i, i ^ bit) for i in range(size)])


def bits_of(size):
    bits = []
    bit = 1
    while bit < size:
        bits.append(bit)
        bit *= 2
    return bits


def gather_start(value, size, axis="tensor"):
    have = {0: value}
    for bit in reversed(bits_of(size)[1:]):
        have.update({k ^ bit: swap(v, bit, size, axis) for k, v in list(have.items())})
    return have


def gather_end(have, size, axis="tensor"):
    have = have | {k ^ 1: swap(v, 1, size, axis) for k, v in have.items()}
    return [have[k] for k in range(size)]


def gather_pieces(value, size, axis="tensor"):
    return gather_end(gather_start(value, size, axis), size, axis)


def gather_stack(value, size, axis):
    value = value[None]
    for bit in bits_of(size):
        value = jnp.concatenate([value, swap(value, bit, size, axis)], axis=0)
    return value


def scatter_stack(value, size, axis):
    for bit in reversed(bits_of(size)):
        value = value[:bit] + swap(value[bit:], bit, size, axis)
    return value[0]


def sum_all(value, size, axis):
    for bit in bits_of(size):
        value = value + swap(value, bit, size, axis)
    return value


def scatter_start(pieces, size):
    have = dict(enumerate(pieces))
    for bit in bits_of(size)[:-1]:
        kept = {}
        for k in sorted(have, reverse=True):
            if not k & bit:
                other = swap(have[k ^ bit].astype(BF16), bit, size)
                kept[k] = have[k].astype(F32) + other.astype(F32)
        have = kept
    kept, sent = (have[k] for k in sorted(have))
    return kept, sent.astype(BF16)


def scatter_end(kept, sent, size):
    return kept.astype(F32) + swap(sent, size // 2, size).astype(F32)


def after(values, *others):
    return lax.optimization_barrier((values, others))[0]


def ring_of(count):
    return list(range(0, count, 2)) + list(range(1, count, 2))[::-1]


def ring_member(place, count):
    place = lax.rem(place + count, count)
    return jnp.where(place < (count + 1) // 2, 2 * place, 2 * (count - 1 - place) + 1)


def ring_place(member, count):
    return jnp.where(member % 2 == 0, member // 2, count - 1 - member // 2)


def ring_step(value, way, count):
    ring = ring_of(count)
    hops = [(ring[i], ring[(i + way) % count]) for i in range(count)]
    return lax.ppermute(value, "dp", hops)


def ring_gather(block, count):
    share, wide = block.shape
    half = wide // 2 // LANES * LANES
    place = ring_place(lax.axis_index("dp"), count)
    whole = jnp.zeros((count * share, wide), block.dtype)

    def put(whole, value, offset, column):
        row = ring_member(place + offset, count) * share
        return lax.dynamic_update_slice(whole, value, (row, column))

    whole = put(whole, block, 0, 0)
    behind = ahead = block
    for hop in range(1, count // 2):
        behind = ring_step(behind, 1, count)
        ahead = ring_step(ahead, -1, count)
        behind, ahead = yield behind, ahead
        whole = put(put(whole, behind, -hop, 0), ahead, hop, 0)
    behind = ring_step(behind[:, :half], 1, count)
    ahead = ring_step(ahead[:, half:], -1, count)
    behind, ahead = yield behind, ahead
    yield put(put(whole, behind, -(count // 2), 0), ahead, count // 2, half)


def ring_scatter(grad, count):
    wide = grad.shape[1]
    share = grad.shape[0] // count
    half = wide // 2 // LANES * LANES
    place = ring_place(lax.axis_index("dp"), count)

    def own(offset):
        row = ring_member(place + offset, count) * share
        return lax.dynamic_slice_in_dim(grad, row, share, 0).astype(F32)

    far = own(count // 2).astype(BF16)
    behind = ring_step(far[:, :half], 1, count)
    ahead = ring_step(far[:, half:], -1, count)
    behind, ahead = yield behind, ahead
    behind = jnp.pad(behind.astype(F32), ((0, 0), (0, wide - half)))
    ahead = jnp.pad(ahead.astype(F32), ((0, 0), (half, 0)))
    for hop in range(count // 2 - 1, 0, -1):
        behind = ring_step((own(hop) + behind).astype(BF16), 1, count)
        ahead = ring_step((own(-hop) + ahead).astype(BF16), -1, count)
        behind, ahead = yield behind, ahead
        behind, ahead = behind.astype(F32), ahead.astype(F32)
    yield own(0) + behind + ahead


def text_start(value, size):
    for bit in bits_of(size)[:-1]:
        if bit > 1:
            value = lax.reduce_precision(value, 8, 7)
            value = value + swap(value.astype(BF16), bit, size).astype(F32)
        else:
            value = value + swap(value, bit, size)
    value = lax.reduce_precision(value, 8, 7)
    return value, value.astype(BF16)


def lane_mask(half, shape):
    lane = lax.broadcasted_iota(jnp.int32, shape, 1)
    return (lane >= HEAD) if half else (lane < HEAD)


def pick(value, half):
    return jnp.where(lane_mask(half, value.shape), value, jnp.zeros_like(value))


def load_rows(refs, store):
    start = 0
    for ref in refs:
        rows = ref.shape[1]
        store[start : start + rows, :] = ref[0]
        start += rows


def attend_kernel(count, *refs):
    queries, keys, values = refs[:count], refs[count : 2 * count], refs[2 * count : 3 * count]
    outs = refs[3 * count : 4 * count]
    sums = refs[4 * count : 5 * count]
    key_all, value_all = refs[5 * count :]
    load_rows(keys, key_all)
    load_rows(values, value_all)
    for index in range(count):
        query = queries[index][0] * jnp.asarray(HEAD**-0.5, BF16)
        halves = []
        for half in range(2):
            scores = dot(key_all[...], pick(query, half), 1, 1)
            highest = jnp.max(scores, axis=0, keepdims=True)
            weights = jnp.exp(scores - highest)
            total = jnp.sum(weights, axis=0, keepdims=True)
            weights = (weights * (1.0 / total)).astype(BF16)
            mixed = dot(value_all[...], weights, 0, 0)
            halves.append(mixed[half * HEAD : (half + 1) * HEAD])
            sums[index][0, 0, half : half + 1, :] = highest + jnp.log(total)
        outs[index][0] = jnp.concatenate(halves, axis=0).T.astype(BF16)


def attend_back_kernel(count, groups, *refs):
    queries, keys, values = refs[:count], refs[count : 2 * count], refs[2 * count : 3 * count]
    upstreams = refs[3 * count : 4 * count]
    sums = refs[4 * count : 5 * count]
    outs = refs[5 * count : 6 * count]
    key_all, value_all, key_grad, value_grad = refs[6 * count :]
    load_rows(keys, key_all)
    load_rows(values, value_all)
    pair = pl.program_id(1)
    scale = jnp.asarray(HEAD**-0.5, BF16)
    query_lanes = pl.ds(pl.multiple_of(pair * LANES, LANES), LANES)
    key_lanes = pl.ds(pl.multiple_of((groups + pair) * LANES, LANES), LANES)
    value_lanes = pl.ds(pl.multiple_of((2 * groups + pair) * LANES, LANES), LANES)
    for index in range(count):
        query = queries[index][0] * scale
        upstream = upstreams[index][0]
        halves = []
        for half in range(2):
            query_half = pick(query, half)
            upstream_half = pick(upstream, half)
            scores = dot(key_all[...], query_half, 1, 1)
            weights = jnp.exp(scores - sums[index][0, 0, half : half + 1, :])
            along = dot(value_all[...], upstream_half, 1, 1)
            value_part = dot(weights.astype(BF16), upstream_half, 1, 0)
            product = weights * along
            score_grad = (product - weights * jnp.sum(product, axis=0, keepdims=True)).astype(BF16)
            key_part = dot(score_grad, query_half, 1, 0)
            if index == 0 and half == 0:
                value_grad[...] = value_part
                key_grad[...] = key_part
            else:
                value_grad[...] += value_part
                key_grad[...] += key_part
            mixed = dot(key_all[...], score_grad, 0, 0)
            halves.append(mixed[half * HEAD : (half + 1) * HEAD])
        query_grad = jnp.concatenate(halves, axis=0).T * HEAD**-0.5
        outs[index][0, :, query_lanes] = query_grad.astype(BF16)
    start = 0
    for index in range(count):
        rows = outs[index].shape[1]
        outs[index][0, :, key_lanes] = key_grad[start : start + rows, :].astype(BF16)
        outs[index][0, :, value_lanes] = value_grad[start : start + rows, :].astype(BF16)
        start += rows


def lane_blocks(parts, offset):
    return [
        pl.BlockSpec((1, part.shape[1], LANES), lambda s, p, o=offset: (s, 0, o + p))
        for part in parts
    ]


def widen(part, copies):
    slots, rows, width = part.shape
    width = width // copies
    extra = -width % LANES
    if not extra:
        return part
    part = jnp.pad(part.reshape(slots, rows, copies, width), ((0, 0), (0, 0), (0, 0), (0, extra)))
    return part.reshape(slots, rows, copies * (width + extra))


def narrow(part, copies, width):
    slots, rows, wide = part.shape
    wide = wide // copies
    if wide == width:
        return part
    return part.reshape(slots, rows, copies, wide)[..., :width].reshape(slots, rows, -1)


def attention_cost(slots, rows, width, products):
    return pl.CostEstimate(
        flops=products * 8 * slots * rows * rows * width,
        transcendentals=slots * rows * rows * (width // HEAD),
        bytes_accessed=slots * rows * width * 2 * (4 + 3 * (products > 2)),
    )


def attend(parts):
    slots = parts[0].shape[0]
    width = parts[0].shape[2] // 3
    parts = [widen(part, 3) for part in parts]
    count = len(parts)
    wide = parts[0].shape[2] // 3
    groups = wide // LANES
    total = sum(part.shape[1] for part in parts)
    outs = pl.pallas_call(
        functools.partial(attend_kernel, count),
        grid=(slots, groups),
        in_specs=lane_blocks(parts, 0) + lane_blocks(parts, groups) + lane_blocks(parts, 2 * groups),
        out_specs=lane_blocks(parts, 0)
        + [
            pl.BlockSpec((1, 1, 2, part.shape[1]), lambda s, p: (s, p, 0, 0)) for part in parts
        ],
        out_shape=[jax.ShapeDtypeStruct((slots, part.shape[1], wide), BF16) for part in parts]
        + [jax.ShapeDtypeStruct((slots, groups, 2, part.shape[1]), F32) for part in parts],
        scratch_shapes=[pltpu.VMEM((total, LANES), BF16)] * 2,
        compiler_params=pltpu.CompilerParams(vmem_limit_bytes=48 * 1024 * 1024),
        cost_estimate=attention_cost(slots, total, wide, 2),
        name="attend",
    )(*parts, *parts, *parts)
    return [narrow(out, 1, width) for out in outs[:count]], outs[count:]


def attend_back(parts, upstreams, sums):
    slots = parts[0].shape[0]
    width = parts[0].shape[2] // 3
    parts = [widen(part, 3) for part in parts]
    upstreams = [widen(part, 1) for part in upstreams]
    count = len(parts)
    wide = parts[0].shape[2] // 3
    groups = wide // LANES
    total = sum(part.shape[1] for part in parts)
    outs = pl.pallas_call(
        functools.partial(attend_back_kernel, count, groups),
        grid=(slots, groups),
        in_specs=lane_blocks(parts, 0)
        + lane_blocks(parts, groups)
        + lane_blocks(parts, 2 * groups)
        + lane_blocks(upstreams, 0)
        + [
            pl.BlockSpec((1, 1, 2, part.shape[1]), lambda s, p: (s, p, 0, 0)) for part in parts
        ],
        out_specs=[
            pl.BlockSpec((1, part.shape[1], 3 * wide), lambda s, p: (s, 0, 0)) for part in parts
        ],
        out_shape=[jax.ShapeDtypeStruct((slots, part.shape[1], 3 * wide), BF16) for part in parts],
        scratch_shapes=[pltpu.VMEM((total, LANES), BF16)] * 2 + [pltpu.VMEM((total, LANES), F32)] * 2,
        compiler_params=pltpu.CompilerParams(vmem_limit_bytes=48 * 1024 * 1024),
        cost_estimate=attention_cost(slots, total, wide, 5),
        name="attend_back",
    )(*parts, *parts, *parts, *upstreams, *sums)
    return [narrow(out, 3, width) for out in outs]


def rows_kernel(count, *refs):
    lefts, rights, out = refs[:count], refs[count : 2 * count], refs[-1]
    total = None
    for left, right in zip(lefts, rights):
        for slot in range(left.shape[0]):
            part = dot(left[slot], right[slot], 0, 0)
            total = part if total is None else total + part
    out[...] = total.astype(BF16)


def weight_grad(pairs):
    joined = None
    rows = pairs[0][0][0].shape[-1]
    wide = sum(rights[0].shape[-1] for _, rights in pairs)
    start = 0
    for lefts, rights in pairs:
        part = rights[0].shape[-1]
        if part % LANES or start % part:
            return jnp.concatenate([plain_grad(*pair) for pair in pairs], axis=1)
        count = len(lefts)
        step = 256
        ins = [
            pl.BlockSpec((left.shape[0], left.shape[1], step), lambda i: (0, 0, i))
            for left in lefts
        ] + [
            pl.BlockSpec(right.shape, lambda i: (0, 0, 0), pipeline_mode=pl.Buffered(1))
            for right in rights
        ]
        operands = (*lefts, *rights)
        if joined is not None:
            ins.append(pl.BlockSpec(memory_space=pl.ANY))
            operands += (joined,)
        joined = pl.pallas_call(
            functools.partial(rows_kernel, count),
            grid=(rows // step,),
            in_specs=ins,
            out_specs=pl.BlockSpec((step, part), lambda i, c=start // part: (i, c)),
            out_shape=jax.ShapeDtypeStruct((rows, wide), BF16),
            input_output_aliases={} if joined is None else {2 * count: 0},
            compiler_params=pltpu.CompilerParams(vmem_limit_bytes=48 * 1024 * 1024),
            cost_estimate=pl.CostEstimate(flops=0, transcendentals=0, bytes_accessed=1024),
            name="weight_grad",
        )(*operands)
        start += part
    return joined


NO_COST = pl.CostEstimate(flops=0, transcendentals=0, bytes_accessed=1024)
LIMIT = pltpu.CompilerParams(vmem_limit_bytes=48 * 1024 * 1024)


def tile_of(wide, start, most):
    return max(t for t in range(LANES, most + 1, LANES) if wide % t == 0 and start % t == 0)


def fits(weight):
    _, start, wide = weight
    return wide % LANES == 0 and start % LANES == 0


def cut(weight):
    array, start, wide = weight
    return array[:, start : start + wide]


def row_blocks(ref):
    slots, rows, columns = ref.shape
    if rows % 16 == 0:
        return [(slice(None), ref[...].reshape(slots * rows, columns))]
    return [(slice(slot, slot + 1), ref[slot]) for slot in range(slots)]


def store_rows(ref, place, value):
    slots = ref.shape[0] if place == slice(None) else 1
    ref[place] = value.reshape(slots, -1, value.shape[-1]).astype(ref.dtype)


def product_kernel(count, weight_dim, *refs):
    pieces, weight, outs = refs[:count], refs[count], refs[count + 1 :]
    for piece, out in zip(pieces, outs):
        for place, rows in row_blocks(piece):
            store_rows(out, place, dot(rows, weight[...], 1, weight_dim))


def whole_block(array):
    return pl.BlockSpec(array.shape, lambda j: (0, 0, 0), pipeline_mode=pl.Buffered(1))


def products_of(pieces, weight, weight_dim, kinds, late=False):
    array, start, wide = weight
    if not fits(weight) or (weight_dim and start % wide):
        return [
            dot(piece, cut(weight), 2, weight_dim).astype(kind)
            for piece, kind in zip(pieces, kinds)
        ]
    count = len(pieces)
    slots, _, depth = pieces[0].shape
    if weight_dim:
        result = array.shape[0]
        tile = tile_of(result, 0, 768)
        block = pl.BlockSpec((tile, wide), lambda j: (j, start // wide))
    else:
        result = wide
        tile = tile_of(wide, start, 768)
        block = pl.BlockSpec((depth, tile), lambda j: (0, start // tile + j))
    rows = slots * sum(piece.shape[1] for piece in pieces)
    cost = pl.CostEstimate(
        flops=4 * rows * depth * result, transcendentals=0, bytes_accessed=4 * rows * result
    )
    return pl.pallas_call(
        functools.partial(product_kernel, count, weight_dim),
        grid=(result // tile,),
        in_specs=[whole_block(piece) for piece in pieces] + [block],
        out_specs=[
            pl.BlockSpec((slots, piece.shape[1], tile), lambda j: (0, 0, j)) for piece in pieces
        ],
        out_shape=[
            jax.ShapeDtypeStruct((slots, piece.shape[1], result), kind)
            for piece, kind in zip(pieces, kinds)
        ],
        compiler_params=LIMIT,
        cost_estimate=cost if late else NO_COST,
        name="products",
    )(*pieces, array)


def hidden_kernel(count, *refs):
    pieces, downs, up, down = refs[:count], refs[count : 2 * count], refs[2 * count], refs[2 * count + 1]
    actives, grads = refs[2 * count + 2 : 3 * count + 2], refs[3 * count + 2 :]
    for piece, upstream, active, grad in zip(pieces, downs, actives, grads):
        for (place, rows), (_, above) in zip(row_blocks(piece), row_blocks(upstream)):
            hidden = dot(rows, up[...], 1, 0)
            active_grad = dot(above, down[...], 1, 0)
            square = hidden * hidden
            scale = (2 / math.pi) ** 0.5
            bend = jnp.tanh(hidden * (scale + scale * 0.044715 * square))
            half = 0.5 + 0.5 * bend
            slope = half + hidden * (0.5 - 0.5 * bend * bend) * (
                scale + scale * 0.134145 * square
            )
            store_rows(active, place, hidden * half)
            store_rows(grad, place, active_grad * slope)


def hidden_both(pieces, downs, up, down):
    count = len(pieces)
    if not (fits(up) and fits(down)):
        hidden = [dot(piece, cut(up), 2, 0) for piece in pieces]
        active_grad = [dot(piece, cut(down), 2, 0) for piece in downs]
        return (
            [gelu_tanh(value).astype(BF16) for value in hidden],
            [
                jax.vjp(gelu_tanh, value)[1](grad)[0].astype(BF16)
                for value, grad in zip(hidden, active_grad)
            ],
        )
    slots, _, depth = pieces[0].shape
    wide = up[2]
    tile = tile_of(wide, math.gcd(up[1], down[1]), 512)
    outs = pl.pallas_call(
        functools.partial(hidden_kernel, count),
        grid=(wide // tile,),
        in_specs=[whole_block(piece) for piece in (*pieces, *downs)]
        + [
            pl.BlockSpec((depth, tile), lambda j, o=block[1] // tile: (0, o + j))
            for block in (up, down)
        ],
        out_specs=[
            pl.BlockSpec((slots, piece.shape[1], tile), lambda j: (0, 0, j)) for piece in pieces
        ]
        * 2,
        out_shape=[
            jax.ShapeDtypeStruct((slots, piece.shape[1], wide), BF16) for piece in pieces
        ]
        * 2,
        compiler_params=LIMIT,
        cost_estimate=NO_COST,
        name="hidden_both",
    )(*pieces, *downs, up[0], down[0])
    return outs[:count], outs[count:]


def plain_grad(lefts, rights):
    left = jnp.concatenate([v.reshape(-1, v.shape[-1]) for v in lefts], axis=0)
    right = jnp.concatenate([v.reshape(-1, v.shape[-1]) for v in rights], axis=0)
    return dot(left, right, 0, 0).astype(BF16)


def on_device(
    group_count,
    tensor_size,
    image_tokens,
    text_tokens,
    condition,
    group_size,
    image_modulation,
    image_attention_in,
    image_attention_out,
    image_hidden_in,
    image_hidden_out,
    text_modulation,
    text_attention_in,
    text_attention_out,
    text_hidden_in,
    text_hidden_out,
    image_cotangent,
    text_cotangent,
):
    size = tensor_size
    slots, image_length, model = image_tokens.shape
    text_length = text_tokens.shape[1]
    share, _, width = image_attention_in.shape
    units = image_hidden_in.shape[1]
    tensor_rank = lax.axis_index("tensor")
    group_rank = lax.axis_index("dp")

    def gathered(*blocks):
        joined = blocks[0] if len(blocks) == 1 else jnp.concatenate(blocks, axis=1)
        return lax.all_gather(joined, "dp", axis=0, tiled=True)

    packed_in = gathered(
        image_attention_in.reshape(share, 3 * width), text_attention_in.reshape(share, 3 * width)
    )
    image_up = gathered(image_hidden_in)
    image_down = gathered(image_hidden_out.T)
    out_ring = ring_gather(
        jnp.concatenate([image_attention_out.T, text_attention_out.T], axis=1), group_count
    )
    out_hop = next(out_ring)
    weight_in = ((packed_in, 0, 3 * width), (packed_in, 3 * width, 3 * width))

    alive = (jnp.arange(slots) < group_size[0]).astype(F32)[:, None, None]
    cond_full = condition.astype(F32)
    activated_low = jax.nn.silu(cond_full).astype(BF16)
    activated_all = gather_stack(activated_low, group_count, "dp").reshape(-1, model)
    activated_own = lax.dynamic_slice_in_dim(activated_all, group_rank * share, share, 1)
    all_slots = activated_own.shape[0]
    mod_parts = jnp.concatenate(
        [
            dot(activated_own, image_modulation.reshape(share, 6 * width), 1, 0),
            dot(activated_own, text_modulation.reshape(share, 6 * width), 1, 0),
        ],
        axis=1,
    ).reshape(group_count, slots, 12 * width)
    mod_own = scatter_stack(mod_parts, group_count, "dp")
    modulations = lax.all_gather(
        mod_own.reshape(slots, 2, 6, width), "tensor", axis=3, tiled=True
    )
    modulations, out_hop = lax.optimization_barrier((modulations, out_hop))
    out_hop = out_ring.send(out_hop)
    mods = (modulations[:, 0], modulations[:, 1])

    tokens = (image_tokens.astype(F32), text_tokens.astype(F32))
    outgoing = (image_cotangent.astype(F32) * alive, text_cotangent.astype(F32) * alive)

    half = size // 2
    near_kinds = [F32] + [BF16] * (half - 1)

    def scattered(grad):
        return lax.psum_scatter(grad, "dp", scatter_dimension=0, tiled=True).astype(F32)

    def row_products(pieces, weight, weight_dim, late=False):
        far = products_of(pieces[half:], weight, weight_dim, near_kinds, late)
        near = products_of(after(pieces[:half], far), weight, weight_dim, near_kinds, late)
        return [*near, *far]

    def image_sum(pieces, weight, weight_dim, late=False):
        products = row_products(pieces, weight, weight_dim, late)
        return scatter_end(*scatter_start(products, size), size)

    def text_sum(piece, weight, weight_dim, late=False):
        (product,) = products_of([piece], weight, weight_dim, [F32], late)
        return scatter_end(*text_start(product, size), size)

    def modulated(values, mod, shift, scale):
        normed, inverse = norm_rows(values)
        rows = normed * (1.0 + spread(mod[:, scale])) + spread(mod[:, shift])
        return normed, inverse, rows.astype(BF16)

    def second_back(stream, second_grad, normed, inverse):
        mod = mods[stream]
        shift_two_grad = jnp.sum(second_grad, axis=1)
        scale_two_grad = jnp.sum(second_grad * normed, axis=1)
        middle_grad = outgoing[stream] + norm_back(
            second_grad * (1.0 + spread(mod[:, 4])), normed, inverse
        )
        low = (middle_grad * spread(mod[:, 2])).astype(BF16)
        return middle_grad, low, shift_two_grad, scale_two_grad

    low_kinds = [BF16] * size

    normed_one, inverse_one, image_first = modulated(tokens[0], mods[0], 0, 1)
    text_normed_one, text_inverse_one, text_first = modulated(tokens[1], mods[1], 0, 1)
    first_pieces = gather_pieces(image_first, size)
    first_pieces, out_hop = lax.optimization_barrier((first_pieces, out_hop))
    out_hop = out_ring.send(out_hop)
    for _ in range(group_count // 2 - 4):
        out_hop = out_ring.send(out_hop)
    packed = products_of(first_pieces, weight_in[0], 0, low_kinds)
    text_packed = products_of([text_first], weight_in[1], 0, [BF16])
    down_rows = [
        (outgoing[stream] * spread(mods[stream][:, 5])).astype(BF16) for stream in range(2)
    ]
    down_have = gather_start(after(down_rows[0], first_pieces), size)
    parts, out_hop = after(([*packed, *text_packed], out_hop), down_have)
    out_hop = out_ring.send(out_hop)
    up_ring = ring_gather(
        after(jnp.concatenate([text_hidden_in, text_hidden_out.T], axis=1), parts), group_count
    )
    up_hop = next(up_ring)
    attended, sums = attend(parts)
    down_pieces = gather_end(after(down_have, attended), size)
    attended, out_hop, up_hop = lax.optimization_barrier((attended, out_hop, up_hop))
    both_out = out_ring.send(out_hop)
    up_hop = up_ring.send(up_hop)
    weight_out = ((both_out, 0, width), (both_out, width, width))
    attended_parts = (attended[:-1], attended[-1:])

    branch = image_sum(attended_parts[0], weight_out[0], 1)
    branch, up_hop = lax.optimization_barrier((branch, up_hop))
    up_hop = up_ring.send(up_hop)
    text_branch = text_sum(attended_parts[1][0], weight_out[1], 1)
    middle = tokens[0] + spread(mods[0][:, 2]) * branch
    normed_two, inverse_two, image_second = modulated(middle, mods[0], 3, 4)
    second_pieces = gather_pieces(image_second, size)
    up_weight, down_weight = (image_up, 0, units), (image_down, 0, units)
    near = hidden_both(second_pieces[:half], down_pieces[:half], up_weight, down_weight)
    far_pieces, up_hop = after((second_pieces[half:], up_hop), near)
    up_hop = up_ring.send(up_hop)
    far = hidden_both(far_pieces, down_pieces[half:], up_weight, down_weight)
    active = [*near[0], *far[0]]
    hidden_grad = [*near[1], *far[1]]
    kept, sent = scatter_start(row_products(hidden_grad, up_weight, 1), size)
    for _ in range(group_count // 2 - 4):
        up_hop = up_ring.send(up_hop)
    up_hop = after(up_hop, sent)
    text_both = up_ring.send(up_hop)

    text_up_weight, text_down_weight = (text_both, 0, units), (text_both, units, units)
    text_middle = tokens[1] + spread(mods[1][:, 2]) * text_branch
    text_normed_two, text_inverse_two, text_second = modulated(text_middle, mods[1], 3, 4)
    text_active, text_hidden_grad = hidden_both(
        [text_second], [down_rows[1]], text_up_weight, text_down_weight
    )
    (text_product,) = products_of(text_hidden_grad, text_up_weight, 1, [F32])
    text_second_grad = scatter_end(*text_start(text_product, size), size)
    image_mlp_grad = weight_grad(
        after([(down_pieces, active), (second_pieces, hidden_grad)], sent)
    )
    second_grad = after(scatter_end(kept, sent, size), image_mlp_grad, text_product)
    image_mlp = scattered(after(image_mlp_grad, second_grad))
    middle_grad, low, shift_two_grad, scale_two_grad = second_back(
        0, second_grad, normed_two, inverse_two
    )
    gate_one_grad = jnp.sum(middle_grad * branch, axis=1)

    branch_grads = gather_pieces(low, size)
    text_mlp_grad = weight_grad(
        after([([down_rows[1]], text_active), ([text_second], text_hidden_grad)], low)
    )
    upstreams = products_of(after(branch_grads, text_mlp_grad), weight_out[0], 0, low_kinds)
    text_middle_grad, text_low, text_shift_two_grad, text_scale_two_grad = second_back(
        1, text_second_grad, text_normed_two, text_inverse_two
    )
    text_gate_one_grad = jnp.sum(text_middle_grad * text_branch, axis=1)
    text_upstream = products_of([text_low], weight_out[1], 0, [BF16])
    text_ring = ring_scatter(after(text_mlp_grad, branch_grads), group_count)
    text_hop = next(text_ring)
    packed_grads = attend_back(parts, [*upstreams, *text_upstream], sums)
    packed_grads, text_hop = lax.optimization_barrier((packed_grads, text_hop))
    text_hop = text_ring.send(text_hop)
    attention_grad = weight_grad(
        [
            (first_pieces, packed_grads[:-1]),
            ([text_first], packed_grads[-1:]),
            (branch_grads, attended_parts[0]),
            ([text_low], attended_parts[1]),
        ]
    )
    attention_sum = scattered(attention_grad)
    packed_grads, text_hop, active, text_active = after(
        (packed_grads, text_hop, active, text_active), attention_grad
    )
    text_hop = text_ring.send(text_hop)

    def first_back(stream, first_grad, normed, inverse, middle_grad):
        mod = mods[stream]
        shift_one_grad = jnp.sum(first_grad, axis=1)
        scale_one_grad = jnp.sum(first_grad * normed, axis=1)
        input_grad = middle_grad + norm_back(
            first_grad * (1.0 + spread(mod[:, 1])), normed, inverse
        )
        return input_grad, shift_one_grad, scale_one_grad

    def finish(stream, middle, branch_two):
        result = middle + spread(mods[stream][:, 5]) * branch_two
        gate_two_grad = jnp.sum(outgoing[stream] * branch_two, axis=1)
        return (result * alive).astype(BF16), gate_two_grad

    first_grad = image_sum(packed_grads[:-1], weight_in[0], 1, True)
    text_first_grad = text_sum(packed_grads[-1], weight_in[1], 1, True)
    branch_two = image_sum(active, down_weight, 1, True)
    text_branch_two = text_sum(text_active[0], text_down_weight, 1, True)
    text_first_grad, text_hop = lax.optimization_barrier((text_first_grad, text_hop))
    text_hop = text_ring.send(text_hop)
    for _ in range(group_count // 2 - 4):
        text_hop = text_ring.send(text_hop)
    first_grad, text_hop = lax.optimization_barrier((first_grad, text_hop))
    text_mlp = text_ring.send(text_hop)
    input_grads = [None, None]
    input_grads[0], shift_one_grad, scale_one_grad = first_back(
        0, first_grad, normed_one, inverse_one, middle_grad
    )
    input_grads[1], text_shift_one_grad, text_scale_one_grad = first_back(
        1, text_first_grad, text_normed_one, text_inverse_one, text_middle_grad
    )
    outputs = [None, None]
    outputs[0], gate_two_grad = finish(0, middle, branch_two)
    outputs[1], text_gate_two_grad = finish(1, text_middle, text_branch_two)
    mod_grads = (
        jnp.stack(
            [
                shift_one_grad,
                scale_one_grad,
                gate_one_grad,
                shift_two_grad,
                scale_two_grad,
                gate_two_grad,
            ],
            axis=1,
        ),
        jnp.stack(
            [
                text_shift_one_grad,
                text_scale_one_grad,
                text_gate_one_grad,
                text_shift_two_grad,
                text_scale_two_grad,
                text_gate_two_grad,
            ],
            axis=1,
        ),
    )

    image_blocks = jnp.stack(
        [
            lax.dynamic_slice_in_dim(mod_grads[0], (tensor_rank ^ k) * width, width, 2)
            for k in range(size)
        ]
    )
    image_share = scatter_stack(image_blocks, size, "tensor")
    text_share = lax.dynamic_slice_in_dim(mod_grads[1], tensor_rank * width, width, 2)
    share_low = jnp.stack([image_share, text_share], axis=1).astype(BF16)
    share_all = gather_stack(share_low, group_count, "dp").reshape(all_slots, 2, 6, width)
    image_all = share_all[:, 0].reshape(all_slots, 6 * width)
    text_all = share_all[:, 1].reshape(all_slots, 6 * width)
    image_ada = dot(activated_own, image_all, 0, 0).reshape(share, 6, width)
    text_ada = dot(activated_own, text_all, 0, 0).reshape(share, 6, width)
    activated_part = dot(image_all, image_modulation.reshape(share, 6 * width), 1, 1) + dot(
        text_all, text_modulation.reshape(share, 6 * width), 1, 1
    )
    activated_part = sum_all(activated_part, size, "tensor").reshape(group_count, slots, share)
    activated_rows = gather_stack(activated_part, group_count, "dp")
    activated_rows = jnp.stack([activated_rows[k, k] for k in range(group_count)])
    group_order = group_rank ^ jnp.arange(group_count)
    activated_grad = jnp.concatenate(
        [
            lax.dynamic_index_in_dim(activated_rows, group_order[k], 0, keepdims=False)
            for k in range(group_count)
        ],
        axis=1,
    )
    condition_gradient = jax.vjp(jax.nn.silu, cond_full)[1](activated_grad)[0]

    return (
        outputs[0],
        outputs[1],
        input_grads[0],
        input_grads[1],
        condition_gradient,
        image_ada,
        attention_sum[:, : 3 * width].reshape(share, 3, width),
        attention_sum[:, 6 * width : 7 * width].T,
        image_mlp[:, units:],
        image_mlp[:, :units].T,
        text_ada,
        attention_sum[:, 3 * width : 6 * width].reshape(share, 3, width),
        attention_sum[:, 7 * width :].T,
        text_mlp[:, units:],
        text_mlp[:, :units].T,
    )


def solution(mesh):
    image = P("dp", "tensor", None)
    text = P("dp", None, None)
    columns = P("dp", None, "tensor")
    rows = P("tensor", "dp")
    plain = P("dp", "tensor")
    weights = (columns, columns, rows, plain, rows)
    return jax.shard_map(
        functools.partial(on_device, mesh.shape["dp"], mesh.shape["tensor"]),
        mesh=mesh,
        in_specs=(image, text, P("dp", None), P("dp")) + weights + weights + (image, text),
        out_specs=(image, text, image, text, P("dp", None)) + weights + weights,
        check_vma=False,
    )
```

```python
import functools
import math

import jax
import jax.numpy as jnp
from jax import lax
from jax.experimental import pallas as pl
from jax.experimental.pallas import tpu as pltpu
from jax.sharding import PartitionSpec as P

HEAD = 64
LANES = 128
F32 = jnp.float32
BF16 = jnp.bfloat16


def norm_rows(values):
    center = values - jnp.mean(values, axis=-1, keepdims=True)
    inverse = lax.rsqrt(jnp.mean(center * center, axis=-1, keepdims=True) + 1e-06)
    return (center * inverse, inverse)


def norm_back(upstream, normed, inverse):
    first = jnp.mean(upstream, axis=-1, keepdims=True)
    second = jnp.mean(upstream * normed, axis=-1, keepdims=True)
    return inverse * (upstream - first - normed * second)


def gelu_tanh(values):
    return jax.nn.gelu(values, approximate=True)


def spread(vector):
    return vector[:, None, :]


def dot(left, right, left_dim, right_dim):
    return lax.dot_general(
        left, right, (((left_dim,), (right_dim,)), ((), ())), preferred_element_type=F32
    )


def swap(value, bit, size, axis="tensor"):
    return lax.ppermute(value, axis, [(i, i ^ bit) for i in range(size)])


def bits_of(size):
    bits = []
    bit = 1
    while bit < size:
        bits.append(bit)
        bit *= 2
    return bits


def gather_start(value, size, axis="tensor"):
    have = {0: value}
    for bit in reversed(bits_of(size)[1:]):
        have.update({k ^ bit: swap(v, bit, size, axis) for k, v in list(have.items())})
    return have


def gather_end(have, size, axis="tensor"):
    have = have | {k ^ 1: swap(v, 1, size, axis) for k, v in have.items()}
    return [have[k] for k in range(size)]


def gather_pieces(value, size, axis="tensor"):
    return gather_end(gather_start(value, size, axis), size, axis)


def gather_stack(value, size, axis):
    value = value[None]
    for bit in bits_of(size):
        value = jnp.concatenate([value, swap(value, bit, size, axis)], axis=0)
    return value


def scatter_stack(value, size, axis):
    for bit in reversed(bits_of(size)):
        value = value[:bit] + swap(value[bit:], bit, size, axis)
    return value[0]


def sum_all(value, size, axis):
    for bit in bits_of(size):
        value = value + swap(value, bit, size, axis)
    return value


def scatter_start(pieces, size):
    have = dict(enumerate(pieces))
    for bit in bits_of(size)[:-1]:
        kept = {}
        for k in sorted(have, reverse=True):
            if not k & bit:
                other = swap(have[k ^ bit].astype(BF16), bit, size)
                kept[k] = have[k].astype(F32) + other.astype(F32)
        have = kept
    kept, sent = (have[k] for k in sorted(have))
    return kept, sent.astype(BF16)


def scatter_end(kept, sent, size):
    return kept.astype(F32) + swap(sent, size // 2, size).astype(F32)


def after(values, *others):
    return lax.optimization_barrier((values, others))[0]


def ring_of(count):
    return list(range(0, count, 2)) + list(range(1, count, 2))[::-1]


def ring_member(place, count):
    place = lax.rem(place + count, count)
    return jnp.where(place < (count + 1) // 2, 2 * place, 2 * (count - 1 - place) + 1)


def ring_place(member, count):
    return jnp.where(member % 2 == 0, member // 2, count - 1 - member // 2)


def ring_step(value, way, count):
    ring = ring_of(count)
    hops = [(ring[i], ring[(i + way) % count]) for i in range(count)]
    return lax.ppermute(value, "dp", hops)


def place_kernel(sizes, *refs):
    count = len(sizes)
    rows, blocks, out, sems = refs[0], refs[1 : count + 1], refs[count + 1], refs[count + 2]
    copies = []
    for index, (share, start, wide) in enumerate(sizes):
        row = pl.multiple_of(rows[index], 16)
        copies.append(
            pltpu.make_async_copy(
                blocks[index],
                out.at[pl.ds(row, share), pl.ds(start, wide)],
                sems.at[index],
            )
        )
        copies[-1].start()
    for copy in copies:
        copy.wait()


def place_blocks(blocks, rows, starts, shape):
    sizes = [(*block.shape, start) for block, start in zip(blocks, starts)]
    sizes = [(share, start, wide) for share, wide, start in sizes]
    anywhere = pl.BlockSpec(memory_space=pl.ANY)
    return pl.pallas_call(
        functools.partial(place_kernel, sizes),
        grid_spec=pltpu.PrefetchScalarGridSpec(
            num_scalar_prefetch=1,
            grid=(1,),
            in_specs=[anywhere] * len(blocks),
            out_specs=anywhere,
            scratch_shapes=[pltpu.SemaphoreType.DMA((len(blocks),))],
        ),
        out_shape=jax.ShapeDtypeStruct(shape, BF16),
        cost_estimate=pl.CostEstimate(flops=0, transcendentals=0, bytes_accessed=1024),
        name="place_blocks",
    )(jnp.stack(rows).astype(jnp.int32), *blocks)


def ring_gather(block, count):
    share, wide = block.shape
    half = wide // 2 // LANES * LANES
    place = ring_place(lax.axis_index("dp"), count)
    blocks, offsets, starts = [block], [0], [0]
    behind = ahead = block
    for hop in range(1, count // 2):
        behind = ring_step(behind, 1, count)
        ahead = ring_step(ahead, -1, count)
        behind, ahead = yield behind, ahead
        blocks += [behind, ahead]
        offsets += [-hop, hop]
        starts += [0, 0]
    behind = ring_step(behind[:, :half], 1, count)
    ahead = ring_step(ahead[:, half:], -1, count)
    behind, ahead = yield behind, ahead
    blocks += [behind, ahead]
    offsets += [-(count // 2), count // 2]
    starts += [0, half]
    rows = [ring_member(place + offset, count) * share for offset in offsets]
    yield place_blocks(blocks, rows, starts, (count * share, wide))


def ring_scatter(grad, count):
    wide = grad.shape[1]
    share = grad.shape[0] // count
    half = wide // 2 // LANES * LANES
    place = ring_place(lax.axis_index("dp"), count)

    def own(offset):
        row = ring_member(place + offset, count) * share
        return lax.dynamic_slice_in_dim(grad, row, share, 0).astype(F32)

    far = own(count // 2).astype(BF16)
    behind = ring_step(far[:, :half], 1, count)
    ahead = ring_step(far[:, half:], -1, count)
    behind, ahead = yield behind, ahead
    behind = jnp.pad(behind.astype(F32), ((0, 0), (0, wide - half)))
    ahead = jnp.pad(ahead.astype(F32), ((0, 0), (half, 0)))
    for hop in range(count // 2 - 1, 0, -1):
        behind = ring_step((own(hop) + behind).astype(BF16), 1, count)
        ahead = ring_step((own(-hop) + ahead).astype(BF16), -1, count)
        behind, ahead = yield behind, ahead
        behind, ahead = behind.astype(F32), ahead.astype(F32)
    yield own(0) + behind + ahead


def text_start(value, size):
    for bit in bits_of(size)[:-1]:
        if bit > 1:
            value = lax.reduce_precision(value, 8, 7)
            value = value + swap(value.astype(BF16), bit, size).astype(F32)
        else:
            value = value + swap(value, bit, size)
    value = lax.reduce_precision(value, 8, 7)
    return value, value.astype(BF16)


def lane_mask(half, shape):
    lane = lax.broadcasted_iota(jnp.int32, shape, 1)
    return (lane >= HEAD) if half else (lane < HEAD)


def pick(value, half):
    return jnp.where(lane_mask(half, value.shape), value, jnp.zeros_like(value))


def load_rows(refs, store):
    start = 0
    for ref in refs:
        rows = ref.shape[1]
        store[start : start + rows, :] = ref[0]
        start += rows


def attend_kernel(count, *refs):
    queries, keys, values = refs[:count], refs[count : 2 * count], refs[2 * count : 3 * count]
    outs = refs[3 * count : 4 * count]
    sums = refs[4 * count : 5 * count]
    key_all, value_all = refs[5 * count :]
    load_rows(keys, key_all)
    load_rows(values, value_all)
    for index in range(count):
        query = queries[index][0] * jnp.asarray(HEAD**-0.5, BF16)
        halves = []
        for half in range(2):
            scores = dot(key_all[...], pick(query, half), 1, 1)
            highest = jnp.max(scores, axis=0, keepdims=True)
            weights = jnp.exp(scores - highest)
            total = jnp.sum(weights, axis=0, keepdims=True)
            weights = (weights * (1.0 / total)).astype(BF16)
            mixed = dot(value_all[...], weights, 0, 0)
            halves.append(mixed[half * HEAD : (half + 1) * HEAD])
            sums[index][0, 0, half : half + 1, :] = highest + jnp.log(total)
        outs[index][0] = jnp.concatenate(halves, axis=0).T.astype(BF16)


def attend_back_kernel(count, groups, *refs):
    queries, keys, values = refs[:count], refs[count : 2 * count], refs[2 * count : 3 * count]
    upstreams = refs[3 * count : 4 * count]
    sums = refs[4 * count : 5 * count]
    outs = refs[5 * count : 6 * count]
    key_all, value_all, key_grad, value_grad = refs[6 * count :]
    load_rows(keys, key_all)
    load_rows(values, value_all)
    pair = pl.program_id(1)
    scale = jnp.asarray(HEAD**-0.5, BF16)
    query_lanes = pl.ds(pl.multiple_of(pair * LANES, LANES), LANES)
    key_lanes = pl.ds(pl.multiple_of((groups + pair) * LANES, LANES), LANES)
    value_lanes = pl.ds(pl.multiple_of((2 * groups + pair) * LANES, LANES), LANES)
    for index in range(count):
        query = queries[index][0] * scale
        upstream = upstreams[index][0]
        halves = []
        for half in range(2):
            query_half = pick(query, half)
            upstream_half = pick(upstream, half)
            scores = dot(key_all[...], query_half, 1, 1)
            weights = jnp.exp(scores - sums[index][0, 0, half : half + 1, :])
            along = dot(value_all[...], upstream_half, 1, 1)
            value_part = dot(weights.astype(BF16), upstream_half, 1, 0)
            product = weights * along
            score_grad = (product - weights * jnp.sum(product, axis=0, keepdims=True)).astype(BF16)
            key_part = dot(score_grad, query_half, 1, 0)
            if index == 0 and half == 0:
                value_grad[...] = value_part
                key_grad[...] = key_part
            else:
                value_grad[...] += value_part
                key_grad[...] += key_part
            mixed = dot(key_all[...], score_grad, 0, 0)
            halves.append(mixed[half * HEAD : (half + 1) * HEAD])
        query_grad = jnp.concatenate(halves, axis=0).T * HEAD**-0.5
        outs[index][0, :, query_lanes] = query_grad.astype(BF16)
    start = 0
    for index in range(count):
        rows = outs[index].shape[1]
        outs[index][0, :, key_lanes] = key_grad[start : start + rows, :].astype(BF16)
        outs[index][0, :, value_lanes] = value_grad[start : start + rows, :].astype(BF16)
        start += rows


def lane_blocks(parts, offset):
    return [
        pl.BlockSpec((1, part.shape[1], LANES), lambda s, p, o=offset: (s, 0, o + p))
        for part in parts
    ]


def widen(part, copies):
    slots, rows, width = part.shape
    width = width // copies
    extra = -width % LANES
    if not extra:
        return part
    part = jnp.pad(part.reshape(slots, rows, copies, width), ((0, 0), (0, 0), (0, 0), (0, extra)))
    return part.reshape(slots, rows, copies * (width + extra))


def narrow(part, copies, width):
    slots, rows, wide = part.shape
    wide = wide // copies
    if wide == width:
        return part
    return part.reshape(slots, rows, copies, wide)[..., :width].reshape(slots, rows, -1)


def attention_cost(slots, rows, width, products):
    return pl.CostEstimate(
        flops=products * 8 * slots * rows * rows * width,
        transcendentals=slots * rows * rows * (width // HEAD),
        bytes_accessed=slots * rows * width * 2 * (4 + 3 * (products > 2)),
    )


def attend(parts):
    slots = parts[0].shape[0]
    width = parts[0].shape[2] // 3
    parts = [widen(part, 3) for part in parts]
    count = len(parts)
    wide = parts[0].shape[2] // 3
    groups = wide // LANES
    total = sum(part.shape[1] for part in parts)
    outs = pl.pallas_call(
        functools.partial(attend_kernel, count),
        grid=(slots, groups),
        in_specs=lane_blocks(parts, 0) + lane_blocks(parts, groups) + lane_blocks(parts, 2 * groups),
        out_specs=lane_blocks(parts, 0)
        + [
            pl.BlockSpec((1, 1, 2, part.shape[1]), lambda s, p: (s, p, 0, 0)) for part in parts
        ],
        out_shape=[jax.ShapeDtypeStruct((slots, part.shape[1], wide), BF16) for part in parts]
        + [jax.ShapeDtypeStruct((slots, groups, 2, part.shape[1]), F32) for part in parts],
        scratch_shapes=[pltpu.VMEM((total, LANES), BF16)] * 2,
        compiler_params=pltpu.CompilerParams(vmem_limit_bytes=48 * 1024 * 1024),
        cost_estimate=attention_cost(slots, total, wide, 2),
        name="attend",
    )(*parts, *parts, *parts)
    return [narrow(out, 1, width) for out in outs[:count]], outs[count:]


def attend_back(parts, upstreams, sums):
    slots = parts[0].shape[0]
    width = parts[0].shape[2] // 3
    parts = [widen(part, 3) for part in parts]
    upstreams = [widen(part, 1) for part in upstreams]
    count = len(parts)
    wide = parts[0].shape[2] // 3
    groups = wide // LANES
    total = sum(part.shape[1] for part in parts)
    outs = pl.pallas_call(
        functools.partial(attend_back_kernel, count, groups),
        grid=(slots, groups),
        in_specs=lane_blocks(parts, 0)
        + lane_blocks(parts, groups)
        + lane_blocks(parts, 2 * groups)
        + lane_blocks(upstreams, 0)
        + [
            pl.BlockSpec((1, 1, 2, part.shape[1]), lambda s, p: (s, p, 0, 0)) for part in parts
        ],
        out_specs=[
            pl.BlockSpec((1, part.shape[1], 3 * wide), lambda s, p: (s, 0, 0)) for part in parts
        ],
        out_shape=[jax.ShapeDtypeStruct((slots, part.shape[1], 3 * wide), BF16) for part in parts],
        scratch_shapes=[pltpu.VMEM((total, LANES), BF16)] * 2 + [pltpu.VMEM((total, LANES), F32)] * 2,
        compiler_params=pltpu.CompilerParams(vmem_limit_bytes=48 * 1024 * 1024),
        cost_estimate=attention_cost(slots, total, wide, 5),
        name="attend_back",
    )(*parts, *parts, *parts, *upstreams, *sums)
    return [narrow(out, 3, width) for out in outs]


def rows_kernel(count, *refs):
    lefts, rights, out = refs[:count], refs[count : 2 * count], refs[-1]
    total = None
    for left, right in zip(lefts, rights):
        for slot in range(left.shape[0]):
            part = dot(left[slot], right[slot], 0, 0)
            total = part if total is None else total + part
    out[...] = total.astype(BF16)


def weight_grad(pairs):
    joined = None
    rows = pairs[0][0][0].shape[-1]
    wide = sum(rights[0].shape[-1] for _, rights in pairs)
    start = 0
    for lefts, rights in pairs:
        part = rights[0].shape[-1]
        if part % LANES or start % part:
            return jnp.concatenate([plain_grad(*pair) for pair in pairs], axis=1)
        count = len(lefts)
        step = 256
        ins = [
            pl.BlockSpec((left.shape[0], left.shape[1], step), lambda i: (0, 0, i))
            for left in lefts
        ] + [
            pl.BlockSpec(right.shape, lambda i: (0, 0, 0), pipeline_mode=pl.Buffered(1))
            for right in rights
        ]
        operands = (*lefts, *rights)
        if joined is not None:
            ins.append(pl.BlockSpec(memory_space=pl.ANY))
            operands += (joined,)
        joined = pl.pallas_call(
            functools.partial(rows_kernel, count),
            grid=(rows // step,),
            in_specs=ins,
            out_specs=pl.BlockSpec((step, part), lambda i, c=start // part: (i, c)),
            out_shape=jax.ShapeDtypeStruct((rows, wide), BF16),
            input_output_aliases={} if joined is None else {2 * count: 0},
            compiler_params=pltpu.CompilerParams(vmem_limit_bytes=48 * 1024 * 1024),
            cost_estimate=pl.CostEstimate(flops=0, transcendentals=0, bytes_accessed=1024),
            name="weight_grad",
        )(*operands)
        start += part
    return joined


NO_COST = pl.CostEstimate(flops=0, transcendentals=0, bytes_accessed=1024)
LIMIT = pltpu.CompilerParams(vmem_limit_bytes=48 * 1024 * 1024)


def tile_of(wide, start, most):
    return max(t for t in range(LANES, most + 1, LANES) if wide % t == 0 and start % t == 0)


def fits(weight):
    _, start, wide = weight
    return wide % LANES == 0 and start % LANES == 0


def cut(weight):
    array, start, wide = weight
    return array[:, start : start + wide]


def row_blocks(ref):
    slots, rows, columns = ref.shape
    if rows % 16 == 0:
        return [(slice(None), ref[...].reshape(slots * rows, columns))]
    return [(slice(slot, slot + 1), ref[slot]) for slot in range(slots)]


def store_rows(ref, place, value):
    slots = ref.shape[0] if place == slice(None) else 1
    ref[place] = value.reshape(slots, -1, value.shape[-1]).astype(ref.dtype)


def product_kernel(count, weight_dim, *refs):
    pieces, weight, outs = refs[:count], refs[count], refs[count + 1 :]
    for piece, out in zip(pieces, outs):
        for place, rows in row_blocks(piece):
            store_rows(out, place, dot(rows, weight[...], 1, weight_dim))


def whole_block(array):
    return pl.BlockSpec(array.shape, lambda j: (0, 0, 0), pipeline_mode=pl.Buffered(1))


def products_of(pieces, weight, weight_dim, kinds, late=False):
    array, start, wide = weight
    if not fits(weight) or (weight_dim and start % wide):
        return [
            dot(piece, cut(weight), 2, weight_dim).astype(kind)
            for piece, kind in zip(pieces, kinds)
        ]
    count = len(pieces)
    slots, _, depth = pieces[0].shape
    if weight_dim:
        result = array.shape[0]
        tile = tile_of(result, 0, 768)
        block = pl.BlockSpec((tile, wide), lambda j: (j, start // wide))
    else:
        result = wide
        tile = tile_of(wide, start, 768)
        block = pl.BlockSpec((depth, tile), lambda j: (0, start // tile + j))
    rows = slots * sum(piece.shape[1] for piece in pieces)
    cost = pl.CostEstimate(
        flops=4 * rows * depth * result, transcendentals=0, bytes_accessed=4 * rows * result
    )
    return pl.pallas_call(
        functools.partial(product_kernel, count, weight_dim),
        grid=(result // tile,),
        in_specs=[whole_block(piece) for piece in pieces] + [block],
        out_specs=[
            pl.BlockSpec((slots, piece.shape[1], tile), lambda j: (0, 0, j)) for piece in pieces
        ],
        out_shape=[
            jax.ShapeDtypeStruct((slots, piece.shape[1], result), kind)
            for piece, kind in zip(pieces, kinds)
        ],
        compiler_params=LIMIT,
        cost_estimate=cost if late else NO_COST,
        name="products",
    )(*pieces, array)


def hidden_kernel(count, *refs):
    pieces, downs, up, down = refs[:count], refs[count : 2 * count], refs[2 * count], refs[2 * count + 1]
    actives, grads = refs[2 * count + 2 : 3 * count + 2], refs[3 * count + 2 :]
    for piece, upstream, active, grad in zip(pieces, downs, actives, grads):
        for (place, rows), (_, above) in zip(row_blocks(piece), row_blocks(upstream)):
            hidden = dot(rows, up[...], 1, 0)
            active_grad = dot(above, down[...], 1, 0)
            square = hidden * hidden
            scale = (2 / math.pi) ** 0.5
            bend = jnp.tanh(hidden * (scale + scale * 0.044715 * square))
            half = 0.5 + 0.5 * bend
            slope = half + hidden * (0.5 - 0.5 * bend * bend) * (
                scale + scale * 0.134145 * square
            )
            store_rows(active, place, hidden * half)
            store_rows(grad, place, active_grad * slope)


def hidden_both(pieces, downs, up, down):
    count = len(pieces)
    if not (fits(up) and fits(down)):
        hidden = [dot(piece, cut(up), 2, 0) for piece in pieces]
        active_grad = [dot(piece, cut(down), 2, 0) for piece in downs]
        return (
            [gelu_tanh(value).astype(BF16) for value in hidden],
            [
                jax.vjp(gelu_tanh, value)[1](grad)[0].astype(BF16)
                for value, grad in zip(hidden, active_grad)
            ],
        )
    slots, _, depth = pieces[0].shape
    wide = up[2]
    tile = tile_of(wide, math.gcd(up[1], down[1]), 512)
    outs = pl.pallas_call(
        functools.partial(hidden_kernel, count),
        grid=(wide // tile,),
        in_specs=[whole_block(piece) for piece in (*pieces, *downs)]
        + [
            pl.BlockSpec((depth, tile), lambda j, o=block[1] // tile: (0, o + j))
            for block in (up, down)
        ],
        out_specs=[
            pl.BlockSpec((slots, piece.shape[1], tile), lambda j: (0, 0, j)) for piece in pieces
        ]
        * 2,
        out_shape=[
            jax.ShapeDtypeStruct((slots, piece.shape[1], wide), BF16) for piece in pieces
        ]
        * 2,
        compiler_params=LIMIT,
        cost_estimate=NO_COST,
        name="hidden_both",
    )(*pieces, *downs, up[0], down[0])
    return outs[:count], outs[count:]


def plain_grad(lefts, rights):
    left = jnp.concatenate([v.reshape(-1, v.shape[-1]) for v in lefts], axis=0)
    right = jnp.concatenate([v.reshape(-1, v.shape[-1]) for v in rights], axis=0)
    return dot(left, right, 0, 0).astype(BF16)


def on_device(
    group_count,
    tensor_size,
    image_tokens,
    text_tokens,
    condition,
    group_size,
    image_modulation,
    image_attention_in,
    image_attention_out,
    image_hidden_in,
    image_hidden_out,
    text_modulation,
    text_attention_in,
    text_attention_out,
    text_hidden_in,
    text_hidden_out,
    image_cotangent,
    text_cotangent,
):
    size = tensor_size
    slots, image_length, model = image_tokens.shape
    text_length = text_tokens.shape[1]
    share, _, width = image_attention_in.shape
    units = image_hidden_in.shape[1]
    tensor_rank = lax.axis_index("tensor")
    group_rank = lax.axis_index("dp")

    def gathered(*blocks):
        joined = blocks[0] if len(blocks) == 1 else jnp.concatenate(blocks, axis=1)
        return lax.all_gather(joined, "dp", axis=0, tiled=True)

    packed_first = gathered(
        image_attention_in.reshape(share, 3 * width),
        text_attention_in.reshape(share, 3 * width),
        image_attention_out.T,
        text_attention_out.T,
    )
    image_up = gathered(image_hidden_in)
    image_down = gathered(image_hidden_out.T)
    weight_in = ((packed_first, 0, 3 * width), (packed_first, 3 * width, 3 * width))
    weight_out = ((packed_first, 6 * width, width), (packed_first, 7 * width, width))

    alive = (jnp.arange(slots) < group_size[0]).astype(F32)[:, None, None]
    cond_full = condition.astype(F32)
    activated_low = jax.nn.silu(cond_full).astype(BF16)
    activated_all = gather_stack(activated_low, group_count, "dp").reshape(-1, model)
    activated_own = lax.dynamic_slice_in_dim(activated_all, group_rank * share, share, 1)
    all_slots = activated_own.shape[0]
    mod_parts = jnp.concatenate(
        [
            dot(activated_own, image_modulation.reshape(share, 6 * width), 1, 0),
            dot(activated_own, text_modulation.reshape(share, 6 * width), 1, 0),
        ],
        axis=1,
    ).reshape(group_count, slots, 12 * width)
    mod_own = scatter_stack(mod_parts, group_count, "dp")
    modulations = lax.all_gather(
        mod_own.reshape(slots, 2, 6, width), "tensor", axis=3, tiled=True
    )
    mods = (modulations[:, 0], modulations[:, 1])

    tokens = (image_tokens.astype(F32), text_tokens.astype(F32))
    outgoing = (image_cotangent.astype(F32) * alive, text_cotangent.astype(F32) * alive)

    half = size // 2
    near_kinds = [F32] + [BF16] * (half - 1)

    def scattered(grad):
        return lax.psum_scatter(grad, "dp", scatter_dimension=0, tiled=True).astype(F32)

    def row_products(pieces, weight, weight_dim, late=False):
        far = products_of(pieces[half:], weight, weight_dim, near_kinds, late)
        near = products_of(after(pieces[:half], far), weight, weight_dim, near_kinds, late)
        return [*near, *far]

    def image_sum(pieces, weight, weight_dim, late=False):
        products = row_products(pieces, weight, weight_dim, late)
        return scatter_end(*scatter_start(products, size), size)

    def text_sum(piece, weight, weight_dim, late=False):
        (product,) = products_of([piece], weight, weight_dim, [F32], late)
        return scatter_end(*text_start(product, size), size)

    def modulated(values, mod, shift, scale):
        normed, inverse = norm_rows(values)
        rows = normed * (1.0 + spread(mod[:, scale])) + spread(mod[:, shift])
        return normed, inverse, rows.astype(BF16)

    def second_back(stream, second_grad, normed, inverse):
        mod = mods[stream]
        shift_two_grad = jnp.sum(second_grad, axis=1)
        scale_two_grad = jnp.sum(second_grad * normed, axis=1)
        middle_grad = outgoing[stream] + norm_back(
            second_grad * (1.0 + spread(mod[:, 4])), normed, inverse
        )
        low = (middle_grad * spread(mod[:, 2])).astype(BF16)
        return middle_grad, low, shift_two_grad, scale_two_grad

    low_kinds = [BF16] * size

    normed_one, inverse_one, image_first = modulated(tokens[0], mods[0], 0, 1)
    text_normed_one, text_inverse_one, text_first = modulated(tokens[1], mods[1], 0, 1)
    first_pieces = gather_pieces(image_first, size)
    packed = products_of(first_pieces, weight_in[0], 0, low_kinds)
    text_packed = products_of([text_first], weight_in[1], 0, [BF16])
    down_rows = [
        (outgoing[stream] * spread(mods[stream][:, 5])).astype(BF16) for stream in range(2)
    ]
    down_have = gather_start(after(down_rows[0], first_pieces), size)
    parts = after([*packed, *text_packed], down_have)
    up_ring = ring_gather(
        after(jnp.concatenate([text_hidden_in, text_hidden_out.T], axis=1), parts), group_count
    )
    up_hop = next(up_ring)
    attended, sums = attend(parts)
    down_pieces = gather_end(after(down_have, attended), size)
    attended, up_hop = lax.optimization_barrier((attended, up_hop))
    up_hop = up_ring.send(up_hop)
    attended_parts = (attended[:-1], attended[-1:])

    branch = image_sum(attended_parts[0], weight_out[0], 1)
    branch, up_hop = lax.optimization_barrier((branch, up_hop))
    up_hop = up_ring.send(up_hop)
    middle = tokens[0] + spread(mods[0][:, 2]) * branch
    normed_two, inverse_two, image_second = modulated(middle, mods[0], 3, 4)
    second_pieces = gather_pieces(image_second, size)
    text_branch = text_sum(after(attended_parts[1][0], second_pieces), weight_out[1], 1)
    up_weight, down_weight = (image_up, 0, units), (image_down, 0, units)
    near = hidden_both(second_pieces[:half], down_pieces[:half], up_weight, down_weight)
    far_pieces, up_hop = after((second_pieces[half:], up_hop), near)
    up_hop = up_ring.send(up_hop)
    far = hidden_both(far_pieces, down_pieces[half:], up_weight, down_weight)
    active = [*near[0], *far[0]]
    hidden_grad = [*near[1], *far[1]]
    kept, sent = scatter_start(row_products(hidden_grad, up_weight, 1), size)
    for _ in range(group_count // 2 - 4):
        up_hop = up_ring.send(up_hop)
    up_hop = after(up_hop, sent)
    text_both = up_ring.send(up_hop)

    text_up_weight, text_down_weight = (text_both, 0, units), (text_both, units, units)
    text_middle = tokens[1] + spread(mods[1][:, 2]) * text_branch
    text_normed_two, text_inverse_two, text_second = modulated(text_middle, mods[1], 3, 4)
    text_active, text_hidden_grad = hidden_both(
        [text_second], [down_rows[1]], text_up_weight, text_down_weight
    )
    (text_product,) = products_of(text_hidden_grad, text_up_weight, 1, [F32])
    text_second_grad = scatter_end(*text_start(text_product, size), size)
    image_mlp_grad = weight_grad(
        after([(down_pieces, active), (second_pieces, hidden_grad)], sent)
    )
    second_grad = after(scatter_end(kept, sent, size), image_mlp_grad, text_product)
    image_mlp = scattered(after(image_mlp_grad, second_grad))
    middle_grad, low, shift_two_grad, scale_two_grad = second_back(
        0, second_grad, normed_two, inverse_two
    )
    gate_one_grad = jnp.sum(middle_grad * branch, axis=1)

    low = after(low, text_second_grad)
    branch_grads = gather_pieces(low, size)
    text_mlp_grad = weight_grad(
        after([([down_rows[1]], text_active), ([text_second], text_hidden_grad)], low)
    )
    upstreams = products_of(after(branch_grads, text_mlp_grad), weight_out[0], 0, low_kinds)
    text_middle_grad, text_low, text_shift_two_grad, text_scale_two_grad = second_back(
        1, text_second_grad, text_normed_two, text_inverse_two
    )
    text_gate_one_grad = jnp.sum(text_middle_grad * text_branch, axis=1)
    text_upstream = products_of([text_low], weight_out[1], 0, [BF16])
    text_ring = ring_scatter(after(text_mlp_grad, branch_grads), group_count)
    text_hop = next(text_ring)
    packed_grads = attend_back(parts, [*upstreams, *text_upstream], sums)
    packed_grads, text_hop = lax.optimization_barrier((packed_grads, text_hop))
    text_hop = text_ring.send(text_hop)
    attention_grad = weight_grad(
        [
            (first_pieces, packed_grads[:-1]),
            ([text_first], packed_grads[-1:]),
            (branch_grads, attended_parts[0]),
            ([text_low], attended_parts[1]),
        ]
    )
    attention_sum = scattered(attention_grad)
    packed_grads, text_hop, active, text_active = after(
        (packed_grads, text_hop, active, text_active), attention_grad
    )
    text_hop = text_ring.send(text_hop)

    def first_back(stream, first_grad, normed, inverse, middle_grad):
        mod = mods[stream]
        shift_one_grad = jnp.sum(first_grad, axis=1)
        scale_one_grad = jnp.sum(first_grad * normed, axis=1)
        input_grad = middle_grad + norm_back(
            first_grad * (1.0 + spread(mod[:, 1])), normed, inverse
        )
        return input_grad, shift_one_grad, scale_one_grad

    def finish(stream, middle, branch_two):
        result = middle + spread(mods[stream][:, 5]) * branch_two
        gate_two_grad = jnp.sum(outgoing[stream] * branch_two, axis=1)
        return (result * alive).astype(BF16), gate_two_grad

    first_grad = image_sum(packed_grads[:-1], weight_in[0], 1, True)
    text_first_grad = text_sum(packed_grads[-1], weight_in[1], 1, True)
    branch_two = image_sum(active, down_weight, 1, True)
    text_branch_two = text_sum(text_active[0], text_down_weight, 1, True)
    text_first_grad, text_hop = lax.optimization_barrier((text_first_grad, text_hop))
    for _ in range(group_count // 2 - 3):
        text_hop = text_ring.send(text_hop)
    first_grad, text_hop = lax.optimization_barrier((first_grad, text_hop))
    text_mlp = text_ring.send(text_hop)
    input_grads = [None, None]
    input_grads[0], shift_one_grad, scale_one_grad = first_back(
        0, first_grad, normed_one, inverse_one, middle_grad
    )
    input_grads[1], text_shift_one_grad, text_scale_one_grad = first_back(
        1, text_first_grad, text_normed_one, text_inverse_one, text_middle_grad
    )
    outputs = [None, None]
    outputs[0], gate_two_grad = finish(0, middle, branch_two)
    outputs[1], text_gate_two_grad = finish(1, text_middle, text_branch_two)
    mod_grads = (
        jnp.stack(
            [
                shift_one_grad,
                scale_one_grad,
                gate_one_grad,
                shift_two_grad,
                scale_two_grad,
                gate_two_grad,
            ],
            axis=1,
        ),
        jnp.stack(
            [
                text_shift_one_grad,
                text_scale_one_grad,
                text_gate_one_grad,
                text_shift_two_grad,
                text_scale_two_grad,
                text_gate_two_grad,
            ],
            axis=1,
        ),
    )

    image_blocks = jnp.stack(
        [
            lax.dynamic_slice_in_dim(mod_grads[0], (tensor_rank ^ k) * width, width, 2)
            for k in range(size)
        ]
    )
    image_share = scatter_stack(image_blocks, size, "tensor")
    text_share = lax.dynamic_slice_in_dim(mod_grads[1], tensor_rank * width, width, 2)
    share_low = jnp.stack([image_share, text_share], axis=1).astype(BF16)
    share_all = gather_stack(share_low, group_count, "dp").reshape(all_slots, 2, 6, width)
    image_all = share_all[:, 0].reshape(all_slots, 6 * width)
    text_all = share_all[:, 1].reshape(all_slots, 6 * width)
    image_ada = dot(activated_own, image_all, 0, 0).reshape(share, 6, width)
    text_ada = dot(activated_own, text_all, 0, 0).reshape(share, 6, width)
    activated_part = dot(image_all, image_modulation.reshape(share, 6 * width), 1, 1) + dot(
        text_all, text_modulation.reshape(share, 6 * width), 1, 1
    )
    activated_part = sum_all(activated_part, size, "tensor").reshape(group_count, slots, share)
    activated_rows = gather_stack(activated_part, group_count, "dp")
    activated_rows = jnp.stack([activated_rows[k, k] for k in range(group_count)])
    activated_grad = jnp.concatenate(
        [
            lax.dynamic_index_in_dim(activated_rows, group_rank ^ k, 0, keepdims=False)
            for k in range(group_count)
        ],
        axis=1,
    )
    condition_gradient = jax.vjp(jax.nn.silu, cond_full)[1](activated_grad)[0]

    return (
        outputs[0],
        outputs[1],
        input_grads[0],
        input_grads[1],
        condition_gradient,
        image_ada,
        attention_sum[:, : 3 * width].reshape(share, 3, width),
        attention_sum[:, 6 * width : 7 * width].T,
        image_mlp[:, units:],
        image_mlp[:, :units].T,
        text_ada,
        attention_sum[:, 3 * width : 6 * width].reshape(share, 3, width),
        attention_sum[:, 7 * width :].T,
        text_mlp[:, units:],
        text_mlp[:, :units].T,
    )


def solution(mesh):
    image = P("dp", "tensor", None)
    text = P("dp", None, None)
    columns = P("dp", None, "tensor")
    rows = P("tensor", "dp")
    plain = P("dp", "tensor")
    weights = (columns, columns, rows, plain, rows)
    return jax.shard_map(
        functools.partial(on_device, mesh.shape["dp"], mesh.shape["tensor"]),
        mesh=mesh,
        in_specs=(image, text, P("dp", None), P("dp")) + weights + weights + (image, text),
        out_specs=(image, text, image, text, P("dp", None)) + weights + weights,
        check_vma=False,
    )
```

```python
import functools
import math

import jax
import jax.numpy as jnp
from jax import lax
from jax.experimental import pallas as pl
from jax.experimental.pallas import tpu as pltpu
from jax.sharding import PartitionSpec as P

HEAD = 64
LANES = 128
F32 = jnp.float32
BF16 = jnp.bfloat16


def norm_rows(values):
    center = values - jnp.mean(values, axis=-1, keepdims=True)
    inverse = lax.rsqrt(jnp.mean(center * center, axis=-1, keepdims=True) + 1e-06)
    return (center * inverse, inverse)


def norm_back(upstream, normed, inverse):
    first = jnp.mean(upstream, axis=-1, keepdims=True)
    second = jnp.mean(upstream * normed, axis=-1, keepdims=True)
    return inverse * (upstream - first - normed * second)


def gelu_tanh(values):
    return jax.nn.gelu(values, approximate=True)


def spread(vector):
    return vector[:, None, :]


def dot(left, right, left_dim, right_dim):
    return lax.dot_general(
        left, right, (((left_dim,), (right_dim,)), ((), ())), preferred_element_type=F32
    )


def swap(value, bit, size, axis="tensor"):
    return lax.ppermute(value, axis, [(i, i ^ bit) for i in range(size)])


def bits_of(size):
    bits = []
    bit = 1
    while bit < size:
        bits.append(bit)
        bit *= 2
    return bits


def gather_start(value, size, axis="tensor"):
    have = {0: value}
    for bit in reversed(bits_of(size)[1:]):
        have.update({k ^ bit: swap(v, bit, size, axis) for k, v in list(have.items())})
    return have


def gather_end(have, size, axis="tensor"):
    have = have | {k ^ 1: swap(v, 1, size, axis) for k, v in have.items()}
    return [have[k] for k in range(size)]


def gather_pieces(value, size, axis="tensor"):
    return gather_end(gather_start(value, size, axis), size, axis)


def gather_stack(value, size, axis):
    value = value[None]
    for bit in bits_of(size):
        value = jnp.concatenate([value, swap(value, bit, size, axis)], axis=0)
    return value


def scatter_stack(value, size, axis):
    for bit in reversed(bits_of(size)):
        value = value[:bit] + swap(value[bit:], bit, size, axis)
    return value[0]


def sum_all(value, size, axis):
    for bit in bits_of(size):
        value = value + swap(value, bit, size, axis)
    return value


def scatter_start(pieces, size):
    have = dict(enumerate(pieces))
    for bit in bits_of(size)[:-1]:
        kept = {}
        for k in sorted(have, reverse=True):
            if not k & bit:
                other = swap(have[k ^ bit].astype(BF16), bit, size)
                kept[k] = have[k].astype(F32) + other.astype(F32)
        have = kept
    kept, sent = (have[k] for k in sorted(have))
    return kept, sent.astype(BF16)


def scatter_end(kept, sent, size):
    return kept.astype(F32) + swap(sent, size // 2, size).astype(F32)


def after(values, *others):
    return lax.optimization_barrier((values, others))[0]


def ring_of(count):
    return list(range(0, count, 2)) + list(range(1, count, 2))[::-1]


def ring_member(place, count):
    place = lax.rem(place + count, count)
    return jnp.where(place < (count + 1) // 2, 2 * place, 2 * (count - 1 - place) + 1)


def ring_place(member, count):
    return jnp.where(member % 2 == 0, member // 2, count - 1 - member // 2)


def ring_step(value, way, count):
    ring = ring_of(count)
    hops = [(ring[i], ring[(i + way) % count]) for i in range(count)]
    return lax.ppermute(value, "dp", hops)


def place_kernel(steps, order, *refs):
    out = refs[-1]
    for step, (inputs, starts) in enumerate(steps):

        @pl.when(pl.program_id(0) == step)
        def _():
            for index, start in zip(inputs, starts):
                out[:, start : start + refs[index].shape[1]] = refs[index][...]


def place_blocks(blocks, steps, order, wide):
    share = blocks[0].shape[0]
    return pl.pallas_call(
        functools.partial(place_kernel, steps),
        grid_spec=pltpu.PrefetchScalarGridSpec(
            num_scalar_prefetch=1,
            grid=(len(steps),),
            in_specs=[
                pl.BlockSpec(block.shape, lambda s, order: (0, 0), pipeline_mode=pl.Buffered(1))
                for block in blocks
            ],
            out_specs=pl.BlockSpec((share, wide), lambda s, order: (order[s], 0)),
        ),
        out_shape=jax.ShapeDtypeStruct((len(steps) * share, wide), BF16),
        compiler_params=pltpu.CompilerParams(vmem_limit_bytes=48 * 1024 * 1024),
        cost_estimate=pl.CostEstimate(flops=0, transcendentals=0, bytes_accessed=1024),
        name="place_blocks",
    )(jnp.stack(order).astype(jnp.int32), *blocks)


def ring_gather(block, count):
    wide = block.shape[1]
    half = wide // 2 // LANES * LANES
    place = ring_place(lax.axis_index("dp"), count)
    blocks, offsets, steps = [block], [0], [((0,), (0,))]
    behind = ahead = block
    for hop in range(1, count // 2):
        behind = ring_step(behind, 1, count)
        ahead = ring_step(ahead, -1, count)
        behind, ahead = yield behind, ahead
        blocks += [behind, ahead]
        offsets += [-hop, hop]
        steps += [((2 * hop - 1,), (0,)), ((2 * hop,), (0,))]
    behind = ring_step(behind[:, :half], 1, count)
    ahead = ring_step(ahead[:, half:], -1, count)
    behind, ahead = yield behind, ahead
    blocks += [behind, ahead]
    offsets.append(count // 2)
    steps.append(((count - 1, count), (0, half)))
    yield place_blocks(
        blocks, steps, [ring_member(place + offset, count) for offset in offsets], wide
    )


def ring_scatter(grad, count):
    wide = grad.shape[1]
    share = grad.shape[0] // count
    half = wide // 2 // LANES * LANES
    place = ring_place(lax.axis_index("dp"), count)

    def own(offset):
        row = ring_member(place + offset, count) * share
        return lax.dynamic_slice_in_dim(grad, row, share, 0).astype(F32)

    far = own(count // 2).astype(BF16)
    behind = ring_step(far[:, :half], 1, count)
    ahead = ring_step(far[:, half:], -1, count)
    behind, ahead = yield behind, ahead
    behind = jnp.pad(behind.astype(F32), ((0, 0), (0, wide - half)))
    ahead = jnp.pad(ahead.astype(F32), ((0, 0), (half, 0)))
    for hop in range(count // 2 - 1, 0, -1):
        behind = ring_step((own(hop) + behind).astype(BF16), 1, count)
        ahead = ring_step((own(-hop) + ahead).astype(BF16), -1, count)
        behind, ahead = yield behind, ahead
        behind, ahead = behind.astype(F32), ahead.astype(F32)
    yield own(0) + behind + ahead


def text_start(value, size):
    for bit in bits_of(size)[:-1]:
        if bit > 1:
            value = lax.reduce_precision(value, 8, 7)
            value = value + swap(value.astype(BF16), bit, size).astype(F32)
        else:
            value = value + swap(value, bit, size)
    value = lax.reduce_precision(value, 8, 7)
    return value, value.astype(BF16)


def lane_mask(half, shape):
    lane = lax.broadcasted_iota(jnp.int32, shape, 1)
    return (lane >= HEAD) if half else (lane < HEAD)


def pick(value, half):
    return jnp.where(lane_mask(half, value.shape), value, jnp.zeros_like(value))


def load_rows(refs, store):
    start = 0
    for ref in refs:
        rows = ref.shape[1]
        store[start : start + rows, :] = ref[0]
        start += rows


def attend_kernel(count, *refs):
    queries, keys, values = refs[:count], refs[count : 2 * count], refs[2 * count : 3 * count]
    outs = refs[3 * count : 4 * count]
    sums = refs[4 * count : 5 * count]
    key_all, value_all = refs[5 * count :]
    load_rows(keys, key_all)
    load_rows(values, value_all)
    for index in range(count):
        query = queries[index][0] * jnp.asarray(HEAD**-0.5, BF16)
        halves = []
        for half in range(2):
            scores = dot(key_all[...], pick(query, half), 1, 1)
            highest = jnp.max(scores, axis=0, keepdims=True)
            weights = jnp.exp(scores - highest)
            total = jnp.sum(weights, axis=0, keepdims=True)
            weights = (weights * (1.0 / total)).astype(BF16)
            mixed = dot(value_all[...], weights, 0, 0)
            halves.append(mixed[half * HEAD : (half + 1) * HEAD])
            sums[index][0, 0, half : half + 1, :] = highest + jnp.log(total)
        outs[index][0] = jnp.concatenate(halves, axis=0).T.astype(BF16)


def attend_back_kernel(count, groups, *refs):
    queries, keys, values = refs[:count], refs[count : 2 * count], refs[2 * count : 3 * count]
    upstreams = refs[3 * count : 4 * count]
    sums = refs[4 * count : 5 * count]
    outs = refs[5 * count : 6 * count]
    key_all, value_all, key_grad, value_grad = refs[6 * count :]
    load_rows(keys, key_all)
    load_rows(values, value_all)
    pair = pl.program_id(1)
    scale = jnp.asarray(HEAD**-0.5, BF16)
    query_lanes = pl.ds(pl.multiple_of(pair * LANES, LANES), LANES)
    key_lanes = pl.ds(pl.multiple_of((groups + pair) * LANES, LANES), LANES)
    value_lanes = pl.ds(pl.multiple_of((2 * groups + pair) * LANES, LANES), LANES)
    for index in range(count):
        query = queries[index][0] * scale
        upstream = upstreams[index][0]
        halves = []
        for half in range(2):
            query_half = pick(query, half)
            upstream_half = pick(upstream, half)
            scores = dot(key_all[...], query_half, 1, 1)
            weights = jnp.exp(scores - sums[index][0, 0, half : half + 1, :])
            along = dot(value_all[...], upstream_half, 1, 1)
            value_part = dot(weights.astype(BF16), upstream_half, 1, 0)
            product = weights * along
            score_grad = (product - weights * jnp.sum(product, axis=0, keepdims=True)).astype(BF16)
            key_part = dot(score_grad, query_half, 1, 0)
            if index == 0 and half == 0:
                value_grad[...] = value_part
                key_grad[...] = key_part
            else:
                value_grad[...] += value_part
                key_grad[...] += key_part
            mixed = dot(key_all[...], score_grad, 0, 0)
            halves.append(mixed[half * HEAD : (half + 1) * HEAD])
        query_grad = jnp.concatenate(halves, axis=0).T * HEAD**-0.5
        outs[index][0, :, query_lanes] = query_grad.astype(BF16)
    start = 0
    for index in range(count):
        rows = outs[index].shape[1]
        outs[index][0, :, key_lanes] = key_grad[start : start + rows, :].astype(BF16)
        outs[index][0, :, value_lanes] = value_grad[start : start + rows, :].astype(BF16)
        start += rows


def lane_blocks(parts, offset):
    return [
        pl.BlockSpec((1, part.shape[1], LANES), lambda s, p, o=offset: (s, 0, o + p))
        for part in parts
    ]


def widen(part, copies):
    slots, rows, width = part.shape
    width = width // copies
    extra = -width % LANES
    if not extra:
        return part
    part = jnp.pad(part.reshape(slots, rows, copies, width), ((0, 0), (0, 0), (0, 0), (0, extra)))
    return part.reshape(slots, rows, copies * (width + extra))


def narrow(part, copies, width):
    slots, rows, wide = part.shape
    wide = wide // copies
    if wide == width:
        return part
    return part.reshape(slots, rows, copies, wide)[..., :width].reshape(slots, rows, -1)


def attention_cost(slots, rows, width, products):
    return pl.CostEstimate(
        flops=products * 8 * slots * rows * rows * width,
        transcendentals=slots * rows * rows * (width // HEAD),
        bytes_accessed=slots * rows * width * 2 * (4 + 3 * (products > 2)),
    )


def attend(parts):
    slots = parts[0].shape[0]
    width = parts[0].shape[2] // 3
    parts = [widen(part, 3) for part in parts]
    count = len(parts)
    wide = parts[0].shape[2] // 3
    groups = wide // LANES
    total = sum(part.shape[1] for part in parts)
    outs = pl.pallas_call(
        functools.partial(attend_kernel, count),
        grid=(slots, groups),
        in_specs=lane_blocks(parts, 0) + lane_blocks(parts, groups) + lane_blocks(parts, 2 * groups),
        out_specs=lane_blocks(parts, 0)
        + [
            pl.BlockSpec((1, 1, 2, part.shape[1]), lambda s, p: (s, p, 0, 0)) for part in parts
        ],
        out_shape=[jax.ShapeDtypeStruct((slots, part.shape[1], wide), BF16) for part in parts]
        + [jax.ShapeDtypeStruct((slots, groups, 2, part.shape[1]), F32) for part in parts],
        scratch_shapes=[pltpu.VMEM((total, LANES), BF16)] * 2,
        compiler_params=pltpu.CompilerParams(vmem_limit_bytes=48 * 1024 * 1024),
        cost_estimate=attention_cost(slots, total, wide, 2),
        name="attend",
    )(*parts, *parts, *parts)
    return [narrow(out, 1, width) for out in outs[:count]], outs[count:]


def attend_back(parts, upstreams, sums):
    slots = parts[0].shape[0]
    width = parts[0].shape[2] // 3
    parts = [widen(part, 3) for part in parts]
    upstreams = [widen(part, 1) for part in upstreams]
    count = len(parts)
    wide = parts[0].shape[2] // 3
    groups = wide // LANES
    total = sum(part.shape[1] for part in parts)
    outs = pl.pallas_call(
        functools.partial(attend_back_kernel, count, groups),
        grid=(slots, groups),
        in_specs=lane_blocks(parts, 0)
        + lane_blocks(parts, groups)
        + lane_blocks(parts, 2 * groups)
        + lane_blocks(upstreams, 0)
        + [
            pl.BlockSpec((1, 1, 2, part.shape[1]), lambda s, p: (s, p, 0, 0)) for part in parts
        ],
        out_specs=[
            pl.BlockSpec((1, part.shape[1], 3 * wide), lambda s, p: (s, 0, 0)) for part in parts
        ],
        out_shape=[jax.ShapeDtypeStruct((slots, part.shape[1], 3 * wide), BF16) for part in parts],
        scratch_shapes=[pltpu.VMEM((total, LANES), BF16)] * 2 + [pltpu.VMEM((total, LANES), F32)] * 2,
        compiler_params=pltpu.CompilerParams(vmem_limit_bytes=48 * 1024 * 1024),
        cost_estimate=attention_cost(slots, total, wide, 5),
        name="attend_back",
    )(*parts, *parts, *parts, *upstreams, *sums)
    return [narrow(out, 3, width) for out in outs]


def rows_kernel(count, *refs):
    lefts, rights, out = refs[:count], refs[count : 2 * count], refs[-1]
    total = None
    for left, right in zip(lefts, rights):
        for slot in range(left.shape[0]):
            part = dot(left[slot], right[slot], 0, 0)
            total = part if total is None else total + part
    out[...] = total.astype(BF16)


def weight_grad(pairs):
    joined = None
    rows = pairs[0][0][0].shape[-1]
    wide = sum(rights[0].shape[-1] for _, rights in pairs)
    start = 0
    for lefts, rights in pairs:
        part = rights[0].shape[-1]
        if part % LANES or start % part:
            return jnp.concatenate([plain_grad(*pair) for pair in pairs], axis=1)
        count = len(lefts)
        step = 256
        ins = [
            pl.BlockSpec((left.shape[0], left.shape[1], step), lambda i: (0, 0, i))
            for left in lefts
        ] + [
            pl.BlockSpec(right.shape, lambda i: (0, 0, 0), pipeline_mode=pl.Buffered(1))
            for right in rights
        ]
        operands = (*lefts, *rights)
        if joined is not None:
            ins.append(pl.BlockSpec(memory_space=pl.ANY))
            operands += (joined,)
        joined = pl.pallas_call(
            functools.partial(rows_kernel, count),
            grid=(rows // step,),
            in_specs=ins,
            out_specs=pl.BlockSpec((step, part), lambda i, c=start // part: (i, c)),
            out_shape=jax.ShapeDtypeStruct((rows, wide), BF16),
            input_output_aliases={} if joined is None else {2 * count: 0},
            compiler_params=pltpu.CompilerParams(vmem_limit_bytes=48 * 1024 * 1024),
            cost_estimate=pl.CostEstimate(flops=0, transcendentals=0, bytes_accessed=1024),
            name="weight_grad",
        )(*operands)
        start += part
    return joined


NO_COST = pl.CostEstimate(flops=0, transcendentals=0, bytes_accessed=1024)
LIMIT = pltpu.CompilerParams(vmem_limit_bytes=48 * 1024 * 1024)


def tile_of(wide, start, most):
    return max(t for t in range(LANES, most + 1, LANES) if wide % t == 0 and start % t == 0)


def fits(weight):
    _, start, wide = weight
    return wide % LANES == 0 and start % LANES == 0


def cut(weight):
    array, start, wide = weight
    return array[:, start : start + wide]


def row_blocks(ref):
    slots, rows, columns = ref.shape
    if rows % 16 == 0:
        return [(slice(None), ref[...].reshape(slots * rows, columns))]
    return [(slice(slot, slot + 1), ref[slot]) for slot in range(slots)]


def store_rows(ref, place, value):
    slots = ref.shape[0] if place == slice(None) else 1
    ref[place] = value.reshape(slots, -1, value.shape[-1]).astype(ref.dtype)


def product_kernel(count, weight_dim, *refs):
    pieces, weight, outs = refs[:count], refs[count], refs[count + 1 :]
    for piece, out in zip(pieces, outs):
        for place, rows in row_blocks(piece):
            store_rows(out, place, dot(rows, weight[...], 1, weight_dim))


def whole_block(array):
    return pl.BlockSpec(array.shape, lambda j: (0, 0, 0), pipeline_mode=pl.Buffered(1))


def products_of(pieces, weight, weight_dim, kinds, late=False):
    array, start, wide = weight
    if not fits(weight) or (weight_dim and start % wide):
        return [
            dot(piece, cut(weight), 2, weight_dim).astype(kind)
            for piece, kind in zip(pieces, kinds)
        ]
    count = len(pieces)
    slots, _, depth = pieces[0].shape
    if weight_dim:
        result = array.shape[0]
        tile = tile_of(result, 0, 768)
        block = pl.BlockSpec((tile, wide), lambda j: (j, start // wide))
    else:
        result = wide
        tile = tile_of(wide, start, 768)
        block = pl.BlockSpec((depth, tile), lambda j: (0, start // tile + j))
    rows = slots * sum(piece.shape[1] for piece in pieces)
    cost = pl.CostEstimate(
        flops=4 * rows * depth * result, transcendentals=0, bytes_accessed=4 * rows * result
    )
    return pl.pallas_call(
        functools.partial(product_kernel, count, weight_dim),
        grid=(result // tile,),
        in_specs=[whole_block(piece) for piece in pieces] + [block],
        out_specs=[
            pl.BlockSpec((slots, piece.shape[1], tile), lambda j: (0, 0, j)) for piece in pieces
        ],
        out_shape=[
            jax.ShapeDtypeStruct((slots, piece.shape[1], result), kind)
            for piece, kind in zip(pieces, kinds)
        ],
        compiler_params=LIMIT,
        cost_estimate=cost if late else NO_COST,
        name="products",
    )(*pieces, array)


def hidden_kernel(count, *refs):
    pieces, downs, up, down = refs[:count], refs[count : 2 * count], refs[2 * count], refs[2 * count + 1]
    actives, grads = refs[2 * count + 2 : 3 * count + 2], refs[3 * count + 2 :]
    for piece, upstream, active, grad in zip(pieces, downs, actives, grads):
        for (place, rows), (_, above) in zip(row_blocks(piece), row_blocks(upstream)):
            hidden = dot(rows, up[...], 1, 0)
            active_grad = dot(above, down[...], 1, 0)
            square = hidden * hidden
            scale = (2 / math.pi) ** 0.5
            bend = jnp.tanh(hidden * (scale + scale * 0.044715 * square))
            half = 0.5 + 0.5 * bend
            slope = half + hidden * (0.5 - 0.5 * bend * bend) * (
                scale + scale * 0.134145 * square
            )
            store_rows(active, place, hidden * half)
            store_rows(grad, place, active_grad * slope)


def hidden_both(pieces, downs, up, down):
    count = len(pieces)
    if not (fits(up) and fits(down)):
        hidden = [dot(piece, cut(up), 2, 0) for piece in pieces]
        active_grad = [dot(piece, cut(down), 2, 0) for piece in downs]
        return (
            [gelu_tanh(value).astype(BF16) for value in hidden],
            [
                jax.vjp(gelu_tanh, value)[1](grad)[0].astype(BF16)
                for value, grad in zip(hidden, active_grad)
            ],
        )
    slots, _, depth = pieces[0].shape
    wide = up[2]
    tile = tile_of(wide, math.gcd(up[1], down[1]), 512)
    outs = pl.pallas_call(
        functools.partial(hidden_kernel, count),
        grid=(wide // tile,),
        in_specs=[whole_block(piece) for piece in (*pieces, *downs)]
        + [
            pl.BlockSpec((depth, tile), lambda j, o=block[1] // tile: (0, o + j))
            for block in (up, down)
        ],
        out_specs=[
            pl.BlockSpec((slots, piece.shape[1], tile), lambda j: (0, 0, j)) for piece in pieces
        ]
        * 2,
        out_shape=[
            jax.ShapeDtypeStruct((slots, piece.shape[1], wide), BF16) for piece in pieces
        ]
        * 2,
        compiler_params=LIMIT,
        cost_estimate=NO_COST,
        name="hidden_both",
    )(*pieces, *downs, up[0], down[0])
    return outs[:count], outs[count:]


def plain_grad(lefts, rights):
    left = jnp.concatenate([v.reshape(-1, v.shape[-1]) for v in lefts], axis=0)
    right = jnp.concatenate([v.reshape(-1, v.shape[-1]) for v in rights], axis=0)
    return dot(left, right, 0, 0).astype(BF16)


def on_device(
    group_count,
    tensor_size,
    image_tokens,
    text_tokens,
    condition,
    group_size,
    image_modulation,
    image_attention_in,
    image_attention_out,
    image_hidden_in,
    image_hidden_out,
    text_modulation,
    text_attention_in,
    text_attention_out,
    text_hidden_in,
    text_hidden_out,
    image_cotangent,
    text_cotangent,
):
    size = tensor_size
    slots, image_length, model = image_tokens.shape
    text_length = text_tokens.shape[1]
    share, _, width = image_attention_in.shape
    units = image_hidden_in.shape[1]
    tensor_rank = lax.axis_index("tensor")
    group_rank = lax.axis_index("dp")

    def gathered(*blocks):
        joined = blocks[0] if len(blocks) == 1 else jnp.concatenate(blocks, axis=1)
        return lax.all_gather(joined, "dp", axis=0, tiled=True)

    packed_in = gathered(
        image_attention_in.reshape(share, 3 * width), text_attention_in.reshape(share, 3 * width)
    )
    both_out = gathered(image_attention_out.T, text_attention_out.T)
    image_up = gathered(image_hidden_in)
    packed_text = gathered(text_hidden_in, text_hidden_out.T)
    down_ring = ring_gather(image_hidden_out.T, group_count)
    down_hop = next(down_ring)
    weight_in = ((packed_in, 0, 3 * width), (packed_in, 3 * width, 3 * width))
    weight_out = ((both_out, 0, width), (both_out, width, width))

    alive = (jnp.arange(slots) < group_size[0]).astype(F32)[:, None, None]
    cond_full = condition.astype(F32)
    activated_low = jax.nn.silu(cond_full).astype(BF16)
    activated_all = gather_stack(activated_low, group_count, "dp").reshape(-1, model)
    activated_own = lax.dynamic_slice_in_dim(activated_all, group_rank * share, share, 1)
    all_slots = activated_own.shape[0]
    mod_parts = jnp.concatenate(
        [
            dot(activated_own, image_modulation.reshape(share, 6 * width), 1, 0),
            dot(activated_own, text_modulation.reshape(share, 6 * width), 1, 0),
        ],
        axis=1,
    ).reshape(group_count, slots, 12 * width)
    mod_own = scatter_stack(mod_parts, group_count, "dp")
    modulations = lax.all_gather(
        mod_own.reshape(slots, 2, 6, width), "tensor", axis=3, tiled=True
    )
    modulations, down_hop = lax.optimization_barrier((modulations, down_hop))
    down_hop = down_ring.send(down_hop)
    mods = (modulations[:, 0], modulations[:, 1])

    tokens = (image_tokens.astype(F32), text_tokens.astype(F32))
    outgoing = (image_cotangent.astype(F32) * alive, text_cotangent.astype(F32) * alive)

    half = size // 2
    near_kinds = [F32] + [BF16] * (half - 1)

    def scattered(grad):
        return lax.psum_scatter(grad, "dp", scatter_dimension=0, tiled=True).astype(F32)

    def row_products(pieces, weight, weight_dim, late=False):
        far = products_of(pieces[half:], weight, weight_dim, near_kinds, late)
        near = products_of(after(pieces[:half], far), weight, weight_dim, near_kinds, late)
        return [*near, *far]

    def image_sum(pieces, weight, weight_dim, late=False):
        products = row_products(pieces, weight, weight_dim, late)
        return scatter_end(*scatter_start(products, size), size)

    def text_sum(piece, weight, weight_dim, late=False):
        (product,) = products_of([piece], weight, weight_dim, [F32], late)
        return scatter_end(*text_start(product, size), size)

    def modulated(values, mod, shift, scale):
        normed, inverse = norm_rows(values)
        rows = normed * (1.0 + spread(mod[:, scale])) + spread(mod[:, shift])
        return normed, inverse, rows.astype(BF16)

    def second_back(stream, second_grad, normed, inverse):
        mod = mods[stream]
        shift_two_grad = jnp.sum(second_grad, axis=1)
        scale_two_grad = jnp.sum(second_grad * normed, axis=1)
        middle_grad = outgoing[stream] + norm_back(
            second_grad * (1.0 + spread(mod[:, 4])), normed, inverse
        )
        low = (middle_grad * spread(mod[:, 2])).astype(BF16)
        return middle_grad, low, shift_two_grad, scale_two_grad

    low_kinds = [BF16] * size

    normed_one, inverse_one, image_first = modulated(tokens[0], mods[0], 0, 1)
    text_normed_one, text_inverse_one, text_first = modulated(tokens[1], mods[1], 0, 1)
    first_pieces = gather_pieces(image_first, size)
    first_pieces, down_hop = lax.optimization_barrier((first_pieces, down_hop))
    down_hop = down_ring.send(down_hop)
    for _ in range(group_count // 2 - 4):
        down_hop = down_ring.send(down_hop)
    packed = products_of(first_pieces, weight_in[0], 0, low_kinds)
    text_packed = products_of([text_first], weight_in[1], 0, [BF16])
    down_rows = [
        (outgoing[stream] * spread(mods[stream][:, 5])).astype(BF16) for stream in range(2)
    ]
    down_have = gather_start(after(down_rows[0], first_pieces), size)
    parts, down_hop = after(([*packed, *text_packed], down_hop), down_have)
    down_hop = down_ring.send(down_hop)
    attended, sums = attend(parts)
    down_pieces = gather_end(after(down_have, attended), size)
    attended, down_hop = lax.optimization_barrier((attended, down_hop))
    image_down = down_ring.send(down_hop)
    attended_parts = (attended[:-1], attended[-1:])

    branch = image_sum(attended_parts[0], weight_out[0], 1)
    middle = tokens[0] + spread(mods[0][:, 2]) * branch
    normed_two, inverse_two, image_second = modulated(middle, mods[0], 3, 4)
    second_pieces = gather_pieces(image_second, size)
    text_branch = text_sum(after(attended_parts[1][0], second_pieces), weight_out[1], 1)
    up_weight, down_weight = (image_up, 0, units), (image_down, 0, units)
    near = hidden_both(second_pieces[:half], down_pieces[:half], up_weight, down_weight)
    far_pieces = after(second_pieces[half:], near)
    far = hidden_both(far_pieces, down_pieces[half:], up_weight, down_weight)
    active = [*near[0], *far[0]]
    hidden_grad = [*near[1], *far[1]]
    kept, sent = scatter_start(row_products(hidden_grad, up_weight, 1), size)
    text_both = after(packed_text, sent)

    text_up_weight, text_down_weight = (text_both, 0, units), (text_both, units, units)
    text_middle = tokens[1] + spread(mods[1][:, 2]) * text_branch
    text_normed_two, text_inverse_two, text_second = modulated(text_middle, mods[1], 3, 4)
    text_active, text_hidden_grad = hidden_both(
        [text_second], [down_rows[1]], text_up_weight, text_down_weight
    )
    (text_product,) = products_of(text_hidden_grad, text_up_weight, 1, [F32])
    text_second_grad = scatter_end(*text_start(text_product, size), size)
    image_mlp_grad = weight_grad(
        after([(down_pieces, active), (second_pieces, hidden_grad)], sent)
    )
    second_grad = after(scatter_end(kept, sent, size), image_mlp_grad, text_product)
    image_mlp = scattered(after(image_mlp_grad, second_grad))
    middle_grad, low, shift_two_grad, scale_two_grad = second_back(
        0, second_grad, normed_two, inverse_two
    )
    gate_one_grad = jnp.sum(middle_grad * branch, axis=1)

    low = after(low, text_second_grad)
    branch_grads = gather_pieces(low, size)
    text_mlp_grad = weight_grad(
        after([([down_rows[1]], text_active), ([text_second], text_hidden_grad)], low)
    )
    upstreams = products_of(after(branch_grads, text_mlp_grad), weight_out[0], 0, low_kinds)
    text_middle_grad, text_low, text_shift_two_grad, text_scale_two_grad = second_back(
        1, text_second_grad, text_normed_two, text_inverse_two
    )
    text_gate_one_grad = jnp.sum(text_middle_grad * text_branch, axis=1)
    text_upstream = products_of([text_low], weight_out[1], 0, [BF16])
    text_ring = ring_scatter(after(text_mlp_grad, branch_grads), group_count)
    text_hop = next(text_ring)
    packed_grads = attend_back(parts, [*upstreams, *text_upstream], sums)
    packed_grads, text_hop = lax.optimization_barrier((packed_grads, text_hop))
    text_hop = text_ring.send(text_hop)
    attention_grad = weight_grad(
        [
            (first_pieces, packed_grads[:-1]),
            ([text_first], packed_grads[-1:]),
        ]
    )
    attention_sum = scattered(attention_grad)
    out_grad = weight_grad(
        after(
            [(branch_grads, attended_parts[0]), ([text_low], attended_parts[1])], attention_grad
        )
    )
    packed_grads, text_hop, active, text_active = after(
        (packed_grads, text_hop, active, text_active), attention_grad
    )
    text_hop, image_mlp = lax.optimization_barrier((text_hop, image_mlp))
    text_hop = text_ring.send(text_hop)
    out_ring = ring_scatter(after(out_grad, image_mlp), group_count)
    out_hop = next(out_ring)

    def first_back(stream, first_grad, normed, inverse, middle_grad):
        mod = mods[stream]
        shift_one_grad = jnp.sum(first_grad, axis=1)
        scale_one_grad = jnp.sum(first_grad * normed, axis=1)
        input_grad = middle_grad + norm_back(
            first_grad * (1.0 + spread(mod[:, 1])), normed, inverse
        )
        return input_grad, shift_one_grad, scale_one_grad

    def finish(stream, middle, branch_two):
        result = middle + spread(mods[stream][:, 5]) * branch_two
        gate_two_grad = jnp.sum(outgoing[stream] * branch_two, axis=1)
        return (result * alive).astype(BF16), gate_two_grad

    first_grad = image_sum(packed_grads[:-1], weight_in[0], 1, True)
    text_first_grad = text_sum(packed_grads[-1], weight_in[1], 1, True)
    branch_two = image_sum(active, down_weight, 1, True)
    text_branch_two = text_sum(text_active[0], text_down_weight, 1, True)
    text_first_grad, text_hop, out_hop = lax.optimization_barrier(
        (text_first_grad, text_hop, out_hop)
    )
    for _ in range(group_count // 2 - 3):
        text_hop = text_ring.send(text_hop)
    out_hop = out_ring.send(out_hop)
    first_grad, text_hop, out_hop = lax.optimization_barrier((first_grad, text_hop, out_hop))
    text_mlp = text_ring.send(text_hop)
    for _ in range(group_count // 2 - 1):
        out_hop = out_ring.send(out_hop)
    out_sum = out_hop
    input_grads = [None, None]
    input_grads[0], shift_one_grad, scale_one_grad = first_back(
        0, first_grad, normed_one, inverse_one, middle_grad
    )
    input_grads[1], text_shift_one_grad, text_scale_one_grad = first_back(
        1, text_first_grad, text_normed_one, text_inverse_one, text_middle_grad
    )
    outputs = [None, None]
    outputs[0], gate_two_grad = finish(0, middle, branch_two)
    outputs[1], text_gate_two_grad = finish(1, text_middle, text_branch_two)
    mod_grads = (
        jnp.stack(
            [
                shift_one_grad,
                scale_one_grad,
                gate_one_grad,
                shift_two_grad,
                scale_two_grad,
                gate_two_grad,
            ],
            axis=1,
        ),
        jnp.stack(
            [
                text_shift_one_grad,
                text_scale_one_grad,
                text_gate_one_grad,
                text_shift_two_grad,
                text_scale_two_grad,
                text_gate_two_grad,
            ],
            axis=1,
        ),
    )

    image_blocks = jnp.stack(
        [
            lax.dynamic_slice_in_dim(mod_grads[0], (tensor_rank ^ k) * width, width, 2)
            for k in range(size)
        ]
    )
    image_share = scatter_stack(image_blocks, size, "tensor")
    text_share = lax.dynamic_slice_in_dim(mod_grads[1], tensor_rank * width, width, 2)
    share_low = jnp.stack([image_share, text_share], axis=1).astype(BF16)
    share_all = gather_stack(share_low, group_count, "dp").reshape(all_slots, 2, 6, width)
    image_all = share_all[:, 0].reshape(all_slots, 6 * width)
    text_all = share_all[:, 1].reshape(all_slots, 6 * width)
    image_ada = dot(activated_own, image_all, 0, 0).reshape(share, 6, width)
    text_ada = dot(activated_own, text_all, 0, 0).reshape(share, 6, width)
    activated_part = dot(image_all, image_modulation.reshape(share, 6 * width), 1, 1) + dot(
        text_all, text_modulation.reshape(share, 6 * width), 1, 1
    )
    activated_part = sum_all(activated_part, size, "tensor").reshape(group_count, slots, share)
    activated_rows = gather_stack(activated_part, group_count, "dp")
    activated_rows = jnp.stack([activated_rows[k, k] for k in range(group_count)])
    activated_grad = jnp.concatenate(
        [
            lax.dynamic_index_in_dim(activated_rows, group_rank ^ k, 0, keepdims=False)
            for k in range(group_count)
        ],
        axis=1,
    )
    condition_gradient = jax.vjp(jax.nn.silu, cond_full)[1](activated_grad)[0]

    return (
        outputs[0],
        outputs[1],
        input_grads[0],
        input_grads[1],
        condition_gradient,
        image_ada,
        attention_sum[:, : 3 * width].reshape(share, 3, width),
        out_sum[:, :width].T,
        image_mlp[:, units:],
        image_mlp[:, :units].T,
        text_ada,
        attention_sum[:, 3 * width :].reshape(share, 3, width),
        out_sum[:, width:].T,
        text_mlp[:, units:],
        text_mlp[:, :units].T,
    )


def solution(mesh):
    image = P("dp", "tensor", None)
    text = P("dp", None, None)
    columns = P("dp", None, "tensor")
    rows = P("tensor", "dp")
    plain = P("dp", "tensor")
    weights = (columns, columns, rows, plain, rows)
    return jax.shard_map(
        functools.partial(on_device, mesh.shape["dp"], mesh.shape["tensor"]),
        mesh=mesh,
        in_specs=(image, text, P("dp", None), P("dp")) + weights + weights + (image, text),
        out_specs=(image, text, image, text, P("dp", None)) + weights + weights,
        check_vma=False,
    )
```

```python
import functools
import math

import jax
import jax.numpy as jnp
from jax import lax
from jax.experimental import pallas as pl
from jax.experimental.pallas import tpu as pltpu
from jax.sharding import PartitionSpec as P

HEAD = 64
LANES = 128
F32 = jnp.float32
BF16 = jnp.bfloat16


def norm_rows(values):
    center = values - jnp.mean(values, axis=-1, keepdims=True)
    inverse = lax.rsqrt(jnp.mean(center * center, axis=-1, keepdims=True) + 1e-06)
    return (center * inverse, inverse)


def norm_back(upstream, normed, inverse):
    first = jnp.mean(upstream, axis=-1, keepdims=True)
    second = jnp.mean(upstream * normed, axis=-1, keepdims=True)
    return inverse * (upstream - first - normed * second)


def gelu_tanh(values):
    return jax.nn.gelu(values, approximate=True)


def spread(vector):
    return vector[:, None, :]


def dot(left, right, left_dim, right_dim):
    return lax.dot_general(
        left, right, (((left_dim,), (right_dim,)), ((), ())), preferred_element_type=F32
    )


def swap(value, bit, size, axis="tensor"):
    return lax.ppermute(value, axis, [(i, i ^ bit) for i in range(size)])


def bits_of(size):
    bits = []
    bit = 1
    while bit < size:
        bits.append(bit)
        bit *= 2
    return bits


def gather_start(value, size, axis="tensor"):
    have = {0: value}
    for bit in reversed(bits_of(size)[1:]):
        have.update({k ^ bit: swap(v, bit, size, axis) for k, v in list(have.items())})
    return have


def gather_end(have, size, first=0, axis="tensor"):
    have = have | {k ^ 1: swap(v, 1, size, axis) for k, v in have.items()}
    return [have[k] for k in range(first, first + len(have))]


def gather_pieces(value, size, reach=None, axis="tensor"):
    have = {0: value}
    for bit in reversed(bits_of(reach or size)):
        have.update({k ^ bit: swap(v, bit, size, axis) for k, v in list(have.items())})
    return [have[k] for k in sorted(have)]


def gather_stack(value, size, axis):
    value = value[None]
    for bit in bits_of(size):
        value = jnp.concatenate([value, swap(value, bit, size, axis)], axis=0)
    return value


def scatter_stack(value, size, axis):
    for bit in reversed(bits_of(size)):
        value = value[:bit] + swap(value[bit:], bit, size, axis)
    return value[0]


def sum_all(value, size, axis):
    for bit in bits_of(size):
        value = value + swap(value, bit, size, axis)
    return value


def scatter_start(pieces, size):
    have = dict(enumerate(pieces))
    for bit in bits_of(size)[:-1]:
        kept = {}
        for k in sorted(have, reverse=True):
            if not k & bit:
                other = swap(have[k ^ bit].astype(BF16), bit, size)
                kept[k] = have[k].astype(F32) + other.astype(F32)
        have = kept
    kept, sent = (have[k] for k in sorted(have))
    return kept, sent.astype(BF16)


def scatter_end(kept, sent, size):
    return kept.astype(F32) + swap(sent, size // 2, size).astype(F32)


def after(values, *others):
    return lax.optimization_barrier((values, others))[0]


def ring_of(count):
    return list(range(0, count, 2)) + list(range(1, count, 2))[::-1]


def ring_member(place, count):
    place = lax.rem(place + count, count)
    return jnp.where(place < (count + 1) // 2, 2 * place, 2 * (count - 1 - place) + 1)


def ring_place(member, count):
    return jnp.where(member % 2 == 0, member // 2, count - 1 - member // 2)


def ring_step(value, way, count):
    ring = ring_of(count)
    hops = [(ring[i], ring[(i + way) % count]) for i in range(count)]
    return lax.ppermute(value, "dp", hops)


def ring_scatter(grad, count):
    wide = grad.shape[1]
    share = grad.shape[0] // count
    half = wide // 2 // LANES * LANES
    place = ring_place(lax.axis_index("dp"), count)

    def own(offset):
        row = ring_member(place + offset, count) * share
        return lax.dynamic_slice_in_dim(grad, row, share, 0).astype(F32)

    far = own(count // 2).astype(BF16)
    behind = ring_step(far[:, :half], 1, count)
    ahead = ring_step(far[:, half:], -1, count)
    behind, ahead = yield behind, ahead
    behind = jnp.pad(behind.astype(F32), ((0, 0), (0, wide - half)))
    ahead = jnp.pad(ahead.astype(F32), ((0, 0), (half, 0)))
    for hop in range(count // 2 - 1, 0, -1):
        behind = ring_step((own(hop) + behind).astype(BF16), 1, count)
        ahead = ring_step((own(-hop) + ahead).astype(BF16), -1, count)
        behind, ahead = yield behind, ahead
        behind, ahead = behind.astype(F32), ahead.astype(F32)
    yield own(0) + behind + ahead


def text_start(value, size):
    for bit in bits_of(size)[:-1]:
        if bit > 1:
            value = lax.reduce_precision(value, 8, 7)
            value = value + swap(value.astype(BF16), bit, size).astype(F32)
        else:
            value = value + swap(value, bit, size)
    value = lax.reduce_precision(value, 8, 7)
    return value, value.astype(BF16)


def lane_mask(half, shape):
    lane = lax.broadcasted_iota(jnp.int32, shape, 1)
    return (lane >= HEAD) if half else (lane < HEAD)


def pick(value, half):
    return jnp.where(lane_mask(half, value.shape), value, jnp.zeros_like(value))


def load_rows(refs, store):
    start = 0
    for ref in refs:
        rows = ref.shape[1]
        store[start : start + rows, :] = ref[0]
        start += rows


def attend_kernel(count, *refs):
    queries, keys, values = refs[:count], refs[count : 2 * count], refs[2 * count : 3 * count]
    outs = refs[3 * count : 4 * count]
    sums = refs[4 * count : 5 * count]
    key_all, value_all = refs[5 * count :]
    load_rows(keys, key_all)
    load_rows(values, value_all)
    for index in range(count):
        query = queries[index][0] * jnp.asarray(HEAD**-0.5, BF16)
        halves = []
        for half in range(2):
            scores = dot(key_all[...], pick(query, half), 1, 1)
            highest = jnp.max(scores, axis=0, keepdims=True)
            weights = jnp.exp(scores - highest)
            total = jnp.sum(weights, axis=0, keepdims=True)
            weights = (weights * (1.0 / total)).astype(BF16)
            mixed = dot(value_all[...], weights, 0, 0)
            halves.append(mixed[half * HEAD : (half + 1) * HEAD])
            sums[index][0, 0, half : half + 1, :] = highest + jnp.log(total)
        outs[index][0] = jnp.concatenate(halves, axis=0).T.astype(BF16)


def attend_back_kernel(count, asked, groups, last, *refs):
    refs = list(refs)

    def take(number):
        return [refs.pop(0) for _ in range(number)]

    keys, values = take(count), take(count)
    queries, upstreams, sums = take(asked), take(asked), take(asked)
    if last:
        before = take(2)
        query_grads = take(count - asked)
        outs = take(count)
    else:
        outs = take(asked)
        totals = take(2)
    key_all, value_all, key_grad, value_grad = refs
    load_rows(keys, key_all)
    load_rows(values, value_all)
    pair = pl.program_id(1)
    scale = jnp.asarray(HEAD**-0.5, BF16)
    for index in range(asked):
        query = queries[index][0] * scale
        upstream = upstreams[index][0]
        halves = []
        for half in range(2):
            query_half = pick(query, half)
            upstream_half = pick(upstream, half)
            scores = dot(key_all[...], query_half, 1, 1)
            weights = jnp.exp(scores - sums[index][0, 0, half : half + 1, :])
            along = dot(value_all[...], upstream_half, 1, 1)
            value_part = dot(weights.astype(BF16), upstream_half, 1, 0)
            product = weights * along
            score_grad = (product - weights * jnp.sum(product, axis=0, keepdims=True)).astype(BF16)
            key_part = dot(score_grad, query_half, 1, 0)
            if index == 0 and half == 0 and last:
                value_grad[...] = before[1][0, 0] + value_part
                key_grad[...] = before[0][0, 0] + key_part
            elif index == 0 and half == 0:
                value_grad[...] = value_part
                key_grad[...] = key_part
            else:
                value_grad[...] += value_part
                key_grad[...] += key_part
            mixed = dot(key_all[...], score_grad, 0, 0)
            halves.append(mixed[half * HEAD : (half + 1) * HEAD])
        query_grad = (jnp.concatenate(halves, axis=0).T * HEAD**-0.5).astype(BF16)
        if last:
            lanes = pl.ds(pl.multiple_of(pair * LANES, LANES), LANES)
            outs[count - asked + index][0, :, lanes] = query_grad
        else:
            outs[index][0] = query_grad
    if not last:
        totals[0][0, 0] = key_grad[...]
        totals[1][0, 0] = value_grad[...]
        return
    for index, query_grad in enumerate(query_grads):
        lanes = pl.ds(pl.multiple_of(pair * LANES, LANES), LANES)
        outs[index][0, :, lanes] = query_grad[0]
    start = 0
    for out in outs:
        rows = out.shape[1]
        for number, grad in ((1, key_grad), (2, value_grad)):
            lanes = pl.ds(pl.multiple_of((number * groups + pair) * LANES, LANES), LANES)
            out[0, :, lanes] = grad[start : start + rows, :].astype(BF16)
        start += rows


def lane_blocks(parts, offset):
    return [
        pl.BlockSpec((1, part.shape[1], LANES), lambda s, p, o=offset: (s, 0, o + p))
        for part in parts
    ]


def widen(part, copies):
    slots, rows, width = part.shape
    width = width // copies
    extra = -width % LANES
    if not extra:
        return part
    part = jnp.pad(part.reshape(slots, rows, copies, width), ((0, 0), (0, 0), (0, 0), (0, extra)))
    return part.reshape(slots, rows, copies * (width + extra))


def narrow(part, copies, width):
    slots, rows, wide = part.shape
    wide = wide // copies
    if wide == width:
        return part
    return part.reshape(slots, rows, copies, wide)[..., :width].reshape(slots, rows, -1)


def attention_cost(slots, rows, width, products):
    return pl.CostEstimate(
        flops=products * 8 * slots * rows * rows * width,
        transcendentals=slots * rows * rows * (width // HEAD),
        bytes_accessed=slots * rows * width * 2 * (4 + 3 * (products > 2)),
    )


def attend(parts):
    slots = parts[0].shape[0]
    width = parts[0].shape[2] // 3
    parts = [widen(part, 3) for part in parts]
    count = len(parts)
    wide = parts[0].shape[2] // 3
    groups = wide // LANES
    total = sum(part.shape[1] for part in parts)
    outs = pl.pallas_call(
        functools.partial(attend_kernel, count),
        grid=(slots, groups),
        in_specs=lane_blocks(parts, 0) + lane_blocks(parts, groups) + lane_blocks(parts, 2 * groups),
        out_specs=lane_blocks(parts, 0)
        + [
            pl.BlockSpec((1, 1, 2, part.shape[1]), lambda s, p: (s, p, 0, 0)) for part in parts
        ],
        out_shape=[jax.ShapeDtypeStruct((slots, part.shape[1], wide), BF16) for part in parts]
        + [jax.ShapeDtypeStruct((slots, groups, 2, part.shape[1]), F32) for part in parts],
        scratch_shapes=[pltpu.VMEM((total, LANES), BF16)] * 2,
        compiler_params=pltpu.CompilerParams(vmem_limit_bytes=48 * 1024 * 1024),
        cost_estimate=attention_cost(slots, total, wide, 2),
        name="attend",
    )(*parts, *parts, *parts)
    return [narrow(out, 1, width) for out in outs[:count]], outs[count:]


def attend_back(parts, asked, upstreams, sums, before=None):
    slots = parts[0].shape[0]
    width = parts[0].shape[2] // 3
    parts = [widen(part, 3) for part in parts]
    upstreams = [widen(part, 1) for part in upstreams]
    last = before is not None
    count = len(parts)
    queries = parts[-asked:] if last else parts[:asked]
    wide = parts[0].shape[2] // 3
    groups = wide // LANES
    total = sum(part.shape[1] for part in parts)
    whole = pl.BlockSpec((1, 1, total, LANES), lambda s, p: (s, p, 0, 0))
    ins = lane_blocks(parts, groups) + lane_blocks(parts, 2 * groups) + lane_blocks(queries, 0)
    ins += lane_blocks(upstreams, 0)
    ins += [pl.BlockSpec((1, 1, 2, part.shape[1]), lambda s, p: (s, p, 0, 0)) for part in queries]
    operands = [*parts, *parts, *queries, *upstreams, *sums]
    if last:
        query_grads, totals = before
        ins += [whole, whole] + lane_blocks(query_grads, 0)
        operands += [*totals, *query_grads]
        out_specs = [
            pl.BlockSpec((1, part.shape[1], 3 * wide), lambda s, p: (s, 0, 0)) for part in parts
        ]
        out_shape = [
            jax.ShapeDtypeStruct((slots, part.shape[1], 3 * wide), BF16) for part in parts
        ]
    else:
        out_specs = lane_blocks(queries, 0) + [whole, whole]
        out_shape = [
            jax.ShapeDtypeStruct((slots, part.shape[1], wide), BF16) for part in queries
        ] + [jax.ShapeDtypeStruct((slots, groups, total, LANES), F32)] * 2
    outs = pl.pallas_call(
        functools.partial(attend_back_kernel, count, asked, groups, last),
        grid=(slots, groups),
        in_specs=ins,
        out_specs=out_specs,
        out_shape=out_shape,
        scratch_shapes=[pltpu.VMEM((total, LANES), BF16)] * 2 + [pltpu.VMEM((total, LANES), F32)] * 2,
        compiler_params=pltpu.CompilerParams(vmem_limit_bytes=48 * 1024 * 1024),
        cost_estimate=attention_cost(slots, total, wide, 2 if last else 5),
        name="attend_back",
    )(*operands)
    if last:
        return [narrow(out, 3, width) for out in outs]
    return outs[:asked], outs[asked:]


def rows_kernel(count, *refs):
    lefts, rights, out = refs[:count], refs[count : 2 * count], refs[-1]
    total = None
    for left, right in zip(lefts, rights):
        for slot in range(left.shape[0]):
            part = dot(left[slot], right[slot], 0, 0)
            total = part if total is None else total + part
    out[...] = total.astype(BF16)


def weight_grad(pairs):
    joined = None
    rows = pairs[0][0][0].shape[-1]
    wide = sum(rights[0].shape[-1] for _, rights in pairs)
    start = 0
    for lefts, rights in pairs:
        part = rights[0].shape[-1]
        if part % LANES or start % part:
            return jnp.concatenate([plain_grad(*pair) for pair in pairs], axis=1)
        count = len(lefts)
        step = 256
        ins = [
            pl.BlockSpec((left.shape[0], left.shape[1], step), lambda i: (0, 0, i))
            for left in lefts
        ] + [
            pl.BlockSpec(right.shape, lambda i: (0, 0, 0), pipeline_mode=pl.Buffered(1))
            for right in rights
        ]
        operands = (*lefts, *rights)
        if joined is not None:
            ins.append(pl.BlockSpec(memory_space=pl.ANY))
            operands += (joined,)
        joined = pl.pallas_call(
            functools.partial(rows_kernel, count),
            grid=(rows // step,),
            in_specs=ins,
            out_specs=pl.BlockSpec((step, part), lambda i, c=start // part: (i, c)),
            out_shape=jax.ShapeDtypeStruct((rows, wide), BF16),
            input_output_aliases={} if joined is None else {2 * count: 0},
            compiler_params=pltpu.CompilerParams(vmem_limit_bytes=48 * 1024 * 1024),
            cost_estimate=pl.CostEstimate(flops=0, transcendentals=0, bytes_accessed=1024),
            name="weight_grad",
        )(*operands)
        start += part
    return joined


NO_COST = pl.CostEstimate(flops=0, transcendentals=0, bytes_accessed=1024)
LIMIT = pltpu.CompilerParams(vmem_limit_bytes=48 * 1024 * 1024)


def tile_of(wide, start, most):
    return max(t for t in range(LANES, most + 1, LANES) if wide % t == 0 and start % t == 0)


def fits(weight):
    _, start, wide = weight
    return wide % LANES == 0 and start % LANES == 0


def cut(weight):
    array, start, wide = weight
    return array[:, start : start + wide]


def row_blocks(ref):
    slots, rows, columns = ref.shape
    if rows % 16 == 0:
        return [(slice(None), ref[...].reshape(slots * rows, columns))]
    return [(slice(slot, slot + 1), ref[slot]) for slot in range(slots)]


def store_rows(ref, place, value):
    slots = ref.shape[0] if place == slice(None) else 1
    ref[place] = value.reshape(slots, -1, value.shape[-1]).astype(ref.dtype)


def product_kernel(count, weight_dim, *refs):
    pieces, weight, outs = refs[:count], refs[count], refs[count + 1 :]
    for piece, out in zip(pieces, outs):
        for place, rows in row_blocks(piece):
            store_rows(out, place, dot(rows, weight[...], 1, weight_dim))


def whole_block(array):
    return pl.BlockSpec(array.shape, lambda j: (0, 0, 0), pipeline_mode=pl.Buffered(1))


def products_of(pieces, weight, weight_dim, kinds, late=False):
    array, start, wide = weight
    if not fits(weight) or (weight_dim and start % wide):
        return [
            dot(piece, cut(weight), 2, weight_dim).astype(kind)
            for piece, kind in zip(pieces, kinds)
        ]
    count = len(pieces)
    slots, _, depth = pieces[0].shape
    if weight_dim:
        result = array.shape[0]
        tile = tile_of(result, 0, 768)
        block = pl.BlockSpec((tile, wide), lambda j: (j, start // wide))
    else:
        result = wide
        tile = tile_of(wide, start, 768)
        block = pl.BlockSpec((depth, tile), lambda j: (0, start // tile + j))
    rows = slots * sum(piece.shape[1] for piece in pieces)
    cost = pl.CostEstimate(
        flops=4 * rows * depth * result, transcendentals=0, bytes_accessed=4 * rows * result
    )
    return pl.pallas_call(
        functools.partial(product_kernel, count, weight_dim),
        grid=(result // tile,),
        in_specs=[whole_block(piece) for piece in pieces] + [block],
        out_specs=[
            pl.BlockSpec((slots, piece.shape[1], tile), lambda j: (0, 0, j)) for piece in pieces
        ],
        out_shape=[
            jax.ShapeDtypeStruct((slots, piece.shape[1], result), kind)
            for piece, kind in zip(pieces, kinds)
        ],
        compiler_params=LIMIT,
        cost_estimate=cost if late else NO_COST,
        name="products",
    )(*pieces, array)


def hidden_kernel(count, *refs):
    pieces, downs, up, down = refs[:count], refs[count : 2 * count], refs[2 * count], refs[2 * count + 1]
    actives, grads = refs[2 * count + 2 : 3 * count + 2], refs[3 * count + 2 :]
    for piece, upstream, active, grad in zip(pieces, downs, actives, grads):
        for (place, rows), (_, above) in zip(row_blocks(piece), row_blocks(upstream)):
            hidden = dot(rows, up[...], 1, 0)
            active_grad = dot(above, down[...], 1, 0)
            square = hidden * hidden
            scale = (2 / math.pi) ** 0.5
            bend = jnp.tanh(hidden * (scale + scale * 0.044715 * square))
            half = 0.5 + 0.5 * bend
            slope = half + hidden * (0.5 - 0.5 * bend * bend) * (
                scale + scale * 0.134145 * square
            )
            store_rows(active, place, hidden * half)
            store_rows(grad, place, active_grad * slope)


def hidden_both(pieces, downs, up, down):
    count = len(pieces)
    if not (fits(up) and fits(down)):
        hidden = [dot(piece, cut(up), 2, 0) for piece in pieces]
        active_grad = [dot(piece, cut(down), 2, 0) for piece in downs]
        return (
            [gelu_tanh(value).astype(BF16) for value in hidden],
            [
                jax.vjp(gelu_tanh, value)[1](grad)[0].astype(BF16)
                for value, grad in zip(hidden, active_grad)
            ],
        )
    slots, _, depth = pieces[0].shape
    wide = up[2]
    tile = tile_of(wide, math.gcd(up[1], down[1]), 512)
    outs = pl.pallas_call(
        functools.partial(hidden_kernel, count),
        grid=(wide // tile,),
        in_specs=[whole_block(piece) for piece in (*pieces, *downs)]
        + [
            pl.BlockSpec((depth, tile), lambda j, o=block[1] // tile: (0, o + j))
            for block in (up, down)
        ],
        out_specs=[
            pl.BlockSpec((slots, piece.shape[1], tile), lambda j: (0, 0, j)) for piece in pieces
        ]
        * 2,
        out_shape=[
            jax.ShapeDtypeStruct((slots, piece.shape[1], wide), BF16) for piece in pieces
        ]
        * 2,
        compiler_params=LIMIT,
        cost_estimate=NO_COST,
        name="hidden_both",
    )(*pieces, *downs, up[0], down[0])
    return outs[:count], outs[count:]


def plain_grad(lefts, rights):
    left = jnp.concatenate([v.reshape(-1, v.shape[-1]) for v in lefts], axis=0)
    right = jnp.concatenate([v.reshape(-1, v.shape[-1]) for v in rights], axis=0)
    return dot(left, right, 0, 0).astype(BF16)


def on_device(
    group_count,
    tensor_size,
    image_tokens,
    text_tokens,
    condition,
    group_size,
    image_modulation,
    image_attention_in,
    image_attention_out,
    image_hidden_in,
    image_hidden_out,
    text_modulation,
    text_attention_in,
    text_attention_out,
    text_hidden_in,
    text_hidden_out,
    image_cotangent,
    text_cotangent,
):
    size = tensor_size
    slots, image_length, model = image_tokens.shape
    text_length = text_tokens.shape[1]
    share, _, width = image_attention_in.shape
    units = image_hidden_in.shape[1]
    tensor_rank = lax.axis_index("tensor")
    group_rank = lax.axis_index("dp")

    def gathered(*blocks):
        joined = blocks[0] if len(blocks) == 1 else jnp.concatenate(blocks, axis=1)
        return lax.all_gather(joined, "dp", axis=0, tiled=True)

    packed_first = gathered(
        image_attention_in.reshape(share, 3 * width),
        text_attention_in.reshape(share, 3 * width),
        image_attention_out.T,
        text_attention_out.T,
    )
    image_up = gathered(image_hidden_in)
    image_down = gathered(image_hidden_out.T)
    packed_text = gathered(text_hidden_in, text_hidden_out.T)
    weight_in = ((packed_first, 0, 3 * width), (packed_first, 3 * width, 3 * width))
    weight_out = ((packed_first, 6 * width, width), (packed_first, 7 * width, width))

    alive = (jnp.arange(slots) < group_size[0]).astype(F32)[:, None, None]
    cond_full = condition.astype(F32)
    activated_low = jax.nn.silu(cond_full).astype(BF16)
    activated_all = gather_stack(activated_low, group_count, "dp").reshape(-1, model)
    activated_own = lax.dynamic_slice_in_dim(activated_all, group_rank * share, share, 1)
    all_slots = activated_own.shape[0]
    mod_parts = jnp.concatenate(
        [
            dot(activated_own, image_modulation.reshape(share, 6 * width), 1, 0),
            dot(activated_own, text_modulation.reshape(share, 6 * width), 1, 0),
        ],
        axis=1,
    ).reshape(group_count, slots, 12 * width)
    mod_own = scatter_stack(mod_parts, group_count, "dp")
    modulations = lax.all_gather(
        mod_own.reshape(slots, 2, 6, width), "tensor", axis=3, tiled=True
    )
    mods = (modulations[:, 0], modulations[:, 1])

    tokens = (image_tokens.astype(F32), text_tokens.astype(F32))
    outgoing = (image_cotangent.astype(F32) * alive, text_cotangent.astype(F32) * alive)

    half = size // 2
    near_kinds = [F32] + [BF16] * (half - 1)

    def scattered(grad):
        return lax.psum_scatter(grad, "dp", scatter_dimension=0, tiled=True).astype(F32)

    def row_products(pieces, weight, weight_dim, late=False):
        far = products_of(pieces[half:], weight, weight_dim, near_kinds, late)
        near = products_of(after(pieces[:half], far), weight, weight_dim, near_kinds, late)
        return [*near, *far]

    def image_sum(pieces, weight, weight_dim, late=False):
        products = row_products(pieces, weight, weight_dim, late)
        return scatter_end(*scatter_start(products, size), size)

    def text_sum(piece, weight, weight_dim, late=False):
        (product,) = products_of([piece], weight, weight_dim, [F32], late)
        return scatter_end(*text_start(product, size), size)

    def modulated(values, mod, shift, scale):
        normed, inverse = norm_rows(values)
        rows = normed * (1.0 + spread(mod[:, scale])) + spread(mod[:, shift])
        return normed, inverse, rows.astype(BF16)

    def second_back(stream, second_grad, normed, inverse):
        mod = mods[stream]
        shift_two_grad = jnp.sum(second_grad, axis=1)
        scale_two_grad = jnp.sum(second_grad * normed, axis=1)
        middle_grad = outgoing[stream] + norm_back(
            second_grad * (1.0 + spread(mod[:, 4])), normed, inverse
        )
        low = (middle_grad * spread(mod[:, 2])).astype(BF16)
        return middle_grad, low, shift_two_grad, scale_two_grad

    low_kinds = [BF16] * size

    normed_one, inverse_one, image_first = modulated(tokens[0], mods[0], 0, 1)
    text_normed_one, text_inverse_one, text_first = modulated(tokens[1], mods[1], 0, 1)
    first_pieces = gather_pieces(image_first, size)
    packed = products_of(first_pieces, weight_in[0], 0, low_kinds)
    text_packed = products_of([text_first], weight_in[1], 0, [BF16])
    down_rows = [
        (outgoing[stream] * spread(mods[stream][:, 5])).astype(BF16) for stream in range(2)
    ]
    down_have = gather_start(after(down_rows[0], first_pieces), size)
    parts = after([*packed, *text_packed], down_have)
    attended, sums = attend(parts)
    down_pieces = gather_end(after(down_have, attended), size)
    attended_parts = (attended[:-1], attended[-1:])

    branch = image_sum(attended_parts[0], weight_out[0], 1)
    middle = tokens[0] + spread(mods[0][:, 2]) * branch
    normed_two, inverse_two, image_second = modulated(middle, mods[0], 3, 4)
    up_weight, down_weight = (image_up, 0, units), (image_down, 0, units)
    near_pieces = gather_pieces(image_second, size, half)
    far_have = gather_start(image_second, size)
    near = hidden_both(near_pieces, down_pieces[:half], up_weight, down_weight)
    far_have = {k: v for k, v in far_have.items() if k >= half}
    far_pieces = gather_end(after(far_have, near), size, half)
    second_pieces = [*near_pieces, *far_pieces]
    far = hidden_both(far_pieces, down_pieces[half:], up_weight, down_weight)
    text_branch = text_sum(after(attended_parts[1][0], far_pieces), weight_out[1], 1)
    active = [*near[0], *far[0]]
    hidden_grad = after([*near[1], *far[1]], text_branch)
    kept, sent = scatter_start(row_products(hidden_grad, up_weight, 1), size)
    image_mlp_grad = weight_grad(
        after([(down_pieces, active), (second_pieces, hidden_grad)], sent)
    )
    second_grad = after(scatter_end(kept, sent, size), image_mlp_grad)
    image_mlp = scattered(after(image_mlp_grad, second_grad))
    middle_grad, low, shift_two_grad, scale_two_grad = second_back(
        0, second_grad, normed_two, inverse_two
    )
    gate_one_grad = jnp.sum(middle_grad * branch, axis=1)

    low_have = gather_start(low, size)
    two_products = row_products(after(active, low), down_weight, 1)
    two_kept, two_sent = scatter_start(two_products, size)
    low_have = after(low_have, two_products)
    branch_grads = gather_end(low_have, size)

    text_both = after(packed_text, low_have)
    text_up_weight, text_down_weight = (text_both, 0, units), (text_both, units, units)
    text_middle = tokens[1] + spread(mods[1][:, 2]) * text_branch
    text_normed_two, text_inverse_two, text_second = modulated(text_middle, mods[1], 3, 4)
    text_active, text_hidden_grad = hidden_both(
        [text_second], [down_rows[1]], text_up_weight, text_down_weight
    )
    (text_product,) = products_of(text_hidden_grad, text_up_weight, 1, [F32])
    text_kept, text_sent = text_start(text_product, size)
    text_mlp_grad = weight_grad(
        after([([down_rows[1]], text_active), ([text_second], text_hidden_grad)], text_product)
    )
    (text_two,) = products_of(after(text_active, text_product), text_down_weight, 1, [F32])

    upstreams = products_of(branch_grads, weight_out[0], 0, low_kinds)
    upstreams = after(upstreams, text_sent, text_mlp_grad, text_two)
    text_ring = ring_scatter(after(text_mlp_grad, branch_grads), group_count)
    text_hop = next(text_ring)
    first_part = attend_back(parts, size, upstreams, sums[:-1])
    branch_two = scatter_end(after(two_kept, first_part), two_sent, size)
    text_second_grad = scatter_end(after(text_kept, first_part), text_sent, size)
    first_part, branch_two, text_hop = lax.optimization_barrier((first_part, branch_two, text_hop))
    text_hop = text_ring.send(text_hop)
    text_middle_grad, text_low, text_shift_two_grad, text_scale_two_grad = second_back(
        1, text_second_grad, text_normed_two, text_inverse_two
    )
    text_gate_one_grad = jnp.sum(text_middle_grad * text_branch, axis=1)
    text_upstream = products_of([text_low], weight_out[1], 0, [BF16])
    packed_grads = attend_back(parts, 1, text_upstream, sums[-1:], first_part)
    attention_grad = weight_grad(
        [
            (first_pieces, packed_grads[:-1]),
            ([text_first], packed_grads[-1:]),
            (branch_grads, attended_parts[0]),
            ([text_low], attended_parts[1]),
        ]
    )
    attention_sum = scattered(attention_grad)
    packed_grads, text_hop, text_two = after((packed_grads, text_hop, text_two), attention_grad)
    text_hop = text_ring.send(text_hop)

    def first_back(stream, first_grad, normed, inverse, middle_grad):
        mod = mods[stream]
        shift_one_grad = jnp.sum(first_grad, axis=1)
        scale_one_grad = jnp.sum(first_grad * normed, axis=1)
        input_grad = middle_grad + norm_back(
            first_grad * (1.0 + spread(mod[:, 1])), normed, inverse
        )
        return input_grad, shift_one_grad, scale_one_grad

    def finish(stream, middle, branch_two):
        result = middle + spread(mods[stream][:, 5]) * branch_two
        gate_two_grad = jnp.sum(outgoing[stream] * branch_two, axis=1)
        return (result * alive).astype(BF16), gate_two_grad

    first_grad = image_sum(packed_grads[:-1], weight_in[0], 1, True)
    text_first_grad = text_sum(packed_grads[-1], weight_in[1], 1, True)
    text_branch_two = scatter_end(*text_start(text_two, size), size)
    text_first_grad, text_hop = lax.optimization_barrier((text_first_grad, text_hop))
    for _ in range(group_count // 2 - 3):
        text_hop = text_ring.send(text_hop)
    first_grad, text_hop = lax.optimization_barrier((first_grad, text_hop))
    text_mlp = text_ring.send(text_hop)
    input_grads = [None, None]
    input_grads[0], shift_one_grad, scale_one_grad = first_back(
        0, first_grad, normed_one, inverse_one, middle_grad
    )
    input_grads[1], text_shift_one_grad, text_scale_one_grad = first_back(
        1, text_first_grad, text_normed_one, text_inverse_one, text_middle_grad
    )
    outputs = [None, None]
    outputs[0], gate_two_grad = finish(0, middle, branch_two)
    outputs[1], text_gate_two_grad = finish(1, text_middle, text_branch_two)
    mod_grads = (
        jnp.stack(
            [
                shift_one_grad,
                scale_one_grad,
                gate_one_grad,
                shift_two_grad,
                scale_two_grad,
                gate_two_grad,
            ],
            axis=1,
        ),
        jnp.stack(
            [
                text_shift_one_grad,
                text_scale_one_grad,
                text_gate_one_grad,
                text_shift_two_grad,
                text_scale_two_grad,
                text_gate_two_grad,
            ],
            axis=1,
        ),
    )

    image_blocks = jnp.stack(
        [
            lax.dynamic_slice_in_dim(mod_grads[0], (tensor_rank ^ k) * width, width, 2)
            for k in range(size)
        ]
    )
    image_share = scatter_stack(image_blocks, size, "tensor")
    text_share = lax.dynamic_slice_in_dim(mod_grads[1], tensor_rank * width, width, 2)
    share_low = jnp.stack([image_share, text_share], axis=1).astype(BF16)
    share_all = gather_stack(share_low, group_count, "dp").reshape(all_slots, 2, 6, width)
    image_all = share_all[:, 0].reshape(all_slots, 6 * width)
    text_all = share_all[:, 1].reshape(all_slots, 6 * width)
    image_ada = dot(activated_own, image_all, 0, 0).reshape(share, 6, width)
    text_ada = dot(activated_own, text_all, 0, 0).reshape(share, 6, width)
    activated_part = dot(image_all, image_modulation.reshape(share, 6 * width), 1, 1) + dot(
        text_all, text_modulation.reshape(share, 6 * width), 1, 1
    )
    activated_part = sum_all(activated_part, size, "tensor").reshape(group_count, slots, share)
    activated_rows = gather_stack(activated_part, group_count, "dp")
    activated_rows = jnp.stack([activated_rows[k, k] for k in range(group_count)])
    activated_grad = jnp.concatenate(
        [
            lax.dynamic_index_in_dim(activated_rows, group_rank ^ k, 0, keepdims=False)
            for k in range(group_count)
        ],
        axis=1,
    )
    condition_gradient = jax.vjp(jax.nn.silu, cond_full)[1](activated_grad)[0]

    return (
        outputs[0],
        outputs[1],
        input_grads[0],
        input_grads[1],
        condition_gradient,
        image_ada,
        attention_sum[:, : 3 * width].reshape(share, 3, width),
        attention_sum[:, 6 * width : 7 * width].T,
        image_mlp[:, units:],
        image_mlp[:, :units].T,
        text_ada,
        attention_sum[:, 3 * width : 6 * width].reshape(share, 3, width),
        attention_sum[:, 7 * width :].T,
        text_mlp[:, units:],
        text_mlp[:, :units].T,
    )


def solution(mesh):
    image = P("dp", "tensor", None)
    text = P("dp", None, None)
    columns = P("dp", None, "tensor")
    rows = P("tensor", "dp")
    plain = P("dp", "tensor")
    weights = (columns, columns, rows, plain, rows)
    return jax.shard_map(
        functools.partial(on_device, mesh.shape["dp"], mesh.shape["tensor"]),
        mesh=mesh,
        in_specs=(image, text, P("dp", None), P("dp")) + weights + weights + (image, text),
        out_specs=(image, text, image, text, P("dp", None)) + weights + weights,
        check_vma=False,
    )
```

```python
import functools
import math

import jax
import jax.numpy as jnp
from jax import lax
from jax.experimental import pallas as pl
from jax.experimental.pallas import tpu as pltpu
from jax.sharding import PartitionSpec as P

HEAD = 64
LANES = 128
F32 = jnp.float32
BF16 = jnp.bfloat16


def norm_rows(values):
    center = values - jnp.mean(values, axis=-1, keepdims=True)
    inverse = lax.rsqrt(jnp.mean(center * center, axis=-1, keepdims=True) + 1e-06)
    return (center * inverse, inverse)


def norm_back(upstream, normed, inverse):
    first = jnp.mean(upstream, axis=-1, keepdims=True)
    second = jnp.mean(upstream * normed, axis=-1, keepdims=True)
    return inverse * (upstream - first - normed * second)


def gelu_tanh(values):
    return jax.nn.gelu(values, approximate=True)


def spread(vector):
    return vector[:, None, :]


def dot(left, right, left_dim, right_dim):
    return lax.dot_general(
        left, right, (((left_dim,), (right_dim,)), ((), ())), preferred_element_type=F32
    )


def swap(value, bit, size, axis="tensor"):
    return lax.ppermute(value, axis, [(i, i ^ bit) for i in range(size)])


def bits_of(size):
    bits = []
    bit = 1
    while bit < size:
        bits.append(bit)
        bit *= 2
    return bits


def gather_start(value, size, axis="tensor"):
    have = {0: value}
    for bit in reversed(bits_of(size)[1:]):
        have.update({k ^ bit: swap(v, bit, size, axis) for k, v in list(have.items())})
    return have


def gather_end(have, size, first=0, axis="tensor"):
    have = have | {k ^ 1: swap(v, 1, size, axis) for k, v in have.items()}
    return [have[k] for k in range(first, first + len(have))]


def gather_pieces(value, size, reach=None, axis="tensor"):
    have = {0: value}
    for bit in reversed(bits_of(reach or size)):
        have.update({k ^ bit: swap(v, bit, size, axis) for k, v in list(have.items())})
    return [have[k] for k in sorted(have)]


def gather_stack(value, size, axis):
    value = value[None]
    for bit in bits_of(size):
        value = jnp.concatenate([value, swap(value, bit, size, axis)], axis=0)
    return value


def scatter_stack(value, size, axis):
    for bit in reversed(bits_of(size)):
        value = value[:bit] + swap(value[bit:], bit, size, axis)
    return value[0]


def sum_all(value, size, axis):
    for bit in bits_of(size):
        value = value + swap(value, bit, size, axis)
    return value


def scatter_start(pieces, size):
    have = dict(enumerate(pieces))
    for bit in bits_of(size)[:-1]:
        kept = {}
        for k in sorted(have, reverse=True):
            if not k & bit:
                other = swap(have[k ^ bit].astype(BF16), bit, size)
                kept[k] = have[k].astype(F32) + other.astype(F32)
        have = kept
    kept, sent = (have[k] for k in sorted(have))
    return kept, sent.astype(BF16)


def scatter_end(kept, sent, size):
    return kept.astype(F32) + swap(sent, size // 2, size).astype(F32)


def after(values, *others):
    return lax.optimization_barrier((values, others))[0]


def ring_of(count):
    return list(range(0, count, 2)) + list(range(1, count, 2))[::-1]


def ring_member(place, count):
    place = lax.rem(place + count, count)
    return jnp.where(place < (count + 1) // 2, 2 * place, 2 * (count - 1 - place) + 1)


def ring_place(member, count):
    return jnp.where(member % 2 == 0, member // 2, count - 1 - member // 2)


def ring_step(value, way, count):
    ring = ring_of(count)
    hops = [(ring[i], ring[(i + way) % count]) for i in range(count)]
    return lax.ppermute(value, "dp", hops)


def place_kernel(steps, order, *refs):
    out = refs[-1]
    for step, (inputs, starts) in enumerate(steps):

        @pl.when(pl.program_id(0) == step)
        def _():
            for index, start in zip(inputs, starts):
                out[:, start : start + refs[index].shape[1]] = refs[index][...]


def place_blocks(blocks, steps, order, wide):
    share = blocks[0].shape[0]
    return pl.pallas_call(
        functools.partial(place_kernel, steps),
        grid_spec=pltpu.PrefetchScalarGridSpec(
            num_scalar_prefetch=1,
            grid=(len(steps),),
            in_specs=[
                pl.BlockSpec(block.shape, lambda s, order: (0, 0), pipeline_mode=pl.Buffered(1))
                for block in blocks
            ],
            out_specs=pl.BlockSpec((share, wide), lambda s, order: (order[s], 0)),
        ),
        out_shape=jax.ShapeDtypeStruct((len(steps) * share, wide), BF16),
        compiler_params=pltpu.CompilerParams(vmem_limit_bytes=48 * 1024 * 1024),
        cost_estimate=pl.CostEstimate(flops=0, transcendentals=0, bytes_accessed=1024),
        name="place_blocks",
    )(jnp.stack(order).astype(jnp.int32), *blocks)


def ring_gather(block, count):
    wide = block.shape[1]
    half = wide // 2 // LANES * LANES
    place = ring_place(lax.axis_index("dp"), count)
    blocks, offsets, steps = [block], [0], [((0,), (0,))]
    behind = ahead = block
    for hop in range(1, count // 2):
        behind = ring_step(behind, 1, count)
        ahead = ring_step(ahead, -1, count)
        behind, ahead = yield behind, ahead
        blocks += [behind, ahead]
        offsets += [-hop, hop]
        steps += [((2 * hop - 1,), (0,)), ((2 * hop,), (0,))]
    behind = ring_step(behind[:, :half], 1, count)
    ahead = ring_step(ahead[:, half:], -1, count)
    behind, ahead = yield behind, ahead
    blocks += [behind, ahead]
    offsets.append(count // 2)
    steps.append(((count - 1, count), (0, half)))
    yield place_blocks(
        blocks, steps, [ring_member(place + offset, count) for offset in offsets], wide
    )


def ring_scatter(grad, count):
    wide = grad.shape[1]
    share = grad.shape[0] // count
    half = wide // 2 // LANES * LANES
    place = ring_place(lax.axis_index("dp"), count)

    def own(offset):
        row = ring_member(place + offset, count) * share
        return lax.dynamic_slice_in_dim(grad, row, share, 0).astype(F32)

    far = own(count // 2).astype(BF16)
    behind = ring_step(far[:, :half], 1, count)
    ahead = ring_step(far[:, half:], -1, count)
    behind, ahead = yield behind, ahead
    behind = jnp.pad(behind.astype(F32), ((0, 0), (0, wide - half)))
    ahead = jnp.pad(ahead.astype(F32), ((0, 0), (half, 0)))
    for hop in range(count // 2 - 1, 0, -1):
        behind = ring_step((own(hop) + behind).astype(BF16), 1, count)
        ahead = ring_step((own(-hop) + ahead).astype(BF16), -1, count)
        behind, ahead = yield behind, ahead
        behind, ahead = behind.astype(F32), ahead.astype(F32)
    yield own(0) + behind + ahead


def text_start(value, size):
    for bit in bits_of(size)[:-1]:
        if bit > 1:
            value = lax.reduce_precision(value, 8, 7)
            value = value + swap(value.astype(BF16), bit, size).astype(F32)
        else:
            value = value + swap(value, bit, size)
    value = lax.reduce_precision(value, 8, 7)
    return value, value.astype(BF16)


def lane_mask(half, shape):
    lane = lax.broadcasted_iota(jnp.int32, shape, 1)
    return (lane >= HEAD) if half else (lane < HEAD)


def pick(value, half):
    return jnp.where(lane_mask(half, value.shape), value, jnp.zeros_like(value))


def load_rows(refs, store):
    start = 0
    for ref in refs:
        rows = ref.shape[1]
        store[start : start + rows, :] = ref[0]
        start += rows


def attend_kernel(count, *refs):
    queries, keys, values = refs[:count], refs[count : 2 * count], refs[2 * count : 3 * count]
    outs = refs[3 * count : 4 * count]
    sums = refs[4 * count : 5 * count]
    key_all, value_all = refs[5 * count :]
    load_rows(keys, key_all)
    load_rows(values, value_all)
    for index in range(count):
        query = queries[index][0] * jnp.asarray(HEAD**-0.5, BF16)
        halves = []
        for half in range(2):
            scores = dot(key_all[...], pick(query, half), 1, 1)
            highest = jnp.max(scores, axis=0, keepdims=True)
            weights = jnp.exp(scores - highest)
            total = jnp.sum(weights, axis=0, keepdims=True)
            weights = (weights * (1.0 / total)).astype(BF16)
            mixed = dot(value_all[...], weights, 0, 0)
            halves.append(mixed[half * HEAD : (half + 1) * HEAD])
            sums[index][0, 0, half : half + 1, :] = highest + jnp.log(total)
        outs[index][0] = jnp.concatenate(halves, axis=0).T.astype(BF16)


def attend_back_kernel(count, asked, groups, last, *refs):
    refs = list(refs)

    def take(number):
        return [refs.pop(0) for _ in range(number)]

    keys, values = take(count), take(count)
    queries, upstreams, sums = take(asked), take(asked), take(asked)
    if last:
        before = take(2)
        query_grads = take(count - asked)
        outs = take(count)
    else:
        outs = take(asked)
        totals = take(2)
    key_all, value_all, key_grad, value_grad = refs
    load_rows(keys, key_all)
    load_rows(values, value_all)
    pair = pl.program_id(1)
    scale = jnp.asarray(HEAD**-0.5, BF16)
    for index in range(asked):
        query = queries[index][0] * scale
        upstream = upstreams[index][0]
        halves = []
        for half in range(2):
            query_half = pick(query, half)
            upstream_half = pick(upstream, half)
            scores = dot(key_all[...], query_half, 1, 1)
            weights = jnp.exp(scores - sums[index][0, 0, half : half + 1, :])
            along = dot(value_all[...], upstream_half, 1, 1)
            value_part = dot(weights.astype(BF16), upstream_half, 1, 0)
            product = weights * along
            score_grad = (product - weights * jnp.sum(product, axis=0, keepdims=True)).astype(BF16)
            key_part = dot(score_grad, query_half, 1, 0)
            if index == 0 and half == 0 and last:
                value_grad[...] = before[1][0, 0] + value_part
                key_grad[...] = before[0][0, 0] + key_part
            elif index == 0 and half == 0:
                value_grad[...] = value_part
                key_grad[...] = key_part
            else:
                value_grad[...] += value_part
                key_grad[...] += key_part
            mixed = dot(key_all[...], score_grad, 0, 0)
            halves.append(mixed[half * HEAD : (half + 1) * HEAD])
        query_grad = (jnp.concatenate(halves, axis=0).T * HEAD**-0.5).astype(BF16)
        if last:
            lanes = pl.ds(pl.multiple_of(pair * LANES, LANES), LANES)
            outs[count - asked + index][0, :, lanes] = query_grad
        else:
            outs[index][0] = query_grad
    if not last:
        totals[0][0, 0] = key_grad[...]
        totals[1][0, 0] = value_grad[...]
        return
    for index, query_grad in enumerate(query_grads):
        lanes = pl.ds(pl.multiple_of(pair * LANES, LANES), LANES)
        outs[index][0, :, lanes] = query_grad[0]
    start = 0
    for out in outs:
        rows = out.shape[1]
        for number, grad in ((1, key_grad), (2, value_grad)):
            lanes = pl.ds(pl.multiple_of((number * groups + pair) * LANES, LANES), LANES)
            out[0, :, lanes] = grad[start : start + rows, :].astype(BF16)
        start += rows


def lane_blocks(parts, offset):
    return [
        pl.BlockSpec((1, part.shape[1], LANES), lambda s, p, o=offset: (s, 0, o + p))
        for part in parts
    ]


def widen(part, copies):
    slots, rows, width = part.shape
    width = width // copies
    extra = -width % LANES
    if not extra:
        return part
    part = jnp.pad(part.reshape(slots, rows, copies, width), ((0, 0), (0, 0), (0, 0), (0, extra)))
    return part.reshape(slots, rows, copies * (width + extra))


def narrow(part, copies, width):
    slots, rows, wide = part.shape
    wide = wide // copies
    if wide == width:
        return part
    return part.reshape(slots, rows, copies, wide)[..., :width].reshape(slots, rows, -1)


def attention_cost(slots, rows, width, products):
    return pl.CostEstimate(
        flops=products * 8 * slots * rows * rows * width,
        transcendentals=slots * rows * rows * (width // HEAD),
        bytes_accessed=slots * rows * width * 2 * (4 + 3 * (products > 2)),
    )


def attend(parts):
    slots = parts[0].shape[0]
    width = parts[0].shape[2] // 3
    parts = [widen(part, 3) for part in parts]
    count = len(parts)
    wide = parts[0].shape[2] // 3
    groups = wide // LANES
    total = sum(part.shape[1] for part in parts)
    outs = pl.pallas_call(
        functools.partial(attend_kernel, count),
        grid=(slots, groups),
        in_specs=lane_blocks(parts, 0) + lane_blocks(parts, groups) + lane_blocks(parts, 2 * groups),
        out_specs=lane_blocks(parts, 0)
        + [
            pl.BlockSpec((1, 1, 2, part.shape[1]), lambda s, p: (s, p, 0, 0)) for part in parts
        ],
        out_shape=[jax.ShapeDtypeStruct((slots, part.shape[1], wide), BF16) for part in parts]
        + [jax.ShapeDtypeStruct((slots, groups, 2, part.shape[1]), F32) for part in parts],
        scratch_shapes=[pltpu.VMEM((total, LANES), BF16)] * 2,
        compiler_params=pltpu.CompilerParams(vmem_limit_bytes=48 * 1024 * 1024),
        cost_estimate=attention_cost(slots, total, wide, 2),
        name="attend",
    )(*parts, *parts, *parts)
    return [narrow(out, 1, width) for out in outs[:count]], outs[count:]


def attend_back(parts, asked, upstreams, sums, before=None):
    slots = parts[0].shape[0]
    width = parts[0].shape[2] // 3
    parts = [widen(part, 3) for part in parts]
    upstreams = [widen(part, 1) for part in upstreams]
    last = before is not None
    count = len(parts)
    queries = parts[-asked:] if last else parts[:asked]
    wide = parts[0].shape[2] // 3
    groups = wide // LANES
    total = sum(part.shape[1] for part in parts)
    whole = pl.BlockSpec((1, 1, total, LANES), lambda s, p: (s, p, 0, 0))
    ins = lane_blocks(parts, groups) + lane_blocks(parts, 2 * groups) + lane_blocks(queries, 0)
    ins += lane_blocks(upstreams, 0)
    ins += [pl.BlockSpec((1, 1, 2, part.shape[1]), lambda s, p: (s, p, 0, 0)) for part in queries]
    operands = [*parts, *parts, *queries, *upstreams, *sums]
    if last:
        query_grads, totals = before
        ins += [whole, whole] + lane_blocks(query_grads, 0)
        operands += [*totals, *query_grads]
        out_specs = [
            pl.BlockSpec((1, part.shape[1], 3 * wide), lambda s, p: (s, 0, 0)) for part in parts
        ]
        out_shape = [
            jax.ShapeDtypeStruct((slots, part.shape[1], 3 * wide), BF16) for part in parts
        ]
    else:
        out_specs = lane_blocks(queries, 0) + [whole, whole]
        out_shape = [
            jax.ShapeDtypeStruct((slots, part.shape[1], wide), BF16) for part in queries
        ] + [jax.ShapeDtypeStruct((slots, groups, total, LANES), F32)] * 2
    outs = pl.pallas_call(
        functools.partial(attend_back_kernel, count, asked, groups, last),
        grid=(slots, groups),
        in_specs=ins,
        out_specs=out_specs,
        out_shape=out_shape,
        scratch_shapes=[pltpu.VMEM((total, LANES), BF16)] * 2 + [pltpu.VMEM((total, LANES), F32)] * 2,
        compiler_params=pltpu.CompilerParams(vmem_limit_bytes=48 * 1024 * 1024),
        cost_estimate=attention_cost(slots, total, wide, 2 if last else 5),
        name="attend_back",
    )(*operands)
    if last:
        return [narrow(out, 3, width) for out in outs]
    return outs[:asked], outs[asked:]


def rows_kernel(count, *refs):
    lefts, rights, out = refs[:count], refs[count : 2 * count], refs[-1]
    total = None
    for left, right in zip(lefts, rights):
        for slot in range(left.shape[0]):
            part = dot(left[slot], right[slot], 0, 0)
            total = part if total is None else total + part
    out[...] = total.astype(BF16)


def weight_grad(pairs):
    joined = None
    rows = pairs[0][0][0].shape[-1]
    wide = sum(rights[0].shape[-1] for _, rights in pairs)
    start = 0
    for lefts, rights in pairs:
        part = rights[0].shape[-1]
        if part % LANES or start % part:
            return jnp.concatenate([plain_grad(*pair) for pair in pairs], axis=1)
        count = len(lefts)
        step = 256
        ins = [
            pl.BlockSpec((left.shape[0], left.shape[1], step), lambda i: (0, 0, i))
            for left in lefts
        ] + [
            pl.BlockSpec(right.shape, lambda i: (0, 0, 0), pipeline_mode=pl.Buffered(1))
            for right in rights
        ]
        operands = (*lefts, *rights)
        if joined is not None:
            ins.append(pl.BlockSpec(memory_space=pl.ANY))
            operands += (joined,)
        joined = pl.pallas_call(
            functools.partial(rows_kernel, count),
            grid=(rows // step,),
            in_specs=ins,
            out_specs=pl.BlockSpec((step, part), lambda i, c=start // part: (i, c)),
            out_shape=jax.ShapeDtypeStruct((rows, wide), BF16),
            input_output_aliases={} if joined is None else {2 * count: 0},
            compiler_params=pltpu.CompilerParams(vmem_limit_bytes=48 * 1024 * 1024),
            cost_estimate=pl.CostEstimate(flops=0, transcendentals=0, bytes_accessed=1024),
            name="weight_grad",
        )(*operands)
        start += part
    return joined


NO_COST = pl.CostEstimate(flops=0, transcendentals=0, bytes_accessed=1024)
LIMIT = pltpu.CompilerParams(vmem_limit_bytes=48 * 1024 * 1024)


def tile_of(wide, start, most):
    return max(t for t in range(LANES, most + 1, LANES) if wide % t == 0 and start % t == 0)


def fits(weight):
    _, start, wide = weight
    return wide % LANES == 0 and start % LANES == 0


def cut(weight):
    array, start, wide = weight
    return array[:, start : start + wide]


def row_blocks(ref):
    slots, rows, columns = ref.shape
    if rows % 16 == 0:
        return [(slice(None), ref[...].reshape(slots * rows, columns))]
    return [(slice(slot, slot + 1), ref[slot]) for slot in range(slots)]


def store_rows(ref, place, value):
    slots = ref.shape[0] if place == slice(None) else 1
    ref[place] = value.reshape(slots, -1, value.shape[-1]).astype(ref.dtype)


def product_kernel(count, weight_dim, *refs):
    pieces, weight, outs = refs[:count], refs[count], refs[count + 1 :]
    for piece, out in zip(pieces, outs):
        for place, rows in row_blocks(piece):
            store_rows(out, place, dot(rows, weight[...], 1, weight_dim))


def whole_block(array):
    return pl.BlockSpec(array.shape, lambda j: (0, 0, 0), pipeline_mode=pl.Buffered(1))


def products_of(pieces, weight, weight_dim, kinds, late=False):
    array, start, wide = weight
    if not fits(weight) or (weight_dim and start % wide):
        return [
            dot(piece, cut(weight), 2, weight_dim).astype(kind)
            for piece, kind in zip(pieces, kinds)
        ]
    count = len(pieces)
    slots, _, depth = pieces[0].shape
    if weight_dim:
        result = array.shape[0]
        tile = tile_of(result, 0, 768)
        block = pl.BlockSpec((tile, wide), lambda j: (j, start // wide))
    else:
        result = wide
        tile = tile_of(wide, start, 768)
        block = pl.BlockSpec((depth, tile), lambda j: (0, start // tile + j))
    rows = slots * sum(piece.shape[1] for piece in pieces)
    cost = pl.CostEstimate(
        flops=4 * rows * depth * result, transcendentals=0, bytes_accessed=4 * rows * result
    )
    return pl.pallas_call(
        functools.partial(product_kernel, count, weight_dim),
        grid=(result // tile,),
        in_specs=[whole_block(piece) for piece in pieces] + [block],
        out_specs=[
            pl.BlockSpec((slots, piece.shape[1], tile), lambda j: (0, 0, j)) for piece in pieces
        ],
        out_shape=[
            jax.ShapeDtypeStruct((slots, piece.shape[1], result), kind)
            for piece, kind in zip(pieces, kinds)
        ],
        compiler_params=LIMIT,
        cost_estimate=cost if late else NO_COST,
        name="products",
    )(*pieces, array)


def hidden_kernel(count, *refs):
    pieces, downs, up, down = refs[:count], refs[count : 2 * count], refs[2 * count], refs[2 * count + 1]
    actives, grads = refs[2 * count + 2 : 3 * count + 2], refs[3 * count + 2 :]
    for piece, upstream, active, grad in zip(pieces, downs, actives, grads):
        for (place, rows), (_, above) in zip(row_blocks(piece), row_blocks(upstream)):
            hidden = dot(rows, up[...], 1, 0)
            active_grad = dot(above, down[...], 1, 0)
            square = hidden * hidden
            scale = (2 / math.pi) ** 0.5
            bend = jnp.tanh(hidden * (scale + scale * 0.044715 * square))
            half = 0.5 + 0.5 * bend
            slope = half + hidden * (0.5 - 0.5 * bend * bend) * (
                scale + scale * 0.134145 * square
            )
            store_rows(active, place, hidden * half)
            store_rows(grad, place, active_grad * slope)


def hidden_both(pieces, downs, up, down):
    count = len(pieces)
    if not (fits(up) and fits(down)):
        hidden = [dot(piece, cut(up), 2, 0) for piece in pieces]
        active_grad = [dot(piece, cut(down), 2, 0) for piece in downs]
        return (
            [gelu_tanh(value).astype(BF16) for value in hidden],
            [
                jax.vjp(gelu_tanh, value)[1](grad)[0].astype(BF16)
                for value, grad in zip(hidden, active_grad)
            ],
        )
    slots, _, depth = pieces[0].shape
    wide = up[2]
    tile = tile_of(wide, math.gcd(up[1], down[1]), 512)
    outs = pl.pallas_call(
        functools.partial(hidden_kernel, count),
        grid=(wide // tile,),
        in_specs=[whole_block(piece) for piece in (*pieces, *downs)]
        + [
            pl.BlockSpec((depth, tile), lambda j, o=block[1] // tile: (0, o + j))
            for block in (up, down)
        ],
        out_specs=[
            pl.BlockSpec((slots, piece.shape[1], tile), lambda j: (0, 0, j)) for piece in pieces
        ]
        * 2,
        out_shape=[
            jax.ShapeDtypeStruct((slots, piece.shape[1], wide), BF16) for piece in pieces
        ]
        * 2,
        compiler_params=LIMIT,
        cost_estimate=NO_COST,
        name="hidden_both",
    )(*pieces, *downs, up[0], down[0])
    return outs[:count], outs[count:]


def plain_grad(lefts, rights):
    left = jnp.concatenate([v.reshape(-1, v.shape[-1]) for v in lefts], axis=0)
    right = jnp.concatenate([v.reshape(-1, v.shape[-1]) for v in rights], axis=0)
    return dot(left, right, 0, 0).astype(BF16)


def on_device(
    group_count,
    tensor_size,
    image_tokens,
    text_tokens,
    condition,
    group_size,
    image_modulation,
    image_attention_in,
    image_attention_out,
    image_hidden_in,
    image_hidden_out,
    text_modulation,
    text_attention_in,
    text_attention_out,
    text_hidden_in,
    text_hidden_out,
    image_cotangent,
    text_cotangent,
):
    size = tensor_size
    slots, image_length, model = image_tokens.shape
    text_length = text_tokens.shape[1]
    share, _, width = image_attention_in.shape
    units = image_hidden_in.shape[1]
    tensor_rank = lax.axis_index("tensor")
    group_rank = lax.axis_index("dp")

    def gathered(*blocks):
        joined = blocks[0] if len(blocks) == 1 else jnp.concatenate(blocks, axis=1)
        return lax.all_gather(joined, "dp", axis=0, tiled=True)

    packed_first = gathered(
        image_attention_in.reshape(share, 3 * width),
        text_attention_in.reshape(share, 3 * width),
        image_attention_out.T,
        text_attention_out.T,
    )
    image_up = gathered(image_hidden_in)
    packed_text = gathered(text_hidden_in, text_hidden_out.T)
    weight_in = ((packed_first, 0, 3 * width), (packed_first, 3 * width, 3 * width))
    weight_out = ((packed_first, 6 * width, width), (packed_first, 7 * width, width))

    alive = (jnp.arange(slots) < group_size[0]).astype(F32)[:, None, None]
    cond_full = condition.astype(F32)
    activated_low = jax.nn.silu(cond_full).astype(BF16)
    activated_all = gather_stack(activated_low, group_count, "dp").reshape(-1, model)
    activated_own = lax.dynamic_slice_in_dim(activated_all, group_rank * share, share, 1)
    all_slots = activated_own.shape[0]
    mod_parts = jnp.concatenate(
        [
            dot(activated_own, image_modulation.reshape(share, 6 * width), 1, 0),
            dot(activated_own, text_modulation.reshape(share, 6 * width), 1, 0),
        ],
        axis=1,
    ).reshape(group_count, slots, 12 * width)
    mod_own = scatter_stack(mod_parts, group_count, "dp")
    modulations = lax.all_gather(
        mod_own.reshape(slots, 2, 6, width), "tensor", axis=3, tiled=True
    )
    down_ring = ring_gather(after(image_hidden_out.T, modulations), group_count)
    down_hop = next(down_ring)
    mods = (modulations[:, 0], modulations[:, 1])

    tokens = (image_tokens.astype(F32), text_tokens.astype(F32))
    outgoing = (image_cotangent.astype(F32) * alive, text_cotangent.astype(F32) * alive)

    half = size // 2
    near_kinds = [F32] + [BF16] * (half - 1)

    def scattered(grad):
        return lax.psum_scatter(grad, "dp", scatter_dimension=0, tiled=True).astype(F32)

    def row_products(pieces, weight, weight_dim, late=False):
        far = products_of(pieces[half:], weight, weight_dim, near_kinds, late)
        near = products_of(after(pieces[:half], far), weight, weight_dim, near_kinds, late)
        return [*near, *far]

    def image_sum(pieces, weight, weight_dim, late=False):
        products = row_products(pieces, weight, weight_dim, late)
        return scatter_end(*scatter_start(products, size), size)

    def text_sum(piece, weight, weight_dim, late=False):
        (product,) = products_of([piece], weight, weight_dim, [F32], late)
        return scatter_end(*text_start(product, size), size)

    def modulated(values, mod, shift, scale):
        normed, inverse = norm_rows(values)
        rows = normed * (1.0 + spread(mod[:, scale])) + spread(mod[:, shift])
        return normed, inverse, rows.astype(BF16)

    def second_back(stream, second_grad, normed, inverse):
        mod = mods[stream]
        shift_two_grad = jnp.sum(second_grad, axis=1)
        scale_two_grad = jnp.sum(second_grad * normed, axis=1)
        middle_grad = outgoing[stream] + norm_back(
            second_grad * (1.0 + spread(mod[:, 4])), normed, inverse
        )
        low = (middle_grad * spread(mod[:, 2])).astype(BF16)
        return middle_grad, low, shift_two_grad, scale_two_grad

    low_kinds = [BF16] * size

    normed_one, inverse_one, image_first = modulated(tokens[0], mods[0], 0, 1)
    text_normed_one, text_inverse_one, text_first = modulated(tokens[1], mods[1], 0, 1)
    first_pieces = gather_pieces(image_first, size)
    first_pieces, down_hop = lax.optimization_barrier((first_pieces, down_hop))
    down_hop = down_ring.send(down_hop)
    for _ in range(group_count // 2 - 4):
        down_hop = down_ring.send(down_hop)
    packed = products_of(first_pieces, weight_in[0], 0, low_kinds)
    text_packed = products_of([text_first], weight_in[1], 0, [BF16])
    down_rows = [
        (outgoing[stream] * spread(mods[stream][:, 5])).astype(BF16) for stream in range(2)
    ]
    down_have = gather_start(after(down_rows[0], first_pieces), size)
    parts, down_hop = after(([*packed, *text_packed], down_hop), down_have)
    down_hop = down_ring.send(down_hop)
    attended, sums = attend(parts)
    attended, down_hop = lax.optimization_barrier((attended, down_hop))
    down_hop = down_ring.send(down_hop)
    down_pieces = gather_end(after(down_have, attended), size)
    attended_parts = (attended[:-1], attended[-1:])

    branch = image_sum(attended_parts[0], weight_out[0], 1)
    branch, down_hop = lax.optimization_barrier((branch, down_hop))
    image_down = down_ring.send(down_hop)
    middle = tokens[0] + spread(mods[0][:, 2]) * branch
    normed_two, inverse_two, image_second = modulated(middle, mods[0], 3, 4)
    up_weight, down_weight = (image_up, 0, units), (image_down, 0, units)
    near_pieces = gather_pieces(image_second, size, half)
    far_have = gather_start(image_second, size)
    near = hidden_both(near_pieces, down_pieces[:half], up_weight, down_weight)
    far_have = {k: v for k, v in far_have.items() if k >= half}
    far_pieces = gather_end(after(far_have, near), size, half)
    second_pieces = [*near_pieces, *far_pieces]
    far = hidden_both(far_pieces, down_pieces[half:], up_weight, down_weight)
    text_branch = text_sum(after(attended_parts[1][0], image_second), weight_out[1], 1)
    active = [*near[0], *far[0]]
    hidden_grad = after([*near[1], *far[1]], text_branch)
    kept, sent = scatter_start(row_products(hidden_grad, up_weight, 1), size)
    image_mlp_grad = weight_grad(
        after([(down_pieces, active), (second_pieces, hidden_grad)], sent)
    )
    second_grad = after(scatter_end(kept, sent, size), image_mlp_grad)
    image_mlp = scattered(after(image_mlp_grad, second_grad))
    middle_grad, low, shift_two_grad, scale_two_grad = second_back(
        0, second_grad, normed_two, inverse_two
    )
    gate_one_grad = jnp.sum(middle_grad * branch, axis=1)

    low_have = gather_start(low, size)
    two_products = row_products(after(active, low), down_weight, 1)
    two_kept, two_sent = scatter_start(two_products, size)
    text_both = after(packed_text, low)
    text_up_weight, text_down_weight = (text_both, 0, units), (text_both, units, units)
    text_middle = tokens[1] + spread(mods[1][:, 2]) * text_branch
    text_normed_two, text_inverse_two, text_second = modulated(text_middle, mods[1], 3, 4)
    text_active, text_hidden_grad = hidden_both(
        [text_second], [down_rows[1]], text_up_weight, text_down_weight
    )
    (text_product,) = products_of(text_hidden_grad, text_up_weight, 1, [F32])
    text_kept, text_sent = text_start(text_product, size)
    low_have = after(low_have, two_products, text_product)
    branch_grads = gather_end(low_have, size)

    upstreams = products_of(branch_grads, weight_out[0], 0, low_kinds)
    ring_grad = weight_grad(
        after(
            [
                ([down_rows[1]], text_active),
                ([text_second], text_hidden_grad),
                (branch_grads, attended_parts[0]),
            ],
            branch_grads,
        )
    )
    upstreams = after(upstreams, text_sent, ring_grad)
    text_ring = ring_scatter(ring_grad, group_count)
    text_hop = next(text_ring)
    first_part = attend_back(parts, size, upstreams, sums[:-1])
    branch_two = scatter_end(after(two_kept, first_part), two_sent, size)
    text_second_grad = scatter_end(after(text_kept, first_part), text_sent, size)
    first_part, branch_two, text_hop = lax.optimization_barrier((first_part, branch_two, text_hop))
    text_hop = text_ring.send(text_hop)
    text_middle_grad, text_low, text_shift_two_grad, text_scale_two_grad = second_back(
        1, text_second_grad, text_normed_two, text_inverse_two
    )
    text_gate_one_grad = jnp.sum(text_middle_grad * text_branch, axis=1)
    text_upstream = products_of([text_low], weight_out[1], 0, [BF16])
    packed_grads = attend_back(parts, 1, text_upstream, sums[-1:], first_part)
    packed_grads, text_hop = lax.optimization_barrier((packed_grads, text_hop))
    text_hop = text_ring.send(text_hop)
    attention_grad = weight_grad(
        [
            (first_pieces, packed_grads[:-1]),
            ([text_first], packed_grads[-1:]),
            ([text_low], attended_parts[1]),
        ]
    )
    attention_sum = scattered(attention_grad)
    packed_grads, text_active = after((packed_grads, text_active), attention_grad)

    def first_back(stream, first_grad, normed, inverse, middle_grad):
        mod = mods[stream]
        shift_one_grad = jnp.sum(first_grad, axis=1)
        scale_one_grad = jnp.sum(first_grad * normed, axis=1)
        input_grad = middle_grad + norm_back(
            first_grad * (1.0 + spread(mod[:, 1])), normed, inverse
        )
        return input_grad, shift_one_grad, scale_one_grad

    def finish(stream, middle, branch_two):
        result = middle + spread(mods[stream][:, 5]) * branch_two
        gate_two_grad = jnp.sum(outgoing[stream] * branch_two, axis=1)
        return (result * alive).astype(BF16), gate_two_grad

    first_grad = image_sum(packed_grads[:-1], weight_in[0], 1, True)
    text_first_grad = text_sum(packed_grads[-1], weight_in[1], 1, True)
    text_branch_two = text_sum(text_active[0], text_down_weight, 1, True)
    text_first_grad, text_hop = lax.optimization_barrier((text_first_grad, text_hop))
    for _ in range(group_count // 2 - 3):
        text_hop = text_ring.send(text_hop)
    first_grad, text_hop = lax.optimization_barrier((first_grad, text_hop))
    text_mlp = text_ring.send(text_hop)
    input_grads = [None, None]
    input_grads[0], shift_one_grad, scale_one_grad = first_back(
        0, first_grad, normed_one, inverse_one, middle_grad
    )
    input_grads[1], text_shift_one_grad, text_scale_one_grad = first_back(
        1, text_first_grad, text_normed_one, text_inverse_one, text_middle_grad
    )
    outputs = [None, None]
    outputs[0], gate_two_grad = finish(0, middle, branch_two)
    outputs[1], text_gate_two_grad = finish(1, text_middle, text_branch_two)
    mod_grads = (
        jnp.stack(
            [
                shift_one_grad,
                scale_one_grad,
                gate_one_grad,
                shift_two_grad,
                scale_two_grad,
                gate_two_grad,
            ],
            axis=1,
        ),
        jnp.stack(
            [
                text_shift_one_grad,
                text_scale_one_grad,
                text_gate_one_grad,
                text_shift_two_grad,
                text_scale_two_grad,
                text_gate_two_grad,
            ],
            axis=1,
        ),
    )

    image_blocks = jnp.stack(
        [
            lax.dynamic_slice_in_dim(mod_grads[0], (tensor_rank ^ k) * width, width, 2)
            for k in range(size)
        ]
    )
    image_share = scatter_stack(image_blocks, size, "tensor")
    text_share = lax.dynamic_slice_in_dim(mod_grads[1], tensor_rank * width, width, 2)
    share_low = jnp.stack([image_share, text_share], axis=1).astype(BF16)
    share_all = gather_stack(share_low, group_count, "dp").reshape(all_slots, 2, 6, width)
    image_all = share_all[:, 0].reshape(all_slots, 6 * width)
    text_all = share_all[:, 1].reshape(all_slots, 6 * width)
    image_ada = dot(activated_own, image_all, 0, 0).reshape(share, 6, width)
    text_ada = dot(activated_own, text_all, 0, 0).reshape(share, 6, width)
    activated_part = dot(image_all, image_modulation.reshape(share, 6 * width), 1, 1) + dot(
        text_all, text_modulation.reshape(share, 6 * width), 1, 1
    )
    activated_part = sum_all(activated_part, size, "tensor").reshape(group_count, slots, share)
    activated_rows = gather_stack(activated_part, group_count, "dp")
    activated_rows = jnp.stack([activated_rows[k, k] for k in range(group_count)])
    activated_grad = jnp.concatenate(
        [
            lax.dynamic_index_in_dim(activated_rows, group_rank ^ k, 0, keepdims=False)
            for k in range(group_count)
        ],
        axis=1,
    )
    condition_gradient = jax.vjp(jax.nn.silu, cond_full)[1](activated_grad)[0]

    return (
        outputs[0],
        outputs[1],
        input_grads[0],
        input_grads[1],
        condition_gradient,
        image_ada,
        attention_sum[:, : 3 * width].reshape(share, 3, width),
        text_mlp[:, 2 * units :].T,
        image_mlp[:, units:],
        image_mlp[:, :units].T,
        text_ada,
        attention_sum[:, 3 * width : 6 * width].reshape(share, 3, width),
        attention_sum[:, 6 * width :].T,
        text_mlp[:, units : 2 * units],
        text_mlp[:, :units].T,
    )


def solution(mesh):
    image = P("dp", "tensor", None)
    text = P("dp", None, None)
    columns = P("dp", None, "tensor")
    rows = P("tensor", "dp")
    plain = P("dp", "tensor")
    weights = (columns, columns, rows, plain, rows)
    return jax.shard_map(
        functools.partial(on_device, mesh.shape["dp"], mesh.shape["tensor"]),
        mesh=mesh,
        in_specs=(image, text, P("dp", None), P("dp")) + weights + weights + (image, text),
        out_specs=(image, text, image, text, P("dp", None)) + weights + weights,
        check_vma=False,
    )
```

```python
import functools
import math

import jax
import jax.numpy as jnp
from jax import lax
from jax.experimental import pallas as pl
from jax.experimental.pallas import tpu as pltpu
from jax.sharding import PartitionSpec as P

HEAD = 64
LANES = 128
F32 = jnp.float32
BF16 = jnp.bfloat16


def norm_rows(values):
    center = values - jnp.mean(values, axis=-1, keepdims=True)
    inverse = lax.rsqrt(jnp.mean(center * center, axis=-1, keepdims=True) + 1e-06)
    return (center * inverse, inverse)


def norm_back(upstream, normed, inverse):
    first = jnp.mean(upstream, axis=-1, keepdims=True)
    second = jnp.mean(upstream * normed, axis=-1, keepdims=True)
    return inverse * (upstream - first - normed * second)


def gelu_tanh(values):
    return jax.nn.gelu(values, approximate=True)


def spread(vector):
    return vector[:, None, :]


def dot(left, right, left_dim, right_dim):
    return lax.dot_general(
        left, right, (((left_dim,), (right_dim,)), ((), ())), preferred_element_type=F32
    )


def swap(value, bit, size, axis="tensor"):
    return lax.ppermute(value, axis, [(i, i ^ bit) for i in range(size)])


def bits_of(size):
    bits = []
    bit = 1
    while bit < size:
        bits.append(bit)
        bit *= 2
    return bits


def gather_start(value, size, axis="tensor"):
    have = {0: value}
    for bit in reversed(bits_of(size)[1:]):
        have.update({k ^ bit: swap(v, bit, size, axis) for k, v in list(have.items())})
    return have


def gather_end(have, size, first=0, axis="tensor"):
    have = have | {k ^ 1: swap(v, 1, size, axis) for k, v in have.items()}
    return [have[k] for k in range(first, first + len(have))]


def gather_pieces(value, size, reach=None, axis="tensor"):
    have = {0: value}
    for bit in reversed(bits_of(reach or size)):
        have.update({k ^ bit: swap(v, bit, size, axis) for k, v in list(have.items())})
    return [have[k] for k in sorted(have)]


def gather_stack(value, size, axis):
    value = value[None]
    for bit in bits_of(size):
        value = jnp.concatenate([value, swap(value, bit, size, axis)], axis=0)
    return value


def scatter_stack(value, size, axis):
    for bit in reversed(bits_of(size)):
        value = value[:bit] + swap(value[bit:], bit, size, axis)
    return value[0]


def sum_all(value, size, axis):
    for bit in bits_of(size):
        value = value + swap(value, bit, size, axis)
    return value


def scatter_start(pieces, size):
    have = dict(enumerate(pieces))
    for bit in bits_of(size)[:-1]:
        kept = {}
        for k in sorted(have, reverse=True):
            if not k & bit:
                other = swap(have[k ^ bit].astype(BF16), bit, size)
                kept[k] = have[k].astype(F32) + other.astype(F32)
        have = kept
    kept, sent = (have[k] for k in sorted(have))
    return kept, sent.astype(BF16)


def scatter_end(kept, sent, size):
    return kept.astype(F32) + swap(sent, size // 2, size).astype(F32)


def after(values, *others):
    return lax.optimization_barrier((values, others))[0]


def ring_of(count):
    return list(range(0, count, 2)) + list(range(1, count, 2))[::-1]


def ring_member(place, count):
    place = lax.rem(place + count, count)
    return jnp.where(place < (count + 1) // 2, 2 * place, 2 * (count - 1 - place) + 1)


def ring_place(member, count):
    return jnp.where(member % 2 == 0, member // 2, count - 1 - member // 2)


def ring_step(value, way, count):
    ring = ring_of(count)
    hops = [(ring[i], ring[(i + way) % count]) for i in range(count)]
    return lax.ppermute(value, "dp", hops)


def ring_scatter(grad, count):
    wide = grad.shape[1]
    share = grad.shape[0] // count
    half = wide // 2 // LANES * LANES
    place = ring_place(lax.axis_index("dp"), count)

    def own(offset):
        row = ring_member(place + offset, count) * share
        return lax.dynamic_slice_in_dim(grad, row, share, 0).astype(F32)

    far = own(count // 2).astype(BF16)
    behind = ring_step(far[:, :half], 1, count)
    ahead = ring_step(far[:, half:], -1, count)
    behind, ahead = yield behind, ahead
    behind = jnp.pad(behind.astype(F32), ((0, 0), (0, wide - half)))
    ahead = jnp.pad(ahead.astype(F32), ((0, 0), (half, 0)))
    for hop in range(count // 2 - 1, 0, -1):
        behind = ring_step((own(hop) + behind).astype(BF16), 1, count)
        ahead = ring_step((own(-hop) + ahead).astype(BF16), -1, count)
        behind, ahead = yield behind, ahead
        behind, ahead = behind.astype(F32), ahead.astype(F32)
    yield own(0) + behind + ahead


def text_start(value, size):
    for bit in bits_of(size)[:-1]:
        if bit > 1:
            value = lax.reduce_precision(value, 8, 7)
            value = value + swap(value.astype(BF16), bit, size).astype(F32)
        else:
            value = value + swap(value, bit, size)
    value = lax.reduce_precision(value, 8, 7)
    return value, value.astype(BF16)


def lane_mask(half, shape):
    lane = lax.broadcasted_iota(jnp.int32, shape, 1)
    return (lane >= HEAD) if half else (lane < HEAD)


def pick(value, half):
    return jnp.where(lane_mask(half, value.shape), value, jnp.zeros_like(value))


def load_rows(refs, store):
    start = 0
    for ref in refs:
        rows = ref.shape[1]
        store[start : start + rows, :] = ref[0]
        start += rows


def attend_kernel(count, *refs):
    queries, keys, values = refs[:count], refs[count : 2 * count], refs[2 * count : 3 * count]
    outs = refs[3 * count : 4 * count]
    sums = refs[4 * count : 5 * count]
    key_all, value_all = refs[5 * count :]
    load_rows(keys, key_all)
    load_rows(values, value_all)
    for index in range(count):
        query = queries[index][0] * jnp.asarray(HEAD**-0.5, BF16)
        halves = []
        for half in range(2):
            scores = dot(key_all[...], pick(query, half), 1, 1)
            highest = jnp.max(scores, axis=0, keepdims=True)
            weights = jnp.exp(scores - highest)
            total = jnp.sum(weights, axis=0, keepdims=True)
            weights = (weights * (1.0 / total)).astype(BF16)
            mixed = dot(value_all[...], weights, 0, 0)
            halves.append(mixed[half * HEAD : (half + 1) * HEAD])
            sums[index][0, 0, half : half + 1, :] = highest + jnp.log(total)
        outs[index][0] = jnp.concatenate(halves, axis=0).T.astype(BF16)


def attend_back_kernel(count, asked, groups, last, *refs):
    refs = list(refs)

    def take(number):
        return [refs.pop(0) for _ in range(number)]

    keys, values = take(count), take(count)
    queries, upstreams, sums = take(asked), take(asked), take(asked)
    if last:
        before = take(2)
        query_grads = take(count - asked)
        outs = take(count)
    else:
        outs = take(asked)
        totals = take(2)
    key_all, value_all, key_grad, value_grad = refs
    load_rows(keys, key_all)
    load_rows(values, value_all)
    pair = pl.program_id(1)
    scale = jnp.asarray(HEAD**-0.5, BF16)
    for index in range(asked):
        query = queries[index][0] * scale
        upstream = upstreams[index][0]
        halves = []
        for half in range(2):
            query_half = pick(query, half)
            upstream_half = pick(upstream, half)
            scores = dot(key_all[...], query_half, 1, 1)
            weights = jnp.exp(scores - sums[index][0, 0, half : half + 1, :])
            along = dot(value_all[...], upstream_half, 1, 1)
            value_part = dot(weights.astype(BF16), upstream_half, 1, 0)
            product = weights * along
            score_grad = (product - weights * jnp.sum(product, axis=0, keepdims=True)).astype(BF16)
            key_part = dot(score_grad, query_half, 1, 0)
            if index == 0 and half == 0 and last:
                value_grad[...] = before[1][0, 0] + value_part
                key_grad[...] = before[0][0, 0] + key_part
            elif index == 0 and half == 0:
                value_grad[...] = value_part
                key_grad[...] = key_part
            else:
                value_grad[...] += value_part
                key_grad[...] += key_part
            mixed = dot(key_all[...], score_grad, 0, 0)
            halves.append(mixed[half * HEAD : (half + 1) * HEAD])
        query_grad = (jnp.concatenate(halves, axis=0).T * HEAD**-0.5).astype(BF16)
        if last:
            lanes = pl.ds(pl.multiple_of(pair * LANES, LANES), LANES)
            outs[count - asked + index][0, :, lanes] = query_grad
        else:
            outs[index][0] = query_grad
    if not last:
        totals[0][0, 0] = key_grad[...]
        totals[1][0, 0] = value_grad[...]
        return
    for index, query_grad in enumerate(query_grads):
        lanes = pl.ds(pl.multiple_of(pair * LANES, LANES), LANES)
        outs[index][0, :, lanes] = query_grad[0]
    start = 0
    for out in outs:
        rows = out.shape[1]
        for number, grad in ((1, key_grad), (2, value_grad)):
            lanes = pl.ds(pl.multiple_of((number * groups + pair) * LANES, LANES), LANES)
            out[0, :, lanes] = grad[start : start + rows, :].astype(BF16)
        start += rows


def lane_blocks(parts, offset):
    return [
        pl.BlockSpec((1, part.shape[1], LANES), lambda s, p, o=offset: (s, 0, o + p))
        for part in parts
    ]


def widen(part, copies):
    slots, rows, width = part.shape
    width = width // copies
    extra = -width % LANES
    if not extra:
        return part
    part = jnp.pad(part.reshape(slots, rows, copies, width), ((0, 0), (0, 0), (0, 0), (0, extra)))
    return part.reshape(slots, rows, copies * (width + extra))


def narrow(part, copies, width):
    slots, rows, wide = part.shape
    wide = wide // copies
    if wide == width:
        return part
    return part.reshape(slots, rows, copies, wide)[..., :width].reshape(slots, rows, -1)


def attention_cost(slots, rows, width, products):
    return pl.CostEstimate(
        flops=products * 8 * slots * rows * rows * width,
        transcendentals=slots * rows * rows * (width // HEAD),
        bytes_accessed=slots * rows * width * 2 * (4 + 3 * (products > 2)),
    )


def attend(parts):
    slots = parts[0].shape[0]
    width = parts[0].shape[2] // 3
    parts = [widen(part, 3) for part in parts]
    count = len(parts)
    wide = parts[0].shape[2] // 3
    groups = wide // LANES
    total = sum(part.shape[1] for part in parts)
    outs = pl.pallas_call(
        functools.partial(attend_kernel, count),
        grid=(slots, groups),
        in_specs=lane_blocks(parts, 0) + lane_blocks(parts, groups) + lane_blocks(parts, 2 * groups),
        out_specs=lane_blocks(parts, 0)
        + [
            pl.BlockSpec((1, 1, 2, part.shape[1]), lambda s, p: (s, p, 0, 0)) for part in parts
        ],
        out_shape=[jax.ShapeDtypeStruct((slots, part.shape[1], wide), BF16) for part in parts]
        + [jax.ShapeDtypeStruct((slots, groups, 2, part.shape[1]), F32) for part in parts],
        scratch_shapes=[pltpu.VMEM((total, LANES), BF16)] * 2,
        compiler_params=pltpu.CompilerParams(vmem_limit_bytes=48 * 1024 * 1024),
        cost_estimate=attention_cost(slots, total, wide, 2),
        name="attend",
    )(*parts, *parts, *parts)
    return [narrow(out, 1, width) for out in outs[:count]], outs[count:]


def attend_back(parts, asked, upstreams, sums, before=None):
    slots = parts[0].shape[0]
    width = parts[0].shape[2] // 3
    parts = [widen(part, 3) for part in parts]
    upstreams = [widen(part, 1) for part in upstreams]
    last = before is not None
    count = len(parts)
    queries = parts[-asked:] if last else parts[:asked]
    wide = parts[0].shape[2] // 3
    groups = wide // LANES
    total = sum(part.shape[1] for part in parts)
    whole = pl.BlockSpec((1, 1, total, LANES), lambda s, p: (s, p, 0, 0))
    ins = lane_blocks(parts, groups) + lane_blocks(parts, 2 * groups) + lane_blocks(queries, 0)
    ins += lane_blocks(upstreams, 0)
    ins += [pl.BlockSpec((1, 1, 2, part.shape[1]), lambda s, p: (s, p, 0, 0)) for part in queries]
    operands = [*parts, *parts, *queries, *upstreams, *sums]
    if last:
        query_grads, totals = before
        ins += [whole, whole] + lane_blocks(query_grads, 0)
        operands += [*totals, *query_grads]
        out_specs = [
            pl.BlockSpec((1, part.shape[1], 3 * wide), lambda s, p: (s, 0, 0)) for part in parts
        ]
        out_shape = [
            jax.ShapeDtypeStruct((slots, part.shape[1], 3 * wide), BF16) for part in parts
        ]
    else:
        out_specs = lane_blocks(queries, 0) + [whole, whole]
        out_shape = [
            jax.ShapeDtypeStruct((slots, part.shape[1], wide), BF16) for part in queries
        ] + [jax.ShapeDtypeStruct((slots, groups, total, LANES), F32)] * 2
    outs = pl.pallas_call(
        functools.partial(attend_back_kernel, count, asked, groups, last),
        grid=(slots, groups),
        in_specs=ins,
        out_specs=out_specs,
        out_shape=out_shape,
        scratch_shapes=[pltpu.VMEM((total, LANES), BF16)] * 2 + [pltpu.VMEM((total, LANES), F32)] * 2,
        compiler_params=pltpu.CompilerParams(vmem_limit_bytes=48 * 1024 * 1024),
        cost_estimate=attention_cost(slots, total, wide, 2 if last else 5),
        name="attend_back",
    )(*operands)
    if last:
        return [narrow(out, 3, width) for out in outs]
    return outs[:asked], outs[asked:]


def rows_kernel(count, *refs):
    lefts, rights, out = refs[:count], refs[count : 2 * count], refs[-1]
    total = None
    for left, right in zip(lefts, rights):
        for slot in range(left.shape[0]):
            part = dot(left[slot], right[slot], 0, 0)
            total = part if total is None else total + part
    out[...] = total.astype(BF16)


def weight_grad(pairs):
    joined = None
    rows = pairs[0][0][0].shape[-1]
    wide = sum(rights[0].shape[-1] for _, rights in pairs)
    start = 0
    for lefts, rights in pairs:
        part = rights[0].shape[-1]
        if part % LANES or start % part:
            return jnp.concatenate([plain_grad(*pair) for pair in pairs], axis=1)
        count = len(lefts)
        step = 256
        ins = [
            pl.BlockSpec((left.shape[0], left.shape[1], step), lambda i: (0, 0, i))
            for left in lefts
        ] + [
            pl.BlockSpec(right.shape, lambda i: (0, 0, 0), pipeline_mode=pl.Buffered(1))
            for right in rights
        ]
        operands = (*lefts, *rights)
        if joined is not None:
            ins.append(pl.BlockSpec(memory_space=pl.ANY))
            operands += (joined,)
        joined = pl.pallas_call(
            functools.partial(rows_kernel, count),
            grid=(rows // step,),
            in_specs=ins,
            out_specs=pl.BlockSpec((step, part), lambda i, c=start // part: (i, c)),
            out_shape=jax.ShapeDtypeStruct((rows, wide), BF16),
            input_output_aliases={} if joined is None else {2 * count: 0},
            compiler_params=pltpu.CompilerParams(vmem_limit_bytes=48 * 1024 * 1024),
            cost_estimate=pl.CostEstimate(flops=0, transcendentals=0, bytes_accessed=1024),
            name="weight_grad",
        )(*operands)
        start += part
    return joined


NO_COST = pl.CostEstimate(flops=0, transcendentals=0, bytes_accessed=1024)
LIMIT = pltpu.CompilerParams(vmem_limit_bytes=48 * 1024 * 1024)


def tile_of(wide, start, most):
    return max(t for t in range(LANES, most + 1, LANES) if wide % t == 0 and start % t == 0)


def fits(weight):
    _, start, wide = weight
    return wide % LANES == 0 and start % LANES == 0


def cut(weight):
    array, start, wide = weight
    return array[:, start : start + wide]


def row_blocks(ref):
    slots, rows, columns = ref.shape
    if rows % 16 == 0:
        return [(slice(None), ref[...].reshape(slots * rows, columns))]
    return [(slice(slot, slot + 1), ref[slot]) for slot in range(slots)]


def store_rows(ref, place, value):
    slots = ref.shape[0] if place == slice(None) else 1
    ref[place] = value.reshape(slots, -1, value.shape[-1]).astype(ref.dtype)


def product_kernel(count, weight_dim, *refs):
    pieces, weight, outs = refs[:count], refs[count], refs[count + 1 :]
    for piece, out in zip(pieces, outs):
        for place, rows in row_blocks(piece):
            store_rows(out, place, dot(rows, weight[...], 1, weight_dim))


def whole_block(array):
    return pl.BlockSpec(array.shape, lambda j: (0, 0, 0), pipeline_mode=pl.Buffered(1))


def products_of(pieces, weight, weight_dim, kinds, late=False):
    array, start, wide = weight
    if not fits(weight) or (weight_dim and start % wide):
        return [
            dot(piece, cut(weight), 2, weight_dim).astype(kind)
            for piece, kind in zip(pieces, kinds)
        ]
    count = len(pieces)
    slots, _, depth = pieces[0].shape
    if weight_dim:
        result = array.shape[0]
        tile = tile_of(result, 0, 768)
        block = pl.BlockSpec((tile, wide), lambda j: (j, start // wide))
    else:
        result = wide
        tile = tile_of(wide, start, 768)
        block = pl.BlockSpec((depth, tile), lambda j: (0, start // tile + j))
    rows = slots * sum(piece.shape[1] for piece in pieces)
    cost = pl.CostEstimate(
        flops=12 * rows * depth * result, transcendentals=0, bytes_accessed=4 * rows * result
    )
    return pl.pallas_call(
        functools.partial(product_kernel, count, weight_dim),
        grid=(result // tile,),
        in_specs=[whole_block(piece) for piece in pieces] + [block],
        out_specs=[
            pl.BlockSpec((slots, piece.shape[1], tile), lambda j: (0, 0, j)) for piece in pieces
        ],
        out_shape=[
            jax.ShapeDtypeStruct((slots, piece.shape[1], result), kind)
            for piece, kind in zip(pieces, kinds)
        ],
        compiler_params=LIMIT,
        cost_estimate=cost if late else NO_COST,
        name="products",
    )(*pieces, array)


def hidden_kernel(count, *refs):
    pieces, downs, up, down = refs[:count], refs[count : 2 * count], refs[2 * count], refs[2 * count + 1]
    actives, grads = refs[2 * count + 2 : 3 * count + 2], refs[3 * count + 2 :]
    for piece, upstream, active, grad in zip(pieces, downs, actives, grads):
        for (place, rows), (_, above) in zip(row_blocks(piece), row_blocks(upstream)):
            hidden = dot(rows, up[...], 1, 0)
            active_grad = dot(above, down[...], 1, 0)
            square = hidden * hidden
            scale = (2 / math.pi) ** 0.5
            bend = jnp.tanh(hidden * (scale + scale * 0.044715 * square))
            half = 0.5 + 0.5 * bend
            slope = half + hidden * (0.5 - 0.5 * bend * bend) * (
                scale + scale * 0.134145 * square
            )
            store_rows(active, place, hidden * half)
            store_rows(grad, place, active_grad * slope)


def hidden_both(pieces, downs, up, down):
    count = len(pieces)
    if not (fits(up) and fits(down)):
        hidden = [dot(piece, cut(up), 2, 0) for piece in pieces]
        active_grad = [dot(piece, cut(down), 2, 0) for piece in downs]
        return (
            [gelu_tanh(value).astype(BF16) for value in hidden],
            [
                jax.vjp(gelu_tanh, value)[1](grad)[0].astype(BF16)
                for value, grad in zip(hidden, active_grad)
            ],
        )
    slots, _, depth = pieces[0].shape
    wide = up[2]
    tile = tile_of(wide, math.gcd(up[1], down[1]), 512)
    outs = pl.pallas_call(
        functools.partial(hidden_kernel, count),
        grid=(wide // tile,),
        in_specs=[whole_block(piece) for piece in (*pieces, *downs)]
        + [
            pl.BlockSpec((depth, tile), lambda j, o=block[1] // tile: (0, o + j))
            for block in (up, down)
        ],
        out_specs=[
            pl.BlockSpec((slots, piece.shape[1], tile), lambda j: (0, 0, j)) for piece in pieces
        ]
        * 2,
        out_shape=[
            jax.ShapeDtypeStruct((slots, piece.shape[1], wide), BF16) for piece in pieces
        ]
        * 2,
        compiler_params=LIMIT,
        cost_estimate=NO_COST,
        name="hidden_both",
    )(*pieces, *downs, up[0], down[0])
    return outs[:count], outs[count:]


def plain_grad(lefts, rights):
    left = jnp.concatenate([v.reshape(-1, v.shape[-1]) for v in lefts], axis=0)
    right = jnp.concatenate([v.reshape(-1, v.shape[-1]) for v in rights], axis=0)
    return dot(left, right, 0, 0).astype(BF16)


def on_device(
    group_count,
    tensor_size,
    image_tokens,
    text_tokens,
    condition,
    group_size,
    image_modulation,
    image_attention_in,
    image_attention_out,
    image_hidden_in,
    image_hidden_out,
    text_modulation,
    text_attention_in,
    text_attention_out,
    text_hidden_in,
    text_hidden_out,
    image_cotangent,
    text_cotangent,
):
    size = tensor_size
    slots, image_length, model = image_tokens.shape
    text_length = text_tokens.shape[1]
    share, _, width = image_attention_in.shape
    units = image_hidden_in.shape[1]
    tensor_rank = lax.axis_index("tensor")
    group_rank = lax.axis_index("dp")

    def gathered(*blocks):
        joined = blocks[0] if len(blocks) == 1 else jnp.concatenate(blocks, axis=1)
        return lax.all_gather(joined, "dp", axis=0, tiled=True)

    packed_first = gathered(
        image_attention_in.reshape(share, 3 * width),
        text_attention_in.reshape(share, 3 * width),
        image_attention_out.T,
        text_attention_out.T,
    )
    image_up = gathered(image_hidden_in)
    image_down = gathered(image_hidden_out.T)
    packed_text = gathered(text_hidden_in, text_hidden_out.T)
    weight_in = ((packed_first, 0, 3 * width), (packed_first, 3 * width, 3 * width))
    weight_out = ((packed_first, 6 * width, width), (packed_first, 7 * width, width))

    alive = (jnp.arange(slots) < group_size[0]).astype(F32)[:, None, None]
    cond_full = condition.astype(F32)
    activated_low = jax.nn.silu(cond_full).astype(BF16)
    activated_all = gather_stack(activated_low, group_count, "dp").reshape(-1, model)
    activated_own = lax.dynamic_slice_in_dim(activated_all, group_rank * share, share, 1)
    all_slots = activated_own.shape[0]
    mod_parts = jnp.concatenate(
        [
            dot(activated_own, image_modulation.reshape(share, 6 * width), 1, 0),
            dot(activated_own, text_modulation.reshape(share, 6 * width), 1, 0),
        ],
        axis=1,
    ).reshape(group_count, slots, 12 * width)
    mod_own = scatter_stack(mod_parts, group_count, "dp")
    modulations = lax.all_gather(
        mod_own.reshape(slots, 2, 6, width), "tensor", axis=3, tiled=True
    )
    mods = (modulations[:, 0], modulations[:, 1])

    tokens = (image_tokens.astype(F32), text_tokens.astype(F32))
    outgoing = (image_cotangent.astype(F32) * alive, text_cotangent.astype(F32) * alive)

    half = size // 2
    near_kinds = [F32] + [BF16] * (half - 1)

    def scattered(grad):
        return lax.psum_scatter(grad, "dp", scatter_dimension=0, tiled=True).astype(F32)

    def row_products(pieces, weight, weight_dim, late=False):
        far = products_of(pieces[half:], weight, weight_dim, near_kinds, late)
        near = products_of(after(pieces[:half], far), weight, weight_dim, near_kinds, late)
        return [*near, *far]

    def image_sum(pieces, weight, weight_dim, late=False):
        products = row_products(pieces, weight, weight_dim, late)
        return scatter_end(*scatter_start(products, size), size)

    def text_sum(piece, weight, weight_dim, late=False):
        (product,) = products_of([piece], weight, weight_dim, [F32], late)
        return scatter_end(*text_start(product, size), size)

    def modulated(values, mod, shift, scale):
        normed, inverse = norm_rows(values)
        rows = normed * (1.0 + spread(mod[:, scale])) + spread(mod[:, shift])
        return normed, inverse, rows.astype(BF16)

    def second_back(stream, second_grad, normed, inverse):
        mod = mods[stream]
        shift_two_grad = jnp.sum(second_grad, axis=1)
        scale_two_grad = jnp.sum(second_grad * normed, axis=1)
        middle_grad = outgoing[stream] + norm_back(
            second_grad * (1.0 + spread(mod[:, 4])), normed, inverse
        )
        low = (middle_grad * spread(mod[:, 2])).astype(BF16)
        return middle_grad, low, shift_two_grad, scale_two_grad

    low_kinds = [BF16] * size

    normed_one, inverse_one, image_first = modulated(tokens[0], mods[0], 0, 1)
    text_normed_one, text_inverse_one, text_first = modulated(tokens[1], mods[1], 0, 1)
    first_pieces = gather_pieces(image_first, size)
    packed = products_of(first_pieces, weight_in[0], 0, low_kinds)
    text_packed = products_of([text_first], weight_in[1], 0, [BF16])
    down_rows = [
        (outgoing[stream] * spread(mods[stream][:, 5])).astype(BF16) for stream in range(2)
    ]
    down_have = gather_start(after(down_rows[0], first_pieces), size)
    parts = after([*packed, *text_packed], down_have)
    attended, sums = attend(parts)
    down_pieces = gather_end(after(down_have, attended), size)
    attended_parts = (attended[:-1], attended[-1:])

    branch = image_sum(attended_parts[0], weight_out[0], 1)
    middle = tokens[0] + spread(mods[0][:, 2]) * branch
    normed_two, inverse_two, image_second = modulated(middle, mods[0], 3, 4)
    up_weight, down_weight = (image_up, 0, units), (image_down, 0, units)
    near_pieces = gather_pieces(image_second, size, half)
    far_have = gather_start(image_second, size)
    near = hidden_both(near_pieces, down_pieces[:half], up_weight, down_weight)
    far_have = {k: v for k, v in far_have.items() if k >= half}
    far_pieces = gather_end(after(far_have, near), size, half)
    second_pieces = [*near_pieces, *far_pieces]
    far = hidden_both(far_pieces, down_pieces[half:], up_weight, down_weight)
    text_branch = text_sum(after(attended_parts[1][0], far_pieces), weight_out[1], 1)
    active = [*near[0], *far[0]]
    hidden_grad = after([*near[1], *far[1]], text_branch)
    kept, sent = scatter_start(row_products(hidden_grad, up_weight, 1), size)
    image_mlp_grad = weight_grad(
        after([(down_pieces, active), (second_pieces, hidden_grad)], sent)
    )
    second_grad = after(scatter_end(kept, sent, size), image_mlp_grad)
    image_mlp = scattered(after(image_mlp_grad, second_grad))
    middle_grad, low, shift_two_grad, scale_two_grad = second_back(
        0, second_grad, normed_two, inverse_two
    )
    gate_one_grad = jnp.sum(middle_grad * branch, axis=1)

    low_have = gather_start(low, size)
    two_products = row_products(after(active, low), down_weight, 1)
    two_kept, two_sent = scatter_start(two_products, size)
    text_both = after(packed_text, low)
    text_up_weight, text_down_weight = (text_both, 0, units), (text_both, units, units)
    text_middle = tokens[1] + spread(mods[1][:, 2]) * text_branch
    text_normed_two, text_inverse_two, text_second = modulated(text_middle, mods[1], 3, 4)
    text_active, text_hidden_grad = hidden_both(
        [text_second], [down_rows[1]], text_up_weight, text_down_weight
    )
    (text_product,) = products_of(text_hidden_grad, text_up_weight, 1, [F32])
    text_kept, text_sent = text_start(text_product, size)
    low_have = after(low_have, two_products, text_product)
    branch_grads = gather_end(low_have, size)

    upstreams = products_of(branch_grads, weight_out[0], 0, low_kinds)
    ring_grad = weight_grad(
        after(
            [
                ([down_rows[1]], text_active),
                ([text_second], text_hidden_grad),
                (branch_grads, attended_parts[0]),
            ],
            branch_grads,
        )
    )
    upstreams = after(upstreams, text_sent, ring_grad)
    text_ring = ring_scatter(ring_grad, group_count)
    text_hop = next(text_ring)
    first_part = attend_back(parts, size, upstreams, sums[:-1])
    branch_two = scatter_end(after(two_kept, first_part), two_sent, size)
    text_second_grad = scatter_end(after(text_kept, first_part), text_sent, size)
    first_part, branch_two, text_hop = lax.optimization_barrier((first_part, branch_two, text_hop))
    text_hop = text_ring.send(text_hop)
    text_middle_grad, text_low, text_shift_two_grad, text_scale_two_grad = second_back(
        1, text_second_grad, text_normed_two, text_inverse_two
    )
    text_gate_one_grad = jnp.sum(text_middle_grad * text_branch, axis=1)
    text_upstream = products_of([text_low], weight_out[1], 0, [BF16])
    packed_grads = attend_back(parts, 1, text_upstream, sums[-1:], first_part)
    attention_grad = weight_grad(
        [
            (first_pieces, packed_grads[:-1]),
            ([text_first], packed_grads[-1:]),
            ([text_low], attended_parts[1]),
        ]
    )
    attention_sum = scattered(attention_grad)
    packed_grads, text_active, text_hop = after(
        (packed_grads, text_active, text_hop), attention_grad
    )
    text_hop = text_ring.send(text_hop)

    def first_back(stream, first_grad, normed, inverse, middle_grad):
        mod = mods[stream]
        shift_one_grad = jnp.sum(first_grad, axis=1)
        scale_one_grad = jnp.sum(first_grad * normed, axis=1)
        input_grad = middle_grad + norm_back(
            first_grad * (1.0 + spread(mod[:, 1])), normed, inverse
        )
        return input_grad, shift_one_grad, scale_one_grad

    def finish(stream, middle, branch_two):
        result = middle + spread(mods[stream][:, 5]) * branch_two
        gate_two_grad = jnp.sum(outgoing[stream] * branch_two, axis=1)
        return (result * alive).astype(BF16), gate_two_grad

    first_grad = image_sum(packed_grads[:-1], weight_in[0], 1, True)
    text_first_grad = text_sum(packed_grads[-1], weight_in[1], 1, True)
    text_branch_two = text_sum(text_active[0], text_down_weight, 1, True)
    first_grad, text_hop = lax.optimization_barrier((first_grad, text_hop))
    for _ in range(group_count // 2 - 2):
        text_hop = text_ring.send(text_hop)
    text_mlp = text_hop
    input_grads = [None, None]
    input_grads[0], shift_one_grad, scale_one_grad = first_back(
        0, first_grad, normed_one, inverse_one, middle_grad
    )
    input_grads[1], text_shift_one_grad, text_scale_one_grad = first_back(
        1, text_first_grad, text_normed_one, text_inverse_one, text_middle_grad
    )
    outputs = [None, None]
    outputs[0], gate_two_grad = finish(0, middle, branch_two)
    outputs[1], text_gate_two_grad = finish(1, text_middle, text_branch_two)
    mod_grads = (
        jnp.stack(
            [
                shift_one_grad,
                scale_one_grad,
                gate_one_grad,
                shift_two_grad,
                scale_two_grad,
                gate_two_grad,
            ],
            axis=1,
        ),
        jnp.stack(
            [
                text_shift_one_grad,
                text_scale_one_grad,
                text_gate_one_grad,
                text_shift_two_grad,
                text_scale_two_grad,
                text_gate_two_grad,
            ],
            axis=1,
        ),
    )

    image_blocks = jnp.stack(
        [
            lax.dynamic_slice_in_dim(mod_grads[0], (tensor_rank ^ k) * width, width, 2)
            for k in range(size)
        ]
    )
    image_share = scatter_stack(image_blocks, size, "tensor")
    text_share = lax.dynamic_slice_in_dim(mod_grads[1], tensor_rank * width, width, 2)
    share_low = jnp.stack([image_share, text_share], axis=1).astype(BF16)
    share_all = gather_stack(share_low, group_count, "dp").reshape(all_slots, 2, 6, width)
    image_all = share_all[:, 0].reshape(all_slots, 6 * width)
    text_all = share_all[:, 1].reshape(all_slots, 6 * width)
    image_ada = dot(activated_own, image_all, 0, 0).reshape(share, 6, width)
    text_ada = dot(activated_own, text_all, 0, 0).reshape(share, 6, width)
    activated_part = dot(image_all, image_modulation.reshape(share, 6 * width), 1, 1) + dot(
        text_all, text_modulation.reshape(share, 6 * width), 1, 1
    )
    activated_part = sum_all(activated_part, size, "tensor").reshape(group_count, slots, share)
    activated_rows = gather_stack(activated_part, group_count, "dp")
    activated_rows = jnp.stack([activated_rows[k, k] for k in range(group_count)])
    activated_grad = jnp.concatenate(
        [
            lax.dynamic_index_in_dim(activated_rows, group_rank ^ k, 0, keepdims=False)
            for k in range(group_count)
        ],
        axis=1,
    )
    condition_gradient = jax.vjp(jax.nn.silu, cond_full)[1](activated_grad)[0]

    return (
        outputs[0],
        outputs[1],
        input_grads[0],
        input_grads[1],
        condition_gradient,
        image_ada,
        attention_sum[:, : 3 * width].reshape(share, 3, width),
        text_mlp[:, 2 * units :].T,
        image_mlp[:, units:],
        image_mlp[:, :units].T,
        text_ada,
        attention_sum[:, 3 * width : 6 * width].reshape(share, 3, width),
        attention_sum[:, 6 * width :].T,
        text_mlp[:, units : 2 * units],
        text_mlp[:, :units].T,
    )


def solution(mesh):
    image = P("dp", "tensor", None)
    text = P("dp", None, None)
    columns = P("dp", None, "tensor")
    rows = P("tensor", "dp")
    plain = P("dp", "tensor")
    weights = (columns, columns, rows, plain, rows)
    return jax.shard_map(
        functools.partial(on_device, mesh.shape["dp"], mesh.shape["tensor"]),
        mesh=mesh,
        in_specs=(image, text, P("dp", None), P("dp")) + weights + weights + (image, text),
        out_specs=(image, text, image, text, P("dp", None)) + weights + weights,
        check_vma=False,
    )
```

```python
import functools
import math

import jax
import jax.numpy as jnp
from jax import lax
from jax.experimental import pallas as pl
from jax.experimental.pallas import tpu as pltpu
from jax.sharding import PartitionSpec as P

HEAD = 64
LANES = 128
F32 = jnp.float32
BF16 = jnp.bfloat16


def norm_rows(values):
    center = values - jnp.mean(values, axis=-1, keepdims=True)
    inverse = lax.rsqrt(jnp.mean(center * center, axis=-1, keepdims=True) + 1e-06)
    return (center * inverse, inverse)


def norm_back(upstream, normed, inverse):
    first = jnp.mean(upstream, axis=-1, keepdims=True)
    second = jnp.mean(upstream * normed, axis=-1, keepdims=True)
    return inverse * (upstream - first - normed * second)


def gelu_tanh(values):
    return jax.nn.gelu(values, approximate=True)


def spread(vector):
    return vector[:, None, :]


def dot(left, right, left_dim, right_dim):
    return lax.dot_general(
        left, right, (((left_dim,), (right_dim,)), ((), ())), preferred_element_type=F32
    )


def swap(value, bit, size, axis="tensor"):
    return lax.ppermute(value, axis, [(i, i ^ bit) for i in range(size)])


def bits_of(size):
    bits = []
    bit = 1
    while bit < size:
        bits.append(bit)
        bit *= 2
    return bits


def gather_start(value, size, axis="tensor"):
    have = {0: value}
    for bit in reversed(bits_of(size)[1:]):
        have.update({k ^ bit: swap(v, bit, size, axis) for k, v in list(have.items())})
    return have


def gather_end(have, size, first=0, axis="tensor"):
    have = have | {k ^ 1: swap(v, 1, size, axis) for k, v in have.items()}
    return [have[k] for k in range(first, first + len(have))]


def gather_pieces(value, size, reach=None, axis="tensor"):
    have = {0: value}
    for bit in reversed(bits_of(reach or size)):
        have.update({k ^ bit: swap(v, bit, size, axis) for k, v in list(have.items())})
    return [have[k] for k in sorted(have)]


def gather_stack(value, size, axis):
    value = value[None]
    for bit in bits_of(size):
        value = jnp.concatenate([value, swap(value, bit, size, axis)], axis=0)
    return value


def scatter_stack(value, size, axis):
    for bit in reversed(bits_of(size)):
        value = value[:bit] + swap(value[bit:], bit, size, axis)
    return value[0]


def sum_all(value, size, axis):
    for bit in bits_of(size):
        value = value + swap(value, bit, size, axis)
    return value


def scatter_start(pieces, size):
    have = dict(enumerate(pieces))
    for bit in bits_of(size)[:-1]:
        kept = {}
        for k in sorted(have, reverse=True):
            if not k & bit:
                other = swap(have[k ^ bit].astype(BF16), bit, size)
                kept[k] = have[k].astype(F32) + other.astype(F32)
        have = kept
    kept, sent = (have[k] for k in sorted(have))
    return kept, sent.astype(BF16)


def scatter_end(kept, sent, size):
    return kept.astype(F32) + swap(sent, size // 2, size).astype(F32)


def after(values, *others):
    return lax.optimization_barrier((values, others))[0]


def ring_of(count):
    return list(range(0, count, 2)) + list(range(1, count, 2))[::-1]


def ring_member(place, count):
    place = lax.rem(place + count, count)
    return jnp.where(place < (count + 1) // 2, 2 * place, 2 * (count - 1 - place) + 1)


def ring_place(member, count):
    return jnp.where(member % 2 == 0, member // 2, count - 1 - member // 2)


def ring_step(value, way, count):
    ring = ring_of(count)
    hops = [(ring[i], ring[(i + way) % count]) for i in range(count)]
    return lax.ppermute(value, "dp", hops)


def ring_scatter(grad, count):
    wide = grad.shape[1]
    share = grad.shape[0] // count
    half = wide // 2 // LANES * LANES
    place = ring_place(lax.axis_index("dp"), count)

    def own(offset):
        row = ring_member(place + offset, count) * share
        return lax.dynamic_slice_in_dim(grad, row, share, 0).astype(F32)

    far = own(count // 2).astype(BF16)
    behind = ring_step(far[:, :half], 1, count)
    ahead = ring_step(far[:, half:], -1, count)
    behind, ahead = yield behind, ahead
    behind = jnp.pad(behind.astype(F32), ((0, 0), (0, wide - half)))
    ahead = jnp.pad(ahead.astype(F32), ((0, 0), (half, 0)))
    for hop in range(count // 2 - 1, 0, -1):
        behind = ring_step((own(hop) + behind).astype(BF16), 1, count)
        ahead = ring_step((own(-hop) + ahead).astype(BF16), -1, count)
        behind, ahead = yield behind, ahead
        behind, ahead = behind.astype(F32), ahead.astype(F32)
    yield own(0) + behind + ahead


def text_start(value, size):
    for bit in bits_of(size)[:-1]:
        if bit > 1:
            value = lax.reduce_precision(value, 8, 7)
            value = value + swap(value.astype(BF16), bit, size).astype(F32)
        else:
            value = value + swap(value, bit, size)
    value = lax.reduce_precision(value, 8, 7)
    return value, value.astype(BF16)


def lane_mask(half, shape):
    lane = lax.broadcasted_iota(jnp.int32, shape, 1)
    return (lane >= HEAD) if half else (lane < HEAD)


def pick(value, half):
    return jnp.where(lane_mask(half, value.shape), value, jnp.zeros_like(value))


def load_rows(refs, store):
    start = 0
    for ref in refs:
        rows = ref.shape[1]
        store[start : start + rows, :] = ref[0]
        start += rows


def attend_kernel(count, *refs):
    queries, keys, values = refs[:count], refs[count : 2 * count], refs[2 * count : 3 * count]
    outs = refs[3 * count : 4 * count]
    sums = refs[4 * count : 5 * count]
    key_all, value_all = refs[5 * count :]
    load_rows(keys, key_all)
    load_rows(values, value_all)
    for index in range(count):
        query = queries[index][0] * jnp.asarray(HEAD**-0.5, BF16)
        halves = []
        for half in range(2):
            scores = dot(key_all[...], pick(query, half), 1, 1)
            highest = jnp.max(scores, axis=0, keepdims=True)
            weights = jnp.exp(scores - highest)
            total = jnp.sum(weights, axis=0, keepdims=True)
            weights = (weights * (1.0 / total)).astype(BF16)
            mixed = dot(value_all[...], weights, 0, 0)
            halves.append(mixed[half * HEAD : (half + 1) * HEAD])
            sums[index][0, 0, half : half + 1, :] = highest + jnp.log(total)
        outs[index][0] = jnp.concatenate(halves, axis=0).T.astype(BF16)


def attend_back_kernel(count, asked, groups, last, *refs):
    refs = list(refs)

    def take(number):
        return [refs.pop(0) for _ in range(number)]

    keys, values = take(count), take(count)
    queries, upstreams, sums = take(asked), take(asked), take(asked)
    if last:
        before = take(2)
        query_grads = take(count - asked)
        outs = take(count)
    else:
        outs = take(asked)
        totals = take(2)
    key_all, value_all, key_grad, value_grad = refs
    load_rows(keys, key_all)
    load_rows(values, value_all)
    pair = pl.program_id(1)
    scale = jnp.asarray(HEAD**-0.5, BF16)
    for index in range(asked):
        query = queries[index][0] * scale
        upstream = upstreams[index][0]
        halves = []
        for half in range(2):
            query_half = pick(query, half)
            upstream_half = pick(upstream, half)
            scores = dot(key_all[...], query_half, 1, 1)
            weights = jnp.exp(scores - sums[index][0, 0, half : half + 1, :])
            along = dot(value_all[...], upstream_half, 1, 1)
            value_part = dot(weights.astype(BF16), upstream_half, 1, 0)
            product = weights * along
            score_grad = (product - weights * jnp.sum(product, axis=0, keepdims=True)).astype(BF16)
            key_part = dot(score_grad, query_half, 1, 0)
            if index == 0 and half == 0 and last:
                value_grad[...] = before[1][0, 0] + value_part
                key_grad[...] = before[0][0, 0] + key_part
            elif index == 0 and half == 0:
                value_grad[...] = value_part
                key_grad[...] = key_part
            else:
                value_grad[...] += value_part
                key_grad[...] += key_part
            mixed = dot(key_all[...], score_grad, 0, 0)
            halves.append(mixed[half * HEAD : (half + 1) * HEAD])
        query_grad = (jnp.concatenate(halves, axis=0).T * HEAD**-0.5).astype(BF16)
        if last:
            lanes = pl.ds(pl.multiple_of(pair * LANES, LANES), LANES)
            outs[count - asked + index][0, :, lanes] = query_grad
        else:
            outs[index][0] = query_grad
    if not last:
        totals[0][0, 0] = key_grad[...]
        totals[1][0, 0] = value_grad[...]
        return
    for index, query_grad in enumerate(query_grads):
        lanes = pl.ds(pl.multiple_of(pair * LANES, LANES), LANES)
        outs[index][0, :, lanes] = query_grad[0]
    start = 0
    for out in outs:
        rows = out.shape[1]
        for number, grad in ((1, key_grad), (2, value_grad)):
            lanes = pl.ds(pl.multiple_of((number * groups + pair) * LANES, LANES), LANES)
            out[0, :, lanes] = grad[start : start + rows, :].astype(BF16)
        start += rows


def lane_blocks(parts, offset):
    return [
        pl.BlockSpec((1, part.shape[1], LANES), lambda s, p, o=offset: (s, 0, o + p))
        for part in parts
    ]


def widen(part, copies):
    slots, rows, width = part.shape
    width = width // copies
    extra = -width % LANES
    if not extra:
        return part
    part = jnp.pad(part.reshape(slots, rows, copies, width), ((0, 0), (0, 0), (0, 0), (0, extra)))
    return part.reshape(slots, rows, copies * (width + extra))


def narrow(part, copies, width):
    slots, rows, wide = part.shape
    wide = wide // copies
    if wide == width:
        return part
    return part.reshape(slots, rows, copies, wide)[..., :width].reshape(slots, rows, -1)


def attention_cost(slots, rows, width, products):
    return pl.CostEstimate(
        flops=products * 8 * slots * rows * rows * width,
        transcendentals=slots * rows * rows * (width // HEAD),
        bytes_accessed=slots * rows * width * 2 * (4 + 3 * (products > 2)),
    )


def attend(parts):
    slots = parts[0].shape[0]
    width = parts[0].shape[2] // 3
    parts = [widen(part, 3) for part in parts]
    count = len(parts)
    wide = parts[0].shape[2] // 3
    groups = wide // LANES
    total = sum(part.shape[1] for part in parts)
    outs = pl.pallas_call(
        functools.partial(attend_kernel, count),
        grid=(slots, groups),
        in_specs=lane_blocks(parts, 0) + lane_blocks(parts, groups) + lane_blocks(parts, 2 * groups),
        out_specs=lane_blocks(parts, 0)
        + [
            pl.BlockSpec((1, 1, 2, part.shape[1]), lambda s, p: (s, p, 0, 0)) for part in parts
        ],
        out_shape=[jax.ShapeDtypeStruct((slots, part.shape[1], wide), BF16) for part in parts]
        + [jax.ShapeDtypeStruct((slots, groups, 2, part.shape[1]), F32) for part in parts],
        scratch_shapes=[pltpu.VMEM((total, LANES), BF16)] * 2,
        compiler_params=pltpu.CompilerParams(vmem_limit_bytes=48 * 1024 * 1024),
        cost_estimate=attention_cost(slots, total, wide, 2),
        name="attend",
    )(*parts, *parts, *parts)
    return [narrow(out, 1, width) for out in outs[:count]], outs[count:]


def attend_back(parts, asked, upstreams, sums, before=None):
    slots = parts[0].shape[0]
    width = parts[0].shape[2] // 3
    parts = [widen(part, 3) for part in parts]
    upstreams = [widen(part, 1) for part in upstreams]
    last = before is not None
    count = len(parts)
    queries = parts[-asked:] if last else parts[:asked]
    wide = parts[0].shape[2] // 3
    groups = wide // LANES
    total = sum(part.shape[1] for part in parts)
    whole = pl.BlockSpec((1, 1, total, LANES), lambda s, p: (s, p, 0, 0))
    ins = lane_blocks(parts, groups) + lane_blocks(parts, 2 * groups) + lane_blocks(queries, 0)
    ins += lane_blocks(upstreams, 0)
    ins += [pl.BlockSpec((1, 1, 2, part.shape[1]), lambda s, p: (s, p, 0, 0)) for part in queries]
    operands = [*parts, *parts, *queries, *upstreams, *sums]
    if last:
        query_grads, totals = before
        ins += [whole, whole] + lane_blocks(query_grads, 0)
        operands += [*totals, *query_grads]
        out_specs = [
            pl.BlockSpec((1, part.shape[1], 3 * wide), lambda s, p: (s, 0, 0)) for part in parts
        ]
        out_shape = [
            jax.ShapeDtypeStruct((slots, part.shape[1], 3 * wide), BF16) for part in parts
        ]
    else:
        out_specs = lane_blocks(queries, 0) + [whole, whole]
        out_shape = [
            jax.ShapeDtypeStruct((slots, part.shape[1], wide), BF16) for part in queries
        ] + [jax.ShapeDtypeStruct((slots, groups, total, LANES), F32)] * 2
    outs = pl.pallas_call(
        functools.partial(attend_back_kernel, count, asked, groups, last),
        grid=(slots, groups),
        in_specs=ins,
        out_specs=out_specs,
        out_shape=out_shape,
        scratch_shapes=[pltpu.VMEM((total, LANES), BF16)] * 2 + [pltpu.VMEM((total, LANES), F32)] * 2,
        compiler_params=pltpu.CompilerParams(vmem_limit_bytes=48 * 1024 * 1024),
        cost_estimate=attention_cost(slots, total, wide, 2 if last else 5),
        name="attend_back",
    )(*operands)
    if last:
        return [narrow(out, 3, width) for out in outs]
    return outs[:asked], outs[asked:]


def rows_kernel(count, *refs):
    lefts, rights, out = refs[:count], refs[count : 2 * count], refs[-1]
    total = None
    for left, right in zip(lefts, rights):
        for slot in range(left.shape[0]):
            part = dot(left[slot], right[slot], 0, 0)
            total = part if total is None else total + part
    out[...] = total.astype(BF16)


def weight_grad(pairs):
    joined = None
    rows = pairs[0][0][0].shape[-1]
    wide = sum(rights[0].shape[-1] for _, rights in pairs)
    start = 0
    for lefts, rights in pairs:
        part = rights[0].shape[-1]
        if part % LANES or start % part:
            return jnp.concatenate([plain_grad(*pair) for pair in pairs], axis=1)
        count = len(lefts)
        step = 256
        ins = [
            pl.BlockSpec((left.shape[0], left.shape[1], step), lambda i: (0, 0, i))
            for left in lefts
        ] + [
            pl.BlockSpec(right.shape, lambda i: (0, 0, 0), pipeline_mode=pl.Buffered(1))
            for right in rights
        ]
        operands = (*lefts, *rights)
        if joined is not None:
            ins.append(pl.BlockSpec(memory_space=pl.ANY))
            operands += (joined,)
        joined = pl.pallas_call(
            functools.partial(rows_kernel, count),
            grid=(rows // step,),
            in_specs=ins,
            out_specs=pl.BlockSpec((step, part), lambda i, c=start // part: (i, c)),
            out_shape=jax.ShapeDtypeStruct((rows, wide), BF16),
            input_output_aliases={} if joined is None else {2 * count: 0},
            compiler_params=pltpu.CompilerParams(vmem_limit_bytes=48 * 1024 * 1024),
            cost_estimate=pl.CostEstimate(flops=0, transcendentals=0, bytes_accessed=1024),
            name="weight_grad",
        )(*operands)
        start += part
    return joined


NO_COST = pl.CostEstimate(flops=0, transcendentals=0, bytes_accessed=1024)
LIMIT = pltpu.CompilerParams(vmem_limit_bytes=48 * 1024 * 1024)


def tile_of(wide, start, most):
    return max(t for t in range(LANES, most + 1, LANES) if wide % t == 0 and start % t == 0)


def fits(weight):
    _, start, wide = weight
    return wide % LANES == 0 and start % LANES == 0


def cut(weight):
    array, start, wide = weight
    return array[:, start : start + wide]


def row_blocks(ref):
    slots, rows, columns = ref.shape
    if rows % 16 == 0:
        return [(slice(None), ref[...].reshape(slots * rows, columns))]
    return [(slice(slot, slot + 1), ref[slot]) for slot in range(slots)]


def store_rows(ref, place, value):
    slots = ref.shape[0] if place == slice(None) else 1
    ref[place] = value.reshape(slots, -1, value.shape[-1]).astype(ref.dtype)


def product_kernel(count, weight_dim, *refs):
    pieces, weight, outs = refs[:count], refs[count], refs[count + 1 :]
    for piece, out in zip(pieces, outs):
        for place, rows in row_blocks(piece):
            store_rows(out, place, dot(rows, weight[...], 1, weight_dim))


def whole_block(array):
    return pl.BlockSpec(array.shape, lambda j: (0, 0, 0), pipeline_mode=pl.Buffered(1))


def products_of(pieces, weight, weight_dim, kinds, late=False):
    array, start, wide = weight
    if not fits(weight) or (weight_dim and start % wide):
        return [
            dot(piece, cut(weight), 2, weight_dim).astype(kind)
            for piece, kind in zip(pieces, kinds)
        ]
    count = len(pieces)
    slots, _, depth = pieces[0].shape
    if weight_dim:
        result = array.shape[0]
        tile = tile_of(result, 0, 768)
        block = pl.BlockSpec((tile, wide), lambda j: (j, start // wide))
    else:
        result = wide
        tile = tile_of(wide, start, 768)
        block = pl.BlockSpec((depth, tile), lambda j: (0, start // tile + j))
    rows = slots * sum(piece.shape[1] for piece in pieces)
    cost = pl.CostEstimate(
        flops=4 * rows * depth * result, transcendentals=0, bytes_accessed=4 * rows * result
    )
    return pl.pallas_call(
        functools.partial(product_kernel, count, weight_dim),
        grid=(result // tile,),
        in_specs=[whole_block(piece) for piece in pieces] + [block],
        out_specs=[
            pl.BlockSpec((slots, piece.shape[1], tile), lambda j: (0, 0, j)) for piece in pieces
        ],
        out_shape=[
            jax.ShapeDtypeStruct((slots, piece.shape[1], result), kind)
            for piece, kind in zip(pieces, kinds)
        ],
        compiler_params=LIMIT,
        cost_estimate=cost if late else NO_COST,
        name="products",
    )(*pieces, array)


def hidden_kernel(count, *refs):
    pieces, downs, up, down = refs[:count], refs[count : 2 * count], refs[2 * count], refs[2 * count + 1]
    actives, grads = refs[2 * count + 2 : 3 * count + 2], refs[3 * count + 2 :]
    for piece, upstream, active, grad in zip(pieces, downs, actives, grads):
        for (place, rows), (_, above) in zip(row_blocks(piece), row_blocks(upstream)):
            hidden = dot(rows, up[...], 1, 0)
            active_grad = dot(above, down[...], 1, 0)
            square = hidden * hidden
            scale = (2 / math.pi) ** 0.5
            bend = jnp.tanh(hidden * (scale + scale * 0.044715 * square))
            half = 0.5 + 0.5 * bend
            slope = half + hidden * (0.5 - 0.5 * bend * bend) * (
                scale + scale * 0.134145 * square
            )
            store_rows(active, place, hidden * half)
            store_rows(grad, place, active_grad * slope)


def hidden_both(pieces, downs, up, down):
    count = len(pieces)
    if not (fits(up) and fits(down)):
        hidden = [dot(piece, cut(up), 2, 0) for piece in pieces]
        active_grad = [dot(piece, cut(down), 2, 0) for piece in downs]
        return (
            [gelu_tanh(value).astype(BF16) for value in hidden],
            [
                jax.vjp(gelu_tanh, value)[1](grad)[0].astype(BF16)
                for value, grad in zip(hidden, active_grad)
            ],
        )
    slots, _, depth = pieces[0].shape
    wide = up[2]
    tile = tile_of(wide, math.gcd(up[1], down[1]), 512)
    outs = pl.pallas_call(
        functools.partial(hidden_kernel, count),
        grid=(wide // tile,),
        in_specs=[whole_block(piece) for piece in (*pieces, *downs)]
        + [
            pl.BlockSpec((depth, tile), lambda j, o=block[1] // tile: (0, o + j))
            for block in (up, down)
        ],
        out_specs=[
            pl.BlockSpec((slots, piece.shape[1], tile), lambda j: (0, 0, j)) for piece in pieces
        ]
        * 2,
        out_shape=[
            jax.ShapeDtypeStruct((slots, piece.shape[1], wide), BF16) for piece in pieces
        ]
        * 2,
        compiler_params=LIMIT,
        cost_estimate=NO_COST,
        name="hidden_both",
    )(*pieces, *downs, up[0], down[0])
    return outs[:count], outs[count:]


def plain_grad(lefts, rights):
    left = jnp.concatenate([v.reshape(-1, v.shape[-1]) for v in lefts], axis=0)
    right = jnp.concatenate([v.reshape(-1, v.shape[-1]) for v in rights], axis=0)
    return dot(left, right, 0, 0).astype(BF16)


def on_device(
    group_count,
    tensor_size,
    image_tokens,
    text_tokens,
    condition,
    group_size,
    image_modulation,
    image_attention_in,
    image_attention_out,
    image_hidden_in,
    image_hidden_out,
    text_modulation,
    text_attention_in,
    text_attention_out,
    text_hidden_in,
    text_hidden_out,
    image_cotangent,
    text_cotangent,
):
    size = tensor_size
    slots, image_length, model = image_tokens.shape
    text_length = text_tokens.shape[1]
    share, _, width = image_attention_in.shape
    units = image_hidden_in.shape[1]
    tensor_rank = lax.axis_index("tensor")
    group_rank = lax.axis_index("dp")

    def gathered(*blocks):
        joined = blocks[0] if len(blocks) == 1 else jnp.concatenate(blocks, axis=1)
        return lax.all_gather(joined, "dp", axis=0, tiled=True)

    packed_first = gathered(
        image_attention_in.reshape(share, 3 * width),
        text_attention_in.reshape(share, 3 * width),
        image_attention_out.T,
        text_attention_out.T,
    )
    packed_image = gathered(image_hidden_in, image_hidden_out.T)
    packed_text = gathered(text_hidden_in, text_hidden_out.T)
    weight_in = ((packed_first, 0, 3 * width), (packed_first, 3 * width, 3 * width))
    weight_out = ((packed_first, 6 * width, width), (packed_first, 7 * width, width))

    alive = (jnp.arange(slots) < group_size[0]).astype(F32)[:, None, None]
    cond_full = condition.astype(F32)
    activated_low = jax.nn.silu(cond_full).astype(BF16)
    activated_all = gather_stack(activated_low, group_count, "dp").reshape(-1, model)
    activated_own = lax.dynamic_slice_in_dim(activated_all, group_rank * share, share, 1)
    all_slots = activated_own.shape[0]
    mod_parts = jnp.concatenate(
        [
            dot(activated_own, image_modulation.reshape(share, 6 * width), 1, 0),
            dot(activated_own, text_modulation.reshape(share, 6 * width), 1, 0),
        ],
        axis=1,
    ).reshape(group_count, slots, 12 * width)
    mod_own = scatter_stack(mod_parts, group_count, "dp")
    modulations = lax.all_gather(
        mod_own.reshape(slots, 2, 6, width), "tensor", axis=3, tiled=True
    )
    mods = (modulations[:, 0], modulations[:, 1])

    tokens = (image_tokens.astype(F32), text_tokens.astype(F32))
    outgoing = (image_cotangent.astype(F32) * alive, text_cotangent.astype(F32) * alive)

    half = size // 2
    near_kinds = [F32] + [BF16] * (half - 1)

    def scattered(grad):
        return lax.psum_scatter(grad, "dp", scatter_dimension=0, tiled=True).astype(F32)

    def row_products(pieces, weight, weight_dim, late=False):
        far = products_of(pieces[half:], weight, weight_dim, near_kinds, late)
        near = products_of(after(pieces[:half], far), weight, weight_dim, near_kinds, late)
        return [*near, *far]

    def image_sum(pieces, weight, weight_dim, late=False):
        products = row_products(pieces, weight, weight_dim, late)
        return scatter_end(*scatter_start(products, size), size)

    def text_sum(piece, weight, weight_dim, late=False):
        (product,) = products_of([piece], weight, weight_dim, [F32], late)
        return scatter_end(*text_start(product, size), size)

    def modulated(values, mod, shift, scale):
        normed, inverse = norm_rows(values)
        rows = normed * (1.0 + spread(mod[:, scale])) + spread(mod[:, shift])
        return normed, inverse, rows.astype(BF16)

    def second_back(stream, second_grad, normed, inverse):
        mod = mods[stream]
        shift_two_grad = jnp.sum(second_grad, axis=1)
        scale_two_grad = jnp.sum(second_grad * normed, axis=1)
        middle_grad = outgoing[stream] + norm_back(
            second_grad * (1.0 + spread(mod[:, 4])), normed, inverse
        )
        low = (middle_grad * spread(mod[:, 2])).astype(BF16)
        return middle_grad, low, shift_two_grad, scale_two_grad

    low_kinds = [BF16] * size

    normed_one, inverse_one, image_first = modulated(tokens[0], mods[0], 0, 1)
    text_normed_one, text_inverse_one, text_first = modulated(tokens[1], mods[1], 0, 1)
    first_pieces = gather_pieces(image_first, size)
    packed = products_of(first_pieces, weight_in[0], 0, low_kinds)
    text_packed = products_of([text_first], weight_in[1], 0, [BF16])
    down_rows = [
        (outgoing[stream] * spread(mods[stream][:, 5])).astype(BF16) for stream in range(2)
    ]
    down_have = gather_start(after(down_rows[0], first_pieces), size)
    parts = after([*packed, *text_packed], down_have)
    attended, sums = attend(parts)
    down_pieces = gather_end(after(down_have, attended), size)
    attended_parts = (attended[:-1], attended[-1:])

    branch = image_sum(attended_parts[0], weight_out[0], 1)
    middle = tokens[0] + spread(mods[0][:, 2]) * branch
    normed_two, inverse_two, image_second = modulated(middle, mods[0], 3, 4)
    up_weight, down_weight = (packed_image, 0, units), (packed_image, units, units)
    near_pieces = gather_pieces(image_second, size, half)
    far_have = gather_start(image_second, size)
    near = hidden_both(near_pieces, down_pieces[:half], up_weight, down_weight)
    far_have = {k: v for k, v in far_have.items() if k >= half}
    far_pieces = gather_end(after(far_have, near), size, half)
    second_pieces = [*near_pieces, *far_pieces]
    far = hidden_both(far_pieces, down_pieces[half:], up_weight, down_weight)
    text_branch = text_sum(after(attended_parts[1][0], far_pieces), weight_out[1], 1)
    active = [*near[0], *far[0]]
    hidden_grad = after([*near[1], *far[1]], text_branch)
    kept, sent = scatter_start(row_products(hidden_grad, up_weight, 1), size)
    image_mlp_grad = weight_grad(
        after([(down_pieces, active), (second_pieces, hidden_grad)], sent)
    )
    second_grad = after(scatter_end(kept, sent, size), image_mlp_grad)
    image_mlp = scattered(after(image_mlp_grad, second_grad))
    middle_grad, low, shift_two_grad, scale_two_grad = second_back(
        0, second_grad, normed_two, inverse_two
    )
    gate_one_grad = jnp.sum(middle_grad * branch, axis=1)

    low_have = gather_start(low, size)
    two_products = row_products(after(active, low), down_weight, 1)
    two_kept, two_sent = scatter_start(two_products, size)
    low_have = after(low_have, two_products)
    branch_grads = gather_end(low_have, size)

    text_both = after(packed_text, low_have)
    text_up_weight, text_down_weight = (text_both, 0, units), (text_both, units, units)
    text_middle = tokens[1] + spread(mods[1][:, 2]) * text_branch
    text_normed_two, text_inverse_two, text_second = modulated(text_middle, mods[1], 3, 4)
    text_active, text_hidden_grad = hidden_both(
        [text_second], [down_rows[1]], text_up_weight, text_down_weight
    )
    (text_product,) = products_of(text_hidden_grad, text_up_weight, 1, [F32])
    text_kept, text_sent = text_start(text_product, size)
    text_mlp_grad = weight_grad(
        after([([down_rows[1]], text_active), ([text_second], text_hidden_grad)], text_product)
    )
    (text_two,) = products_of(after(text_active, text_product), text_down_weight, 1, [F32])

    upstreams = products_of(branch_grads, weight_out[0], 0, low_kinds)
    upstreams = after(upstreams, text_sent, text_mlp_grad, text_two)
    text_ring = ring_scatter(after(text_mlp_grad, branch_grads), group_count)
    text_hop = next(text_ring)
    first_part = attend_back(parts, size, upstreams, sums[:-1])
    branch_two = scatter_end(after(two_kept, first_part), two_sent, size)
    text_second_grad = scatter_end(after(text_kept, first_part), text_sent, size)
    first_part, branch_two, text_hop = lax.optimization_barrier((first_part, branch_two, text_hop))
    text_hop = text_ring.send(text_hop)
    text_middle_grad, text_low, text_shift_two_grad, text_scale_two_grad = second_back(
        1, text_second_grad, text_normed_two, text_inverse_two
    )
    text_gate_one_grad = jnp.sum(text_middle_grad * text_branch, axis=1)
    text_upstream = products_of([text_low], weight_out[1], 0, [BF16])
    packed_grads = attend_back(parts, 1, text_upstream, sums[-1:], first_part)
    attention_grad = weight_grad(
        [
            (first_pieces, packed_grads[:-1]),
            ([text_first], packed_grads[-1:]),
            (branch_grads, attended_parts[0]),
            ([text_low], attended_parts[1]),
        ]
    )
    attention_sum = scattered(attention_grad)
    packed_grads, text_hop, text_two = after((packed_grads, text_hop, text_two), attention_grad)
    text_hop = text_ring.send(text_hop)

    def first_back(stream, first_grad, normed, inverse, middle_grad):
        mod = mods[stream]
        shift_one_grad = jnp.sum(first_grad, axis=1)
        scale_one_grad = jnp.sum(first_grad * normed, axis=1)
        input_grad = middle_grad + norm_back(
            first_grad * (1.0 + spread(mod[:, 1])), normed, inverse
        )
        return input_grad, shift_one_grad, scale_one_grad

    def finish(stream, middle, branch_two):
        result = middle + spread(mods[stream][:, 5]) * branch_two
        gate_two_grad = jnp.sum(outgoing[stream] * branch_two, axis=1)
        return (result * alive).astype(BF16), gate_two_grad

    first_grad = image_sum(packed_grads[:-1], weight_in[0], 1, True)
    text_first_grad = text_sum(packed_grads[-1], weight_in[1], 1, True)
    text_branch_two = scatter_end(*text_start(text_two, size), size)
    text_first_grad, text_hop = lax.optimization_barrier((text_first_grad, text_hop))
    for _ in range(group_count // 2 - 3):
        text_hop = text_ring.send(text_hop)
    first_grad, text_hop = lax.optimization_barrier((first_grad, text_hop))
    text_mlp = text_ring.send(text_hop)
    input_grads = [None, None]
    input_grads[0], shift_one_grad, scale_one_grad = first_back(
        0, first_grad, normed_one, inverse_one, middle_grad
    )
    input_grads[1], text_shift_one_grad, text_scale_one_grad = first_back(
        1, text_first_grad, text_normed_one, text_inverse_one, text_middle_grad
    )
    outputs = [None, None]
    outputs[0], gate_two_grad = finish(0, middle, branch_two)
    outputs[1], text_gate_two_grad = finish(1, text_middle, text_branch_two)
    mod_grads = (
        jnp.stack(
            [
                shift_one_grad,
                scale_one_grad,
                gate_one_grad,
                shift_two_grad,
                scale_two_grad,
                gate_two_grad,
            ],
            axis=1,
        ),
        jnp.stack(
            [
                text_shift_one_grad,
                text_scale_one_grad,
                text_gate_one_grad,
                text_shift_two_grad,
                text_scale_two_grad,
                text_gate_two_grad,
            ],
            axis=1,
        ),
    )

    image_blocks = jnp.stack(
        [
            lax.dynamic_slice_in_dim(mod_grads[0], (tensor_rank ^ k) * width, width, 2)
            for k in range(size)
        ]
    )
    image_share = scatter_stack(image_blocks, size, "tensor")
    text_share = lax.dynamic_slice_in_dim(mod_grads[1], tensor_rank * width, width, 2)
    share_low = jnp.stack([image_share, text_share], axis=1).astype(BF16)
    share_all = gather_stack(share_low, group_count, "dp").reshape(all_slots, 2, 6, width)
    image_all = share_all[:, 0].reshape(all_slots, 6 * width)
    text_all = share_all[:, 1].reshape(all_slots, 6 * width)
    image_ada = dot(activated_own, image_all, 0, 0).reshape(share, 6, width)
    text_ada = dot(activated_own, text_all, 0, 0).reshape(share, 6, width)
    activated_part = dot(image_all, image_modulation.reshape(share, 6 * width), 1, 1) + dot(
        text_all, text_modulation.reshape(share, 6 * width), 1, 1
    )
    activated_part = sum_all(activated_part, size, "tensor").reshape(group_count, slots, share)
    activated_rows = gather_stack(activated_part, group_count, "dp")
    activated_rows = jnp.stack([activated_rows[k, k] for k in range(group_count)])
    activated_grad = jnp.concatenate(
        [
            lax.dynamic_index_in_dim(activated_rows, group_rank ^ k, 0, keepdims=False)
            for k in range(group_count)
        ],
        axis=1,
    )
    condition_gradient = jax.vjp(jax.nn.silu, cond_full)[1](activated_grad)[0]

    return (
        outputs[0],
        outputs[1],
        input_grads[0],
        input_grads[1],
        condition_gradient,
        image_ada,
        attention_sum[:, : 3 * width].reshape(share, 3, width),
        attention_sum[:, 6 * width : 7 * width].T,
        image_mlp[:, units:],
        image_mlp[:, :units].T,
        text_ada,
        attention_sum[:, 3 * width : 6 * width].reshape(share, 3, width),
        attention_sum[:, 7 * width :].T,
        text_mlp[:, units:],
        text_mlp[:, :units].T,
    )


def solution(mesh):
    image = P("dp", "tensor", None)
    text = P("dp", None, None)
    columns = P("dp", None, "tensor")
    rows = P("tensor", "dp")
    plain = P("dp", "tensor")
    weights = (columns, columns, rows, plain, rows)
    return jax.shard_map(
        functools.partial(on_device, mesh.shape["dp"], mesh.shape["tensor"]),
        mesh=mesh,
        in_specs=(image, text, P("dp", None), P("dp")) + weights + weights + (image, text),
        out_specs=(image, text, image, text, P("dp", None)) + weights + weights,
        check_vma=False,
    )
```

```python
import functools
import math

import jax
import jax.numpy as jnp
from jax import lax
from jax.experimental import pallas as pl
from jax.experimental.pallas import tpu as pltpu
from jax.sharding import PartitionSpec as P

HEAD = 64
LANES = 128
F32 = jnp.float32
BF16 = jnp.bfloat16


def norm_rows(values):
    center = values - jnp.mean(values, axis=-1, keepdims=True)
    inverse = lax.rsqrt(jnp.mean(center * center, axis=-1, keepdims=True) + 1e-06)
    return (center * inverse, inverse)


def norm_back(upstream, normed, inverse):
    first = jnp.mean(upstream, axis=-1, keepdims=True)
    second = jnp.mean(upstream * normed, axis=-1, keepdims=True)
    return inverse * (upstream - first - normed * second)


def gelu_tanh(values):
    return jax.nn.gelu(values, approximate=True)


def spread(vector):
    return vector[:, None, :]


def dot(left, right, left_dim, right_dim):
    return lax.dot_general(
        left, right, (((left_dim,), (right_dim,)), ((), ())), preferred_element_type=F32
    )


def swap(value, bit, size, axis="tensor"):
    return lax.ppermute(value, axis, [(i, i ^ bit) for i in range(size)])


def bits_of(size):
    bits = []
    bit = 1
    while bit < size:
        bits.append(bit)
        bit *= 2
    return bits


def gather_start(value, size, axis="tensor"):
    have = {0: value}
    for bit in reversed(bits_of(size)[1:]):
        have.update({k ^ bit: swap(v, bit, size, axis) for k, v in list(have.items())})
    return have


def gather_end(have, size, first=0, axis="tensor"):
    have = have | {k ^ 1: swap(v, 1, size, axis) for k, v in have.items()}
    return [have[k] for k in range(first, first + len(have))]


def gather_pieces(value, size, reach=None, axis="tensor"):
    have = {0: value}
    for bit in reversed(bits_of(reach or size)):
        have.update({k ^ bit: swap(v, bit, size, axis) for k, v in list(have.items())})
    return [have[k] for k in sorted(have)]


def gather_stack(value, size, axis):
    value = value[None]
    for bit in bits_of(size):
        value = jnp.concatenate([value, swap(value, bit, size, axis)], axis=0)
    return value


def scatter_stack(value, size, axis):
    for bit in reversed(bits_of(size)):
        value = value[:bit] + swap(value[bit:], bit, size, axis)
    return value[0]


def sum_all(value, size, axis):
    for bit in bits_of(size):
        value = value + swap(value, bit, size, axis)
    return value


def scatter_start(pieces, size):
    have = dict(enumerate(pieces))
    for bit in bits_of(size)[:-1]:
        kept = {}
        for k in sorted(have, reverse=True):
            if not k & bit:
                other = swap(have[k ^ bit].astype(BF16), bit, size)
                kept[k] = have[k].astype(F32) + other.astype(F32)
        have = kept
    kept, sent = (have[k] for k in sorted(have))
    return kept, sent.astype(BF16)


def scatter_end(kept, sent, size):
    return kept.astype(F32) + swap(sent, size // 2, size).astype(F32)


def after(values, *others):
    return lax.optimization_barrier((values, others))[0]


def ring_of(count):
    return list(range(0, count, 2)) + list(range(1, count, 2))[::-1]


def ring_member(place, count):
    place = lax.rem(place + count, count)
    return jnp.where(place < (count + 1) // 2, 2 * place, 2 * (count - 1 - place) + 1)


def ring_place(member, count):
    return jnp.where(member % 2 == 0, member // 2, count - 1 - member // 2)


def ring_step(value, way, count):
    ring = ring_of(count)
    hops = [(ring[i], ring[(i + way) % count]) for i in range(count)]
    return lax.ppermute(value, "dp", hops)


def ring_scatter(grad, count):
    wide = grad.shape[1]
    share = grad.shape[0] // count
    half = wide // 2 // LANES * LANES
    place = ring_place(lax.axis_index("dp"), count)

    def own(offset):
        row = ring_member(place + offset, count) * share
        return lax.dynamic_slice_in_dim(grad, row, share, 0).astype(F32)

    far = own(count // 2).astype(BF16)
    behind = ring_step(far[:, :half], 1, count)
    ahead = ring_step(far[:, half:], -1, count)
    behind, ahead = yield behind, ahead
    behind = jnp.pad(behind.astype(F32), ((0, 0), (0, wide - half)))
    ahead = jnp.pad(ahead.astype(F32), ((0, 0), (half, 0)))
    for hop in range(count // 2 - 1, 0, -1):
        behind = ring_step((own(hop) + behind).astype(BF16), 1, count)
        ahead = ring_step((own(-hop) + ahead).astype(BF16), -1, count)
        behind, ahead = yield behind, ahead
        behind, ahead = behind.astype(F32), ahead.astype(F32)
    yield own(0) + behind + ahead


def text_start(value, size):
    for bit in bits_of(size)[:-1]:
        if bit > 1:
            value = lax.reduce_precision(value, 8, 7)
            value = value + swap(value.astype(BF16), bit, size).astype(F32)
        else:
            value = value + swap(value, bit, size)
    value = lax.reduce_precision(value, 8, 7)
    return value, value.astype(BF16)


def lane_mask(half, shape):
    lane = lax.broadcasted_iota(jnp.int32, shape, 1)
    return (lane >= HEAD) if half else (lane < HEAD)


def pick(value, half):
    return jnp.where(lane_mask(half, value.shape), value, jnp.zeros_like(value))


def load_rows(refs, store):
    start = 0
    for ref in refs:
        rows = ref.shape[1]
        store[start : start + rows, :] = ref[0]
        start += rows


def attend_kernel(count, *refs):
    queries, keys, values = refs[:count], refs[count : 2 * count], refs[2 * count : 3 * count]
    outs = refs[3 * count : 4 * count]
    sums = refs[4 * count : 5 * count]
    key_all, value_all = refs[5 * count :]
    load_rows(keys, key_all)
    load_rows(values, value_all)
    for index in range(count):
        query = queries[index][0] * jnp.asarray(HEAD**-0.5, BF16)
        halves = []
        for half in range(2):
            scores = dot(key_all[...], pick(query, half), 1, 1)
            highest = jnp.max(scores, axis=0, keepdims=True)
            weights = jnp.exp(scores - highest)
            total = jnp.sum(weights, axis=0, keepdims=True)
            weights = (weights * (1.0 / total)).astype(BF16)
            mixed = dot(value_all[...], weights, 0, 0)
            halves.append(mixed[half * HEAD : (half + 1) * HEAD])
            sums[index][0, 0, half : half + 1, :] = highest + jnp.log(total)
        outs[index][0] = jnp.concatenate(halves, axis=0).T.astype(BF16)


def attend_back_kernel(count, asked, groups, last, *refs):
    refs = list(refs)

    def take(number):
        return [refs.pop(0) for _ in range(number)]

    keys, values = take(count), take(count)
    queries, upstreams, sums = take(asked), take(asked), take(asked)
    if last:
        before = take(2)
        query_grads = take(count - asked)
        outs = take(count)
    else:
        outs = take(asked)
        totals = take(2)
    key_all, value_all, key_grad, value_grad = refs
    load_rows(keys, key_all)
    load_rows(values, value_all)
    pair = pl.program_id(1)
    scale = jnp.asarray(HEAD**-0.5, BF16)
    for index in range(asked):
        query = queries[index][0] * scale
        upstream = upstreams[index][0]
        halves = []
        for half in range(2):
            query_half = pick(query, half)
            upstream_half = pick(upstream, half)
            scores = dot(key_all[...], query_half, 1, 1)
            weights = jnp.exp(scores - sums[index][0, 0, half : half + 1, :])
            along = dot(value_all[...], upstream_half, 1, 1)
            value_part = dot(weights.astype(BF16), upstream_half, 1, 0)
            product = weights * along
            score_grad = (product - weights * jnp.sum(product, axis=0, keepdims=True)).astype(BF16)
            key_part = dot(score_grad, query_half, 1, 0)
            if index == 0 and half == 0 and last:
                value_grad[...] = before[1][0, 0] + value_part
                key_grad[...] = before[0][0, 0] + key_part
            elif index == 0 and half == 0:
                value_grad[...] = value_part
                key_grad[...] = key_part
            else:
                value_grad[...] += value_part
                key_grad[...] += key_part
            mixed = dot(key_all[...], score_grad, 0, 0)
            halves.append(mixed[half * HEAD : (half + 1) * HEAD])
        query_grad = (jnp.concatenate(halves, axis=0).T * HEAD**-0.5).astype(BF16)
        if last:
            lanes = pl.ds(pl.multiple_of(pair * LANES, LANES), LANES)
            outs[count - asked + index][0, :, lanes] = query_grad
        else:
            outs[index][0] = query_grad
    if not last:
        totals[0][0, 0] = key_grad[...]
        totals[1][0, 0] = value_grad[...]
        return
    for index, query_grad in enumerate(query_grads):
        lanes = pl.ds(pl.multiple_of(pair * LANES, LANES), LANES)
        outs[index][0, :, lanes] = query_grad[0]
    start = 0
    for out in outs:
        rows = out.shape[1]
        for number, grad in ((1, key_grad), (2, value_grad)):
            lanes = pl.ds(pl.multiple_of((number * groups + pair) * LANES, LANES), LANES)
            out[0, :, lanes] = grad[start : start + rows, :].astype(BF16)
        start += rows


def lane_blocks(parts, offset):
    return [
        pl.BlockSpec((1, part.shape[1], LANES), lambda s, p, o=offset: (s, 0, o + p))
        for part in parts
    ]


def widen(part, copies):
    slots, rows, width = part.shape
    width = width // copies
    extra = -width % LANES
    if not extra:
        return part
    part = jnp.pad(part.reshape(slots, rows, copies, width), ((0, 0), (0, 0), (0, 0), (0, extra)))
    return part.reshape(slots, rows, copies * (width + extra))


def narrow(part, copies, width):
    slots, rows, wide = part.shape
    wide = wide // copies
    if wide == width:
        return part
    return part.reshape(slots, rows, copies, wide)[..., :width].reshape(slots, rows, -1)


def attention_cost(slots, rows, width, products):
    return pl.CostEstimate(
        flops=products * 8 * slots * rows * rows * width,
        transcendentals=slots * rows * rows * (width // HEAD),
        bytes_accessed=slots * rows * width * 2 * (4 + 3 * (products > 2)),
    )


def attend(parts):
    slots = parts[0].shape[0]
    width = parts[0].shape[2] // 3
    parts = [widen(part, 3) for part in parts]
    count = len(parts)
    wide = parts[0].shape[2] // 3
    groups = wide // LANES
    total = sum(part.shape[1] for part in parts)
    outs = pl.pallas_call(
        functools.partial(attend_kernel, count),
        grid=(slots, groups),
        in_specs=lane_blocks(parts, 0) + lane_blocks(parts, groups) + lane_blocks(parts, 2 * groups),
        out_specs=lane_blocks(parts, 0)
        + [
            pl.BlockSpec((1, 1, 2, part.shape[1]), lambda s, p: (s, p, 0, 0)) for part in parts
        ],
        out_shape=[jax.ShapeDtypeStruct((slots, part.shape[1], wide), BF16) for part in parts]
        + [jax.ShapeDtypeStruct((slots, groups, 2, part.shape[1]), F32) for part in parts],
        scratch_shapes=[pltpu.VMEM((total, LANES), BF16)] * 2,
        compiler_params=pltpu.CompilerParams(vmem_limit_bytes=48 * 1024 * 1024),
        cost_estimate=attention_cost(slots, total, wide, 2),
        name="attend",
    )(*parts, *parts, *parts)
    return [narrow(out, 1, width) for out in outs[:count]], outs[count:]


def attend_back(parts, asked, upstreams, sums, before=None):
    slots = parts[0].shape[0]
    width = parts[0].shape[2] // 3
    parts = [widen(part, 3) for part in parts]
    upstreams = [widen(part, 1) for part in upstreams]
    last = before is not None
    count = len(parts)
    queries = parts[-asked:] if last else parts[:asked]
    wide = parts[0].shape[2] // 3
    groups = wide // LANES
    total = sum(part.shape[1] for part in parts)
    whole = pl.BlockSpec((1, 1, total, LANES), lambda s, p: (s, p, 0, 0))
    ins = lane_blocks(parts, groups) + lane_blocks(parts, 2 * groups) + lane_blocks(queries, 0)
    ins += lane_blocks(upstreams, 0)
    ins += [pl.BlockSpec((1, 1, 2, part.shape[1]), lambda s, p: (s, p, 0, 0)) for part in queries]
    operands = [*parts, *parts, *queries, *upstreams, *sums]
    if last:
        query_grads, totals = before
        ins += [whole, whole] + lane_blocks(query_grads, 0)
        operands += [*totals, *query_grads]
        out_specs = [
            pl.BlockSpec((1, part.shape[1], 3 * wide), lambda s, p: (s, 0, 0)) for part in parts
        ]
        out_shape = [
            jax.ShapeDtypeStruct((slots, part.shape[1], 3 * wide), BF16) for part in parts
        ]
    else:
        out_specs = lane_blocks(queries, 0) + [whole, whole]
        out_shape = [
            jax.ShapeDtypeStruct((slots, part.shape[1], wide), BF16) for part in queries
        ] + [jax.ShapeDtypeStruct((slots, groups, total, LANES), F32)] * 2
    outs = pl.pallas_call(
        functools.partial(attend_back_kernel, count, asked, groups, last),
        grid=(slots, groups),
        in_specs=ins,
        out_specs=out_specs,
        out_shape=out_shape,
        scratch_shapes=[pltpu.VMEM((total, LANES), BF16)] * 2 + [pltpu.VMEM((total, LANES), F32)] * 2,
        compiler_params=pltpu.CompilerParams(vmem_limit_bytes=48 * 1024 * 1024),
        cost_estimate=attention_cost(slots, total, wide, 2 if last else 5),
        name="attend_back",
    )(*operands)
    if last:
        return [narrow(out, 3, width) for out in outs]
    return outs[:asked], outs[asked:]


def rows_kernel(count, *refs):
    lefts, rights, out = refs[:count], refs[count : 2 * count], refs[-1]
    total = None
    for left, right in zip(lefts, rights):
        for slot in range(left.shape[0]):
            part = dot(left[slot], right[slot], 0, 0)
            total = part if total is None else total + part
    out[...] = total.astype(BF16)


def weight_grad(pairs):
    joined = None
    rows = pairs[0][0][0].shape[-1]
    wide = sum(rights[0].shape[-1] for _, rights in pairs)
    start = 0
    for lefts, rights in pairs:
        part = rights[0].shape[-1]
        if part % LANES or start % part:
            return jnp.concatenate([plain_grad(*pair) for pair in pairs], axis=1)
        count = len(lefts)
        step = 256
        ins = [
            pl.BlockSpec((left.shape[0], left.shape[1], step), lambda i: (0, 0, i))
            for left in lefts
        ] + [
            pl.BlockSpec(right.shape, lambda i: (0, 0, 0), pipeline_mode=pl.Buffered(1))
            for right in rights
        ]
        operands = (*lefts, *rights)
        if joined is not None:
            ins.append(pl.BlockSpec(memory_space=pl.ANY))
            operands += (joined,)
        joined = pl.pallas_call(
            functools.partial(rows_kernel, count),
            grid=(rows // step,),
            in_specs=ins,
            out_specs=pl.BlockSpec((step, part), lambda i, c=start // part: (i, c)),
            out_shape=jax.ShapeDtypeStruct((rows, wide), BF16),
            input_output_aliases={} if joined is None else {2 * count: 0},
            compiler_params=pltpu.CompilerParams(vmem_limit_bytes=48 * 1024 * 1024),
            cost_estimate=pl.CostEstimate(flops=0, transcendentals=0, bytes_accessed=1024),
            name="weight_grad",
        )(*operands)
        start += part
    return joined


NO_COST = pl.CostEstimate(flops=0, transcendentals=0, bytes_accessed=1024)
LIMIT = pltpu.CompilerParams(vmem_limit_bytes=48 * 1024 * 1024)


def tile_of(wide, start, most):
    return max(t for t in range(LANES, most + 1, LANES) if wide % t == 0 and start % t == 0)


def fits(weight):
    _, start, wide = weight
    return wide % LANES == 0 and start % LANES == 0


def cut(weight):
    array, start, wide = weight
    return array[:, start : start + wide]


def row_blocks(ref):
    slots, rows, columns = ref.shape
    if rows % 16 == 0:
        return [(slice(None), ref[...].reshape(slots * rows, columns))]
    return [(slice(slot, slot + 1), ref[slot]) for slot in range(slots)]


def store_rows(ref, place, value):
    slots = ref.shape[0] if place == slice(None) else 1
    ref[place] = value.reshape(slots, -1, value.shape[-1]).astype(ref.dtype)


def product_kernel(count, weight_dim, *refs):
    pieces, weight, outs = refs[:count], refs[count], refs[count + 1 :]
    for piece, out in zip(pieces, outs):
        for place, rows in row_blocks(piece):
            store_rows(out, place, dot(rows, weight[...], 1, weight_dim))


def whole_block(array):
    return pl.BlockSpec(array.shape, lambda j: (0, 0, 0), pipeline_mode=pl.Buffered(1))


def products_of(pieces, weight, weight_dim, kinds, late=False):
    array, start, wide = weight
    if not fits(weight) or (weight_dim and start % wide):
        return [
            dot(piece, cut(weight), 2, weight_dim).astype(kind)
            for piece, kind in zip(pieces, kinds)
        ]
    count = len(pieces)
    slots, _, depth = pieces[0].shape
    if weight_dim:
        result = array.shape[0]
        tile = tile_of(result, 0, 768)
        block = pl.BlockSpec((tile, wide), lambda j: (j, start // wide))
    else:
        result = wide
        tile = tile_of(wide, start, 768)
        block = pl.BlockSpec((depth, tile), lambda j: (0, start // tile + j))
    rows = slots * sum(piece.shape[1] for piece in pieces)
    cost = pl.CostEstimate(
        flops=4 * rows * depth * result, transcendentals=0, bytes_accessed=4 * rows * result
    )
    return pl.pallas_call(
        functools.partial(product_kernel, count, weight_dim),
        grid=(result // tile,),
        in_specs=[whole_block(piece) for piece in pieces] + [block],
        out_specs=[
            pl.BlockSpec((slots, piece.shape[1], tile), lambda j: (0, 0, j)) for piece in pieces
        ],
        out_shape=[
            jax.ShapeDtypeStruct((slots, piece.shape[1], result), kind)
            for piece, kind in zip(pieces, kinds)
        ],
        compiler_params=LIMIT,
        cost_estimate=cost if late else NO_COST,
        name="products",
    )(*pieces, array)


def hidden_kernel(count, *refs):
    pieces, downs, up, down = refs[:count], refs[count : 2 * count], refs[2 * count], refs[2 * count + 1]
    actives, grads = refs[2 * count + 2 : 3 * count + 2], refs[3 * count + 2 :]
    for piece, upstream, active, grad in zip(pieces, downs, actives, grads):
        for (place, rows), (_, above) in zip(row_blocks(piece), row_blocks(upstream)):
            hidden = dot(rows, up[...], 1, 0)
            active_grad = dot(above, down[...], 1, 0)
            square = hidden * hidden
            scale = (2 / math.pi) ** 0.5
            bend = jnp.tanh(hidden * (scale + scale * 0.044715 * square))
            half = 0.5 + 0.5 * bend
            slope = half + hidden * (0.5 - 0.5 * bend * bend) * (
                scale + scale * 0.134145 * square
            )
            store_rows(active, place, hidden * half)
            store_rows(grad, place, active_grad * slope)


def hidden_both(pieces, downs, up, down):
    count = len(pieces)
    if not (fits(up) and fits(down)):
        hidden = [dot(piece, cut(up), 2, 0) for piece in pieces]
        active_grad = [dot(piece, cut(down), 2, 0) for piece in downs]
        return (
            [gelu_tanh(value).astype(BF16) for value in hidden],
            [
                jax.vjp(gelu_tanh, value)[1](grad)[0].astype(BF16)
                for value, grad in zip(hidden, active_grad)
            ],
        )
    slots, _, depth = pieces[0].shape
    wide = up[2]
    tile = tile_of(wide, math.gcd(up[1], down[1]), 512)
    outs = pl.pallas_call(
        functools.partial(hidden_kernel, count),
        grid=(wide // tile,),
        in_specs=[whole_block(piece) for piece in (*pieces, *downs)]
        + [
            pl.BlockSpec((depth, tile), lambda j, o=block[1] // tile: (0, o + j))
            for block in (up, down)
        ],
        out_specs=[
            pl.BlockSpec((slots, piece.shape[1], tile), lambda j: (0, 0, j)) for piece in pieces
        ]
        * 2,
        out_shape=[
            jax.ShapeDtypeStruct((slots, piece.shape[1], wide), BF16) for piece in pieces
        ]
        * 2,
        compiler_params=LIMIT,
        cost_estimate=NO_COST,
        name="hidden_both",
    )(*pieces, *downs, up[0], down[0])
    return outs[:count], outs[count:]


def plain_grad(lefts, rights):
    left = jnp.concatenate([v.reshape(-1, v.shape[-1]) for v in lefts], axis=0)
    right = jnp.concatenate([v.reshape(-1, v.shape[-1]) for v in rights], axis=0)
    return dot(left, right, 0, 0).astype(BF16)


def on_device(
    group_count,
    tensor_size,
    image_tokens,
    text_tokens,
    condition,
    group_size,
    image_modulation,
    image_attention_in,
    image_attention_out,
    image_hidden_in,
    image_hidden_out,
    text_modulation,
    text_attention_in,
    text_attention_out,
    text_hidden_in,
    text_hidden_out,
    image_cotangent,
    text_cotangent,
):
    size = tensor_size
    slots, image_length, model = image_tokens.shape
    text_length = text_tokens.shape[1]
    share, _, width = image_attention_in.shape
    units = image_hidden_in.shape[1]
    tensor_rank = lax.axis_index("tensor")
    group_rank = lax.axis_index("dp")

    def gathered(*blocks):
        joined = blocks[0] if len(blocks) == 1 else jnp.concatenate(blocks, axis=1)
        return lax.all_gather(joined, "dp", axis=0, tiled=True)

    packed_first = gathered(
        image_attention_in.reshape(share, 3 * width),
        text_attention_in.reshape(share, 3 * width),
        image_attention_out.T,
        text_attention_out.T,
    )
    packed_image = gathered(image_hidden_in, image_hidden_out.T)
    packed_text = gathered(text_hidden_in, text_hidden_out.T)
    weight_in = ((packed_first, 0, 3 * width), (packed_first, 3 * width, 3 * width))
    weight_out = ((packed_first, 6 * width, width), (packed_first, 7 * width, width))

    alive = (jnp.arange(slots) < group_size[0]).astype(F32)[:, None, None]
    cond_full = condition.astype(F32)
    activated_low = jax.nn.silu(cond_full).astype(BF16)
    activated_all = gather_stack(activated_low, group_count, "dp").reshape(-1, model)
    activated_own = lax.dynamic_slice_in_dim(activated_all, group_rank * share, share, 1)
    all_slots = activated_own.shape[0]
    mod_parts = jnp.concatenate(
        [
            dot(activated_own, image_modulation.reshape(share, 6 * width), 1, 0),
            dot(activated_own, text_modulation.reshape(share, 6 * width), 1, 0),
        ],
        axis=1,
    ).reshape(group_count, slots, 12 * width)
    mod_own = scatter_stack(mod_parts, group_count, "dp")
    modulations = lax.all_gather(
        mod_own.reshape(slots, 2, 6, width), "tensor", axis=3, tiled=True
    )
    mods = (modulations[:, 0], modulations[:, 1])

    tokens = (image_tokens.astype(F32), text_tokens.astype(F32))
    outgoing = (image_cotangent.astype(F32) * alive, text_cotangent.astype(F32) * alive)

    half = size // 2
    near_kinds = [F32] + [BF16] * (half - 1)

    def scattered(grad):
        return lax.psum_scatter(grad, "dp", scatter_dimension=0, tiled=True).astype(F32)

    def row_products(pieces, weight, weight_dim, late=False):
        far = products_of(pieces[half:], weight, weight_dim, near_kinds, late)
        near = products_of(after(pieces[:half], far), weight, weight_dim, near_kinds, late)
        return [*near, *far]

    def image_sum(pieces, weight, weight_dim, late=False):
        products = row_products(pieces, weight, weight_dim, late)
        return scatter_end(*scatter_start(products, size), size)

    def text_sum(piece, weight, weight_dim, late=False):
        (product,) = products_of([piece], weight, weight_dim, [F32], late)
        return scatter_end(*text_start(product, size), size)

    def modulated(values, mod, shift, scale):
        normed, inverse = norm_rows(values)
        rows = normed * (1.0 + spread(mod[:, scale])) + spread(mod[:, shift])
        return normed, inverse, rows.astype(BF16)

    def second_back(stream, second_grad, normed, inverse):
        mod = mods[stream]
        shift_two_grad = jnp.sum(second_grad, axis=1)
        scale_two_grad = jnp.sum(second_grad * normed, axis=1)
        middle_grad = outgoing[stream] + norm_back(
            second_grad * (1.0 + spread(mod[:, 4])), normed, inverse
        )
        low = (middle_grad * spread(mod[:, 2])).astype(BF16)
        return middle_grad, low, shift_two_grad, scale_two_grad

    low_kinds = [BF16] * size

    normed_one, inverse_one, image_first = modulated(tokens[0], mods[0], 0, 1)
    text_normed_one, text_inverse_one, text_first = modulated(tokens[1], mods[1], 0, 1)
    first_pieces = gather_pieces(image_first, size)
    packed = products_of(first_pieces, weight_in[0], 0, low_kinds)
    text_packed = products_of([text_first], weight_in[1], 0, [BF16])
    down_rows = [
        (outgoing[stream] * spread(mods[stream][:, 5])).astype(BF16) for stream in range(2)
    ]
    down_have = gather_start(after(down_rows[0], first_pieces), size)
    parts = after([*packed, *text_packed], down_have)
    attended, sums = attend(parts)
    down_pieces = gather_end(after(down_have, attended), size)
    attended_parts = (attended[:-1], attended[-1:])

    branch = image_sum(attended_parts[0], weight_out[0], 1)
    middle = tokens[0] + spread(mods[0][:, 2]) * branch
    normed_two, inverse_two, image_second = modulated(middle, mods[0], 3, 4)
    up_weight, down_weight = (packed_image, 0, units), (packed_image, units, units)
    near_pieces = gather_pieces(image_second, size, half)
    far_have = gather_start(image_second, size)
    near = hidden_both(near_pieces, down_pieces[:half], up_weight, down_weight)
    far_have = {k: v for k, v in far_have.items() if k >= half}
    far_pieces = gather_end(after(far_have, near), size, half)
    second_pieces = [*near_pieces, *far_pieces]
    far = hidden_both(far_pieces, down_pieces[half:], up_weight, down_weight)
    text_branch = text_sum(after(attended_parts[1][0], far_pieces), weight_out[1], 1)
    active = [*near[0], *far[0]]
    hidden_grad = after([*near[1], *far[1]], text_branch)
    kept, sent = scatter_start(row_products(hidden_grad, up_weight, 1), size)
    image_mlp_grad = weight_grad(
        after([(down_pieces, active), (second_pieces, hidden_grad)], sent)
    )
    second_grad = after(scatter_end(kept, sent, size), image_mlp_grad)
    image_mlp = scattered(after(image_mlp_grad, second_grad))
    middle_grad, low, shift_two_grad, scale_two_grad = second_back(
        0, second_grad, normed_two, inverse_two
    )
    gate_one_grad = jnp.sum(middle_grad * branch, axis=1)

    low_have = gather_start(low, size)
    two_products = row_products(after(active, low), down_weight, 1)
    two_kept, two_sent = scatter_start(two_products, size)

    text_both = after(packed_text, low)
    text_up_weight, text_down_weight = (text_both, 0, units), (text_both, units, units)
    text_middle = tokens[1] + spread(mods[1][:, 2]) * text_branch
    text_normed_two, text_inverse_two, text_second = modulated(text_middle, mods[1], 3, 4)
    text_active, text_hidden_grad = hidden_both(
        [text_second], [down_rows[1]], text_up_weight, text_down_weight
    )
    (text_product,) = products_of(text_hidden_grad, text_up_weight, 1, [F32])
    text_kept, text_sent = text_start(text_product, size)
    low_have = after(low_have, two_products, text_product)
    branch_grads = gather_end(low_have, size)
    text_mlp_grad = weight_grad(
        after([([down_rows[1]], text_active), ([text_second], text_hidden_grad)], low_have)
    )
    (text_two,) = products_of(after(text_active, text_product), text_down_weight, 1, [F32])

    upstreams = products_of(branch_grads, weight_out[0], 0, low_kinds)
    upstreams = after(upstreams, text_sent, text_mlp_grad, text_two)
    text_ring = ring_scatter(after(text_mlp_grad, low_have), group_count)
    text_hop = next(text_ring)
    first_part = attend_back(parts, size, upstreams, sums[:-1])
    branch_two = scatter_end(after(two_kept, first_part), two_sent, size)
    text_second_grad = scatter_end(after(text_kept, first_part), text_sent, size)
    first_part, branch_two, text_hop = lax.optimization_barrier((first_part, branch_two, text_hop))
    text_hop = text_ring.send(text_hop)
    text_middle_grad, text_low, text_shift_two_grad, text_scale_two_grad = second_back(
        1, text_second_grad, text_normed_two, text_inverse_two
    )
    text_gate_one_grad = jnp.sum(text_middle_grad * text_branch, axis=1)
    text_upstream = products_of([text_low], weight_out[1], 0, [BF16])
    packed_grads = attend_back(parts, 1, text_upstream, sums[-1:], first_part)
    attention_grad = weight_grad(
        [
            (first_pieces, packed_grads[:-1]),
            ([text_first], packed_grads[-1:]),
            (branch_grads, attended_parts[0]),
            ([text_low], attended_parts[1]),
        ]
    )
    attention_sum = scattered(attention_grad)
    packed_grads, text_hop, text_two = after((packed_grads, text_hop, text_two), attention_grad)
    text_hop = text_ring.send(text_hop)

    def first_back(stream, first_grad, normed, inverse, middle_grad):
        mod = mods[stream]
        shift_one_grad = jnp.sum(first_grad, axis=1)
        scale_one_grad = jnp.sum(first_grad * normed, axis=1)
        input_grad = middle_grad + norm_back(
            first_grad * (1.0 + spread(mod[:, 1])), normed, inverse
        )
        return input_grad, shift_one_grad, scale_one_grad

    def finish(stream, middle, branch_two):
        result = middle + spread(mods[stream][:, 5]) * branch_two
        gate_two_grad = jnp.sum(outgoing[stream] * branch_two, axis=1)
        return (result * alive).astype(BF16), gate_two_grad

    first_grad = image_sum(packed_grads[:-1], weight_in[0], 1, True)
    text_first_grad = text_sum(packed_grads[-1], weight_in[1], 1, True)
    text_branch_two = scatter_end(*text_start(text_two, size), size)
    text_first_grad, text_hop = lax.optimization_barrier((text_first_grad, text_hop))
    for _ in range(group_count // 2 - 3):
        text_hop = text_ring.send(text_hop)
    first_grad, text_hop = lax.optimization_barrier((first_grad, text_hop))
    text_mlp = text_ring.send(text_hop)
    input_grads = [None, None]
    input_grads[0], shift_one_grad, scale_one_grad = first_back(
        0, first_grad, normed_one, inverse_one, middle_grad
    )
    input_grads[1], text_shift_one_grad, text_scale_one_grad = first_back(
        1, text_first_grad, text_normed_one, text_inverse_one, text_middle_grad
    )
    outputs = [None, None]
    outputs[0], gate_two_grad = finish(0, middle, branch_two)
    outputs[1], text_gate_two_grad = finish(1, text_middle, text_branch_two)
    mod_grads = (
        jnp.stack(
            [
                shift_one_grad,
                scale_one_grad,
                gate_one_grad,
                shift_two_grad,
                scale_two_grad,
                gate_two_grad,
            ],
            axis=1,
        ),
        jnp.stack(
            [
                text_shift_one_grad,
                text_scale_one_grad,
                text_gate_one_grad,
                text_shift_two_grad,
                text_scale_two_grad,
                text_gate_two_grad,
            ],
            axis=1,
        ),
    )

    image_blocks = jnp.stack(
        [
            lax.dynamic_slice_in_dim(mod_grads[0], (tensor_rank ^ k) * width, width, 2)
            for k in range(size)
        ]
    )
    image_share = scatter_stack(image_blocks, size, "tensor")
    text_share = lax.dynamic_slice_in_dim(mod_grads[1], tensor_rank * width, width, 2)
    share_low = jnp.stack([image_share, text_share], axis=1).astype(BF16)
    share_all = gather_stack(share_low, group_count, "dp").reshape(all_slots, 2, 6, width)
    image_all = share_all[:, 0].reshape(all_slots, 6 * width)
    text_all = share_all[:, 1].reshape(all_slots, 6 * width)
    image_ada = dot(activated_own, image_all, 0, 0).reshape(share, 6, width)
    text_ada = dot(activated_own, text_all, 0, 0).reshape(share, 6, width)
    activated_part = dot(image_all, image_modulation.reshape(share, 6 * width), 1, 1) + dot(
        text_all, text_modulation.reshape(share, 6 * width), 1, 1
    )
    activated_part = sum_all(activated_part, size, "tensor").reshape(group_count, slots, share)
    activated_rows = gather_stack(activated_part, group_count, "dp")
    activated_rows = jnp.stack([activated_rows[k, k] for k in range(group_count)])
    activated_grad = jnp.concatenate(
        [
            lax.dynamic_index_in_dim(activated_rows, group_rank ^ k, 0, keepdims=False)
            for k in range(group_count)
        ],
        axis=1,
    )
    condition_gradient = jax.vjp(jax.nn.silu, cond_full)[1](activated_grad)[0]

    return (
        outputs[0],
        outputs[1],
        input_grads[0],
        input_grads[1],
        condition_gradient,
        image_ada,
        attention_sum[:, : 3 * width].reshape(share, 3, width),
        attention_sum[:, 6 * width : 7 * width].T,
        image_mlp[:, units:],
        image_mlp[:, :units].T,
        text_ada,
        attention_sum[:, 3 * width : 6 * width].reshape(share, 3, width),
        attention_sum[:, 7 * width :].T,
        text_mlp[:, units:],
        text_mlp[:, :units].T,
    )


def solution(mesh):
    image = P("dp", "tensor", None)
    text = P("dp", None, None)
    columns = P("dp", None, "tensor")
    rows = P("tensor", "dp")
    plain = P("dp", "tensor")
    weights = (columns, columns, rows, plain, rows)
    return jax.shard_map(
        functools.partial(on_device, mesh.shape["dp"], mesh.shape["tensor"]),
        mesh=mesh,
        in_specs=(image, text, P("dp", None), P("dp")) + weights + weights + (image, text),
        out_specs=(image, text, image, text, P("dp", None)) + weights + weights,
        check_vma=False,
    )
```

```python
import functools
import math

import jax
import jax.numpy as jnp
from jax import lax
from jax.experimental import pallas as pl
from jax.experimental.pallas import tpu as pltpu
from jax.sharding import PartitionSpec as P

HEAD = 64
LANES = 128
F32 = jnp.float32
BF16 = jnp.bfloat16


def norm_rows(values):
    center = values - jnp.mean(values, axis=-1, keepdims=True)
    inverse = lax.rsqrt(jnp.mean(center * center, axis=-1, keepdims=True) + 1e-06)
    return (center * inverse, inverse)


def norm_back(upstream, normed, inverse):
    first = jnp.mean(upstream, axis=-1, keepdims=True)
    second = jnp.mean(upstream * normed, axis=-1, keepdims=True)
    return inverse * (upstream - first - normed * second)


def gelu_tanh(values):
    return jax.nn.gelu(values, approximate=True)


def spread(vector):
    return vector[:, None, :]


def dot(left, right, left_dim, right_dim):
    return lax.dot_general(
        left, right, (((left_dim,), (right_dim,)), ((), ())), preferred_element_type=F32
    )


def swap(value, bit, size, axis="tensor"):
    return lax.ppermute(value, axis, [(i, i ^ bit) for i in range(size)])


def bits_of(size):
    bits = []
    bit = 1
    while bit < size:
        bits.append(bit)
        bit *= 2
    return bits


def gather_start(value, size, axis="tensor"):
    have = {0: value}
    for bit in reversed(bits_of(size)[1:]):
        have.update({k ^ bit: swap(v, bit, size, axis) for k, v in list(have.items())})
    return have


def gather_end(have, size, first=0, axis="tensor"):
    have = have | {k ^ 1: swap(v, 1, size, axis) for k, v in have.items()}
    return [have[k] for k in range(first, first + len(have))]


def gather_pieces(value, size, reach=None, axis="tensor"):
    have = {0: value}
    for bit in reversed(bits_of(reach or size)):
        have.update({k ^ bit: swap(v, bit, size, axis) for k, v in list(have.items())})
    return [have[k] for k in sorted(have)]


def gather_stack(value, size, axis):
    value = value[None]
    for bit in bits_of(size):
        value = jnp.concatenate([value, swap(value, bit, size, axis)], axis=0)
    return value


def scatter_stack(value, size, axis):
    for bit in reversed(bits_of(size)):
        value = value[:bit] + swap(value[bit:], bit, size, axis)
    return value[0]


def sum_all(value, size, axis):
    for bit in bits_of(size):
        value = value + swap(value, bit, size, axis)
    return value


def scatter_start(pieces, size):
    have = dict(enumerate(pieces))
    for bit in bits_of(size)[:-1]:
        kept = {}
        for k in sorted(have, reverse=True):
            if not k & bit:
                other = swap(have[k ^ bit].astype(BF16), bit, size)
                kept[k] = have[k].astype(F32) + other.astype(F32)
        have = kept
    kept, sent = (have[k] for k in sorted(have))
    return kept, sent.astype(BF16)


def scatter_end(kept, sent, size):
    return kept.astype(F32) + swap(sent, size // 2, size).astype(F32)


def after(values, *others):
    return lax.optimization_barrier((values, others))[0]


def ring_of(count):
    return list(range(0, count, 2)) + list(range(1, count, 2))[::-1]


def ring_member(place, count):
    place = lax.rem(place + count, count)
    return jnp.where(place < (count + 1) // 2, 2 * place, 2 * (count - 1 - place) + 1)


def ring_place(member, count):
    return jnp.where(member % 2 == 0, member // 2, count - 1 - member // 2)


def ring_step(value, way, count):
    ring = ring_of(count)
    hops = [(ring[i], ring[(i + way) % count]) for i in range(count)]
    return lax.ppermute(value, "dp", hops)


def ring_scatter(grad, count):
    wide = grad.shape[1]
    share = grad.shape[0] // count
    half = wide // 2 // LANES * LANES
    place = ring_place(lax.axis_index("dp"), count)

    def own(offset):
        row = ring_member(place + offset, count) * share
        return lax.dynamic_slice_in_dim(grad, row, share, 0).astype(F32)

    far = own(count // 2).astype(BF16)
    behind = ring_step(far[:, :half], 1, count)
    ahead = ring_step(far[:, half:], -1, count)
    behind, ahead = yield behind, ahead
    behind = jnp.pad(behind.astype(F32), ((0, 0), (0, wide - half)))
    ahead = jnp.pad(ahead.astype(F32), ((0, 0), (half, 0)))
    for hop in range(count // 2 - 1, 0, -1):
        behind = ring_step((own(hop) + behind).astype(BF16), 1, count)
        ahead = ring_step((own(-hop) + ahead).astype(BF16), -1, count)
        behind, ahead = yield behind, ahead
        behind, ahead = behind.astype(F32), ahead.astype(F32)
    yield own(0) + behind + ahead


def text_start(value, size):
    for bit in bits_of(size)[:-1]:
        if bit > 1:
            value = lax.reduce_precision(value, 8, 7)
            value = value + swap(value.astype(BF16), bit, size).astype(F32)
        else:
            value = value + swap(value, bit, size)
    value = lax.reduce_precision(value, 8, 7)
    return value, value.astype(BF16)


def lane_mask(half, shape):
    lane = lax.broadcasted_iota(jnp.int32, shape, 1)
    return (lane >= HEAD) if half else (lane < HEAD)


def pick(value, half):
    return jnp.where(lane_mask(half, value.shape), value, jnp.zeros_like(value))


def load_rows(refs, store):
    start = 0
    for ref in refs:
        rows = ref.shape[1]
        store[start : start + rows, :] = ref[0]
        start += rows


def attend_kernel(count, *refs):
    queries, keys, values = refs[:count], refs[count : 2 * count], refs[2 * count : 3 * count]
    outs = refs[3 * count : 4 * count]
    sums = refs[4 * count : 5 * count]
    key_all, value_all = refs[5 * count :]
    load_rows(keys, key_all)
    load_rows(values, value_all)
    for index in range(count):
        query = queries[index][0] * jnp.asarray(HEAD**-0.5, BF16)
        halves = []
        for half in range(2):
            scores = dot(key_all[...], pick(query, half), 1, 1)
            highest = jnp.max(scores, axis=0, keepdims=True)
            weights = jnp.exp(scores - highest)
            total = jnp.sum(weights, axis=0, keepdims=True)
            weights = (weights * (1.0 / total)).astype(BF16)
            mixed = dot(value_all[...], weights, 0, 0)
            halves.append(mixed[half * HEAD : (half + 1) * HEAD])
            sums[index][0, 0, half : half + 1, :] = highest + jnp.log(total)
        outs[index][0] = jnp.concatenate(halves, axis=0).T.astype(BF16)


def attend_back_kernel(count, asked, groups, last, *refs):
    refs = list(refs)

    def take(number):
        return [refs.pop(0) for _ in range(number)]

    keys, values = take(count), take(count)
    queries, upstreams, sums = take(asked), take(asked), take(asked)
    if last:
        before = take(2)
        query_grads = take(count - asked)
        outs = take(count)
    else:
        outs = take(asked)
        totals = take(2)
    key_all, value_all, key_grad, value_grad = refs
    load_rows(keys, key_all)
    load_rows(values, value_all)
    pair = pl.program_id(1)
    scale = jnp.asarray(HEAD**-0.5, BF16)
    for index in range(asked):
        query = queries[index][0] * scale
        upstream = upstreams[index][0]
        halves = []
        for half in range(2):
            query_half = pick(query, half)
            upstream_half = pick(upstream, half)
            scores = dot(key_all[...], query_half, 1, 1)
            weights = jnp.exp(scores - sums[index][0, 0, half : half + 1, :])
            along = dot(value_all[...], upstream_half, 1, 1)
            value_part = dot(weights.astype(BF16), upstream_half, 1, 0)
            product = weights * along
            score_grad = (product - weights * jnp.sum(product, axis=0, keepdims=True)).astype(BF16)
            key_part = dot(score_grad, query_half, 1, 0)
            if index == 0 and half == 0 and last:
                value_grad[...] = before[1][0, 0] + value_part
                key_grad[...] = before[0][0, 0] + key_part
            elif index == 0 and half == 0:
                value_grad[...] = value_part
                key_grad[...] = key_part
            else:
                value_grad[...] += value_part
                key_grad[...] += key_part
            mixed = dot(key_all[...], score_grad, 0, 0)
            halves.append(mixed[half * HEAD : (half + 1) * HEAD])
        query_grad = (jnp.concatenate(halves, axis=0).T * HEAD**-0.5).astype(BF16)
        if last:
            lanes = pl.ds(pl.multiple_of(pair * LANES, LANES), LANES)
            outs[count - asked + index][0, :, lanes] = query_grad
        else:
            outs[index][0] = query_grad
    if not last:
        totals[0][0, 0] = key_grad[...]
        totals[1][0, 0] = value_grad[...]
        return
    for index, query_grad in enumerate(query_grads):
        lanes = pl.ds(pl.multiple_of(pair * LANES, LANES), LANES)
        outs[index][0, :, lanes] = query_grad[0]
    start = 0
    for out in outs:
        rows = out.shape[1]
        for number, grad in ((1, key_grad), (2, value_grad)):
            lanes = pl.ds(pl.multiple_of((number * groups + pair) * LANES, LANES), LANES)
            out[0, :, lanes] = grad[start : start + rows, :].astype(BF16)
        start += rows


def lane_blocks(parts, offset):
    return [
        pl.BlockSpec((1, part.shape[1], LANES), lambda s, p, o=offset: (s, 0, o + p))
        for part in parts
    ]


def widen(part, copies):
    slots, rows, width = part.shape
    width = width // copies
    extra = -width % LANES
    if not extra:
        return part
    part = jnp.pad(part.reshape(slots, rows, copies, width), ((0, 0), (0, 0), (0, 0), (0, extra)))
    return part.reshape(slots, rows, copies * (width + extra))


def narrow(part, copies, width):
    slots, rows, wide = part.shape
    wide = wide // copies
    if wide == width:
        return part
    return part.reshape(slots, rows, copies, wide)[..., :width].reshape(slots, rows, -1)


def attention_cost(slots, rows, width, products):
    return pl.CostEstimate(
        flops=products * 8 * slots * rows * rows * width,
        transcendentals=slots * rows * rows * (width // HEAD),
        bytes_accessed=slots * rows * width * 2 * (4 + 3 * (products > 2)),
    )


def attend(parts):
    slots = parts[0].shape[0]
    width = parts[0].shape[2] // 3
    parts = [widen(part, 3) for part in parts]
    count = len(parts)
    wide = parts[0].shape[2] // 3
    groups = wide // LANES
    total = sum(part.shape[1] for part in parts)
    outs = pl.pallas_call(
        functools.partial(attend_kernel, count),
        grid=(slots, groups),
        in_specs=lane_blocks(parts, 0) + lane_blocks(parts, groups) + lane_blocks(parts, 2 * groups),
        out_specs=lane_blocks(parts, 0)
        + [
            pl.BlockSpec((1, 1, 2, part.shape[1]), lambda s, p: (s, p, 0, 0)) for part in parts
        ],
        out_shape=[jax.ShapeDtypeStruct((slots, part.shape[1], wide), BF16) for part in parts]
        + [jax.ShapeDtypeStruct((slots, groups, 2, part.shape[1]), F32) for part in parts],
        scratch_shapes=[pltpu.VMEM((total, LANES), BF16)] * 2,
        compiler_params=pltpu.CompilerParams(vmem_limit_bytes=48 * 1024 * 1024),
        cost_estimate=attention_cost(slots, total, wide, 2),
        name="attend",
    )(*parts, *parts, *parts)
    return [narrow(out, 1, width) for out in outs[:count]], outs[count:]


def attend_back(parts, asked, upstreams, sums, before=None):
    slots = parts[0].shape[0]
    width = parts[0].shape[2] // 3
    parts = [widen(part, 3) for part in parts]
    upstreams = [widen(part, 1) for part in upstreams]
    last = before is not None
    count = len(parts)
    queries = parts[-asked:] if last else parts[:asked]
    wide = parts[0].shape[2] // 3
    groups = wide // LANES
    total = sum(part.shape[1] for part in parts)
    whole = pl.BlockSpec((1, 1, total, LANES), lambda s, p: (s, p, 0, 0))
    ins = lane_blocks(parts, groups) + lane_blocks(parts, 2 * groups) + lane_blocks(queries, 0)
    ins += lane_blocks(upstreams, 0)
    ins += [pl.BlockSpec((1, 1, 2, part.shape[1]), lambda s, p: (s, p, 0, 0)) for part in queries]
    operands = [*parts, *parts, *queries, *upstreams, *sums]
    if last:
        query_grads, totals = before
        ins += [whole, whole] + lane_blocks(query_grads, 0)
        operands += [*totals, *query_grads]
        out_specs = [
            pl.BlockSpec((1, part.shape[1], 3 * wide), lambda s, p: (s, 0, 0)) for part in parts
        ]
        out_shape = [
            jax.ShapeDtypeStruct((slots, part.shape[1], 3 * wide), BF16) for part in parts
        ]
    else:
        out_specs = lane_blocks(queries, 0) + [whole, whole]
        out_shape = [
            jax.ShapeDtypeStruct((slots, part.shape[1], wide), BF16) for part in queries
        ] + [jax.ShapeDtypeStruct((slots, groups, total, LANES), F32)] * 2
    outs = pl.pallas_call(
        functools.partial(attend_back_kernel, count, asked, groups, last),
        grid=(slots, groups),
        in_specs=ins,
        out_specs=out_specs,
        out_shape=out_shape,
        scratch_shapes=[pltpu.VMEM((total, LANES), BF16)] * 2 + [pltpu.VMEM((total, LANES), F32)] * 2,
        compiler_params=pltpu.CompilerParams(vmem_limit_bytes=48 * 1024 * 1024),
        cost_estimate=attention_cost(slots, total, wide, 2 if last else 5),
        name="attend_back",
    )(*operands)
    if last:
        return [narrow(out, 3, width) for out in outs]
    return outs[:asked], outs[asked:]


def rows_kernel(count, *refs):
    lefts, rights, out = refs[:count], refs[count : 2 * count], refs[-1]
    total = None
    for left, right in zip(lefts, rights):
        for slot in range(left.shape[0]):
            part = dot(left[slot], right[slot], 0, 0)
            total = part if total is None else total + part
    out[...] = total.astype(BF16)


def weight_grad(pairs):
    joined = None
    rows = pairs[0][0][0].shape[-1]
    wide = sum(rights[0].shape[-1] for _, rights in pairs)
    start = 0
    for lefts, rights in pairs:
        part = rights[0].shape[-1]
        if part % LANES or start % part:
            return jnp.concatenate([plain_grad(*pair) for pair in pairs], axis=1)
        count = len(lefts)
        step = 256
        ins = [
            pl.BlockSpec((left.shape[0], left.shape[1], step), lambda i: (0, 0, i))
            for left in lefts
        ] + [
            pl.BlockSpec(right.shape, lambda i: (0, 0, 0), pipeline_mode=pl.Buffered(1))
            for right in rights
        ]
        operands = (*lefts, *rights)
        if joined is not None:
            ins.append(pl.BlockSpec(memory_space=pl.ANY))
            operands += (joined,)
        joined = pl.pallas_call(
            functools.partial(rows_kernel, count),
            grid=(rows // step,),
            in_specs=ins,
            out_specs=pl.BlockSpec((step, part), lambda i, c=start // part: (i, c)),
            out_shape=jax.ShapeDtypeStruct((rows, wide), BF16),
            input_output_aliases={} if joined is None else {2 * count: 0},
            compiler_params=pltpu.CompilerParams(vmem_limit_bytes=48 * 1024 * 1024),
            cost_estimate=pl.CostEstimate(flops=0, transcendentals=0, bytes_accessed=1024),
            name="weight_grad",
        )(*operands)
        start += part
    return joined


NO_COST = pl.CostEstimate(flops=0, transcendentals=0, bytes_accessed=1024)
LIMIT = pltpu.CompilerParams(vmem_limit_bytes=48 * 1024 * 1024)


def tile_of(wide, start, most):
    return max(t for t in range(LANES, most + 1, LANES) if wide % t == 0 and start % t == 0)


def fits(weight):
    _, start, wide = weight
    return wide % LANES == 0 and start % LANES == 0


def cut(weight):
    array, start, wide = weight
    return array[:, start : start + wide]


def row_blocks(ref):
    slots, rows, columns = ref.shape
    if rows % 16 == 0:
        return [(slice(None), ref[...].reshape(slots * rows, columns))]
    return [(slice(slot, slot + 1), ref[slot]) for slot in range(slots)]


def store_rows(ref, place, value):
    slots = ref.shape[0] if place == slice(None) else 1
    ref[place] = value.reshape(slots, -1, value.shape[-1]).astype(ref.dtype)


def product_kernel(count, weight_dim, *refs):
    pieces, weight, outs = refs[:count], refs[count], refs[count + 1 :]
    for piece, out in zip(pieces, outs):
        for place, rows in row_blocks(piece):
            store_rows(out, place, dot(rows, weight[...], 1, weight_dim))


def whole_block(array):
    return pl.BlockSpec(array.shape, lambda j: (0, 0, 0), pipeline_mode=pl.Buffered(1))


def products_of(pieces, weight, weight_dim, kinds, late=False):
    array, start, wide = weight
    if not fits(weight) or (weight_dim and start % wide):
        return [
            dot(piece, cut(weight), 2, weight_dim).astype(kind)
            for piece, kind in zip(pieces, kinds)
        ]
    count = len(pieces)
    slots, _, depth = pieces[0].shape
    if weight_dim:
        result = array.shape[0]
        tile = tile_of(result, 0, 768)
        block = pl.BlockSpec((tile, wide), lambda j: (j, start // wide))
    else:
        result = wide
        tile = tile_of(wide, start, 768)
        block = pl.BlockSpec((depth, tile), lambda j: (0, start // tile + j))
    rows = slots * sum(piece.shape[1] for piece in pieces)
    cost = pl.CostEstimate(
        flops=4 * rows * depth * result, transcendentals=0, bytes_accessed=4 * rows * result
    )
    return pl.pallas_call(
        functools.partial(product_kernel, count, weight_dim),
        grid=(result // tile,),
        in_specs=[whole_block(piece) for piece in pieces] + [block],
        out_specs=[
            pl.BlockSpec((slots, piece.shape[1], tile), lambda j: (0, 0, j)) for piece in pieces
        ],
        out_shape=[
            jax.ShapeDtypeStruct((slots, piece.shape[1], result), kind)
            for piece, kind in zip(pieces, kinds)
        ],
        compiler_params=LIMIT,
        cost_estimate=cost if late else NO_COST,
        name="products",
    )(*pieces, array)


def hidden_kernel(count, *refs):
    pieces, downs, up, down = refs[:count], refs[count : 2 * count], refs[2 * count], refs[2 * count + 1]
    actives, grads = refs[2 * count + 2 : 3 * count + 2], refs[3 * count + 2 :]
    for piece, upstream, active, grad in zip(pieces, downs, actives, grads):
        for (place, rows), (_, above) in zip(row_blocks(piece), row_blocks(upstream)):
            hidden = dot(rows, up[...], 1, 0)
            active_grad = dot(above, down[...], 1, 0)
            square = hidden * hidden
            scale = (2 / math.pi) ** 0.5
            bend = jnp.tanh(hidden * (scale + scale * 0.044715 * square))
            half = 0.5 + 0.5 * bend
            slope = half + hidden * (0.5 - 0.5 * bend * bend) * (
                scale + scale * 0.134145 * square
            )
            store_rows(active, place, hidden * half)
            store_rows(grad, place, active_grad * slope)


def hidden_both(pieces, downs, up, down):
    count = len(pieces)
    if not (fits(up) and fits(down)):
        hidden = [dot(piece, cut(up), 2, 0) for piece in pieces]
        active_grad = [dot(piece, cut(down), 2, 0) for piece in downs]
        return (
            [gelu_tanh(value).astype(BF16) for value in hidden],
            [
                jax.vjp(gelu_tanh, value)[1](grad)[0].astype(BF16)
                for value, grad in zip(hidden, active_grad)
            ],
        )
    slots, _, depth = pieces[0].shape
    wide = up[2]
    tile = tile_of(wide, math.gcd(up[1], down[1]), 512)
    outs = pl.pallas_call(
        functools.partial(hidden_kernel, count),
        grid=(wide // tile,),
        in_specs=[whole_block(piece) for piece in (*pieces, *downs)]
        + [
            pl.BlockSpec((depth, tile), lambda j, o=block[1] // tile: (0, o + j))
            for block in (up, down)
        ],
        out_specs=[
            pl.BlockSpec((slots, piece.shape[1], tile), lambda j: (0, 0, j)) for piece in pieces
        ]
        * 2,
        out_shape=[
            jax.ShapeDtypeStruct((slots, piece.shape[1], wide), BF16) for piece in pieces
        ]
        * 2,
        compiler_params=LIMIT,
        cost_estimate=NO_COST,
        name="hidden_both",
    )(*pieces, *downs, up[0], down[0])
    return outs[:count], outs[count:]


def plain_grad(lefts, rights):
    left = jnp.concatenate([v.reshape(-1, v.shape[-1]) for v in lefts], axis=0)
    right = jnp.concatenate([v.reshape(-1, v.shape[-1]) for v in rights], axis=0)
    return dot(left, right, 0, 0).astype(BF16)


def on_device(
    group_count,
    tensor_size,
    image_tokens,
    text_tokens,
    condition,
    group_size,
    image_modulation,
    image_attention_in,
    image_attention_out,
    image_hidden_in,
    image_hidden_out,
    text_modulation,
    text_attention_in,
    text_attention_out,
    text_hidden_in,
    text_hidden_out,
    image_cotangent,
    text_cotangent,
):
    size = tensor_size
    slots, image_length, model = image_tokens.shape
    text_length = text_tokens.shape[1]
    share, _, width = image_attention_in.shape
    units = image_hidden_in.shape[1]
    tensor_rank = lax.axis_index("tensor")
    group_rank = lax.axis_index("dp")

    def gathered(*blocks):
        joined = blocks[0] if len(blocks) == 1 else jnp.concatenate(blocks, axis=1)
        return lax.all_gather(joined, "dp", axis=0, tiled=True)

    packed_first = gathered(
        image_attention_in.reshape(share, 3 * width),
        text_attention_in.reshape(share, 3 * width),
        image_attention_out.T,
        text_attention_out.T,
    )
    packed_image = gathered(image_hidden_in, image_hidden_out.T)
    packed_text = gathered(text_hidden_in, text_hidden_out.T)
    weight_in = ((packed_first, 0, 3 * width), (packed_first, 3 * width, 3 * width))
    weight_out = ((packed_first, 6 * width, width), (packed_first, 7 * width, width))

    alive = (jnp.arange(slots) < group_size[0]).astype(F32)[:, None, None]
    cond_full = condition.astype(F32)
    activated_low = jax.nn.silu(cond_full).astype(BF16)
    activated_all = gather_stack(activated_low, group_count, "dp").reshape(-1, model)
    activated_own = lax.dynamic_slice_in_dim(activated_all, group_rank * share, share, 1)
    all_slots = activated_own.shape[0]
    mod_parts = jnp.concatenate(
        [
            dot(activated_own, image_modulation.reshape(share, 6 * width), 1, 0),
            dot(activated_own, text_modulation.reshape(share, 6 * width), 1, 0),
        ],
        axis=1,
    ).reshape(group_count, slots, 12 * width)
    mod_own = scatter_stack(mod_parts, group_count, "dp")
    modulations = lax.all_gather(
        mod_own.reshape(slots, 2, 6, width), "tensor", axis=3, tiled=True
    )
    mods = (modulations[:, 0], modulations[:, 1])

    tokens = (image_tokens.astype(F32), text_tokens.astype(F32))
    outgoing = (image_cotangent.astype(F32) * alive, text_cotangent.astype(F32) * alive)

    half = size // 2
    near_kinds = [F32] + [BF16] * (half - 1)

    def scattered(grad):
        return lax.psum_scatter(grad, "dp", scatter_dimension=0, tiled=True).astype(F32)

    def row_products(pieces, weight, weight_dim, late=False):
        far = products_of(pieces[half:], weight, weight_dim, near_kinds, late)
        near = products_of(after(pieces[:half], far), weight, weight_dim, near_kinds, late)
        return [*near, *far]

    def image_sum(pieces, weight, weight_dim, late=False):
        products = row_products(pieces, weight, weight_dim, late)
        return scatter_end(*scatter_start(products, size), size)

    def text_sum(piece, weight, weight_dim, late=False):
        (product,) = products_of([piece], weight, weight_dim, [F32], late)
        return scatter_end(*text_start(product, size), size)

    def modulated(values, mod, shift, scale):
        normed, inverse = norm_rows(values)
        rows = normed * (1.0 + spread(mod[:, scale])) + spread(mod[:, shift])
        return normed, inverse, rows.astype(BF16)

    def second_back(stream, second_grad, normed, inverse):
        mod = mods[stream]
        shift_two_grad = jnp.sum(second_grad, axis=1)
        scale_two_grad = jnp.sum(second_grad * normed, axis=1)
        middle_grad = outgoing[stream] + norm_back(
            second_grad * (1.0 + spread(mod[:, 4])), normed, inverse
        )
        low = (middle_grad * spread(mod[:, 2])).astype(BF16)
        return middle_grad, low, shift_two_grad, scale_two_grad

    low_kinds = [BF16] * size

    normed_one, inverse_one, image_first = modulated(tokens[0], mods[0], 0, 1)
    text_normed_one, text_inverse_one, text_first = modulated(tokens[1], mods[1], 0, 1)
    first_pieces = gather_pieces(image_first, size)
    packed = products_of(first_pieces, weight_in[0], 0, low_kinds)
    text_packed = products_of([text_first], weight_in[1], 0, [BF16])
    down_rows = [
        (outgoing[stream] * spread(mods[stream][:, 5])).astype(BF16) for stream in range(2)
    ]
    down_have = gather_start(after(down_rows[0], first_pieces), size)
    parts = after([*packed, *text_packed], down_have)
    attended, sums = attend(parts)
    down_pieces = gather_end(after(down_have, attended), size)
    attended_parts = (attended[:-1], attended[-1:])

    branch = image_sum(attended_parts[0], weight_out[0], 1)
    middle = tokens[0] + spread(mods[0][:, 2]) * branch
    normed_two, inverse_two, image_second = modulated(middle, mods[0], 3, 4)
    up_weight, down_weight = (packed_image, 0, units), (packed_image, units, units)
    near_pieces = gather_pieces(image_second, size, half)
    far_have = gather_start(image_second, size)
    near = hidden_both(near_pieces, down_pieces[:half], up_weight, down_weight)
    far_have = {k: v for k, v in far_have.items() if k >= half}
    far_pieces = gather_end(after(far_have, near), size, half)
    second_pieces = [*near_pieces, *far_pieces]
    far = hidden_both(far_pieces, down_pieces[half:], up_weight, down_weight)
    text_branch = text_sum(after(attended_parts[1][0], far_pieces), weight_out[1], 1)
    active = [*near[0], *far[0]]
    hidden_grad = after([*near[1], *far[1]], text_branch)
    kept, sent = scatter_start(row_products(hidden_grad, up_weight, 1), size)
    image_mlp_grad = weight_grad(
        after([(down_pieces, active), (second_pieces, hidden_grad)], sent)
    )
    second_grad = after(scatter_end(kept, sent, size), image_mlp_grad)
    image_mlp = scattered(after(image_mlp_grad, second_grad))
    middle_grad, low, shift_two_grad, scale_two_grad = second_back(
        0, second_grad, normed_two, inverse_two
    )
    gate_one_grad = jnp.sum(middle_grad * branch, axis=1)

    low_have = gather_start(low, size)
    two_products = row_products(after(active, low), down_weight, 1)
    two_kept, two_sent = scatter_start(two_products, size)

    text_both = after(packed_text, low)
    text_up_weight, text_down_weight = (text_both, 0, units), (text_both, units, units)
    text_middle = tokens[1] + spread(mods[1][:, 2]) * text_branch
    text_normed_two, text_inverse_two, text_second = modulated(text_middle, mods[1], 3, 4)
    text_active, text_hidden_grad = hidden_both(
        [text_second], [down_rows[1]], text_up_weight, text_down_weight
    )
    (text_product,) = products_of(text_hidden_grad, text_up_weight, 1, [F32])
    text_kept, text_sent = text_start(text_product, size)
    low_have = after(low_have, two_products, text_product)
    branch_grads = gather_end(low_have, size)
    text_mlp_grad = weight_grad(
        after(
            [
                ([down_rows[1]], text_active),
                ([text_second], text_hidden_grad),
                (branch_grads, attended_parts[0]),
            ],
            low_have,
        )
    )
    (text_two,) = products_of(after(text_active, text_product), text_down_weight, 1, [F32])

    upstreams = products_of(branch_grads, weight_out[0], 0, low_kinds)
    upstreams = after(upstreams, text_sent, text_mlp_grad, text_two)
    text_ring = ring_scatter(after(text_mlp_grad, low_have), group_count)
    text_hop = next(text_ring)
    first_part = attend_back(parts, size, upstreams, sums[:-1])
    branch_two = scatter_end(after(two_kept, first_part), two_sent, size)
    text_second_grad = scatter_end(after(text_kept, first_part), text_sent, size)
    first_part, branch_two, text_hop = lax.optimization_barrier((first_part, branch_two, text_hop))
    text_hop = text_ring.send(text_hop)
    text_middle_grad, text_low, text_shift_two_grad, text_scale_two_grad = second_back(
        1, text_second_grad, text_normed_two, text_inverse_two
    )
    text_gate_one_grad = jnp.sum(text_middle_grad * text_branch, axis=1)
    text_upstream = products_of([text_low], weight_out[1], 0, [BF16])
    packed_grads = attend_back(parts, 1, text_upstream, sums[-1:], first_part)
    attention_grad = weight_grad(
        [
            (first_pieces, packed_grads[:-1]),
            ([text_first], packed_grads[-1:]),
            ([text_low], attended_parts[1]),
        ]
    )
    attention_sum = scattered(attention_grad)
    packed_grads, text_hop, text_two = after((packed_grads, text_hop, text_two), attention_grad)
    text_hop = text_ring.send(text_hop)

    def first_back(stream, first_grad, normed, inverse, middle_grad):
        mod = mods[stream]
        shift_one_grad = jnp.sum(first_grad, axis=1)
        scale_one_grad = jnp.sum(first_grad * normed, axis=1)
        input_grad = middle_grad + norm_back(
            first_grad * (1.0 + spread(mod[:, 1])), normed, inverse
        )
        return input_grad, shift_one_grad, scale_one_grad

    def finish(stream, middle, branch_two):
        result = middle + spread(mods[stream][:, 5]) * branch_two
        gate_two_grad = jnp.sum(outgoing[stream] * branch_two, axis=1)
        return (result * alive).astype(BF16), gate_two_grad

    first_grad = image_sum(packed_grads[:-1], weight_in[0], 1, True)
    text_first_grad = text_sum(packed_grads[-1], weight_in[1], 1, True)
    text_branch_two = scatter_end(*text_start(text_two, size), size)
    text_first_grad, text_hop = lax.optimization_barrier((text_first_grad, text_hop))
    for _ in range(group_count // 2 - 3):
        text_hop = text_ring.send(text_hop)
    first_grad, text_hop = lax.optimization_barrier((first_grad, text_hop))
    text_mlp = text_ring.send(text_hop)
    input_grads = [None, None]
    input_grads[0], shift_one_grad, scale_one_grad = first_back(
        0, first_grad, normed_one, inverse_one, middle_grad
    )
    input_grads[1], text_shift_one_grad, text_scale_one_grad = first_back(
        1, text_first_grad, text_normed_one, text_inverse_one, text_middle_grad
    )
    outputs = [None, None]
    outputs[0], gate_two_grad = finish(0, middle, branch_two)
    outputs[1], text_gate_two_grad = finish(1, text_middle, text_branch_two)
    mod_grads = (
        jnp.stack(
            [
                shift_one_grad,
                scale_one_grad,
                gate_one_grad,
                shift_two_grad,
                scale_two_grad,
                gate_two_grad,
            ],
            axis=1,
        ),
        jnp.stack(
            [
                text_shift_one_grad,
                text_scale_one_grad,
                text_gate_one_grad,
                text_shift_two_grad,
                text_scale_two_grad,
                text_gate_two_grad,
            ],
            axis=1,
        ),
    )

    image_blocks = jnp.stack(
        [
            lax.dynamic_slice_in_dim(mod_grads[0], (tensor_rank ^ k) * width, width, 2)
            for k in range(size)
        ]
    )
    image_share = scatter_stack(image_blocks, size, "tensor")
    text_share = lax.dynamic_slice_in_dim(mod_grads[1], tensor_rank * width, width, 2)
    share_low = jnp.stack([image_share, text_share], axis=1).astype(BF16)
    share_all = gather_stack(share_low, group_count, "dp").reshape(all_slots, 2, 6, width)
    image_all = share_all[:, 0].reshape(all_slots, 6 * width)
    text_all = share_all[:, 1].reshape(all_slots, 6 * width)
    image_ada = dot(activated_own, image_all, 0, 0).reshape(share, 6, width)
    text_ada = dot(activated_own, text_all, 0, 0).reshape(share, 6, width)
    activated_part = dot(image_all, image_modulation.reshape(share, 6 * width), 1, 1) + dot(
        text_all, text_modulation.reshape(share, 6 * width), 1, 1
    )
    activated_part = sum_all(activated_part, size, "tensor").reshape(group_count, slots, share)
    activated_rows = gather_stack(activated_part, group_count, "dp")
    activated_rows = jnp.stack([activated_rows[k, k] for k in range(group_count)])
    activated_grad = jnp.concatenate(
        [
            lax.dynamic_index_in_dim(activated_rows, group_rank ^ k, 0, keepdims=False)
            for k in range(group_count)
        ],
        axis=1,
    )
    condition_gradient = jax.vjp(jax.nn.silu, cond_full)[1](activated_grad)[0]

    return (
        outputs[0],
        outputs[1],
        input_grads[0],
        input_grads[1],
        condition_gradient,
        image_ada,
        attention_sum[:, : 3 * width].reshape(share, 3, width),
        text_mlp[:, 2 * units :].T,
        image_mlp[:, units:],
        image_mlp[:, :units].T,
        text_ada,
        attention_sum[:, 3 * width : 6 * width].reshape(share, 3, width),
        attention_sum[:, 6 * width :].T,
        text_mlp[:, units : 2 * units],
        text_mlp[:, :units].T,
    )


def solution(mesh):
    image = P("dp", "tensor", None)
    text = P("dp", None, None)
    columns = P("dp", None, "tensor")
    rows = P("tensor", "dp")
    plain = P("dp", "tensor")
    weights = (columns, columns, rows, plain, rows)
    return jax.shard_map(
        functools.partial(on_device, mesh.shape["dp"], mesh.shape["tensor"]),
        mesh=mesh,
        in_specs=(image, text, P("dp", None), P("dp")) + weights + weights + (image, text),
        out_specs=(image, text, image, text, P("dp", None)) + weights + weights,
        check_vma=False,
    )
```
